32 devices in a mesh: ctx: 8 (over z, x), fsdp: 4 (over y, core).
Axes of the slice: x: 2, y: 2, z: 4, core: 2. Of those that a mesh axis runs over, the one named last changes fastest.
Arguments:
- layer_input: bfloat16 [2, 4, 1024, 1024], P(None, 'fsdp', 'ctx'), may hold values from -6 to 6
- segments: int32 [2, 4, 1024], P(None, 'fsdp', 'ctx'), may hold values from 0 to 15, never falling along the last dimension, each value on 1 to 512 neighbouring positions
- cotangent: bfloat16 [2, 4, 1024, 1024], P(None, 'fsdp', 'ctx'), may hold values from -6 to 6
- query_weight: bfloat16 [1024, 1024], P('fsdp'), may hold values from -0.1875 to 0.1875
- key_weight: bfloat16 [1024, 1024], P('fsdp'), may hold values from -0.1875 to 0.1875
- value_weight: bfloat16 [1024, 1024], P('fsdp'), may hold values from -0.1875 to 0.1875
- output_weight: bfloat16 [1024, 1024], P('fsdp'), may hold values from -0.75 to 0.75
- expand_weight: bfloat16 [1024, 4096], P('fsdp'), may hold values from -0.1875 to 0.1875
- contract_weight: bfloat16 [4096, 1024], P('fsdp'), may hold values from -0.09375 to 0.09375
- query_bias: bfloat16 [1024], P('fsdp'), may hold values from -3 to 3
- value_bias: bfloat16 [1024], P('fsdp'), may hold values from -3 to 3
- output_bias: bfloat16 [1024], P('fsdp'), may hold values from -3 to 3
- first_gain: bfloat16 [1024], P('fsdp'), may hold values from 0.099609375 to 1.8984375
- first_shift: bfloat16 [1024], P('fsdp'), may hold values from -3 to 3
- expand_bias: bfloat16 [4096], P('fsdp'), may hold values from -3 to 3
- contract_bias: bfloat16 [1024], P('fsdp'), may hold values from -3 to 3
- second_gain: bfloat16 [1024], P('fsdp'), may hold values from 0.099609375 to 1.8984375
- second_shift: bfloat16 [1024], P('fsdp'), may hold values from -3 to 3
Outputs:
- layer_output: bfloat16 [2, 4, 1024, 1024], P(None, 'fsdp', 'ctx')
- input_grad: float32 [2, 4, 1024, 1024], P(None, 'fsdp', 'ctx')
- query_weight_grad: float32 [1024, 1024], P('fsdp')
- key_weight_grad: float32 [1024, 1024], P('fsdp')
- value_weight_grad: float32 [1024, 1024], P('fsdp')
- output_weight_grad: float32 [1024, 1024], P('fsdp')
- expand_weight_grad: float32 [1024, 4096], P('fsdp')
- contract_weight_grad: float32 [4096, 1024], P('fsdp')
- query_bias_grad: float32 [1024], P('fsdp')
- value_bias_grad: float32 [1024], P('fsdp')
- output_bias_grad: float32 [1024], P('fsdp')
- first_gain_grad: float32 [1024], P('fsdp')
- first_shift_grad: float32 [1024], P('fsdp')
- expand_bias_grad: float32 [4096], P('fsdp')
- contract_bias_grad: float32 [1024], P('fsdp')
- second_gain_grad: float32 [1024], P('fsdp')
- second_shift_grad: float32 [1024], P('fsdp')
The draws below stay inside these ranges and needn't reach their ends.
Inputs may be any that keep to these rules, and one draw needn't show every extreme that they name: `segments`: in each sequence the ids never fall along the positions; each document holds 1 to 512 positions, and one holds exactly 512.
All inputs are finite; a program needn't handle non-finite values.
Results may differ from the reference program's by a relative error of at most 0.025.
Values may be sent and summed in bfloat16 or wider, within the bound.
A program may use at most 192 MiB of HBM per device.

```python
import math
import jax
import jax.numpy as jnp
import numpy as np
from jax import lax

D = 1024
HEADS = 16
HEAD_DIM = 64
FF = 4096
MB = 2
SEGS = 16
NSEQ = 4
SEQ_LEN = 1024
SEG_MOST = 512


def block_scale(own_key, extent, split, smallest, largest):
    loudness = 1.0
    for dim, blocks in split:
        heights = jax.random.uniform(jax.random.fold_in(jax.random.fold_in(own_key, 6), dim), (blocks,), jnp.float32, smallest / len(split), largest / len(split))
        loudness = loudness * jnp.repeat(jnp.exp(heights), extent[dim] // blocks).reshape((-1,) + (1,) * (len(extent) - 1 - dim))
    return loudness


def profile(number_of, total, limit, slope):
    weights = [(1 << 20) // math.isqrt(rank ** slope) + 1 for rank in range(2, number_of + 1)]
    rest, counts = total - limit - (number_of - 1), [1] * (number_of - 1)
    while rest > 0:
        free = [i for i in range(number_of - 1) if counts[i] < limit]
        mass, remaining = sum([weights[i] for i in free]), rest
        for i in free:
            extra = min(limit - counts[i], max(1, remaining * weights[i] // mass), rest)
            counts[i] = counts[i] + extra
            rest = rest - extra
    return np.array([limit] + counts)


def uneven_parts(key, number_of, total, most, slope):
    if number_of == 2:
        one = jax.random.randint(key, (), max(1, total - most), min(most, total - 1) + 1)
        return jnp.stack([one, total - one])
    lengths = jnp.asarray(profile(number_of, total, most, slope), jnp.int32)
    couples = (number_of - 1) // 2
    donor, taker = lengths[1:1 + 2 * couples:2], lengths[2:2 + 2 * couples:2]
    room = jnp.minimum(donor - 1, most - taker)
    moved = jax.random.randint(jax.random.fold_in(key, 1), (couples,), 0, 1 << 20) % (room + 1)
    lengths = lengths.at[1:1 + 2 * couples:2].set(donor - moved).at[2:2 + 2 * couples:2].set(taker + moved)
    return lengths[jax.random.permutation(jax.random.fold_in(key, 2), number_of)]


def normal_values(key, dims, deviation, reach, cuts=(), kind=jnp.bfloat16):
    factor_of = block_scale(key, dims, cuts, -0.22, 0.18) if cuts else 1.0
    drawn = jax.random.normal(key, dims, jnp.float32) * deviation * factor_of
    return jnp.minimum(jnp.maximum(drawn, -reach), reach).astype(kind)


def setup_inputs(seed: int = 0) -> dict:
    streams_of = jax.random.split(jax.random.key(seed), 19)
    return {
        "layer_input": normal_values(streams_of[0], (MB, NSEQ, SEQ_LEN, D), 1.0, 6.0, ((1, 4), (2, 8))),
        "segments": jax.vmap(lambda own: jnp.searchsorted(jnp.cumsum(uneven_parts(own, SEGS, SEQ_LEN, SEG_MOST, 2)), jnp.arange(SEQ_LEN), side="right"))(jax.random.split(streams_of[1], MB * NSEQ)).reshape((MB, NSEQ, SEQ_LEN)).astype(jnp.int32),
        "cotangent": normal_values(streams_of[2], (MB, NSEQ, SEQ_LEN, D), 1.0, 6.0, ((1, 4), (2, 8))),
        "query_weight": normal_values(streams_of[3], (D, D), D ** -0.5, 0.1875, ((0, 4),)),
        "key_weight": normal_values(streams_of[4], (D, D), D ** -0.5, 0.1875, ((0, 4),)),
        "value_weight": normal_values(streams_of[5], (D, D), D ** -0.5, 0.1875, ((0, 4),)),
        "output_weight": normal_values(streams_of[6], (D, D), (D // 16) ** -0.5, 0.75, ((0, 4),)),
        "expand_weight": normal_values(streams_of[7], (D, FF), D ** -0.5, 0.1875, ((0, 4),)),
        "contract_weight": normal_values(streams_of[8], (FF, D), FF ** -0.5, 0.09375, ((0, 4),)),
        "query_bias": normal_values(streams_of[9], (D,), 0.5, 3.0, ((0, 4),)),
        "value_bias": normal_values(streams_of[10], (D,), 0.5, 3.0, ((0, 4),)),
        "output_bias": normal_values(streams_of[11], (D,), 0.5, 3.0, ((0, 4),)),
        "first_gain": jnp.clip(1.0 + 0.18 * jax.random.normal(streams_of[12], (D,), jnp.float32), 0.099609375, 1.8984375).astype(jnp.bfloat16),
        "first_shift": normal_values(streams_of[13], (D,), 0.5, 3.0, ((0, 4),)),
        "expand_bias": normal_values(streams_of[14], (FF,), 0.5, 3.0, ((0, 4),)),
        "contract_bias": normal_values(streams_of[15], (D,), 0.5, 3.0, ((0, 4),)),
        "second_gain": jnp.clip(1.0 + 0.18 * jax.random.normal(streams_of[16], (D,), jnp.float32), 0.099609375, 1.8984375).astype(jnp.bfloat16),
        "second_shift": normal_values(streams_of[17], (D,), 0.5, 3.0, ((0, 4),)),
    }


@jax.custom_vjp
def low(v):
    return lax.optimization_barrier(v.astype(jnp.bfloat16)).astype(jnp.float32)

@jax.custom_vjp
def low_back(v):
    return v

def low_keep(v):
    return (low(v), None)

def low_pass(kept, grad):
    return (grad,)

def back_keep(v):
    return (v, None)

def back_low(kept, grad):
    return (low(grad),)
low.defvjp(low_keep, low_pass)
low_back.defvjp(back_keep, back_low)

def matmul(left_side, right_side):
    return jnp.dot(left_side, right_side, precision=lax.Precision.HIGHEST, preferred_element_type=jnp.float32)

def norm_rows(hidden, gain_row, offset_row):
    centre = hidden - lax.optimization_barrier(jnp.mean(hidden, axis=-1, keepdims=True))
    spread = lax.optimization_barrier(jnp.mean(centre * centre, axis=-1, keepdims=True))
    return centre * lax.rsqrt(spread + 1e-05) * gain_row + offset_row

def forward_one(inputs, params, seg_ids):
    query_weight, key_weight, value_weight, output_weight, expand_weight, contract_weight, query_bias, value_bias, output_bias, first_gain, first_shift, expand_bias, contract_bias, second_gain, second_shift = params
    length = inputs.shape[0]
    score_scale = HEAD_DIM ** (-0.5)
    rounded = low(inputs)
    queries = low(low_back(matmul(rounded, query_weight) + query_bias))
    keyed = low(low_back(matmul(rounded, key_weight)))
    valued = low(low_back(matmul(rounded, value_weight) + value_bias))
    key_heads = keyed.reshape(length, HEADS, HEAD_DIM)
    value_heads = valued.reshape(length, HEADS, HEAD_DIM)
    block_len = min(512, length)

    def attend(pair_in):
        query_block, seg_block = pair_in
        scores = jnp.einsum('rhd,khd->hrk', query_block, key_heads, precision=lax.Precision.HIGHEST) * score_scale
        scores = low_back(scores)
        same_doc = seg_block[:, None] == seg_ids[None, :]
        scores = jnp.where(same_doc[None], scores, -1e+30)
        softmaxed = low(jax.nn.softmax(scores, axis=-1))
        return jnp.einsum('hrk,khd->rhd', softmaxed, value_heads, precision=lax.Precision.HIGHEST)
    blocks = length // block_len
    context = lax.map(jax.checkpoint(attend), (queries.reshape(blocks, block_len, HEADS, HEAD_DIM), seg_ids.reshape(blocks, block_len)))
    context = low(low_back(context.reshape(length, HEADS * HEAD_DIM)))
    attn_out = low_back(matmul(context, output_weight) + output_bias)
    first_out = norm_rows(inputs + attn_out, first_gain, first_shift)
    hidden = low_back(matmul(low(first_out), expand_weight) + expand_bias)
    gelled = low(jax.nn.gelu(hidden, approximate=False))
    branch = low_back(matmul(gelled, contract_weight) + contract_bias)
    return norm_rows(first_out + branch, second_gain, second_shift)

def reference(layer_input, segments, cotangent, query_weight, key_weight, value_weight, output_weight, expand_weight, contract_weight, query_bias, value_bias, output_bias, first_gain, first_shift, expand_bias, contract_bias, second_gain, second_shift):
    params = tuple((weight.astype(jnp.float32) for weight in (query_weight, key_weight, value_weight, output_weight, expand_weight, contract_weight, query_bias, value_bias, output_bias, first_gain, first_shift, expand_bias, contract_bias, second_gain, second_shift)))
    seq_total = MB * NSEQ
    inputs = layer_input.astype(jnp.float32).reshape(seq_total, SEQ_LEN, D)
    seg_every = segments.reshape(seq_total, SEQ_LEN)
    cot_every = cotangent.astype(jnp.float32).reshape(seq_total, SEQ_LEN, D)

    def one_seq(running, seq_item):
        seq_in, seq_seg, seq_cot = seq_item
        result, pullback = jax.vjp(lambda values, weights: forward_one(values, weights, seq_seg), seq_in, params)
        grad_in, grad_params = pullback(seq_cot)
        running = jax.tree.map(lambda left_side, right_side: left_side + right_side, running, grad_params)
        return (running, (result.astype(jnp.bfloat16), grad_in))
    initial = tuple((jnp.zeros_like(weight) for weight in params))
    grad_sums, (results, grad_inputs) = lax.scan(one_seq, initial, (inputs, seg_every, cot_every))
    layer_output = results.reshape(MB, NSEQ, SEQ_LEN, D)
    input_grad = grad_inputs.reshape(MB, NSEQ, SEQ_LEN, D)
    return (layer_output, input_grad, grad_sums[0], grad_sums[1], grad_sums[2], grad_sums[3], grad_sums[4], grad_sums[5], grad_sums[6], grad_sums[7], grad_sums[8], grad_sums[9], grad_sums[10], grad_sums[11], grad_sums[12], grad_sums[13], grad_sums[14])
```

```python
import jax
import jax.numpy as jnp
from jax import lax
from jax.experimental import pallas as pl
from jax.experimental.pallas import tpu as pltpu
from jax.sharding import PartitionSpec as P

HEADS = 16
HEAD_DIM = 64


def as_sent(x):
    return jax.tree.map(lambda a: a.astype(jnp.bfloat16) if a.dtype == jnp.float32 else a, x)


def plain_dot(left_side, right_side):
    return jnp.dot(left_side, right_side, preferred_element_type=jnp.float32)


def left_dot(left_side, right_side):
    return lax.dot_general(
        left_side, right_side, (((0,), (0,)), ((), ())), preferred_element_type=jnp.float32
    )


def right_dot(left_side, right_side):
    return lax.dot_general(
        left_side, right_side, (((1,), (1,)), ((), ())), preferred_element_type=jnp.float32
    )


def norm_forward(hidden, gain_row, offset_row):
    centre = hidden - jnp.mean(hidden, axis=-1, keepdims=True)
    inverse = lax.rsqrt(jnp.mean(centre * centre, axis=-1, keepdims=True) + 1e-05)
    normed = centre * inverse
    return (normed * gain_row.astype(jnp.float32) + offset_row.astype(jnp.float32), normed, inverse)


def norm_backward(grad_out, normed, inverse, gain_row):
    scaled = grad_out * gain_row.astype(jnp.float32)
    grad_in = inverse * (
        scaled
        - jnp.mean(scaled, axis=-1, keepdims=True)
        - normed * jnp.mean(scaled * normed, axis=-1, keepdims=True)
    )
    return (grad_in, jnp.sum(grad_out * normed, axis=0), jnp.sum(grad_out, axis=0))


def gather_weights(shards):
    return (
        lax.all_gather(shards[0], "fsdp", axis=0, tiled=True),
        lax.all_gather(shards[1], "fsdp", axis=0, tiled=True),
        lax.all_gather(shards[2], "fsdp", axis=0, tiled=True),
        lax.all_gather(shards[3], "fsdp", axis=0, tiled=True),
        lax.all_gather(shards[4], "fsdp", axis=0, tiled=True),
        lax.all_gather(shards[5], "fsdp", axis=0, tiled=True),
        lax.all_gather(shards[6], "fsdp", axis=0, tiled=True),
        lax.all_gather(shards[7], "fsdp", axis=0, tiled=True),
        lax.all_gather(shards[8], "fsdp", axis=0, tiled=True),
        lax.all_gather(shards[9], "fsdp", axis=0, tiled=True),
        lax.all_gather(shards[10], "fsdp", axis=0, tiled=True),
        lax.all_gather(shards[11], "fsdp", axis=0, tiled=True),
        lax.all_gather(shards[12], "fsdp", axis=0, tiled=True),
        lax.all_gather(shards[13], "fsdp", axis=0, tiled=True),
        lax.all_gather(shards[14], "fsdp", axis=0, tiled=True),
    )


def attend_forward(query_bf, key_bf, value_bf, seg_local):
    row_count = query_bf.shape[0]
    score_scale = HEAD_DIM ** (-0.5)
    query_heads = query_bf.reshape(row_count, HEADS, HEAD_DIM)
    run_max = jnp.full((HEADS, row_count), -1e30, jnp.float32)
    key_rows = lax.all_gather(key_bf, "ctx", axis=0, tiled=True)
    value_rows = lax.all_gather(value_bf, "ctx", axis=0, tiled=True)
    key_seg = lax.all_gather(seg_local, "ctx", axis=0, tiled=True)
    piece_rows = key_rows.shape[0]
    key_heads = key_rows.reshape(piece_rows, HEADS, HEAD_DIM)
    value_heads = value_rows.reshape(piece_rows, HEADS, HEAD_DIM)
    scores = (
        jnp.einsum("rhd,khd->hrk", query_heads, key_heads, preferred_element_type=jnp.float32)
        * score_scale
    )
    same_doc = seg_local[:, None] == key_seg[None, :]
    scores = jnp.where(same_doc[None], scores, -1e30)
    new_max = jnp.maximum(run_max, jnp.max(scores, axis=-1))
    numerators = jnp.exp(scores - new_max[..., None])
    run_sum = jnp.sum(numerators, axis=-1)
    accumulated = jnp.einsum(
        "hrk,khd->hrd",
        numerators.astype(jnp.bfloat16),
        value_heads,
        preferred_element_type=jnp.float32,
    )
    run_max, run_sum, accumulated = (new_max, run_sum, accumulated)
    context = jnp.transpose(accumulated / run_sum[..., None], (1, 0, 2)).reshape(
        row_count, HEADS * HEAD_DIM
    )
    return (context, run_max + jnp.log(run_sum))


def block_grads(
    query_heads, grad_heads, query_seg, log_sum, row_delta, key_heads, value_heads, key_seg
):
    score_scale = HEAD_DIM ** (-0.5)
    scores = (
        jnp.einsum("rhd,khd->hrk", query_heads, key_heads, preferred_element_type=jnp.float32)
        * score_scale
    )
    same_doc = query_seg[:, None] == key_seg[None, :]
    scores = jnp.where(same_doc[None], scores, -1e30)
    probs_full = jnp.exp(scores - log_sum[..., None])
    grad_probs = jnp.einsum(
        "rhd,khd->hrk", grad_heads, value_heads, preferred_element_type=jnp.float32
    )
    grad_scores = (probs_full * (grad_probs - row_delta[..., None])).astype(jnp.bfloat16)
    return (probs_full, grad_scores)


def attend_backward(query_bf, key_bf, value_bf, seg_local, context, log_sum, grad_context):
    row_count = query_bf.shape[0]
    score_scale = HEAD_DIM ** (-0.5)
    key_every, value_every, seg_every = (
        lax.all_gather(key_bf, "ctx", axis=0, tiled=True),
        lax.all_gather(value_bf, "ctx", axis=0, tiled=True),
        lax.all_gather(seg_local, "ctx", axis=0, tiled=True),
    )
    length = key_every.shape[0]
    block_len = min(512, length)
    query_heads = query_bf.reshape(row_count, HEADS, HEAD_DIM)
    grad_heads = grad_context.reshape(row_count, HEADS, HEAD_DIM)
    row_delta = jnp.sum(
        (grad_context.astype(jnp.float32) * context).reshape(row_count, HEADS, HEAD_DIM), axis=-1
    ).T

    def visit_block(grad_query, block_num):
        first_row = block_num * block_len
        key_heads = lax.dynamic_slice_in_dim(key_every, first_row, block_len, 0).reshape(
            block_len, HEADS, HEAD_DIM
        )
        value_heads = lax.dynamic_slice_in_dim(value_every, first_row, block_len, 0).reshape(
            block_len, HEADS, HEAD_DIM
        )
        key_seg = lax.dynamic_slice_in_dim(seg_every, first_row, block_len, 0)
        probs_full, grad_scores = block_grads(
            query_heads, grad_heads, seg_local, log_sum, row_delta, key_heads, value_heads, key_seg
        )
        grad_query = (
            grad_query
            + jnp.einsum("hrk,khd->rhd", grad_scores, key_heads, preferred_element_type=jnp.float32)
            * score_scale
        )
        grad_keys = (
            jnp.einsum("hrk,rhd->khd", grad_scores, query_heads, preferred_element_type=jnp.float32)
            * score_scale
        )
        grad_values = jnp.einsum(
            "hrk,rhd->khd",
            probs_full.astype(jnp.bfloat16),
            grad_heads,
            preferred_element_type=jnp.float32,
        )
        stacked = jnp.stack(
            (
                grad_keys.reshape(block_len, HEADS * HEAD_DIM),
                grad_values.reshape(block_len, HEADS * HEAD_DIM),
            ),
            axis=1,
        )
        return (grad_query, stacked)

    grad_query, pieces = lax.scan(
        visit_block,
        jnp.zeros((row_count, HEADS, HEAD_DIM), jnp.float32),
        jnp.arange(length // block_len),
    )
    key_terms = pieces.reshape(length, 2, HEADS * HEAD_DIM)
    own_rows = lax.psum_scatter(
        key_terms.astype(jnp.bfloat16), "ctx", scatter_dimension=0, tiled=True
    ).astype(jnp.float32)
    grad_keyed = own_rows[:, 0].astype(jnp.bfloat16)
    grad_valued = own_rows[:, 1].astype(jnp.bfloat16)
    grad_queries = grad_query.reshape(row_count, HEADS * HEAD_DIM).astype(jnp.bfloat16)
    return (grad_queries, grad_keyed, grad_valued)


def layer_forward(inputs, seg_local, full_weights):
    (
        query_weight,
        key_weight,
        value_weight,
        output_weight,
        expand_weight,
        contract_weight,
        query_bias,
        value_bias,
        output_bias,
        first_gain,
        first_shift,
        expand_bias,
        contract_bias,
        second_gain,
        second_shift,
    ) = full_weights
    query_bf = (plain_dot(inputs, query_weight) + query_bias.astype(jnp.float32)).astype(
        jnp.bfloat16
    )
    key_bf = plain_dot(inputs, key_weight).astype(jnp.bfloat16)
    value_bf = (plain_dot(inputs, value_weight) + value_bias.astype(jnp.float32)).astype(
        jnp.bfloat16
    )
    context, log_sum = attend_forward(query_bf, key_bf, value_bf, seg_local)
    context_bf = context.astype(jnp.bfloat16)
    first_sum = (
        inputs.astype(jnp.float32)
        + plain_dot(context_bf, output_weight)
        + output_bias.astype(jnp.float32)
    )
    first_out, normed_one, inverse_one = norm_forward(first_sum, first_gain, first_shift)
    first_bf = first_out.astype(jnp.bfloat16)
    hidden = plain_dot(first_bf, expand_weight) + expand_bias.astype(jnp.float32)
    gelled_bf = jax.nn.gelu(hidden, approximate=False).astype(jnp.bfloat16)
    second_sum = (
        first_out + plain_dot(gelled_bf, contract_weight) + contract_bias.astype(jnp.float32)
    )
    result, normed_two, inverse_two = norm_forward(second_sum, second_gain, second_shift)
    kept_state = (
        query_bf,
        key_bf,
        value_bf,
        context,
        log_sum,
        context_bf,
        normed_one,
        inverse_one,
        first_bf,
        hidden,
        gelled_bf,
        normed_two,
        inverse_two,
    )
    return (result.astype(jnp.bfloat16), kept_state)


def layer_backward(inputs, seg_local, grad_out, kept_state, full_weights):
    (
        query_weight,
        key_weight,
        value_weight,
        output_weight,
        expand_weight,
        contract_weight,
        query_bias,
        value_bias,
        output_bias,
        first_gain,
        first_shift,
        expand_bias,
        contract_bias,
        second_gain,
        second_shift,
    ) = full_weights
    (
        query_bf,
        key_bf,
        value_bf,
        context,
        log_sum,
        context_bf,
        normed_one,
        inverse_one,
        first_bf,
        hidden,
        gelled_bf,
        normed_two,
        inverse_two,
    ) = kept_state
    grad_second, second_gain_grad, second_shift_grad = norm_backward(
        grad_out.astype(jnp.float32), normed_two, inverse_two, second_gain
    )
    grad_branch = grad_second.astype(jnp.bfloat16)
    contract_weight_grad = left_dot(gelled_bf, grad_branch)
    contract_bias_grad = jnp.sum(grad_branch.astype(jnp.float32), axis=0)
    grad_gelled = right_dot(grad_branch, contract_weight)
    gelu_pull = jax.vjp(lambda values: jax.nn.gelu(values, approximate=False), hidden)[1]
    grad_hidden = gelu_pull(grad_gelled)[0].astype(jnp.bfloat16)
    expand_weight_grad = left_dot(first_bf, grad_hidden)
    expand_bias_grad = jnp.sum(grad_hidden.astype(jnp.float32), axis=0)
    grad_first = grad_second + right_dot(grad_hidden, expand_weight)
    grad_attn, first_gain_grad, first_shift_grad = norm_backward(
        grad_first, normed_one, inverse_one, first_gain
    )
    grad_attn_low = grad_attn.astype(jnp.bfloat16)
    output_weight_grad = left_dot(context_bf, grad_attn_low)
    output_bias_grad = jnp.sum(grad_attn_low.astype(jnp.float32), axis=0)
    grad_context = right_dot(grad_attn_low, output_weight).astype(jnp.bfloat16)
    grad_queries, grad_keyed, grad_valued = attend_backward(
        query_bf, key_bf, value_bf, seg_local, context, log_sum, grad_context
    )
    query_weight_grad = left_dot(inputs, grad_queries)
    key_weight_grad = left_dot(inputs, grad_keyed)
    value_weight_grad = left_dot(inputs, grad_valued)
    query_bias_grad = jnp.sum(grad_queries.astype(jnp.float32), axis=0)
    value_bias_grad = jnp.sum(grad_valued.astype(jnp.float32), axis=0)
    grad_input = (
        grad_attn
        + right_dot(grad_queries, query_weight)
        + right_dot(grad_keyed, key_weight)
        + right_dot(grad_valued, value_weight)
    )
    grad_terms = (
        query_weight_grad,
        key_weight_grad,
        value_weight_grad,
        output_weight_grad,
        expand_weight_grad,
        contract_weight_grad,
        query_bias_grad,
        value_bias_grad,
        output_bias_grad,
        first_gain_grad,
        first_shift_grad,
        expand_bias_grad,
        contract_bias_grad,
        second_gain_grad,
        second_shift_grad,
    )
    return (grad_input, grad_terms)


def per_device(
    layer_input,
    segments,
    cotangent,
    query_weight,
    key_weight,
    value_weight,
    output_weight,
    expand_weight,
    contract_weight,
    query_bias,
    value_bias,
    output_bias,
    first_gain,
    first_shift,
    expand_bias,
    contract_bias,
    second_gain,
    second_shift,
):
    shards = (
        query_weight,
        key_weight,
        value_weight,
        output_weight,
        expand_weight,
        contract_weight,
        query_bias,
        value_bias,
        output_bias,
        first_gain,
        first_shift,
        expand_bias,
        contract_bias,
        second_gain,
        second_shift,
    )
    micro_count = layer_input.shape[0]
    results = []
    grad_inputs = []
    totals = None
    for micro_step in range(micro_count):
        inputs = layer_input[micro_step, 0]
        seg_local = segments[micro_step, 0].astype(jnp.bfloat16)
        front_weights = gather_weights(shards)
        result, kept_state = layer_forward(inputs, seg_local, front_weights)
        behind = gather_weights(shards)
        grad_input, grad_terms = layer_backward(
            inputs, seg_local, cotangent[micro_step, 0], kept_state, behind
        )
        results.append(result)
        grad_inputs.append(grad_input)
        if totals is None:
            totals = grad_terms
        else:
            totals = tuple(
                (left_side + right_side for left_side, right_side in zip(totals, grad_terms))
            )
    reduced = jax.tree.map(
        lambda part: part.astype(jnp.float32),
        lax.psum_scatter(as_sent(totals), "fsdp", scatter_dimension=0, tiled=True),
    )
    summed = jax.tree.map(lambda part: part.astype(jnp.float32), lax.psum(as_sent(reduced), "ctx"))
    layer_output = jnp.stack(results, axis=0)[:, None]
    input_grad = jnp.stack(grad_inputs, axis=0)[:, None]
    return (
        layer_output,
        input_grad,
        summed[0],
        summed[1],
        summed[2],
        summed[3],
        summed[4],
        summed[5],
        summed[6],
        summed[7],
        summed[8],
        summed[9],
        summed[10],
        summed[11],
        summed[12],
        summed[13],
        summed[14],
    )


MESH = pl.DeviceIdType.MESH
BF = jnp.bfloat16
F32 = jnp.float32
CHUNKS = 24
SLOTS = 3


def coords():
    c, f = lax.axis_index("ctx"), lax.axis_index("fsdp")
    return c // 2, c % 2, f // 2, f % 2


def dev(z, x, y, k):
    return (z * 2 + x, y * 2 + k)


def greet(z, x, y, k):
    barrier = pltpu.get_barrier_semaphore()
    for step in range(1, 8):
        place = (z * 2 + k + step) % 8
        pl.semaphore_signal(
            barrier, inc=1, device_id=dev(place // 2, x, y, place % 2), device_id_type=MESH
        )
    pl.semaphore_signal(barrier, inc=1, device_id=dev(z, 1 - x, y, k), device_id_type=MESH)
    pl.semaphore_signal(barrier, inc=1, device_id=dev(z, x, 1 - y, k), device_id_type=MESH)
    pl.semaphore_wait(barrier, 9)


def remote(src, dst, send, recv, to):
    return pltpu.make_async_remote_copy(
        src_ref=src, dst_ref=dst, send_sem=send, recv_sem=recv, device_id=to, device_id_type=MESH
    )


def rows_of(start, size, unit=16):
    return pl.ds(pl.multiple_of(start, unit), size)


def gather_kernel(
    inp, cot, seg, wq, wk, wv, wo, we, wc, vec,
    xf, cotf, segf, fq, fk, fv, fo, fe, fc, vecf,
    a_send, a_recv, g_send, g_recv, w_send, w_recv, v_send, v_recv,
):
    z, x, y, k = coords()
    f = y * 2 + k
    other = (1 - y) * 2 + k
    sib, xn, yn = dev(z, x, y, 1 - k), dev(z, 1 - x, y, k), dev(z, x, 1 - y, k)
    zn = dev(z + 1 - 2 * (z % 2), x, y, k)
    color = (z % 2) * 2 + x
    c_x, c_z, c_o = color + 1 - 2 * x, (color + 2) % 4, 3 - color
    greet(z, x, y, k)

    def block_moves(mb):
        to_z, to_k = mb * 2 + k, z // 2
        row = x * 512 + z * 128
        slot = z % 2
        mine = (to_z == z) & (to_k == k)
        moves = (
            (inp.at[mb, 0], xf.at[rows_of(row, 128)], 0),
            (seg.at[mb], segf.at[x * 4 + z], 1),
            (cot.at[mb, 0], cotf.at[rows_of(slot * 128, 128)], 2),
        )
        return mine, dev(to_z, x, y, to_k), slot, moves

    def start_blocks(which):
        for mb in range(2):
            mine, to, slot, moves = block_moves(mb)
            for src, dst, n in moves:
                if n not in which:
                    continue

                @pl.when(mine)
                def _():
                    pltpu.make_async_copy(src, dst, a_recv.at[n, slot]).start()

                @pl.when(jnp.logical_not(mine))
                def _():
                    remote(src, dst, a_send.at[n, mb], a_recv.at[n, slot], to).start()

    def finish_blocks(which):
        for mb in range(2):
            mine, to, slot, moves = block_moves(mb)
            for src, dst, n in moves:
                if n not in which:
                    continue

                @pl.when(jnp.logical_not(mine))
                def _():
                    remote(src, dst, a_send.at[n, mb], a_recv.at[n, slot], to).wait_send()

    def arrive_blocks(which):
        for slot in range(2):
            zz = 2 * k + slot
            for n in which:
                if n == 0:
                    dst = xf.at[rows_of(x * 512 + zz * 128, 128)]
                elif n == 1:
                    dst = segf.at[x * 4 + zz]
                else:
                    dst = cotf.at[pl.ds(slot * 128, 128)]
                pltpu.make_async_copy(dst, dst, a_recv.at[n, slot]).wait()

    def group_copy(step):
        who = x if step < 2 else 1 - x
        src = xf.at[rows_of(who * 512 + k * 256, 256)]
        sseg = segf.at[pl.ds(who * 4 + k * 2, 2)]
        to = (sib, xn, sib)[step]
        return (
            remote(src, src, g_send.at[0, step], g_recv.at[0, step], to),
            remote(sseg, sseg, g_send.at[1, step], g_recv.at[1, step], to),
        )

    def group_arrive(step):
        who = (x, 1 - x, 1 - x)[step]
        kk = (1 - k, k, 1 - k)[step]
        src = xf.at[rows_of(who * 512 + kk * 256, 256)]
        sseg = segf.at[pl.ds(who * 4 + kk * 2, 2)]
        pltpu.make_async_copy(src, src, g_recv.at[0, step]).wait()
        pltpu.make_async_copy(sseg, sseg, g_recv.at[1, step]).wait()

    items = []
    for shard, full in ((wq, fq), (wk, fk), (wv, fv), (wo, fo)):
        items.append((shard, full, 0, 0, 256))
    for j in range(4):
        items.append((we, fe, 0, j * 1024, 256))
    for j in range(4):
        items.append((wc, fc, j * 256, 0, 1024))
    n_items = len(items)

    def part(i, quarter, start, size, own_src=False):
        shard, full, row, col, step = items[i]
        if own_src:
            return shard.at[rows_of(row + start, size), pl.ds(col, 1024)]
        return full.at[rows_of(quarter * step + row + start, size), pl.ds(col, 1024)]

    def send_copy(i, kind):
        sems = (w_send.at[kind, i], w_recv.at[kind, i])
        if kind == 0:
            return remote(part(i, f, color * 64, 64, True), part(i, f, color * 64, 64), *sems, yn)
        if kind == 1:
            return remote(part(i, f, c_o * 64, 32, True), part(i, f, c_o * 64, 32), *sems, yn)
        if kind == 2:
            src = part(i, other, color * 64, 64)
            return remote(src, src, *sems, xn)
        if kind == 3:
            src = part(i, other, c_z * 64 + 32, 16)
            return remote(src, src, *sems, xn)
        if kind == 4:
            src = part(i, other, color * 64, 64)
            return remote(src, src, *sems, zn)
        if kind == 5:
            src = part(i, other, c_x * 64 + 48, 16)
            return remote(src, src, *sems, zn)
        if kind == 6:
            return remote(part(i, f, 0, 256, True), part(i, f, 0, 256), *sems, sib)
        src = part(i, other, 0, 256)
        return remote(src, src, *sems, sib)

    def arrive(i, kind):
        if kind == 0:
            dst = part(i, other, color * 64, 64)
        elif kind == 1:
            dst = part(i, other, c_o * 64, 32)
        elif kind == 2:
            dst = part(i, other, c_x * 64, 64)
        elif kind == 3:
            dst = part(i, other, c_o * 64 + 32, 16)
        elif kind == 4:
            dst = part(i, other, c_z * 64, 64)
        elif kind == 5:
            dst = part(i, other, c_o * 64 + 48, 16)
        elif kind == 6:
            dst = part(i, y * 2 + 1 - k, 0, 256)
        else:
            dst = part(i, (1 - y) * 2 + 1 - k, 0, 256)
        pltpu.make_async_copy(dst, dst, w_recv.at[kind, i]).wait()

    def own_copy(i):
        return pltpu.make_async_copy(
            part(i, f, 0, 256, True), part(i, f, 0, 256), w_recv.at[8, i]
        )

    vec_copies = (
        remote(vec, vecf.at[f], v_send.at[0], v_recv.at[0], yn),
        remote(vec, vecf.at[f], v_send.at[1], v_recv.at[1], sib),
        remote(vecf.at[other], vecf.at[other], v_send.at[2], v_recv.at[2], sib),
    )
    vec_own = pltpu.make_async_copy(vec, vecf.at[f], v_recv.at[3])

    start_blocks((0, 1))
    vec_own.start()
    vec_copies[0].start()
    vec_copies[1].start()
    for t in range(n_items + 3):
        if t < n_items:
            send_copy(t, 0).start()
            send_copy(t, 1).start()
            send_copy(t, 6).start()
            own_copy(t).start()
        if t == 1:
            arrive_blocks((0, 1))
            for step in range(2):
                for move in group_copy(step):
                    move.start()
            pltpu.make_async_copy(vecf.at[other], vecf.at[other], v_recv.at[0]).wait()
            vec_copies[2].start()
        if t == 4:
            group_arrive(1)
            for move in group_copy(2):
                move.start()
            start_blocks((2,))
        if 1 <= t <= n_items:
            i = t - 1
            arrive(i, 0)
            send_copy(i, 2).start()
            send_copy(i, 4).start()
        if 2 <= t <= n_items + 1:
            i = t - 2
            arrive(i, 4)
            send_copy(i, 3).start()
            arrive(i, 2)
            send_copy(i, 5).start()
        if 3 <= t:
            i = t - 3
            arrive(i, 1)
            arrive(i, 3)
            arrive(i, 5)
            send_copy(i, 7).start()
    for i in range(n_items):
        arrive(i, 6)
        arrive(i, 7)
        own_copy(i).wait()
        for kind in range(8):
            send_copy(i, kind).wait_send()
    arrive_blocks((2,))
    finish_blocks((0, 1, 2))
    group_arrive(0)
    group_arrive(2)
    for step in range(3):
        for move in group_copy(step):
            move.wait_send()
    sib_own, sib_other = vecf.at[y * 2 + 1 - k], vecf.at[(1 - y) * 2 + 1 - k]
    pltpu.make_async_copy(sib_own, sib_own, v_recv.at[1]).wait()
    pltpu.make_async_copy(sib_other, sib_other, v_recv.at[2]).wait()
    for move in vec_copies:
        move.wait_send()
    vec_own.wait()


def gather_call(inp, cot, seg, weights, vec):
    any_spec = pl.BlockSpec(memory_space=pl.ANY)
    outs = [
        jax.ShapeDtypeStruct((1024, 1024), BF),
        jax.ShapeDtypeStruct((256, 1024), BF),
        jax.ShapeDtypeStruct((8, 1, 128), jnp.int32),
    ]
    outs += [jax.ShapeDtypeStruct((1024, 1024), BF)] * 4
    outs += [
        jax.ShapeDtypeStruct((1024, 4096), BF),
        jax.ShapeDtypeStruct((4096, 1024), BF),
        jax.ShapeDtypeStruct((4, 32, 128), BF),
    ]
    dma = pltpu.SemaphoreType.DMA
    return pl.pallas_call(
        gather_kernel,
        out_shape=outs,
        in_specs=[any_spec] * 10,
        out_specs=[any_spec] * 10,
        scratch_shapes=[
            dma((3, 2)), dma((3, 2)), dma((2, 3)), dma((2, 3)),
            dma((8, 12)), dma((9, 12)), dma((3,)), dma((4,)),
        ],
        compiler_params=pltpu.CompilerParams(collective_id=0, has_side_effects=True),
        name="gather_all",
    )(inp, cot, seg, *weights, vec)


def two_heads(block):
    lane = lax.broadcasted_iota(jnp.int32, block.shape, 1)
    zero = jnp.zeros_like(block)
    return jnp.concatenate(
        [jnp.where(lane < HEAD_DIM, block, zero), jnp.where(lane >= HEAD_DIM, block, zero)], axis=0
    )


def one_block(pair):
    rows = pair.shape[0] // 2
    lane = lax.broadcasted_iota(jnp.int32, (rows, pair.shape[1]), 1)
    return jnp.where(lane < HEAD_DIM, pair[:rows], pair[rows:])


def softmax_pair(q_ref, k_ref, same_ref):
    queries = two_heads(q_ref[...] * BF(HEAD_DIM**-0.5))
    scores = right_dot(queries, k_ref[...])
    same = same_ref[...]
    scores = jnp.where(jnp.concatenate([same, same], axis=0) > 0, scores, -1e30)
    numer = jnp.exp(scores - jnp.max(scores, axis=-1, keepdims=True))
    return queries, numer * (1.0 / jnp.sum(numer, axis=-1, keepdims=True))


def attend_kernel(q_ref, k_ref, v_ref, sq_ref, sk_ref, o_ref, same_ref):
    @pl.when(pl.program_id(0) == 0)
    def _():
        same_ref[...] = (sq_ref[...] == sk_ref[...]).astype(F32)

    probs = softmax_pair(q_ref, k_ref, same_ref)[1]
    o_ref[...] = one_block(plain_dot(probs.astype(BF), v_ref[...])).astype(BF)


def attend_back_kernel(
    q_ref, k_ref, v_ref, g_ref, sq_ref, sk_ref, dq_ref, dk_ref, dv_ref, same_ref
):
    @pl.when(pl.program_id(0) == 0)
    def _():
        same_ref[...] = (sq_ref[...] == sk_ref[...]).astype(F32)

    queries, probs = softmax_pair(q_ref, k_ref, same_ref)
    grads = two_heads(g_ref[...])
    grad_probs = right_dot(grads, v_ref[...])
    delta = jnp.sum(probs * grad_probs, axis=-1, keepdims=True)
    grad_scores = (probs * (grad_probs - delta)).astype(BF)
    dv_ref[...] = left_dot(probs.astype(BF), grads).astype(BF)
    dk_ref[...] = left_dot(grad_scores, queries).astype(BF)
    dq = one_block(plain_dot(grad_scores, k_ref[...]))
    dq_ref[...] = (dq * HEAD_DIM**-0.5).astype(BF)


def attention_specs():
    rows = pl.BlockSpec((256, 128), lambda h: (0, h))
    full = pl.BlockSpec((1024, 128), lambda h: (0, h))
    sq = pl.BlockSpec((256, 1), lambda h: (0, 0))
    sk = pl.BlockSpec((1, 1024), lambda h: (0, 0))
    return rows, full, sq, sk


def attend(q, k, v, sq, sk):
    rows, full, sqs, sks = attention_specs()
    return pl.pallas_call(
        attend_kernel,
        grid=(8,),
        out_shape=jax.ShapeDtypeStruct((256, 1024), BF),
        in_specs=[rows, full, full, sqs, sks],
        out_specs=rows,
        scratch_shapes=[pltpu.VMEM((256, 1024), F32)],
        compiler_params=pltpu.CompilerParams(vmem_limit_bytes=40 << 20),
        name="attend",
    )(q, k, v, sq, sk)


def attend_back(q, k, v, g, sq, sk):
    rows, full, sqs, sks = attention_specs()
    return pl.pallas_call(
        attend_back_kernel,
        grid=(8,),
        out_shape=[
            jax.ShapeDtypeStruct((256, 1024), BF),
            jax.ShapeDtypeStruct((1024, 1024), BF),
            jax.ShapeDtypeStruct((1024, 1024), BF),
        ],
        in_specs=[rows, full, full, rows, sqs, sks],
        out_specs=[rows, full, full],
        scratch_shapes=[pltpu.VMEM((256, 1024), F32)],
        compiler_params=pltpu.CompilerParams(vmem_limit_bytes=40 << 20),
        name="attend_back",
    )(q, k, v, g, sq, sk)


def reduce_kernel(
    gel, gb, fb, gh, ctx, gal, xo, dq, xf, dk, dv, dxo, dxp, res,
    out, resf, dxf,
    s_d, l_d, r_d, b_y, r_y, b_x, r_x, b_1, r_1, b_2, r_2,
    dx_r, dx_s, dx_y, dx_b,
    ss, rs, ds, dr, a_send, a_recv,
):
    z, x, y, k = coords()
    sib, xn, yn = dev(z, x, y, 1 - k), dev(z, 1 - x, y, k), dev(z, x, 1 - y, k)
    bit1, bit2 = z % 2, z // 2
    z1 = dev(z + 1 - 2 * bit1, x, y, k)
    z2 = dev((z + 2) % 4, x, y, k)
    greet(z, x, y, k)

    def back(n, slot):
        to_z = 2 * k + slot
        to_k = z % 2
        mb = z // 2
        mine = (to_z == z) & (to_k == k)
        src = (res, dx_b)[n].at[pl.ds(slot * 128, 128)]
        dst = (resf, dxf)[n].at[mb, 0]

        def far():
            return remote(
                src, dst, a_send.at[n, slot], a_recv.at[n, mb], dev(to_z, x, y, to_k)
            )

        def near():
            return pltpu.make_async_copy(src, dst, a_recv.at[n, mb])

        return mine, far, near

    def start_back(n):
        for slot in range(2):
            mine, far, near = back(n, slot)

            @pl.when(mine)
            def _():
                near().start()

            @pl.when(jnp.logical_not(mine))
            def _():
                far().start()

    def finish_back(n):
        for slot in range(2):
            mine, far, _ = back(n, slot)

            @pl.when(jnp.logical_not(mine))
            def _():
                far().wait_send()

        for mb in range(2):
            dst = (resf, dxf)[n].at[mb, 0]
            pltpu.make_async_copy(dst, dst, a_recv.at[n, mb]).wait()

    start_back(0)

    def dx_core(g):
        who = x if g == 0 else 1 - x
        src = dxp.at[rows_of(who * 512 + (1 - k) * 256, 256)]
        return remote(src, dx_r.at[g], ds.at[g], dr.at[g], sib)

    dx_far = remote(dx_s, dx_y, ds.at[2], dr.at[2], xn)
    dx_core(1).start()
    dx_core(0).start()

    def send(stage, i, src, dst, to):
        return remote(src, dst, ss.at[stage, i % SLOTS], rs.at[stage, i], to)

    def landed(stage, i, dst):
        pltpu.make_async_copy(dst, dst, rs.at[stage, i]).wait()

    def copies(stage, i):
        slot = i % SLOTS
        if stage == 0:
            return send(0, i, s_d.at[slot], r_d.at[i], sib)
        if stage == 1:
            return send(1, i, b_y.at[slot, 1 - y], r_y.at[i], yn)
        if stage == 2:
            return send(2, i, b_x.at[slot, rows_of((1 - x) * 64, 64)], r_x.at[i], xn)
        if stage == 3:
            return send(3, i, b_1.at[slot, rows_of((1 - bit1) * 32, 32)], r_1.at[i], z1)
        if stage == 4:
            return send(4, i, b_2.at[slot, rows_of((1 - bit2) * 16, 16)], r_2.at[i], z2)
        if stage == 5:
            own = out.at[i, rows_of(x * 64 + bit1 * 32 + bit2 * 16, 16)]
            return send(5, i, own, own, z2)
        if stage == 6:
            own = out.at[i, rows_of(x * 64 + bit1 * 32, 32)]
            return send(6, i, own, own, z1)
        own = out.at[i, rows_of(x * 64, 64)]
        return send(7, i, own, own, xn)

    def launch(stage, i):
        copies(stage, i).start()

    def clear(stage, i):
        @pl.when(i >= SLOTS)
        def _():
            copies(stage, i - SLOTS).wait_send()

    def add(a, b):
        return (a.astype(F32) + b.astype(F32)).astype(BF)

    def terms(i, a_ref, b_ref, a_base, a_step, b_col):
        slot = i % SLOTS
        right = b_ref[:, b_col]
        for plane in range(2):
            for core in range(2):
                quarter = plane * 2 + (k if core == 0 else 1 - k)
                left = a_ref[:, pl.ds(pl.multiple_of(a_base + quarter * a_step, 128), 128)]
                product = left_dot(left, right).astype(BF)
                if core == 0:
                    l_d[slot, plane] = product
                else:
                    s_d[slot, plane] = product

    every = pl.ds(0, 1024)

    def tick(t, carry):
        def at(stage):
            i = t - stage
            return i, (i >= 0) & (i < CHUNKS)

        i0, live0 = at(0)

        @pl.when(live0)
        def _():
            clear(0, i0)

        @pl.when(i0 < 8)
        def _():
            terms(i0, gel, gb, i0 * 128, 1024, every)

        @pl.when((i0 >= 8) & (i0 < 16))
        def _():
            j = i0 - 8
            terms(i0, fb, gh, (j % 2) * 128, 256, rows_of((j // 2) * 1024, 1024, 1024))

        @pl.when((i0 >= 16) & (i0 < 18))
        def _():
            terms(i0, ctx, gal, (i0 - 16) * 128, 256, every)

        @pl.when((i0 >= 18) & (i0 < 20))
        def _():
            terms(i0, xo, dq, (i0 - 18) * 128, 256, every)

        @pl.when((i0 >= 20) & (i0 < 22))
        def _():
            terms(i0, xf, dk, (i0 - 20) * 128, 256, every)

        @pl.when((i0 >= 22) & (i0 < 24))
        def _():
            terms(i0, xf, dv, (i0 - 22) * 128, 256, every)

        @pl.when(live0)
        def _():
            launch(0, i0)

        i1, live1 = at(1)

        @pl.when(live1)
        def _():
            slot = i1 % SLOTS
            clear(1, i1)
            landed(0, i1, r_d.at[i1])
            for plane in range(2):
                b_y[slot, plane] = add(l_d[slot, plane], r_d[i1, plane])
            launch(1, i1)

        i2, live2 = at(2)

        @pl.when(live2)
        def _():
            slot = i2 % SLOTS
            clear(2, i2)
            landed(1, i2, r_y.at[i2])
            b_x[slot] = add(b_y[slot, y], r_y[i2])
            launch(2, i2)

        i3, live3 = at(3)

        @pl.when(live3)
        def _():
            slot = i3 % SLOTS
            clear(3, i3)
            landed(2, i3, r_x.at[i3])
            b_1[slot] = add(b_x[slot, rows_of(x * 64, 64)], r_x[i3])
            launch(3, i3)

        i4, live4 = at(4)

        @pl.when(live4)
        def _():
            slot = i4 % SLOTS
            clear(4, i4)
            landed(3, i4, r_1.at[i4])
            b_2[slot] = add(b_1[slot, rows_of(bit1 * 32, 32)], r_1[i4])
            launch(4, i4)

        i5, live5 = at(5)

        @pl.when(live5)
        def _():
            slot = i5 % SLOTS
            clear(5, i5)
            landed(4, i5, r_2.at[i5])
            out[i5, rows_of(x * 64 + bit1 * 32 + bit2 * 16, 16)] = add(
                b_2[slot, rows_of(bit2 * 16, 16)], r_2[i5]
            )
            launch(5, i5)

        i6, live6 = at(6)

        @pl.when(live6)
        def _():
            clear(6, i6)
            landed(5, i6, out.at[i6, rows_of(x * 64 + bit1 * 32 + (1 - bit2) * 16, 16)])
            launch(6, i6)

        i7, live7 = at(7)

        @pl.when(live7)
        def _():
            clear(7, i7)
            landed(6, i7, out.at[i7, rows_of(x * 64 + (1 - bit1) * 32, 32)])
            launch(7, i7)

        i8, live8 = at(8)

        @pl.when(live8)
        def _():
            landed(7, i8, out.at[i8, rows_of((1 - x) * 64, 64)])

        @pl.when(t == 1)
        def _():
            pltpu.make_async_copy(dx_r.at[1], dx_r.at[1], dr.at[1]).wait()
            dx_s[...] = add(dxp[rows_of((1 - x) * 512 + k * 256, 256)], dx_r[1])
            dx_far.start()

        @pl.when(t == 5)
        def _():
            pltpu.make_async_copy(dx_r.at[0], dx_r.at[0], dr.at[0]).wait()
            pltpu.make_async_copy(dx_y, dx_y, dr.at[2]).wait()
            dx_b[...] = (dxo[...] + dx_r[0].astype(F32) + dx_y[...].astype(F32)).astype(BF)
            start_back(1)

        return carry

    lax.fori_loop(0, CHUNKS + 8, tick, 0)
    for stage in range(8):
        for i in range(CHUNKS - SLOTS, CHUNKS):
            copies(stage, i).wait_send()
    dx_core(0).wait_send()
    dx_core(1).wait_send()
    dx_far.wait_send()
    finish_back(0)
    finish_back(1)


def reduce_call(*operands):
    vmem = pl.BlockSpec(memory_space=pltpu.VMEM)
    any_spec = pl.BlockSpec(memory_space=pl.ANY)
    dma = pltpu.SemaphoreType.DMA
    return pl.pallas_call(
        reduce_kernel,
        out_shape=[
            jax.ShapeDtypeStruct((CHUNKS, 128, 1024), BF),
            jax.ShapeDtypeStruct((2, 1, 128, 1024), BF),
            jax.ShapeDtypeStruct((2, 1, 128, 1024), BF),
        ],
        in_specs=[vmem] * 14,
        out_specs=[vmem, any_spec, any_spec],
        scratch_shapes=[
            pltpu.VMEM((SLOTS, 2, 128, 1024), BF),
            pltpu.VMEM((SLOTS, 2, 128, 1024), BF),
            pltpu.VMEM((CHUNKS, 2, 128, 1024), BF),
            pltpu.VMEM((SLOTS, 2, 128, 1024), BF),
            pltpu.VMEM((CHUNKS, 128, 1024), BF),
            pltpu.VMEM((SLOTS, 128, 1024), BF),
            pltpu.VMEM((CHUNKS, 64, 1024), BF),
            pltpu.VMEM((SLOTS, 64, 1024), BF),
            pltpu.VMEM((CHUNKS, 32, 1024), BF),
            pltpu.VMEM((SLOTS, 32, 1024), BF),
            pltpu.VMEM((CHUNKS, 16, 1024), BF),
            pltpu.VMEM((2, 256, 1024), BF),
            pltpu.VMEM((256, 1024), BF),
            pltpu.VMEM((256, 1024), BF),
            pltpu.VMEM((256, 1024), BF),
            dma((8, SLOTS)), dma((8, CHUNKS)), dma((3,)), dma((3,)), dma((2, 2)), dma((2, 2)),
        ],
        compiler_params=pltpu.CompilerParams(
            collective_id=1, has_side_effects=True, vmem_limit_bytes=61 << 20
        ),
        name="reduce_all",
    )(*operands)


def per_group_device(
    layer_input, segments, cotangent,
    query_weight, key_weight, value_weight, output_weight, expand_weight, contract_weight,
    query_bias, value_bias, output_bias, first_gain, first_shift, expand_bias, contract_bias,
    second_gain, second_shift,
):
    weights = (
        query_weight, key_weight, value_weight, output_weight, expand_weight, contract_weight
    )
    packed = jnp.concatenate(
        [
            query_bias, value_bias, output_bias, first_gain, first_shift, contract_bias,
            second_gain, second_shift, expand_bias, jnp.zeros((1024,), BF),
        ]
    ).reshape(32, 128)
    xf, cot, seg, wq, wk, wv, wo, we, wc, vecs = gather_call(
        layer_input, cotangent, segments, weights, packed
    )
    small = [vecs[:, 2 * i : 2 * i + 2].reshape(1024).astype(F32) for i in range(8)]
    bq, bv, bo, gain_one, shift_one, bc, gain_two, shift_two = small
    be = vecs[:, 16:24].reshape(4096).astype(F32)
    z, x, y, k = coords()
    own = x * 512 + k * 256
    xo = lax.dynamic_slice_in_dim(xf, own, 256, 0)
    sk = seg.reshape(1, 1024)
    sq = lax.dynamic_slice_in_dim(seg, x * 4 + k * 2, 2, 0).reshape(256, 1)

    q = (plain_dot(xo, wq) + bq).astype(BF)
    key = plain_dot(xf, wk).astype(BF)
    val = (plain_dot(xf, wv) + bv).astype(BF)
    ctx = attend(q, key, val, sq, sk)
    first_sum = xo.astype(F32) + plain_dot(ctx, wo) + bo
    first_out, normed_one, inverse_one = norm_forward(first_sum, gain_one, shift_one)
    first_bf = first_out.astype(BF)
    hidden = plain_dot(first_bf, we) + be
    gelled = jax.nn.gelu(hidden, approximate=False).astype(BF)
    second_sum = first_out + plain_dot(gelled, wc) + bc
    result, normed_two, inverse_two = norm_forward(second_sum, gain_two, shift_two)
    grad_out = cot.astype(F32)
    grad_second, gain_two_grad, shift_two_grad = norm_backward(
        grad_out, normed_two, inverse_two, gain_two
    )
    gb = grad_second.astype(BF)
    grad_gelled = right_dot(gb, wc)
    gelu_pull = jax.vjp(lambda values: jax.nn.gelu(values, approximate=False), hidden)[1]
    gh = gelu_pull(grad_gelled)[0].astype(BF)
    grad_first = grad_second + right_dot(gh, we)
    grad_attn, gain_one_grad, shift_one_grad = norm_backward(
        grad_first, normed_one, inverse_one, gain_one
    )
    gal = grad_attn.astype(BF)
    grad_ctx = right_dot(gal, wo).astype(BF)
    dq, dk, dv = attend_back(q, key, val, grad_ctx, sq, sk)
    dxp = right_dot(dk, wk) + right_dot(dv, wv)
    dxo = grad_attn + right_dot(dq, wq) + lax.dynamic_slice_in_dim(dxp, own, 256, 0)

    def column(v):
        return jnp.sum(v.astype(F32), axis=0)

    terms = [
        column(dq), column(dv), column(gal), gain_one_grad, shift_one_grad, column(gb),
        gain_two_grad, shift_two_grad,
    ]
    sums = jnp.concatenate(
        [v.reshape(4, 256) for v in terms] + [column(gh).reshape(4, 1024)], axis=1
    )
    sums = lax.psum(sums, ("ctx", "fsdp"))
    mine = lax.dynamic_slice_in_dim(sums, y * 2 + k, 1, 0)[0]
    vec_grads = [mine[i * 256 : (i + 1) * 256] for i in range(8)]

    out, resf, dxf = reduce_call(
        gelled, gb, first_bf, gh, ctx, gal, xo, dq, xf, dk, dv, dxo, dxp.astype(BF),
        result.astype(BF),
    )
    grads = out.astype(F32)

    def square(start):
        return grads[start : start + 2].reshape(256, 1024)

    expand_grad = grads[8:16].reshape(4, 256, 1024).transpose(1, 0, 2).reshape(256, 4096)
    return (
        resf,
        dxf.astype(F32),
        square(18),
        square(20),
        square(22),
        square(16),
        expand_grad,
        grads[0:8].reshape(1024, 1024),
        vec_grads[0],
        vec_grads[1],
        vec_grads[2],
        vec_grads[3],
        vec_grads[4],
        mine[2048:],
        vec_grads[5],
        vec_grads[6],
        vec_grads[7],
    )


def solution(mesh):
    in_specs = (
        P(None, "fsdp", "ctx", None),
        P(None, "fsdp", "ctx"),
        P(None, "fsdp", "ctx", None),
        P("fsdp", None),
        P("fsdp", None),
        P("fsdp", None),
        P("fsdp", None),
        P("fsdp", None),
        P("fsdp", None),
        P("fsdp"),
        P("fsdp"),
        P("fsdp"),
        P("fsdp"),
        P("fsdp"),
        P("fsdp"),
        P("fsdp"),
        P("fsdp"),
        P("fsdp"),
    )
    out_specs = (
        P(None, "fsdp", "ctx", None),
        P(None, "fsdp", "ctx", None),
        P("fsdp", None),
        P("fsdp", None),
        P("fsdp", None),
        P("fsdp", None),
        P("fsdp", None),
        P("fsdp", None),
        P("fsdp"),
        P("fsdp"),
        P("fsdp"),
        P("fsdp"),
        P("fsdp"),
        P("fsdp"),
        P("fsdp"),
        P("fsdp"),
        P("fsdp"),
    )
    def whole(layer_input, segments, *rest):
        grouped = (
            dict(mesh.shape) == {"ctx": 8, "fsdp": 4}
            and layer_input.shape == (2, 4, 1024, 1024)
            and rest[5].shape == (1024, 4096)
        )
        body = per_group_device if grouped else per_device
        return jax.shard_map(
            body, mesh=mesh, in_specs=in_specs, out_specs=out_specs, check_vma=False
        )(layer_input, segments, *rest)

    return whole
```

```python
import jax
import jax.numpy as jnp
from jax import lax
from jax.experimental import pallas as pl
from jax.experimental.pallas import tpu as pltpu
from jax.sharding import PartitionSpec as P

HEADS = 16
HEAD_DIM = 64


def as_sent(x):
    return jax.tree.map(lambda a: a.astype(jnp.bfloat16) if a.dtype == jnp.float32 else a, x)


def plain_dot(left_side, right_side):
    return jnp.dot(left_side, right_side, preferred_element_type=jnp.float32)


def left_dot(left_side, right_side):
    return lax.dot_general(
        left_side, right_side, (((0,), (0,)), ((), ())), preferred_element_type=jnp.float32
    )


def right_dot(left_side, right_side):
    return lax.dot_general(
        left_side, right_side, (((1,), (1,)), ((), ())), preferred_element_type=jnp.float32
    )


def norm_forward(hidden, gain_row, offset_row):
    centre = hidden - jnp.mean(hidden, axis=-1, keepdims=True)
    inverse = lax.rsqrt(jnp.mean(centre * centre, axis=-1, keepdims=True) + 1e-05)
    normed = centre * inverse
    return (normed * gain_row.astype(jnp.float32) + offset_row.astype(jnp.float32), normed, inverse)


def norm_backward(grad_out, normed, inverse, gain_row):
    scaled = grad_out * gain_row.astype(jnp.float32)
    grad_in = inverse * (
        scaled
        - jnp.mean(scaled, axis=-1, keepdims=True)
        - normed * jnp.mean(scaled * normed, axis=-1, keepdims=True)
    )
    return (grad_in, jnp.sum(grad_out * normed, axis=0), jnp.sum(grad_out, axis=0))


def gather_weights(shards):
    return (
        lax.all_gather(shards[0], "fsdp", axis=0, tiled=True),
        lax.all_gather(shards[1], "fsdp", axis=0, tiled=True),
        lax.all_gather(shards[2], "fsdp", axis=0, tiled=True),
        lax.all_gather(shards[3], "fsdp", axis=0, tiled=True),
        lax.all_gather(shards[4], "fsdp", axis=0, tiled=True),
        lax.all_gather(shards[5], "fsdp", axis=0, tiled=True),
        lax.all_gather(shards[6], "fsdp", axis=0, tiled=True),
        lax.all_gather(shards[7], "fsdp", axis=0, tiled=True),
        lax.all_gather(shards[8], "fsdp", axis=0, tiled=True),
        lax.all_gather(shards[9], "fsdp", axis=0, tiled=True),
        lax.all_gather(shards[10], "fsdp", axis=0, tiled=True),
        lax.all_gather(shards[11], "fsdp", axis=0, tiled=True),
        lax.all_gather(shards[12], "fsdp", axis=0, tiled=True),
        lax.all_gather(shards[13], "fsdp", axis=0, tiled=True),
        lax.all_gather(shards[14], "fsdp", axis=0, tiled=True),
    )


def attend_forward(query_bf, key_bf, value_bf, seg_local):
    row_count = query_bf.shape[0]
    score_scale = HEAD_DIM ** (-0.5)
    query_heads = query_bf.reshape(row_count, HEADS, HEAD_DIM)
    run_max = jnp.full((HEADS, row_count), -1e30, jnp.float32)
    key_rows = lax.all_gather(key_bf, "ctx", axis=0, tiled=True)
    value_rows = lax.all_gather(value_bf, "ctx", axis=0, tiled=True)
    key_seg = lax.all_gather(seg_local, "ctx", axis=0, tiled=True)
    piece_rows = key_rows.shape[0]
    key_heads = key_rows.reshape(piece_rows, HEADS, HEAD_DIM)
    value_heads = value_rows.reshape(piece_rows, HEADS, HEAD_DIM)
    scores = (
        jnp.einsum("rhd,khd->hrk", query_heads, key_heads, preferred_element_type=jnp.float32)
        * score_scale
    )
    same_doc = seg_local[:, None] == key_seg[None, :]
    scores = jnp.where(same_doc[None], scores, -1e30)
    new_max = jnp.maximum(run_max, jnp.max(scores, axis=-1))
    numerators = jnp.exp(scores - new_max[..., None])
    run_sum = jnp.sum(numerators, axis=-1)
    accumulated = jnp.einsum(
        "hrk,khd->hrd",
        numerators.astype(jnp.bfloat16),
        value_heads,
        preferred_element_type=jnp.float32,
    )
    run_max, run_sum, accumulated = (new_max, run_sum, accumulated)
    context = jnp.transpose(accumulated / run_sum[..., None], (1, 0, 2)).reshape(
        row_count, HEADS * HEAD_DIM
    )
    return (context, run_max + jnp.log(run_sum))


def block_grads(
    query_heads, grad_heads, query_seg, log_sum, row_delta, key_heads, value_heads, key_seg
):
    score_scale = HEAD_DIM ** (-0.5)
    scores = (
        jnp.einsum("rhd,khd->hrk", query_heads, key_heads, preferred_element_type=jnp.float32)
        * score_scale
    )
    same_doc = query_seg[:, None] == key_seg[None, :]
    scores = jnp.where(same_doc[None], scores, -1e30)
    probs_full = jnp.exp(scores - log_sum[..., None])
    grad_probs = jnp.einsum(
        "rhd,khd->hrk", grad_heads, value_heads, preferred_element_type=jnp.float32
    )
    grad_scores = (probs_full * (grad_probs - row_delta[..., None])).astype(jnp.bfloat16)
    return (probs_full, grad_scores)


def attend_backward(query_bf, key_bf, value_bf, seg_local, context, log_sum, grad_context):
    row_count = query_bf.shape[0]
    score_scale = HEAD_DIM ** (-0.5)
    key_every, value_every, seg_every = (
        lax.all_gather(key_bf, "ctx", axis=0, tiled=True),
        lax.all_gather(value_bf, "ctx", axis=0, tiled=True),
        lax.all_gather(seg_local, "ctx", axis=0, tiled=True),
    )
    length = key_every.shape[0]
    block_len = min(512, length)
    query_heads = query_bf.reshape(row_count, HEADS, HEAD_DIM)
    grad_heads = grad_context.reshape(row_count, HEADS, HEAD_DIM)
    row_delta = jnp.sum(
        (grad_context.astype(jnp.float32) * context).reshape(row_count, HEADS, HEAD_DIM), axis=-1
    ).T

    def visit_block(grad_query, block_num):
        first_row = block_num * block_len
        key_heads = lax.dynamic_slice_in_dim(key_every, first_row, block_len, 0).reshape(
            block_len, HEADS, HEAD_DIM
        )
        value_heads = lax.dynamic_slice_in_dim(value_every, first_row, block_len, 0).reshape(
            block_len, HEADS, HEAD_DIM
        )
        key_seg = lax.dynamic_slice_in_dim(seg_every, first_row, block_len, 0)
        probs_full, grad_scores = block_grads(
            query_heads, grad_heads, seg_local, log_sum, row_delta, key_heads, value_heads, key_seg
        )
        grad_query = (
            grad_query
            + jnp.einsum("hrk,khd->rhd", grad_scores, key_heads, preferred_element_type=jnp.float32)
            * score_scale
        )
        grad_keys = (
            jnp.einsum("hrk,rhd->khd", grad_scores, query_heads, preferred_element_type=jnp.float32)
            * score_scale
        )
        grad_values = jnp.einsum(
            "hrk,rhd->khd",
            probs_full.astype(jnp.bfloat16),
            grad_heads,
            preferred_element_type=jnp.float32,
        )
        stacked = jnp.stack(
            (
                grad_keys.reshape(block_len, HEADS * HEAD_DIM),
                grad_values.reshape(block_len, HEADS * HEAD_DIM),
            ),
            axis=1,
        )
        return (grad_query, stacked)

    grad_query, pieces = lax.scan(
        visit_block,
        jnp.zeros((row_count, HEADS, HEAD_DIM), jnp.float32),
        jnp.arange(length // block_len),
    )
    key_terms = pieces.reshape(length, 2, HEADS * HEAD_DIM)
    own_rows = lax.psum_scatter(
        key_terms.astype(jnp.bfloat16), "ctx", scatter_dimension=0, tiled=True
    ).astype(jnp.float32)
    grad_keyed = own_rows[:, 0].astype(jnp.bfloat16)
    grad_valued = own_rows[:, 1].astype(jnp.bfloat16)
    grad_queries = grad_query.reshape(row_count, HEADS * HEAD_DIM).astype(jnp.bfloat16)
    return (grad_queries, grad_keyed, grad_valued)


def layer_forward(inputs, seg_local, full_weights):
    (
        query_weight,
        key_weight,
        value_weight,
        output_weight,
        expand_weight,
        contract_weight,
        query_bias,
        value_bias,
        output_bias,
        first_gain,
        first_shift,
        expand_bias,
        contract_bias,
        second_gain,
        second_shift,
    ) = full_weights
    query_bf = (plain_dot(inputs, query_weight) + query_bias.astype(jnp.float32)).astype(
        jnp.bfloat16
    )
    key_bf = plain_dot(inputs, key_weight).astype(jnp.bfloat16)
    value_bf = (plain_dot(inputs, value_weight) + value_bias.astype(jnp.float32)).astype(
        jnp.bfloat16
    )
    context, log_sum = attend_forward(query_bf, key_bf, value_bf, seg_local)
    context_bf = context.astype(jnp.bfloat16)
    first_sum = (
        inputs.astype(jnp.float32)
        + plain_dot(context_bf, output_weight)
        + output_bias.astype(jnp.float32)
    )
    first_out, normed_one, inverse_one = norm_forward(first_sum, first_gain, first_shift)
    first_bf = first_out.astype(jnp.bfloat16)
    hidden = plain_dot(first_bf, expand_weight) + expand_bias.astype(jnp.float32)
    gelled_bf = jax.nn.gelu(hidden, approximate=False).astype(jnp.bfloat16)
    second_sum = (
        first_out + plain_dot(gelled_bf, contract_weight) + contract_bias.astype(jnp.float32)
    )
    result, normed_two, inverse_two = norm_forward(second_sum, second_gain, second_shift)
    kept_state = (
        query_bf,
        key_bf,
        value_bf,
        context,
        log_sum,
        context_bf,
        normed_one,
        inverse_one,
        first_bf,
        hidden,
        gelled_bf,
        normed_two,
        inverse_two,
    )
    return (result.astype(jnp.bfloat16), kept_state)


def layer_backward(inputs, seg_local, grad_out, kept_state, full_weights):
    (
        query_weight,
        key_weight,
        value_weight,
        output_weight,
        expand_weight,
        contract_weight,
        query_bias,
        value_bias,
        output_bias,
        first_gain,
        first_shift,
        expand_bias,
        contract_bias,
        second_gain,
        second_shift,
    ) = full_weights
    (
        query_bf,
        key_bf,
        value_bf,
        context,
        log_sum,
        context_bf,
        normed_one,
        inverse_one,
        first_bf,
        hidden,
        gelled_bf,
        normed_two,
        inverse_two,
    ) = kept_state
    grad_second, second_gain_grad, second_shift_grad = norm_backward(
        grad_out.astype(jnp.float32), normed_two, inverse_two, second_gain
    )
    grad_branch = grad_second.astype(jnp.bfloat16)
    contract_weight_grad = left_dot(gelled_bf, grad_branch)
    contract_bias_grad = jnp.sum(grad_branch.astype(jnp.float32), axis=0)
    grad_gelled = right_dot(grad_branch, contract_weight)
    gelu_pull = jax.vjp(lambda values: jax.nn.gelu(values, approximate=False), hidden)[1]
    grad_hidden = gelu_pull(grad_gelled)[0].astype(jnp.bfloat16)
    expand_weight_grad = left_dot(first_bf, grad_hidden)
    expand_bias_grad = jnp.sum(grad_hidden.astype(jnp.float32), axis=0)
    grad_first = grad_second + right_dot(grad_hidden, expand_weight)
    grad_attn, first_gain_grad, first_shift_grad = norm_backward(
        grad_first, normed_one, inverse_one, first_gain
    )
    grad_attn_low = grad_attn.astype(jnp.bfloat16)
    output_weight_grad = left_dot(context_bf, grad_attn_low)
    output_bias_grad = jnp.sum(grad_attn_low.astype(jnp.float32), axis=0)
    grad_context = right_dot(grad_attn_low, output_weight).astype(jnp.bfloat16)
    grad_queries, grad_keyed, grad_valued = attend_backward(
        query_bf, key_bf, value_bf, seg_local, context, log_sum, grad_context
    )
    query_weight_grad = left_dot(inputs, grad_queries)
    key_weight_grad = left_dot(inputs, grad_keyed)
    value_weight_grad = left_dot(inputs, grad_valued)
    query_bias_grad = jnp.sum(grad_queries.astype(jnp.float32), axis=0)
    value_bias_grad = jnp.sum(grad_valued.astype(jnp.float32), axis=0)
    grad_input = (
        grad_attn
        + right_dot(grad_queries, query_weight)
        + right_dot(grad_keyed, key_weight)
        + right_dot(grad_valued, value_weight)
    )
    grad_terms = (
        query_weight_grad,
        key_weight_grad,
        value_weight_grad,
        output_weight_grad,
        expand_weight_grad,
        contract_weight_grad,
        query_bias_grad,
        value_bias_grad,
        output_bias_grad,
        first_gain_grad,
        first_shift_grad,
        expand_bias_grad,
        contract_bias_grad,
        second_gain_grad,
        second_shift_grad,
    )
    return (grad_input, grad_terms)


def per_device(
    layer_input,
    segments,
    cotangent,
    query_weight,
    key_weight,
    value_weight,
    output_weight,
    expand_weight,
    contract_weight,
    query_bias,
    value_bias,
    output_bias,
    first_gain,
    first_shift,
    expand_bias,
    contract_bias,
    second_gain,
    second_shift,
):
    shards = (
        query_weight,
        key_weight,
        value_weight,
        output_weight,
        expand_weight,
        contract_weight,
        query_bias,
        value_bias,
        output_bias,
        first_gain,
        first_shift,
        expand_bias,
        contract_bias,
        second_gain,
        second_shift,
    )
    micro_count = layer_input.shape[0]
    results = []
    grad_inputs = []
    totals = None
    for micro_step in range(micro_count):
        inputs = layer_input[micro_step, 0]
        seg_local = segments[micro_step, 0].astype(jnp.bfloat16)
        front_weights = gather_weights(shards)
        result, kept_state = layer_forward(inputs, seg_local, front_weights)
        behind = gather_weights(shards)
        grad_input, grad_terms = layer_backward(
            inputs, seg_local, cotangent[micro_step, 0], kept_state, behind
        )
        results.append(result)
        grad_inputs.append(grad_input)
        if totals is None:
            totals = grad_terms
        else:
            totals = tuple(
                (left_side + right_side for left_side, right_side in zip(totals, grad_terms))
            )
    reduced = jax.tree.map(
        lambda part: part.astype(jnp.float32),
        lax.psum_scatter(as_sent(totals), "fsdp", scatter_dimension=0, tiled=True),
    )
    summed = jax.tree.map(lambda part: part.astype(jnp.float32), lax.psum(as_sent(reduced), "ctx"))
    layer_output = jnp.stack(results, axis=0)[:, None]
    input_grad = jnp.stack(grad_inputs, axis=0)[:, None]
    return (
        layer_output,
        input_grad,
        summed[0],
        summed[1],
        summed[2],
        summed[3],
        summed[4],
        summed[5],
        summed[6],
        summed[7],
        summed[8],
        summed[9],
        summed[10],
        summed[11],
        summed[12],
        summed[13],
        summed[14],
    )


MESH = pl.DeviceIdType.MESH
BF = jnp.bfloat16
F32 = jnp.float32
CHUNKS = 24
SLOTS = 3
LAND = 4


def coords():
    c, f = lax.axis_index("ctx"), lax.axis_index("fsdp")
    return c // 2, c % 2, f // 2, f % 2


def dev(z, x, y, k):
    return (z * 2 + x, y * 2 + k)


def greet(z, x, y, k):
    barrier = pltpu.get_barrier_semaphore()
    for step in range(1, 8):
        place = (z * 2 + k + step) % 8
        pl.semaphore_signal(
            barrier, inc=1, device_id=dev(place // 2, x, y, place % 2), device_id_type=MESH
        )
    pl.semaphore_signal(barrier, inc=1, device_id=dev(z, 1 - x, y, k), device_id_type=MESH)
    pl.semaphore_signal(barrier, inc=1, device_id=dev(z, x, 1 - y, k), device_id_type=MESH)
    pl.semaphore_wait(barrier, 9)


def remote(src, dst, send, recv, to):
    return pltpu.make_async_remote_copy(
        src_ref=src, dst_ref=dst, send_sem=send, recv_sem=recv, device_id=to, device_id_type=MESH
    )


def rows_of(start, size, unit=16):
    return pl.ds(pl.multiple_of(start, unit), size)


def gather_kernel(
    inp, cot, seg, wq, wk, wv, wo, we, wc, vec,
    xf, cotf, segf, fq, fk, fv, fo, fe, fc, vecf,
    own, a_send, a_recv, g_send, g_recv, w_send, w_recv, v_send, v_recv,
):
    z, x, y, k = coords()
    f = y * 2 + k
    other = (1 - y) * 2 + k
    sib, xn, yn = dev(z, x, y, 1 - k), dev(z, 1 - x, y, k), dev(z, x, 1 - y, k)
    zn = dev(z + 1 - 2 * (z % 2), x, y, k)
    color = (z % 2) * 2 + x
    c_x, c_z, c_o = color + 1 - 2 * x, (color + 2) % 4, 3 - color
    greet(z, x, y, k)

    def block_moves(mb):
        to_z, to_k = mb * 2 + k, z // 2
        row = x * 512 + z * 128
        slot = z % 2
        mine = (to_z == z) & (to_k == k)
        moves = (
            (inp.at[mb, 0], xf.at[rows_of(row, 128)], 0),
            (seg.at[mb], segf.at[x * 4 + z], 1),
            (cot.at[mb, 0], cotf.at[rows_of(slot * 128, 128)], 2),
        )
        return mine, dev(to_z, x, y, to_k), slot, moves

    def start_blocks(which):
        for mb in range(2):
            mine, to, slot, moves = block_moves(mb)
            for src, dst, n in moves:
                if n not in which:
                    continue

                @pl.when(mine)
                def _():
                    pltpu.make_async_copy(src, dst, a_recv.at[n, slot]).start()

                @pl.when(jnp.logical_not(mine))
                def _():
                    remote(src, dst, a_send.at[n, mb], a_recv.at[n, slot], to).start()

    def finish_blocks(which):
        for mb in range(2):
            mine, to, slot, moves = block_moves(mb)
            for src, dst, n in moves:
                if n not in which:
                    continue

                @pl.when(jnp.logical_not(mine))
                def _():
                    remote(src, dst, a_send.at[n, mb], a_recv.at[n, slot], to).wait_send()

    def arrive_blocks(which):
        for slot in range(2):
            zz = 2 * k + slot
            for n in which:
                if n == 0:
                    dst = xf.at[rows_of(x * 512 + zz * 128, 128)]
                elif n == 1:
                    dst = segf.at[x * 4 + zz]
                else:
                    dst = cotf.at[pl.ds(slot * 128, 128)]
                pltpu.make_async_copy(dst, dst, a_recv.at[n, slot]).wait()

    def group_copy(step):
        who = x if step < 2 else 1 - x
        src = xf.at[rows_of(who * 512 + k * 256, 256)]
        sseg = segf.at[pl.ds(who * 4 + k * 2, 2)]
        to = (sib, xn, sib)[step]
        return (
            remote(src, src, g_send.at[0, step], g_recv.at[0, step], to),
            remote(sseg, sseg, g_send.at[1, step], g_recv.at[1, step], to),
        )

    def group_arrive(step):
        who = (x, 1 - x, 1 - x)[step]
        kk = (1 - k, k, 1 - k)[step]
        src = xf.at[rows_of(who * 512 + kk * 256, 256)]
        sseg = segf.at[pl.ds(who * 4 + kk * 2, 2)]
        pltpu.make_async_copy(src, src, g_recv.at[0, step]).wait()
        pltpu.make_async_copy(sseg, sseg, g_recv.at[1, step]).wait()

    items = []
    for shard, full in ((wq, fq), (wk, fk), (wv, fv), (wo, fo)):
        items.append((shard, full, 0, 0, 256))
    for j in range(4):
        items.append((we, fe, 0, j * 1024, 256))
    for j in range(4):
        items.append((wc, fc, j * 256, 0, 1024))
    n_items = len(items)

    def part(i, quarter, start, size, own_src=False):
        shard, full, row, col, step = items[i]
        if own_src:
            return shard.at[rows_of(row + start, size), pl.ds(col, 1024)]
        return full.at[rows_of(quarter * step + row + start, size), pl.ds(col, 1024)]

    def send_copy(i, kind):
        sems = (w_send.at[kind, i], w_recv.at[kind, i])
        if kind == 0:
            return remote(part(i, f, color * 64, 64, True), part(i, f, color * 64, 64), *sems, yn)
        if kind == 1:
            return remote(part(i, f, c_o * 64, 32, True), part(i, f, c_o * 64, 32), *sems, yn)
        if kind == 2:
            src = part(i, other, color * 64, 64)
            return remote(src, src, *sems, xn)
        if kind == 3:
            src = part(i, other, c_z * 64 + 32, 16)
            return remote(src, src, *sems, xn)
        if kind == 4:
            src = part(i, other, color * 64, 64)
            return remote(src, src, *sems, zn)
        if kind == 5:
            src = part(i, other, c_x * 64 + 48, 16)
            return remote(src, src, *sems, zn)
        if kind == 6:
            return remote(part(i, f, 0, 256, True), part(i, f, 0, 256), *sems, sib)
        src = part(i, other, 0, 256)
        return remote(src, src, *sems, sib)

    def arrive(i, kind):
        if kind == 0:
            dst = part(i, other, color * 64, 64)
        elif kind == 1:
            dst = part(i, other, c_o * 64, 32)
        elif kind == 2:
            dst = part(i, other, c_x * 64, 64)
        elif kind == 3:
            dst = part(i, other, c_o * 64 + 32, 16)
        elif kind == 4:
            dst = part(i, other, c_z * 64, 64)
        elif kind == 5:
            dst = part(i, other, c_o * 64 + 48, 16)
        elif kind == 6:
            dst = part(i, y * 2 + 1 - k, 0, 256)
        else:
            dst = part(i, (1 - y) * 2 + 1 - k, 0, 256)
        pltpu.make_async_copy(dst, dst, w_recv.at[kind, i]).wait()

    def own_in(i):
        return pltpu.make_async_copy(part(i, f, 0, 256, True), own.at[i], w_recv.at[8, i])

    def own_out(i):
        return pltpu.make_async_copy(own.at[i], part(i, f, 0, 256), w_recv.at[9, i])

    vec_copies = (
        remote(vec, vecf.at[f], v_send.at[0], v_recv.at[0], yn),
        remote(vec, vecf.at[f], v_send.at[1], v_recv.at[1], sib),
        remote(vecf.at[other], vecf.at[other], v_send.at[2], v_recv.at[2], sib),
    )
    vec_own = pltpu.make_async_copy(vec, vecf.at[f], v_recv.at[3])

    start_blocks((0, 1))
    vec_own.start()
    for i in range(n_items):
        own_in(i).start()
    vec_copies[0].start()
    vec_copies[1].start()
    for t in range(n_items + 3):
        if t < n_items:
            send_copy(t, 0).start()
            send_copy(t, 1).start()
            send_copy(t, 6).start()
        if t == 1:
            arrive_blocks((0, 1))
            for step in range(2):
                for move in group_copy(step):
                    move.start()
            pltpu.make_async_copy(vecf.at[other], vecf.at[other], v_recv.at[0]).wait()
            vec_copies[2].start()
        if t == 4:
            group_arrive(1)
            for move in group_copy(2):
                move.start()
            start_blocks((2,))
        if 1 <= t <= n_items:
            i = t - 1
            own_in(i).wait()
            own_out(i).start()
            arrive(i, 0)
            send_copy(i, 2).start()
            send_copy(i, 4).start()
        if 2 <= t <= n_items + 1:
            i = t - 2
            arrive(i, 4)
            send_copy(i, 3).start()
            arrive(i, 2)
            send_copy(i, 5).start()
        if 3 <= t:
            i = t - 3
            arrive(i, 1)
            arrive(i, 3)
            arrive(i, 5)
            send_copy(i, 7).start()
    for i in range(n_items):
        arrive(i, 6)
        arrive(i, 7)
        own_out(i).wait()
        for kind in range(8):
            send_copy(i, kind).wait_send()
    arrive_blocks((2,))
    finish_blocks((0, 1, 2))
    group_arrive(0)
    group_arrive(2)
    for step in range(3):
        for move in group_copy(step):
            move.wait_send()
    sib_own, sib_other = vecf.at[y * 2 + 1 - k], vecf.at[(1 - y) * 2 + 1 - k]
    pltpu.make_async_copy(sib_own, sib_own, v_recv.at[1]).wait()
    pltpu.make_async_copy(sib_other, sib_other, v_recv.at[2]).wait()
    for move in vec_copies:
        move.wait_send()
    vec_own.wait()


def gather_call(inp, cot, seg, weights, vec):
    any_spec = pl.BlockSpec(memory_space=pl.ANY)
    outs = [
        jax.ShapeDtypeStruct((1024, 1024), BF),
        jax.ShapeDtypeStruct((256, 1024), BF),
        jax.ShapeDtypeStruct((8, 1, 128), jnp.int32),
    ]
    outs += [jax.ShapeDtypeStruct((1024, 1024), BF)] * 4
    outs += [
        jax.ShapeDtypeStruct((1024, 4096), BF),
        jax.ShapeDtypeStruct((4096, 1024), BF),
        jax.ShapeDtypeStruct((4, 32, 128), BF),
    ]
    dma = pltpu.SemaphoreType.DMA
    return pl.pallas_call(
        gather_kernel,
        out_shape=outs,
        in_specs=[any_spec] * 10,
        out_specs=[any_spec] * 10,
        scratch_shapes=[
            pltpu.VMEM((12, 256, 1024), BF),
            dma((3, 2)), dma((3, 2)), dma((2, 3)), dma((2, 3)),
            dma((8, 12)), dma((10, 12)), dma((3,)), dma((4,)),
        ],
        compiler_params=pltpu.CompilerParams(
            collective_id=0, has_side_effects=True, vmem_limit_bytes=32 << 20
        ),
        name="gather_all",
    )(inp, cot, seg, *weights, vec)


def two_heads(block):
    lane = lax.broadcasted_iota(jnp.int32, block.shape, 1)
    zero = jnp.zeros_like(block)
    return jnp.concatenate(
        [jnp.where(lane < HEAD_DIM, block, zero), jnp.where(lane >= HEAD_DIM, block, zero)], axis=0
    )


def one_block(pair):
    rows = pair.shape[0] // 2
    lane = lax.broadcasted_iota(jnp.int32, (rows, pair.shape[1]), 1)
    return jnp.where(lane < HEAD_DIM, pair[:rows], pair[rows:])


def softmax_pair(q_ref, k_ref, same_ref):
    queries = two_heads(q_ref[...] * BF(HEAD_DIM**-0.5))
    scores = right_dot(queries, k_ref[...])
    same = same_ref[...]
    scores = jnp.where(jnp.concatenate([same, same], axis=0) > 0, scores, -1e30)
    numer = jnp.exp(scores - jnp.max(scores, axis=-1, keepdims=True))
    return queries, numer * (1.0 / jnp.sum(numer, axis=-1, keepdims=True))


def attend_kernel(q_ref, k_ref, v_ref, sq_ref, sk_ref, o_ref, same_ref):
    @pl.when(pl.program_id(0) == 0)
    def _():
        same_ref[...] = (sq_ref[...] == sk_ref[...]).astype(F32)

    probs = softmax_pair(q_ref, k_ref, same_ref)[1]
    o_ref[...] = one_block(plain_dot(probs.astype(BF), v_ref[...])).astype(BF)


def attend_back_kernel(
    q_ref, k_ref, v_ref, g_ref, sq_ref, sk_ref, dq_ref, dk_ref, dv_ref, same_ref
):
    @pl.when(pl.program_id(0) == 0)
    def _():
        same_ref[...] = (sq_ref[...] == sk_ref[...]).astype(F32)

    queries, probs = softmax_pair(q_ref, k_ref, same_ref)
    grads = two_heads(g_ref[...])
    grad_probs = right_dot(grads, v_ref[...])
    delta = jnp.sum(probs * grad_probs, axis=-1, keepdims=True)
    grad_scores = (probs * (grad_probs - delta)).astype(BF)
    dv_ref[...] = left_dot(probs.astype(BF), grads).astype(BF)
    dk_ref[...] = left_dot(grad_scores, queries).astype(BF)
    dq = one_block(plain_dot(grad_scores, k_ref[...]))
    dq_ref[...] = (dq * HEAD_DIM**-0.5).astype(BF)


def attention_specs():
    rows = pl.BlockSpec((256, 128), lambda h: (0, h))
    full = pl.BlockSpec((1024, 128), lambda h: (0, h))
    sq = pl.BlockSpec((256, 1), lambda h: (0, 0))
    sk = pl.BlockSpec((1, 1024), lambda h: (0, 0))
    return rows, full, sq, sk


def attend(q, k, v, sq, sk):
    rows, full, sqs, sks = attention_specs()
    return pl.pallas_call(
        attend_kernel,
        grid=(8,),
        out_shape=jax.ShapeDtypeStruct((256, 1024), BF),
        in_specs=[rows, full, full, sqs, sks],
        out_specs=rows,
        scratch_shapes=[pltpu.VMEM((256, 1024), F32)],
        compiler_params=pltpu.CompilerParams(vmem_limit_bytes=40 << 20),
        name="attend",
    )(q, k, v, sq, sk)


def attend_back(q, k, v, g, sq, sk):
    rows, full, sqs, sks = attention_specs()
    return pl.pallas_call(
        attend_back_kernel,
        grid=(8,),
        out_shape=[
            jax.ShapeDtypeStruct((256, 1024), BF),
            jax.ShapeDtypeStruct((1024, 1024), BF),
            jax.ShapeDtypeStruct((1024, 1024), BF),
        ],
        in_specs=[rows, full, full, rows, sqs, sks],
        out_specs=[rows, full, full],
        scratch_shapes=[pltpu.VMEM((256, 1024), F32)],
        compiler_params=pltpu.CompilerParams(vmem_limit_bytes=40 << 20),
        name="attend_back",
    )(q, k, v, g, sq, sk)


def reduce_kernel(
    gel, gb, fb, gh, ctx, gal, xo, dq, xf, dk, dv, dxo, dxp, res, vec,
    out, resf, dxf, vec_out,
    s_d, l_d, r_d, b_y, r_y, b_x, r_x, b_1, r_1, b_2, r_2,
    dx_r, dx_s, dx_y, dx_b, v_s, v_d, v_r,
    ss, rs, ds, dr, a_send, a_recv, v_send, v_recv,
):
    z, x, y, k = coords()
    sib, xn, yn = dev(z, x, y, 1 - k), dev(z, 1 - x, y, k), dev(z, x, 1 - y, k)
    bit1, bit2 = z % 2, z // 2
    z1 = dev(z + 1 - 2 * bit1, x, y, k)
    z2 = dev((z + 2) % 4, x, y, k)
    greet(z, x, y, k)

    def back(n, slot):
        to_z = 2 * k + slot
        to_k = z % 2
        mb = z // 2
        mine = (to_z == z) & (to_k == k)
        src = (res, dx_b)[n].at[pl.ds(slot * 128, 128)]
        dst = (resf, dxf)[n].at[mb, 0]

        def far():
            return remote(
                src, dst, a_send.at[n, slot], a_recv.at[n, mb], dev(to_z, x, y, to_k)
            )

        def near():
            return pltpu.make_async_copy(src, dst, a_recv.at[n, mb])

        return mine, far, near

    def start_back(n):
        for slot in range(2):
            mine, far, near = back(n, slot)

            @pl.when(mine)
            def _():
                near().start()

            @pl.when(jnp.logical_not(mine))
            def _():
                far().start()

    def finish_back(n):
        for slot in range(2):
            mine, far, _ = back(n, slot)

            @pl.when(jnp.logical_not(mine))
            def _():
                far().wait_send()

        for mb in range(2):
            dst = (resf, dxf)[n].at[mb, 0]
            pltpu.make_async_copy(dst, dst, a_recv.at[n, mb]).wait()

    start_back(0)

    def dx_core(g):
        who = x if g == 0 else 1 - x
        src = dxp.at[rows_of(who * 512 + (1 - k) * 256, 256)]
        return remote(src, dx_r.at[g], ds.at[g], dr.at[g], sib)

    dx_far = remote(dx_s, dx_y, ds.at[2], dr.at[2], xn)
    dx_core(1).start()
    dx_core(0).start()

    v_peers = (sib, yn, xn, z1, z2)

    def v_copy(stage):
        if stage == 0:
            return remote(v_d.at[1], v_d.at[2], v_send.at[0], v_recv.at[0], sib)
        src = v_s.at[0, 1 - y] if stage == 1 else v_s.at[stage - 1, 0]
        return remote(src, v_r.at[stage - 1], v_send.at[stage], v_recv.at[stage], v_peers[stage])

    def v_step(stage):
        if stage == 0:
            for plane in range(2):
                v_d[0, plane] = vec[plane * 2 + k]
                v_d[1, plane] = vec[plane * 2 + 1 - k]
        elif stage == 1:
            pltpu.make_async_copy(v_d.at[2], v_d.at[2], v_recv.at[0]).wait()
            v_s[0] = v_d[0] + v_d[2]
        else:
            dst = v_r.at[stage - 2]
            pltpu.make_async_copy(dst, dst, v_recv.at[stage - 1]).wait()
            mine = v_s[0, y] if stage == 2 else v_s[stage - 2, 0]
            total = mine + v_r[stage - 2]
            if stage == 5:
                vec_out[...] = total
            else:
                v_s[stage - 1, 0] = total
        if stage < 5:
            v_copy(stage).start()

    def send(stage, i, src, dst, to):
        return remote(src, dst, ss.at[stage, i % SLOTS], rs.at[stage, i % LAND], to)

    def landed(stage, i, dst):
        pltpu.make_async_copy(dst, dst, rs.at[stage, i % LAND]).wait()

    def copies(stage, i):
        slot = i % SLOTS
        if stage == 0:
            return send(0, i, s_d.at[slot], r_d.at[i % LAND], sib)
        if stage == 1:
            return send(1, i, b_y.at[slot, 1 - y], r_y.at[i % LAND], yn)
        if stage == 2:
            return send(2, i, b_x.at[slot, rows_of((1 - x) * 64, 64)], r_x.at[i % LAND], xn)
        if stage == 3:
            return send(3, i, b_1.at[slot, rows_of((1 - bit1) * 32, 32)], r_1.at[i % LAND], z1)
        if stage == 4:
            return send(4, i, b_2.at[slot, rows_of((1 - bit2) * 16, 16)], r_2.at[i % LAND], z2)
        if stage == 5:
            own = out.at[i, rows_of(x * 64 + bit1 * 32 + bit2 * 16, 16)]
            return send(5, i, own, own, z2)
        if stage == 6:
            own = out.at[i, rows_of(x * 64 + bit1 * 32, 32)]
            return send(6, i, own, own, z1)
        own = out.at[i, rows_of(x * 64, 64)]
        return send(7, i, own, own, xn)

    def launch(stage, i):
        copies(stage, i).start()

    def clear(stage, i):
        @pl.when(i >= SLOTS)
        def _():
            copies(stage, i - SLOTS).wait_send()

    def add(a, b):
        return (a.astype(F32) + b.astype(F32)).astype(BF)

    def terms(i, a_ref, b_ref, a_base, a_step, b_col):
        slot = i % SLOTS
        right = b_ref[:, b_col]
        for plane in range(2):
            for core in range(2):
                quarter = plane * 2 + (k if core == 0 else 1 - k)
                left = a_ref[:, pl.ds(pl.multiple_of(a_base + quarter * a_step, 128), 128)]
                product = left_dot(left, right).astype(BF)
                if core == 0:
                    l_d[slot, plane] = product
                else:
                    s_d[slot, plane] = product

    every = pl.ds(0, 1024)

    def tick(t, carry):
        def at(stage):
            i = t - stage
            return i, (i >= 0) & (i < CHUNKS)

        i0, live0 = at(0)

        @pl.when(live0)
        def _():
            clear(0, i0)

        @pl.when(i0 < 8)
        def _():
            terms(i0, gel, gb, i0 * 128, 1024, every)

        @pl.when((i0 >= 8) & (i0 < 16))
        def _():
            j = i0 - 8
            terms(i0, fb, gh, (j % 2) * 128, 256, rows_of((j // 2) * 1024, 1024, 1024))

        @pl.when((i0 >= 16) & (i0 < 18))
        def _():
            terms(i0, ctx, gal, (i0 - 16) * 128, 256, every)

        @pl.when((i0 >= 18) & (i0 < 20))
        def _():
            terms(i0, xo, dq, (i0 - 18) * 128, 256, every)

        @pl.when((i0 >= 20) & (i0 < 22))
        def _():
            terms(i0, xf, dk, (i0 - 20) * 128, 256, every)

        @pl.when((i0 >= 22) & (i0 < 24))
        def _():
            terms(i0, xf, dv, (i0 - 22) * 128, 256, every)

        @pl.when(live0)
        def _():
            launch(0, i0)

        i1, live1 = at(1)

        @pl.when(live1)
        def _():
            slot = i1 % SLOTS
            clear(1, i1)
            landed(0, i1, r_d.at[i1 % LAND])
            for plane in range(2):
                b_y[slot, plane] = add(l_d[slot, plane], r_d[i1 % LAND, plane])
            launch(1, i1)

        i2, live2 = at(2)

        @pl.when(live2)
        def _():
            slot = i2 % SLOTS
            clear(2, i2)
            landed(1, i2, r_y.at[i2 % LAND])
            b_x[slot] = add(b_y[slot, y], r_y[i2 % LAND])
            launch(2, i2)

        i3, live3 = at(3)

        @pl.when(live3)
        def _():
            slot = i3 % SLOTS
            clear(3, i3)
            landed(2, i3, r_x.at[i3 % LAND])
            b_1[slot] = add(b_x[slot, rows_of(x * 64, 64)], r_x[i3 % LAND])
            launch(3, i3)

        i4, live4 = at(4)

        @pl.when(live4)
        def _():
            slot = i4 % SLOTS
            clear(4, i4)
            landed(3, i4, r_1.at[i4 % LAND])
            b_2[slot] = add(b_1[slot, rows_of(bit1 * 32, 32)], r_1[i4 % LAND])
            launch(4, i4)

        i5, live5 = at(5)

        @pl.when(live5)
        def _():
            slot = i5 % SLOTS
            clear(5, i5)
            landed(4, i5, r_2.at[i5 % LAND])
            out[i5, rows_of(x * 64 + bit1 * 32 + bit2 * 16, 16)] = add(
                b_2[slot, rows_of(bit2 * 16, 16)], r_2[i5 % LAND]
            )
            launch(5, i5)

        i6, live6 = at(6)

        @pl.when(live6)
        def _():
            clear(6, i6)
            landed(5, i6, out.at[i6, rows_of(x * 64 + bit1 * 32 + (1 - bit2) * 16, 16)])
            launch(6, i6)

        i7, live7 = at(7)

        @pl.when(live7)
        def _():
            clear(7, i7)
            landed(6, i7, out.at[i7, rows_of(x * 64 + (1 - bit1) * 32, 32)])
            launch(7, i7)

        i8, live8 = at(8)

        @pl.when(live8)
        def _():
            landed(7, i8, out.at[i8, rows_of((1 - x) * 64, 64)])

        for stage in range(6):

            @pl.when(t == 2 * stage)
            def _():
                v_step(stage)

        @pl.when(t == 1)
        def _():
            pltpu.make_async_copy(dx_r.at[1], dx_r.at[1], dr.at[1]).wait()
            dx_s[...] = add(dxp[rows_of((1 - x) * 512 + k * 256, 256)], dx_r[1])
            dx_far.start()

        @pl.when(t == 5)
        def _():
            pltpu.make_async_copy(dx_r.at[0], dx_r.at[0], dr.at[0]).wait()
            pltpu.make_async_copy(dx_y, dx_y, dr.at[2]).wait()
            dx_b[...] = (dxo[...] + dx_r[0].astype(F32) + dx_y[...].astype(F32)).astype(BF)
            start_back(1)

        return carry

    lax.fori_loop(0, CHUNKS + 8, tick, 0)
    for stage in range(8):
        for i in range(CHUNKS - SLOTS, CHUNKS):
            copies(stage, i).wait_send()
    for stage in range(5):
        v_copy(stage).wait_send()
    dx_core(0).wait_send()
    dx_core(1).wait_send()
    dx_far.wait_send()
    finish_back(0)
    finish_back(1)


def reduce_call(*operands):
    vmem = pl.BlockSpec(memory_space=pltpu.VMEM)
    any_spec = pl.BlockSpec(memory_space=pl.ANY)
    dma = pltpu.SemaphoreType.DMA
    return pl.pallas_call(
        reduce_kernel,
        out_shape=[
            jax.ShapeDtypeStruct((CHUNKS, 128, 1024), BF),
            jax.ShapeDtypeStruct((2, 1, 128, 1024), BF),
            jax.ShapeDtypeStruct((2, 1, 128, 1024), BF),
            jax.ShapeDtypeStruct((24, 128), F32),
        ],
        in_specs=[vmem] * 15,
        out_specs=[vmem, any_spec, any_spec, vmem],
        scratch_shapes=[
            pltpu.VMEM((SLOTS, 2, 128, 1024), BF),
            pltpu.VMEM((SLOTS, 2, 128, 1024), BF),
            pltpu.VMEM((LAND, 2, 128, 1024), BF),
            pltpu.VMEM((SLOTS, 2, 128, 1024), BF),
            pltpu.VMEM((LAND, 128, 1024), BF),
            pltpu.VMEM((SLOTS, 128, 1024), BF),
            pltpu.VMEM((LAND, 64, 1024), BF),
            pltpu.VMEM((SLOTS, 64, 1024), BF),
            pltpu.VMEM((LAND, 32, 1024), BF),
            pltpu.VMEM((SLOTS, 32, 1024), BF),
            pltpu.VMEM((LAND, 16, 1024), BF),
            pltpu.VMEM((2, 256, 1024), BF),
            pltpu.VMEM((256, 1024), BF),
            pltpu.VMEM((256, 1024), BF),
            pltpu.VMEM((256, 1024), BF),
            pltpu.VMEM((4, 2, 24, 128), F32),
            pltpu.VMEM((3, 2, 24, 128), F32),
            pltpu.VMEM((4, 24, 128), F32),
            dma((8, SLOTS)), dma((8, LAND)), dma((3,)), dma((3,)), dma((2, 2)), dma((2, 2)),
            dma((5,)), dma((5,)),
        ],
        compiler_params=pltpu.CompilerParams(
            collective_id=1, has_side_effects=True, vmem_limit_bytes=61 << 20
        ),
        name="reduce_all",
    )(*operands)


def per_group_device(
    layer_input, segments, cotangent,
    query_weight, key_weight, value_weight, output_weight, expand_weight, contract_weight,
    query_bias, value_bias, output_bias, first_gain, first_shift, expand_bias, contract_bias,
    second_gain, second_shift,
):
    weights = (
        query_weight, key_weight, value_weight, output_weight, expand_weight, contract_weight
    )
    packed = jnp.concatenate(
        [
            query_bias, value_bias, output_bias, first_gain, first_shift, contract_bias,
            second_gain, second_shift, expand_bias, jnp.zeros((1024,), BF),
        ]
    ).reshape(32, 128)
    xf, cot, seg, wq, wk, wv, wo, we, wc, vecs = gather_call(
        layer_input, cotangent, segments, weights, packed
    )
    small = [vecs[:, 2 * i : 2 * i + 2].reshape(1024).astype(F32) for i in range(8)]
    bq, bv, bo, gain_one, shift_one, bc, gain_two, shift_two = small
    be = vecs[:, 16:24].reshape(4096).astype(F32)
    z, x, y, k = coords()
    own = x * 512 + k * 256
    xo = lax.dynamic_slice_in_dim(xf, own, 256, 0)
    sk = seg.reshape(1, 1024)
    sq = lax.dynamic_slice_in_dim(seg, x * 4 + k * 2, 2, 0).reshape(256, 1)

    q = (plain_dot(xo, wq) + bq).astype(BF)
    key = plain_dot(xf, wk).astype(BF)
    val = (plain_dot(xf, wv) + bv).astype(BF)
    ctx = attend(q, key, val, sq, sk)
    first_sum = xo.astype(F32) + plain_dot(ctx, wo) + bo
    first_out, normed_one, inverse_one = norm_forward(first_sum, gain_one, shift_one)
    first_bf = first_out.astype(BF)
    hidden = plain_dot(first_bf, we) + be
    gelled = jax.nn.gelu(hidden, approximate=False).astype(BF)
    second_sum = first_out + plain_dot(gelled, wc) + bc
    result, normed_two, inverse_two = norm_forward(second_sum, gain_two, shift_two)
    grad_out = cot.astype(F32)
    grad_second, gain_two_grad, shift_two_grad = norm_backward(
        grad_out, normed_two, inverse_two, gain_two
    )
    gb = grad_second.astype(BF)
    grad_gelled = right_dot(gb, wc)
    gelu_pull = jax.vjp(lambda values: jax.nn.gelu(values, approximate=False), hidden)[1]
    gh = gelu_pull(grad_gelled)[0].astype(BF)
    grad_first = grad_second + right_dot(gh, we)
    grad_attn, gain_one_grad, shift_one_grad = norm_backward(
        grad_first, normed_one, inverse_one, gain_one
    )
    gal = grad_attn.astype(BF)
    grad_ctx = right_dot(gal, wo).astype(BF)
    dq, dk, dv = attend_back(q, key, val, grad_ctx, sq, sk)
    dxp = right_dot(dk, wk) + right_dot(dv, wv)
    dxo = grad_attn + right_dot(dq, wq) + lax.dynamic_slice_in_dim(dxp, own, 256, 0)

    def column(v):
        return jnp.sum(v.astype(F32), axis=0)

    terms = [
        column(dq), column(dv), column(gal), gain_one_grad, shift_one_grad, column(gb),
        gain_two_grad, shift_two_grad,
    ]
    sums = jnp.concatenate(
        [v.reshape(4, 256) for v in terms] + [column(gh).reshape(4, 1024)], axis=1
    )
    out, resf, dxf, vec = reduce_call(
        gelled, gb, first_bf, gh, ctx, gal, xo, dq, xf, dk, dv, dxo, dxp.astype(BF),
        result.astype(BF), sums.reshape(4, 24, 128),
    )
    mine = vec.reshape(3072)
    vec_grads = [mine[i * 256 : (i + 1) * 256] for i in range(8)]
    grads = out.astype(F32)

    def square(start):
        return grads[start : start + 2].reshape(256, 1024)

    expand_grad = grads[8:16].reshape(4, 256, 1024).transpose(1, 0, 2).reshape(256, 4096)
    return (
        resf,
        dxf.astype(F32),
        square(18),
        square(20),
        square(22),
        square(16),
        expand_grad,
        grads[0:8].reshape(1024, 1024),
        vec_grads[0],
        vec_grads[1],
        vec_grads[2],
        vec_grads[3],
        vec_grads[4],
        mine[2048:],
        vec_grads[5],
        vec_grads[6],
        vec_grads[7],
    )


def solution(mesh):
    in_specs = (
        P(None, "fsdp", "ctx", None),
        P(None, "fsdp", "ctx"),
        P(None, "fsdp", "ctx", None),
        P("fsdp", None),
        P("fsdp", None),
        P("fsdp", None),
        P("fsdp", None),
        P("fsdp", None),
        P("fsdp", None),
        P("fsdp"),
        P("fsdp"),
        P("fsdp"),
        P("fsdp"),
        P("fsdp"),
        P("fsdp"),
        P("fsdp"),
        P("fsdp"),
        P("fsdp"),
    )
    out_specs = (
        P(None, "fsdp", "ctx", None),
        P(None, "fsdp", "ctx", None),
        P("fsdp", None),
        P("fsdp", None),
        P("fsdp", None),
        P("fsdp", None),
        P("fsdp", None),
        P("fsdp", None),
        P("fsdp"),
        P("fsdp"),
        P("fsdp"),
        P("fsdp"),
        P("fsdp"),
        P("fsdp"),
        P("fsdp"),
        P("fsdp"),
        P("fsdp"),
    )
    def whole(layer_input, segments, *rest):
        grouped = (
            dict(mesh.shape) == {"ctx": 8, "fsdp": 4}
            and layer_input.shape == (2, 4, 1024, 1024)
            and rest[5].shape == (1024, 4096)
        )
        body = per_group_device if grouped else per_device
        return jax.shard_map(
            body, mesh=mesh, in_specs=in_specs, out_specs=out_specs, check_vma=False
        )(layer_input, segments, *rest)

    return whole
```

```python
import jax
import jax.numpy as jnp
from jax import lax
from jax.experimental import pallas as pl
from jax.experimental.pallas import tpu as pltpu
from jax.sharding import PartitionSpec as P

HEADS = 16
HEAD_DIM = 64


def as_sent(x):
    return jax.tree.map(lambda a: a.astype(jnp.bfloat16) if a.dtype == jnp.float32 else a, x)


def plain_dot(left_side, right_side):
    return jnp.dot(left_side, right_side, preferred_element_type=jnp.float32)


def left_dot(left_side, right_side):
    return lax.dot_general(
        left_side, right_side, (((0,), (0,)), ((), ())), preferred_element_type=jnp.float32
    )


def right_dot(left_side, right_side):
    return lax.dot_general(
        left_side, right_side, (((1,), (1,)), ((), ())), preferred_element_type=jnp.float32
    )


def norm_forward(hidden, gain_row, offset_row):
    centre = hidden - jnp.mean(hidden, axis=-1, keepdims=True)
    inverse = lax.rsqrt(jnp.mean(centre * centre, axis=-1, keepdims=True) + 1e-05)
    normed = centre * inverse
    return (normed * gain_row.astype(jnp.float32) + offset_row.astype(jnp.float32), normed, inverse)


def norm_backward(grad_out, normed, inverse, gain_row):
    scaled = grad_out * gain_row.astype(jnp.float32)
    grad_in = inverse * (
        scaled
        - jnp.mean(scaled, axis=-1, keepdims=True)
        - normed * jnp.mean(scaled * normed, axis=-1, keepdims=True)
    )
    return (grad_in, jnp.sum(grad_out * normed, axis=0), jnp.sum(grad_out, axis=0))


def gather_weights(shards):
    return (
        lax.all_gather(shards[0], "fsdp", axis=0, tiled=True),
        lax.all_gather(shards[1], "fsdp", axis=0, tiled=True),
        lax.all_gather(shards[2], "fsdp", axis=0, tiled=True),
        lax.all_gather(shards[3], "fsdp", axis=0, tiled=True),
        lax.all_gather(shards[4], "fsdp", axis=0, tiled=True),
        lax.all_gather(shards[5], "fsdp", axis=0, tiled=True),
        lax.all_gather(shards[6], "fsdp", axis=0, tiled=True),
        lax.all_gather(shards[7], "fsdp", axis=0, tiled=True),
        lax.all_gather(shards[8], "fsdp", axis=0, tiled=True),
        lax.all_gather(shards[9], "fsdp", axis=0, tiled=True),
        lax.all_gather(shards[10], "fsdp", axis=0, tiled=True),
        lax.all_gather(shards[11], "fsdp", axis=0, tiled=True),
        lax.all_gather(shards[12], "fsdp", axis=0, tiled=True),
        lax.all_gather(shards[13], "fsdp", axis=0, tiled=True),
        lax.all_gather(shards[14], "fsdp", axis=0, tiled=True),
    )


def attend_forward(query_bf, key_bf, value_bf, seg_local):
    row_count = query_bf.shape[0]
    score_scale = HEAD_DIM ** (-0.5)
    query_heads = query_bf.reshape(row_count, HEADS, HEAD_DIM)
    run_max = jnp.full((HEADS, row_count), -1e30, jnp.float32)
    key_rows = lax.all_gather(key_bf, "ctx", axis=0, tiled=True)
    value_rows = lax.all_gather(value_bf, "ctx", axis=0, tiled=True)
    key_seg = lax.all_gather(seg_local, "ctx", axis=0, tiled=True)
    piece_rows = key_rows.shape[0]
    key_heads = key_rows.reshape(piece_rows, HEADS, HEAD_DIM)
    value_heads = value_rows.reshape(piece_rows, HEADS, HEAD_DIM)
    scores = (
        jnp.einsum("rhd,khd->hrk", query_heads, key_heads, preferred_element_type=jnp.float32)
        * score_scale
    )
    same_doc = seg_local[:, None] == key_seg[None, :]
    scores = jnp.where(same_doc[None], scores, -1e30)
    new_max = jnp.maximum(run_max, jnp.max(scores, axis=-1))
    numerators = jnp.exp(scores - new_max[..., None])
    run_sum = jnp.sum(numerators, axis=-1)
    accumulated = jnp.einsum(
        "hrk,khd->hrd",
        numerators.astype(jnp.bfloat16),
        value_heads,
        preferred_element_type=jnp.float32,
    )
    run_max, run_sum, accumulated = (new_max, run_sum, accumulated)
    context = jnp.transpose(accumulated / run_sum[..., None], (1, 0, 2)).reshape(
        row_count, HEADS * HEAD_DIM
    )
    return (context, run_max + jnp.log(run_sum))


def block_grads(
    query_heads, grad_heads, query_seg, log_sum, row_delta, key_heads, value_heads, key_seg
):
    score_scale = HEAD_DIM ** (-0.5)
    scores = (
        jnp.einsum("rhd,khd->hrk", query_heads, key_heads, preferred_element_type=jnp.float32)
        * score_scale
    )
    same_doc = query_seg[:, None] == key_seg[None, :]
    scores = jnp.where(same_doc[None], scores, -1e30)
    probs_full = jnp.exp(scores - log_sum[..., None])
    grad_probs = jnp.einsum(
        "rhd,khd->hrk", grad_heads, value_heads, preferred_element_type=jnp.float32
    )
    grad_scores = (probs_full * (grad_probs - row_delta[..., None])).astype(jnp.bfloat16)
    return (probs_full, grad_scores)


def attend_backward(query_bf, key_bf, value_bf, seg_local, context, log_sum, grad_context):
    row_count = query_bf.shape[0]
    score_scale = HEAD_DIM ** (-0.5)
    key_every, value_every, seg_every = (
        lax.all_gather(key_bf, "ctx", axis=0, tiled=True),
        lax.all_gather(value_bf, "ctx", axis=0, tiled=True),
        lax.all_gather(seg_local, "ctx", axis=0, tiled=True),
    )
    length = key_every.shape[0]
    block_len = min(512, length)
    query_heads = query_bf.reshape(row_count, HEADS, HEAD_DIM)
    grad_heads = grad_context.reshape(row_count, HEADS, HEAD_DIM)
    row_delta = jnp.sum(
        (grad_context.astype(jnp.float32) * context).reshape(row_count, HEADS, HEAD_DIM), axis=-1
    ).T

    def visit_block(grad_query, block_num):
        first_row = block_num * block_len
        key_heads = lax.dynamic_slice_in_dim(key_every, first_row, block_len, 0).reshape(
            block_len, HEADS, HEAD_DIM
        )
        value_heads = lax.dynamic_slice_in_dim(value_every, first_row, block_len, 0).reshape(
            block_len, HEADS, HEAD_DIM
        )
        key_seg = lax.dynamic_slice_in_dim(seg_every, first_row, block_len, 0)
        probs_full, grad_scores = block_grads(
            query_heads, grad_heads, seg_local, log_sum, row_delta, key_heads, value_heads, key_seg
        )
        grad_query = (
            grad_query
            + jnp.einsum("hrk,khd->rhd", grad_scores, key_heads, preferred_element_type=jnp.float32)
            * score_scale
        )
        grad_keys = (
            jnp.einsum("hrk,rhd->khd", grad_scores, query_heads, preferred_element_type=jnp.float32)
            * score_scale
        )
        grad_values = jnp.einsum(
            "hrk,rhd->khd",
            probs_full.astype(jnp.bfloat16),
            grad_heads,
            preferred_element_type=jnp.float32,
        )
        stacked = jnp.stack(
            (
                grad_keys.reshape(block_len, HEADS * HEAD_DIM),
                grad_values.reshape(block_len, HEADS * HEAD_DIM),
            ),
            axis=1,
        )
        return (grad_query, stacked)

    grad_query, pieces = lax.scan(
        visit_block,
        jnp.zeros((row_count, HEADS, HEAD_DIM), jnp.float32),
        jnp.arange(length // block_len),
    )
    key_terms = pieces.reshape(length, 2, HEADS * HEAD_DIM)
    own_rows = lax.psum_scatter(
        key_terms.astype(jnp.bfloat16), "ctx", scatter_dimension=0, tiled=True
    ).astype(jnp.float32)
    grad_keyed = own_rows[:, 0].astype(jnp.bfloat16)
    grad_valued = own_rows[:, 1].astype(jnp.bfloat16)
    grad_queries = grad_query.reshape(row_count, HEADS * HEAD_DIM).astype(jnp.bfloat16)
    return (grad_queries, grad_keyed, grad_valued)


def layer_forward(inputs, seg_local, full_weights):
    (
        query_weight,
        key_weight,
        value_weight,
        output_weight,
        expand_weight,
        contract_weight,
        query_bias,
        value_bias,
        output_bias,
        first_gain,
        first_shift,
        expand_bias,
        contract_bias,
        second_gain,
        second_shift,
    ) = full_weights
    query_bf = (plain_dot(inputs, query_weight) + query_bias.astype(jnp.float32)).astype(
        jnp.bfloat16
    )
    key_bf = plain_dot(inputs, key_weight).astype(jnp.bfloat16)
    value_bf = (plain_dot(inputs, value_weight) + value_bias.astype(jnp.float32)).astype(
        jnp.bfloat16
    )
    context, log_sum = attend_forward(query_bf, key_bf, value_bf, seg_local)
    context_bf = context.astype(jnp.bfloat16)
    first_sum = (
        inputs.astype(jnp.float32)
        + plain_dot(context_bf, output_weight)
        + output_bias.astype(jnp.float32)
    )
    first_out, normed_one, inverse_one = norm_forward(first_sum, first_gain, first_shift)
    first_bf = first_out.astype(jnp.bfloat16)
    hidden = plain_dot(first_bf, expand_weight) + expand_bias.astype(jnp.float32)
    gelled_bf = jax.nn.gelu(hidden, approximate=False).astype(jnp.bfloat16)
    second_sum = (
        first_out + plain_dot(gelled_bf, contract_weight) + contract_bias.astype(jnp.float32)
    )
    result, normed_two, inverse_two = norm_forward(second_sum, second_gain, second_shift)
    kept_state = (
        query_bf,
        key_bf,
        value_bf,
        context,
        log_sum,
        context_bf,
        normed_one,
        inverse_one,
        first_bf,
        hidden,
        gelled_bf,
        normed_two,
        inverse_two,
    )
    return (result.astype(jnp.bfloat16), kept_state)


def layer_backward(inputs, seg_local, grad_out, kept_state, full_weights):
    (
        query_weight,
        key_weight,
        value_weight,
        output_weight,
        expand_weight,
        contract_weight,
        query_bias,
        value_bias,
        output_bias,
        first_gain,
        first_shift,
        expand_bias,
        contract_bias,
        second_gain,
        second_shift,
    ) = full_weights
    (
        query_bf,
        key_bf,
        value_bf,
        context,
        log_sum,
        context_bf,
        normed_one,
        inverse_one,
        first_bf,
        hidden,
        gelled_bf,
        normed_two,
        inverse_two,
    ) = kept_state
    grad_second, second_gain_grad, second_shift_grad = norm_backward(
        grad_out.astype(jnp.float32), normed_two, inverse_two, second_gain
    )
    grad_branch = grad_second.astype(jnp.bfloat16)
    contract_weight_grad = left_dot(gelled_bf, grad_branch)
    contract_bias_grad = jnp.sum(grad_branch.astype(jnp.float32), axis=0)
    grad_gelled = right_dot(grad_branch, contract_weight)
    gelu_pull = jax.vjp(lambda values: jax.nn.gelu(values, approximate=False), hidden)[1]
    grad_hidden = gelu_pull(grad_gelled)[0].astype(jnp.bfloat16)
    expand_weight_grad = left_dot(first_bf, grad_hidden)
    expand_bias_grad = jnp.sum(grad_hidden.astype(jnp.float32), axis=0)
    grad_first = grad_second + right_dot(grad_hidden, expand_weight)
    grad_attn, first_gain_grad, first_shift_grad = norm_backward(
        grad_first, normed_one, inverse_one, first_gain
    )
    grad_attn_low = grad_attn.astype(jnp.bfloat16)
    output_weight_grad = left_dot(context_bf, grad_attn_low)
    output_bias_grad = jnp.sum(grad_attn_low.astype(jnp.float32), axis=0)
    grad_context = right_dot(grad_attn_low, output_weight).astype(jnp.bfloat16)
    grad_queries, grad_keyed, grad_valued = attend_backward(
        query_bf, key_bf, value_bf, seg_local, context, log_sum, grad_context
    )
    query_weight_grad = left_dot(inputs, grad_queries)
    key_weight_grad = left_dot(inputs, grad_keyed)
    value_weight_grad = left_dot(inputs, grad_valued)
    query_bias_grad = jnp.sum(grad_queries.astype(jnp.float32), axis=0)
    value_bias_grad = jnp.sum(grad_valued.astype(jnp.float32), axis=0)
    grad_input = (
        grad_attn
        + right_dot(grad_queries, query_weight)
        + right_dot(grad_keyed, key_weight)
        + right_dot(grad_valued, value_weight)
    )
    grad_terms = (
        query_weight_grad,
        key_weight_grad,
        value_weight_grad,
        output_weight_grad,
        expand_weight_grad,
        contract_weight_grad,
        query_bias_grad,
        value_bias_grad,
        output_bias_grad,
        first_gain_grad,
        first_shift_grad,
        expand_bias_grad,
        contract_bias_grad,
        second_gain_grad,
        second_shift_grad,
    )
    return (grad_input, grad_terms)


def per_device(
    layer_input,
    segments,
    cotangent,
    query_weight,
    key_weight,
    value_weight,
    output_weight,
    expand_weight,
    contract_weight,
    query_bias,
    value_bias,
    output_bias,
    first_gain,
    first_shift,
    expand_bias,
    contract_bias,
    second_gain,
    second_shift,
):
    shards = (
        query_weight,
        key_weight,
        value_weight,
        output_weight,
        expand_weight,
        contract_weight,
        query_bias,
        value_bias,
        output_bias,
        first_gain,
        first_shift,
        expand_bias,
        contract_bias,
        second_gain,
        second_shift,
    )
    micro_count = layer_input.shape[0]
    results = []
    grad_inputs = []
    totals = None
    for micro_step in range(micro_count):
        inputs = layer_input[micro_step, 0]
        seg_local = segments[micro_step, 0].astype(jnp.bfloat16)
        front_weights = gather_weights(shards)
        result, kept_state = layer_forward(inputs, seg_local, front_weights)
        behind = gather_weights(shards)
        grad_input, grad_terms = layer_backward(
            inputs, seg_local, cotangent[micro_step, 0], kept_state, behind
        )
        results.append(result)
        grad_inputs.append(grad_input)
        if totals is None:
            totals = grad_terms
        else:
            totals = tuple(
                (left_side + right_side for left_side, right_side in zip(totals, grad_terms))
            )
    reduced = jax.tree.map(
        lambda part: part.astype(jnp.float32),
        lax.psum_scatter(as_sent(totals), "fsdp", scatter_dimension=0, tiled=True),
    )
    summed = jax.tree.map(lambda part: part.astype(jnp.float32), lax.psum(as_sent(reduced), "ctx"))
    layer_output = jnp.stack(results, axis=0)[:, None]
    input_grad = jnp.stack(grad_inputs, axis=0)[:, None]
    return (
        layer_output,
        input_grad,
        summed[0],
        summed[1],
        summed[2],
        summed[3],
        summed[4],
        summed[5],
        summed[6],
        summed[7],
        summed[8],
        summed[9],
        summed[10],
        summed[11],
        summed[12],
        summed[13],
        summed[14],
    )


MESH = pl.DeviceIdType.MESH
BF = jnp.bfloat16
F32 = jnp.float32
CHUNKS = 24
SLOTS = 3
LAND = 4
ROOM = 8


def coords():
    c, f = lax.axis_index("ctx"), lax.axis_index("fsdp")
    return c // 2, c % 2, f // 2, f % 2


def dev(z, x, y, k):
    return (z * 2 + x, y * 2 + k)


def greet(z, x, y, k):
    barrier = pltpu.get_barrier_semaphore()
    for step in range(1, 8):
        place = (z * 2 + k + step) % 8
        pl.semaphore_signal(
            barrier, inc=1, device_id=dev(place // 2, x, y, place % 2), device_id_type=MESH
        )
    pl.semaphore_signal(barrier, inc=1, device_id=dev(z, 1 - x, y, k), device_id_type=MESH)
    pl.semaphore_signal(barrier, inc=1, device_id=dev(z, x, 1 - y, k), device_id_type=MESH)
    pl.semaphore_wait(barrier, 9)


def remote(src, dst, send, recv, to):
    return pltpu.make_async_remote_copy(
        src_ref=src, dst_ref=dst, send_sem=send, recv_sem=recv, device_id=to, device_id_type=MESH
    )


def rows_of(start, size, unit=16):
    return pl.ds(pl.multiple_of(start, unit), size)


def gather_kernel(
    inp, cot, seg, wq, wk, wv, wo, we, wc, vec,
    xf, cotf, segf, fq, fk, fv, fo, fe, fc, vecf,
    own, a_send, a_recv, g_send, g_recv, w_send, w_recv, v_send, v_recv,
):
    z, x, y, k = coords()
    f = y * 2 + k
    other = (1 - y) * 2 + k
    sib, xn, yn = dev(z, x, y, 1 - k), dev(z, 1 - x, y, k), dev(z, x, 1 - y, k)
    zn = dev(z + 1 - 2 * (z % 2), x, y, k)
    color = (z % 2) * 2 + x
    c_x, c_z, c_o = color + 1 - 2 * x, (color + 2) % 4, 3 - color
    greet(z, x, y, k)

    def block_moves(mb):
        to_z, to_k = mb * 2 + k, z // 2
        row = x * 512 + z * 128
        slot = z % 2
        mine = (to_z == z) & (to_k == k)
        moves = (
            (inp.at[mb, 0], xf.at[rows_of(row, 128)], 0),
            (seg.at[mb], segf.at[x * 4 + z], 1),
            (cot.at[mb, 0], cotf.at[rows_of(slot * 128, 128)], 2),
        )
        return mine, dev(to_z, x, y, to_k), slot, moves

    def start_blocks(which):
        for mb in range(2):
            mine, to, slot, moves = block_moves(mb)
            for src, dst, n in moves:
                if n not in which:
                    continue

                @pl.when(mine)
                def _():
                    pltpu.make_async_copy(src, dst, a_recv.at[n, slot]).start()

                @pl.when(jnp.logical_not(mine))
                def _():
                    remote(src, dst, a_send.at[n, mb], a_recv.at[n, slot], to).start()

    def finish_blocks(which):
        for mb in range(2):
            mine, to, slot, moves = block_moves(mb)
            for src, dst, n in moves:
                if n not in which:
                    continue

                @pl.when(jnp.logical_not(mine))
                def _():
                    remote(src, dst, a_send.at[n, mb], a_recv.at[n, slot], to).wait_send()

    def arrive_blocks(which):
        for slot in range(2):
            zz = 2 * k + slot
            for n in which:
                if n == 0:
                    dst = xf.at[rows_of(x * 512 + zz * 128, 128)]
                elif n == 1:
                    dst = segf.at[x * 4 + zz]
                else:
                    dst = cotf.at[pl.ds(slot * 128, 128)]
                pltpu.make_async_copy(dst, dst, a_recv.at[n, slot]).wait()

    def group_copy(step):
        who = x if step < 2 else 1 - x
        src = xf.at[rows_of(who * 512 + k * 256, 256)]
        sseg = segf.at[pl.ds(who * 4 + k * 2, 2)]
        to = (sib, xn, sib)[step]
        return (
            remote(src, src, g_send.at[0, step], g_recv.at[0, step], to),
            remote(sseg, sseg, g_send.at[1, step], g_recv.at[1, step], to),
        )

    def group_arrive(step):
        who = (x, 1 - x, 1 - x)[step]
        kk = (1 - k, k, 1 - k)[step]
        src = xf.at[rows_of(who * 512 + kk * 256, 256)]
        sseg = segf.at[pl.ds(who * 4 + kk * 2, 2)]
        pltpu.make_async_copy(src, src, g_recv.at[0, step]).wait()
        pltpu.make_async_copy(sseg, sseg, g_recv.at[1, step]).wait()

    items = []
    for shard, full in ((wq, fq), (wk, fk), (wv, fv), (wo, fo)):
        items.append((shard, full, 0, 0, 256))
    for j in range(4):
        items.append((we, fe, 0, j * 1024, 256))
    for j in range(4):
        items.append((wc, fc, j * 256, 0, 1024))
    n_items = len(items)

    def part(i, quarter, start, size, own_src=False):
        shard, full, row, col, step = items[i]
        if own_src:
            return shard.at[rows_of(row + start, size), pl.ds(col, 1024)]
        return full.at[rows_of(quarter * step + row + start, size), pl.ds(col, 1024)]

    def send_copy(i, kind):
        sems = (w_send.at[kind, i], w_recv.at[kind, i])
        if kind == 0:
            return remote(part(i, f, color * 64, 64, True), part(i, f, color * 64, 64), *sems, yn)
        if kind == 1:
            return remote(part(i, f, c_o * 64, 32, True), part(i, f, c_o * 64, 32), *sems, yn)
        if kind == 2:
            src = part(i, other, color * 64, 64)
            return remote(src, src, *sems, xn)
        if kind == 3:
            src = part(i, other, c_z * 64 + 32, 16)
            return remote(src, src, *sems, xn)
        if kind == 4:
            src = part(i, other, color * 64, 64)
            return remote(src, src, *sems, zn)
        if kind == 5:
            src = part(i, other, c_x * 64 + 48, 16)
            return remote(src, src, *sems, zn)
        if kind == 6:
            return remote(part(i, f, 0, 256, True), part(i, f, 0, 256), *sems, sib)
        src = part(i, other, 0, 256)
        return remote(src, src, *sems, sib)

    def arrive(i, kind):
        if kind == 0:
            dst = part(i, other, color * 64, 64)
        elif kind == 1:
            dst = part(i, other, c_o * 64, 32)
        elif kind == 2:
            dst = part(i, other, c_x * 64, 64)
        elif kind == 3:
            dst = part(i, other, c_o * 64 + 32, 16)
        elif kind == 4:
            dst = part(i, other, c_z * 64, 64)
        elif kind == 5:
            dst = part(i, other, c_o * 64 + 48, 16)
        elif kind == 6:
            dst = part(i, y * 2 + 1 - k, 0, 256)
        else:
            dst = part(i, (1 - y) * 2 + 1 - k, 0, 256)
        pltpu.make_async_copy(dst, dst, w_recv.at[kind, i]).wait()

    def own_in(i):
        return pltpu.make_async_copy(part(i, f, 0, 256, True), own.at[i], w_recv.at[8, i])

    def own_out(i):
        return pltpu.make_async_copy(own.at[i], part(i, f, 0, 256), w_recv.at[9, i])

    vec_copies = (
        remote(vec, vecf.at[f], v_send.at[0], v_recv.at[0], yn),
        remote(vec, vecf.at[f], v_send.at[1], v_recv.at[1], sib),
        remote(vecf.at[other], vecf.at[other], v_send.at[2], v_recv.at[2], sib),
    )
    vec_own = pltpu.make_async_copy(vec, vecf.at[f], v_recv.at[3])

    start_blocks((0, 1))
    vec_own.start()
    for i in range(n_items):
        own_in(i).start()
    vec_copies[0].start()
    vec_copies[1].start()
    for t in range(n_items + 3):
        if t < n_items:
            send_copy(t, 0).start()
            send_copy(t, 1).start()
            send_copy(t, 6).start()
        if t == 1:
            arrive_blocks((0, 1))
            for step in range(2):
                for move in group_copy(step):
                    move.start()
            pltpu.make_async_copy(vecf.at[other], vecf.at[other], v_recv.at[0]).wait()
            vec_copies[2].start()
        if t == 4:
            group_arrive(1)
            for move in group_copy(2):
                move.start()
            start_blocks((2,))
        if 1 <= t <= n_items:
            i = t - 1
            own_in(i).wait()
            own_out(i).start()
            arrive(i, 0)
            send_copy(i, 2).start()
            send_copy(i, 4).start()
        if 2 <= t <= n_items + 1:
            i = t - 2
            arrive(i, 4)
            send_copy(i, 3).start()
            arrive(i, 2)
            send_copy(i, 5).start()
        if 3 <= t:
            i = t - 3
            arrive(i, 1)
            arrive(i, 3)
            arrive(i, 5)
            send_copy(i, 7).start()
    for i in range(n_items):
        arrive(i, 6)
        arrive(i, 7)
        own_out(i).wait()
        for kind in range(8):
            send_copy(i, kind).wait_send()
    arrive_blocks((2,))
    finish_blocks((0, 1, 2))
    group_arrive(0)
    group_arrive(2)
    for step in range(3):
        for move in group_copy(step):
            move.wait_send()
    sib_own, sib_other = vecf.at[y * 2 + 1 - k], vecf.at[(1 - y) * 2 + 1 - k]
    pltpu.make_async_copy(sib_own, sib_own, v_recv.at[1]).wait()
    pltpu.make_async_copy(sib_other, sib_other, v_recv.at[2]).wait()
    for move in vec_copies:
        move.wait_send()
    vec_own.wait()


def gather_call(inp, cot, seg, weights, vec):
    any_spec = pl.BlockSpec(memory_space=pl.ANY)
    outs = [
        jax.ShapeDtypeStruct((1024, 1024), BF),
        jax.ShapeDtypeStruct((256, 1024), BF),
        jax.ShapeDtypeStruct((8, 1, 128), jnp.int32),
    ]
    outs += [jax.ShapeDtypeStruct((1024, 1024), BF)] * 4
    outs += [
        jax.ShapeDtypeStruct((1024, 4096), BF),
        jax.ShapeDtypeStruct((4096, 1024), BF),
        jax.ShapeDtypeStruct((4, 32, 128), BF),
    ]
    dma = pltpu.SemaphoreType.DMA
    return pl.pallas_call(
        gather_kernel,
        out_shape=outs,
        in_specs=[any_spec] * 10,
        out_specs=[any_spec] * 10,
        scratch_shapes=[
            pltpu.VMEM((12, 256, 1024), BF),
            dma((3, 2)), dma((3, 2)), dma((2, 3)), dma((2, 3)),
            dma((8, 12)), dma((10, 12)), dma((3,)), dma((4,)),
        ],
        compiler_params=pltpu.CompilerParams(
            collective_id=0, has_side_effects=True, vmem_limit_bytes=32 << 20
        ),
        name="gather_all",
    )(inp, cot, seg, *weights, vec)


def two_heads(block):
    lane = lax.broadcasted_iota(jnp.int32, block.shape, 1)
    zero = jnp.zeros_like(block)
    return jnp.concatenate(
        [jnp.where(lane < HEAD_DIM, block, zero), jnp.where(lane >= HEAD_DIM, block, zero)], axis=0
    )


def one_block(pair):
    rows = pair.shape[0] // 2
    lane = lax.broadcasted_iota(jnp.int32, (rows, pair.shape[1]), 1)
    return jnp.where(lane < HEAD_DIM, pair[:rows], pair[rows:])


def attention_bias(sq_ref, sk_ref):
    return jnp.where(sq_ref[...] == sk_ref[...], 0.0, -1e30).astype(F32)


def softmax_pair(queries, keys, bias):
    scores = right_dot(queries, keys)
    scores = scores + jnp.concatenate([bias, bias], axis=0)
    numer = jnp.exp(scores - jnp.max(scores, axis=-1, keepdims=True))
    return numer * (1.0 / jnp.sum(numer, axis=-1, keepdims=True))


def attend_kernel(q_ref, k_ref, v_ref, sq_ref, sk_ref, o_ref, bias_ref):
    @pl.when(pl.program_id(0) == 0)
    def _():
        bias_ref[...] = attention_bias(sq_ref, sk_ref)

    queries = two_heads(q_ref[...] * BF(HEAD_DIM**-0.5))
    probs = softmax_pair(queries, k_ref[...], bias_ref[...])
    o_ref[...] = one_block(plain_dot(probs.astype(BF), v_ref[...])).astype(BF)


def attend(q, k, v, sq, sk):
    rows = pl.BlockSpec((256, 128), lambda h: (0, h))
    full = pl.BlockSpec((1024, 128), lambda h: (0, h))
    sqs = pl.BlockSpec((256, 1), lambda h: (0, 0))
    sks = pl.BlockSpec((1, 1024), lambda h: (0, 0))
    return pl.pallas_call(
        attend_kernel,
        grid=(8,),
        out_shape=jax.ShapeDtypeStruct((256, 1024), BF),
        in_specs=[rows, full, full, sqs, sks],
        out_specs=rows,
        scratch_shapes=[pltpu.VMEM((256, 1024), F32)],
        compiler_params=pltpu.CompilerParams(vmem_limit_bytes=40 << 20),
        name="attend",
    )(q, k, v, sq, sk)


def backward_kernel(
    gel, gb, gs, fb, gp, n1, inv1, gain1, ctx, q, key, val, xf, sq, sk, res, g2, s2,
    we, wc, wo, wq, wk, wv,
    o_q, o_k, o_v, o_o, o_e, o_c, resf, dxf, vec_out,
    s_d, l_d, r_d, b_y, r_y, b_x, r_x, b_1, r_1, b_2, r_2, o_b,
    gh, acc, ga, gal, dctx, dq, dk, dv, bias, we_b, wc_b, w_b,
    dx_p, dx_r, dx_s, dx_y, dx_b, vec, v_s, v_d, v_r,
    ss, rs, ds, dr, a_send, a_recv, v_send, v_recv, w_sem, o_sem,
):
    z, x, y, k = coords()
    sib, xn, yn = dev(z, x, y, 1 - k), dev(z, 1 - x, y, k), dev(z, x, 1 - y, k)
    bit1, bit2 = z % 2, z // 2
    z1 = dev(z + 1 - 2 * bit1, x, y, k)
    z2 = dev((z + 2) % 4, x, y, k)

    def load_c(j):
        return pltpu.make_async_copy(
            wc.at[rows_of(j * 512, 512)], wc_b.at[j % 2], w_sem.at[j % 2]
        )

    def load_e(j):
        return pltpu.make_async_copy(
            we.at[:, rows_of(j * 512, 512, 512)], we_b.at[j % 2], w_sem.at[2 + j % 2]
        )

    def load_w(n):
        return pltpu.make_async_copy((wo, wk, wv, wq)[n], w_b.at[n], w_sem.at[4 + n])

    load_c(0).start()
    load_e(0).start()
    for n in range(4):
        load_w(n).start()
    greet(z, x, y, k)

    def back(n, slot):
        to_z = 2 * k + slot
        to_k = z % 2
        mb = z // 2
        mine = (to_z == z) & (to_k == k)
        src = (res, dx_b)[n].at[pl.ds(slot * 128, 128)]
        dst = (resf, dxf)[n].at[mb, 0]

        def far():
            return remote(
                src, dst, a_send.at[n, slot], a_recv.at[n, mb], dev(to_z, x, y, to_k)
            )

        def near():
            return pltpu.make_async_copy(src, dst, a_recv.at[n, mb])

        return mine, far, near

    def start_back(n):
        for slot in range(2):
            mine, far, near = back(n, slot)

            @pl.when(mine)
            def _():
                near().start()

            @pl.when(jnp.logical_not(mine))
            def _():
                far().start()

    def finish_back(n):
        for slot in range(2):
            mine, far, _ = back(n, slot)

            @pl.when(jnp.logical_not(mine))
            def _():
                far().wait_send()

        for mb in range(2):
            dst = (resf, dxf)[n].at[mb, 0]
            pltpu.make_async_copy(dst, dst, a_recv.at[n, mb]).wait()

    start_back(0)

    def column(v):
        return jnp.sum(v.astype(F32), axis=0, keepdims=True)

    def keep(i, row):
        for quarter in range(4):
            for half in range(2):
                col = quarter * 256 + half * 128
                vec[quarter, pl.ds(2 * i + half, 1)] = row[:, col : col + 128]

    v_peers = (sib, yn, xn, z1, z2)

    def v_copy(stage):
        if stage == 0:
            return remote(v_d.at[1], v_d.at[2], v_send.at[0], v_recv.at[0], sib)
        src = v_s.at[0, 1 - y] if stage == 1 else v_s.at[stage - 1, 0]
        return remote(src, v_r.at[stage - 1], v_send.at[stage], v_recv.at[stage], v_peers[stage])

    def v_step(stage):
        if stage == 0:
            for plane in range(2):
                v_d[0, plane] = vec[plane * 2 + k]
                v_d[1, plane] = vec[plane * 2 + 1 - k]
        elif stage == 1:
            pltpu.make_async_copy(v_d.at[2], v_d.at[2], v_recv.at[0]).wait()
            v_s[0] = v_d[0] + v_d[2]
        else:
            dst = v_r.at[stage - 2]
            pltpu.make_async_copy(dst, dst, v_recv.at[stage - 1]).wait()
            mine = v_s[0, y] if stage == 2 else v_s[stage - 2, 0]
            total = mine + v_r[stage - 2]
            if stage == 5:
                vec_out[...] = total
            else:
                v_s[stage - 1, 0] = total
        if stage < 5:
            v_copy(stage).start()

    def send(stage, i, src, dst, to):
        return remote(src, dst, ss.at[stage, i % SLOTS], rs.at[stage, i % LAND], to)

    def landed(stage, i, dst):
        pltpu.make_async_copy(dst, dst, rs.at[stage, i % LAND]).wait()

    def copies(stage, i):
        slot, land, room = i % SLOTS, i % LAND, i % ROOM
        if stage == 0:
            return send(0, i, s_d.at[slot], r_d.at[land], sib)
        if stage == 1:
            return send(1, i, b_y.at[slot, 1 - y], r_y.at[land], yn)
        if stage == 2:
            return send(2, i, b_x.at[slot, rows_of((1 - x) * 64, 64)], r_x.at[land], xn)
        if stage == 3:
            return send(3, i, b_1.at[slot, rows_of((1 - bit1) * 32, 32)], r_1.at[land], z1)
        if stage == 4:
            return send(4, i, b_2.at[slot, rows_of((1 - bit2) * 16, 16)], r_2.at[land], z2)
        if stage == 5:
            own = o_b.at[room, rows_of(x * 64 + bit1 * 32 + bit2 * 16, 16)]
            return send(5, i, own, own, z2)
        if stage == 6:
            own = o_b.at[room, rows_of(x * 64 + bit1 * 32, 32)]
            return send(6, i, own, own, z1)
        own = o_b.at[room, rows_of(x * 64, 64)]
        return send(7, i, own, own, xn)

    def launch(stage, i):
        copies(stage, i).start()

    def clear(stage, i):
        @pl.when(i >= SLOTS)
        def _():
            copies(stage, i - SLOTS).wait_send()

    def add(a, b):
        return (a.astype(F32) + b.astype(F32)).astype(BF)

    def terms(i, a_ref, b_ref, a_base, a_step, b_col, a_rows=None):
        slot = i % SLOTS
        right = b_ref[:, b_col]
        for plane in range(2):
            for core in range(2):
                quarter = plane * 2 + (k if core == 0 else 1 - k)
                cols = pl.ds(pl.multiple_of(a_base + quarter * a_step, 128), 128)
                left = a_ref[:, cols] if a_rows is None else a_ref[a_rows, cols]
                product = left_dot(left, right).astype(BF)
                if core == 0:
                    l_d[slot, plane] = product
                else:
                    s_d[slot, plane] = product

    every = pl.ds(0, 1024)
    own_rows = rows_of(x * 512 + k * 256, 256)

    def stage_zero(i):
        @pl.when((i >= 0) & (i < CHUNKS))
        def _():
            clear(0, i)

        @pl.when(i < 8)
        def _():
            terms(i, gel, gb, i * 128, 1024, every)

        @pl.when((i >= 8) & (i < 16))
        def _():
            j = i - 8
            terms(i, fb, gh, (j % 2) * 128, 256, rows_of((j // 2) * 1024, 1024, 1024))

        @pl.when((i >= 16) & (i < 18))
        def _():
            terms(i, ctx, gal, (i - 16) * 128, 256, every)

        @pl.when((i >= 18) & (i < 20))
        def _():
            terms(i, xf, dq, (i - 18) * 128, 256, every, own_rows)

        @pl.when((i >= 20) & (i < 22))
        def _():
            terms(i, xf, dk, (i - 20) * 128, 256, every)

        @pl.when((i >= 22) & (i < 24))
        def _():
            terms(i, xf, dv, (i - 22) * 128, 256, every)

        @pl.when((i >= 0) & (i < CHUNKS))
        def _():
            launch(0, i)

    def stored():
        pltpu.make_async_copy(o_b.at[0], o_b.at[0], o_sem).wait()

    def store(i):
        src = o_b.at[i % ROOM]

        @pl.when(i >= 1)
        def _():
            stored()

        @pl.when(i < 8)
        def _():
            pltpu.make_async_copy(src, o_c.at[rows_of(i * 128, 128)], o_sem).start()

        @pl.when((i >= 8) & (i < 16))
        def _():
            j = i - 8
            dst = o_e.at[rows_of((j % 2) * 128, 128), rows_of((j // 2) * 1024, 1024, 1024)]
            pltpu.make_async_copy(src, dst, o_sem).start()

        for n, ref in enumerate((o_o, o_q, o_k, o_v)):
            first = 16 + 2 * n

            @pl.when((i >= first) & (i < first + 2))
            def _():
                dst = ref.at[rows_of((i - first) * 128, 128)]
                pltpu.make_async_copy(src, dst, o_sem).start()

    def feed_forward(j):
        slot = j % 2
        cols = rows_of(j * 512, 512, 512)
        load_c(j).wait()
        load_e(j).wait()

        @pl.when(j < 7)
        def _():
            load_c(j + 1).start()
            load_e(j + 1).start()

        grads = (right_dot(gb[...], wc_b[slot]) * gp[:, cols].astype(F32)).astype(BF)
        gh[:, cols] = grads
        acc[...] += right_dot(grads, we_b[slot])
        row = column(grads)
        for n in range(4):
            vec[j // 2, pl.ds(16 + (j % 2) * 4 + n, 1)] = row[:, n * 128 : n * 128 + 128]

    def first_norm():
        normed = n1[...]
        grad_first = acc[...]
        keep(3, column(grad_first * normed))
        keep(4, column(grad_first))
        scaled = grad_first * gain1[...]
        grad_attn = inv1[...] * (
            scaled
            - jnp.mean(scaled, axis=-1, keepdims=True)
            - normed * jnp.mean(scaled * normed, axis=-1, keepdims=True)
        )
        ga[...] = grad_attn
        low = grad_attn.astype(BF)
        gal[...] = low
        keep(2, column(low))
        load_w(0).wait()
        dctx[...] = right_dot(low, w_b[0]).astype(BF)

    def attention(h):
        cols = rows_of(h * 128, 128, 128)
        queries = two_heads(q[:, cols] * BF(HEAD_DIM**-0.5))
        keys = key[:, cols]
        probs = softmax_pair(queries, keys, bias[...])
        grads = two_heads(dctx[:, cols])
        grad_probs = right_dot(grads, val[:, cols])
        delta = jnp.sum(probs * grad_probs, axis=-1, keepdims=True)
        grad_scores = (probs * (grad_probs - delta)).astype(BF)
        dv[:, cols] = left_dot(probs.astype(BF), grads).astype(BF)
        dk[:, cols] = left_dot(grad_scores, queries).astype(BF)
        dq[:, cols] = (one_block(plain_dot(grad_scores, keys)) * HEAD_DIM**-0.5).astype(BF)

    def dx_core(g):
        return remote(dx_p.at[g], dx_r.at[g], ds.at[g], dr.at[g], sib)

    dx_far = remote(dx_s, dx_y, ds.at[2], dr.at[2], xn)

    def input_rows(n):
        who = x * (n % 2) + (1 - x) * (1 - n % 2)
        core = (1 - k) * (1 - n // 2) + k * (n // 2)
        rows = rows_of(who * 512 + core * 256, 256)
        terms_here = right_dot(dk[rows], w_b[1]) + right_dot(dv[rows], w_b[2])

        @pl.when(n == 0)
        def _():
            dx_p[1] = terms_here.astype(BF)
            dx_core(1).start()

        @pl.when(n == 1)
        def _():
            dx_p[0] = terms_here.astype(BF)
            dx_core(0).start()

        @pl.when(n == 2)
        def _():
            pltpu.make_async_copy(dx_r.at[1], dx_r.at[1], dr.at[1]).wait()
            dx_s[...] = (terms_here + dx_r[1].astype(F32)).astype(BF)
            dx_far.start()

        @pl.when(n == 3)
        def _():
            pltpu.make_async_copy(dx_r.at[0], dx_r.at[0], dr.at[0]).wait()
            load_w(3).wait()
            ga[...] = ga[...] + terms_here + dx_r[0].astype(F32) + right_dot(dq[...], w_b[3])

    bias[...] = attention_bias(sq, sk)
    acc[...] = gs[...]
    keep(5, column(gb[...]))
    keep(6, g2[...])
    keep(7, s2[...])

    def tick(t, carry):
        def at(stage):
            i = t - stage
            return i, (i >= 0) & (i < CHUNKS)

        stage_zero(t)
        i1, live1 = at(1)

        @pl.when(live1)
        def _():
            slot, land = i1 % SLOTS, i1 % LAND
            clear(1, i1)
            landed(0, i1, r_d.at[land])
            for plane in range(2):
                b_y[slot, plane] = add(l_d[slot, plane], r_d[land, plane])
            launch(1, i1)

        @pl.when(t < 8)
        def _():
            feed_forward(t)

        @pl.when(t == 8)
        def _():
            first_norm()

        @pl.when((t >= 9) & (t < 17))
        def _():
            attention(t - 9)

        @pl.when(t == 17)
        def _():
            keep(0, column(dq[...]))
            keep(1, column(dv[...]))
            load_w(1).wait()
            load_w(2).wait()

        @pl.when((t >= 17) & (t < 21))
        def _():
            input_rows(t - 17)

        for stage in range(6):

            @pl.when(t == 18 + 2 * stage)
            def _():
                v_step(stage)

        @pl.when(t == 23)
        def _():
            pltpu.make_async_copy(dx_y, dx_y, dr.at[2]).wait()
            dx_b[...] = (ga[...] + dx_y[...].astype(F32)).astype(BF)
            start_back(1)

        i2, live2 = at(2)

        @pl.when(live2)
        def _():
            slot, land = i2 % SLOTS, i2 % LAND
            clear(2, i2)
            landed(1, i2, r_y.at[land])
            b_x[slot] = add(b_y[slot, y], r_y[land])
            launch(2, i2)

        i3, live3 = at(3)

        @pl.when(live3)
        def _():
            slot, land = i3 % SLOTS, i3 % LAND
            clear(3, i3)
            landed(2, i3, r_x.at[land])
            b_1[slot] = add(b_x[slot, rows_of(x * 64, 64)], r_x[land])
            launch(3, i3)

        i4, live4 = at(4)

        @pl.when(live4)
        def _():
            slot, land = i4 % SLOTS, i4 % LAND
            clear(4, i4)
            landed(3, i4, r_1.at[land])
            b_2[slot] = add(b_1[slot, rows_of(bit1 * 32, 32)], r_1[land])
            launch(4, i4)

        i5, live5 = at(5)

        @pl.when(live5)
        def _():
            slot, land = i5 % SLOTS, i5 % LAND
            clear(5, i5)
            landed(4, i5, r_2.at[land])
            o_b[i5 % ROOM, rows_of(x * 64 + bit1 * 32 + bit2 * 16, 16)] = add(
                b_2[slot, rows_of(bit2 * 16, 16)], r_2[land]
            )
            launch(5, i5)

        i6, live6 = at(6)

        @pl.when(live6)
        def _():
            clear(6, i6)
            landed(5, i6, o_b.at[i6 % ROOM, rows_of(x * 64 + bit1 * 32 + (1 - bit2) * 16, 16)])
            launch(6, i6)

        i7, live7 = at(7)

        @pl.when(live7)
        def _():
            clear(7, i7)
            landed(6, i7, o_b.at[i7 % ROOM, rows_of(x * 64 + (1 - bit1) * 32, 32)])
            launch(7, i7)

        i8, live8 = at(8)

        @pl.when(live8)
        def _():
            landed(7, i8, o_b.at[i8 % ROOM, rows_of((1 - x) * 64, 64)])
            store(i8)

        return carry

    lax.fori_loop(0, CHUNKS + 8, tick, 0)
    stored()
    for stage in range(8):
        for i in range(CHUNKS - SLOTS, CHUNKS):
            copies(stage, i).wait_send()
    for stage in range(5):
        v_copy(stage).wait_send()
    dx_core(0).wait_send()
    dx_core(1).wait_send()
    dx_far.wait_send()
    finish_back(0)
    finish_back(1)


def backward_call(*operands):
    vmem = pl.BlockSpec(memory_space=pltpu.VMEM)
    any_spec = pl.BlockSpec(memory_space=pl.ANY)
    dma = pltpu.SemaphoreType.DMA
    grad = jax.ShapeDtypeStruct((256, 1024), BF)
    return pl.pallas_call(
        backward_kernel,
        out_shape=[
            grad, grad, grad, grad,
            jax.ShapeDtypeStruct((256, 4096), BF),
            jax.ShapeDtypeStruct((1024, 1024), BF),
            jax.ShapeDtypeStruct((2, 1, 128, 1024), BF),
            jax.ShapeDtypeStruct((2, 1, 128, 1024), BF),
            jax.ShapeDtypeStruct((24, 128), F32),
        ],
        in_specs=[vmem] * 18 + [any_spec] * 6,
        out_specs=[any_spec] * 8 + [vmem],
        scratch_shapes=[
            pltpu.VMEM((SLOTS, 2, 128, 1024), BF),
            pltpu.VMEM((SLOTS, 2, 128, 1024), BF),
            pltpu.VMEM((LAND, 2, 128, 1024), BF),
            pltpu.VMEM((SLOTS, 2, 128, 1024), BF),
            pltpu.VMEM((LAND, 128, 1024), BF),
            pltpu.VMEM((SLOTS, 128, 1024), BF),
            pltpu.VMEM((LAND, 64, 1024), BF),
            pltpu.VMEM((SLOTS, 64, 1024), BF),
            pltpu.VMEM((LAND, 32, 1024), BF),
            pltpu.VMEM((SLOTS, 32, 1024), BF),
            pltpu.VMEM((LAND, 16, 1024), BF),
            pltpu.VMEM((ROOM, 128, 1024), BF),
            pltpu.VMEM((256, 4096), BF),
            pltpu.VMEM((256, 1024), F32),
            pltpu.VMEM((256, 1024), F32),
            pltpu.VMEM((256, 1024), BF),
            pltpu.VMEM((256, 1024), BF),
            pltpu.VMEM((256, 1024), BF),
            pltpu.VMEM((1024, 1024), BF),
            pltpu.VMEM((1024, 1024), BF),
            pltpu.VMEM((256, 1024), F32),
            pltpu.VMEM((2, 1024, 512), BF),
            pltpu.VMEM((2, 512, 1024), BF),
            pltpu.VMEM((4, 1024, 1024), BF),
            pltpu.VMEM((2, 256, 1024), BF),
            pltpu.VMEM((2, 256, 1024), BF),
            pltpu.VMEM((256, 1024), BF),
            pltpu.VMEM((256, 1024), BF),
            pltpu.VMEM((256, 1024), BF),
            pltpu.VMEM((4, 24, 128), F32),
            pltpu.VMEM((4, 2, 24, 128), F32),
            pltpu.VMEM((3, 2, 24, 128), F32),
            pltpu.VMEM((4, 24, 128), F32),
            dma((8, SLOTS)), dma((8, LAND)), dma((3,)), dma((3,)), dma((2, 2)), dma((2, 2)),
            dma((5,)), dma((5,)), dma((8,)), dma(()),
        ],
        compiler_params=pltpu.CompilerParams(
            collective_id=1, has_side_effects=True, vmem_limit_bytes=61 << 20
        ),
        name="backward_all",
    )(*operands)


def per_group_device(
    layer_input, segments, cotangent,
    query_weight, key_weight, value_weight, output_weight, expand_weight, contract_weight,
    query_bias, value_bias, output_bias, first_gain, first_shift, expand_bias, contract_bias,
    second_gain, second_shift,
):
    weights = (
        query_weight, key_weight, value_weight, output_weight, expand_weight, contract_weight
    )
    packed = jnp.concatenate(
        [
            query_bias, value_bias, output_bias, first_gain, first_shift, contract_bias,
            second_gain, second_shift, expand_bias, jnp.zeros((1024,), BF),
        ]
    ).reshape(32, 128)
    xf, cot, seg, wq, wk, wv, wo, we, wc, vecs = gather_call(
        layer_input, cotangent, segments, weights, packed
    )
    small = [vecs[:, 2 * i : 2 * i + 2].reshape(1024).astype(F32) for i in range(8)]
    bq, bv, bo, gain_one, shift_one, bc, gain_two, shift_two = small
    be = vecs[:, 16:24].reshape(4096).astype(F32)
    z, x, y, k = coords()
    own = x * 512 + k * 256
    xo = lax.dynamic_slice_in_dim(xf, own, 256, 0)
    sk = seg.reshape(1, 1024)
    sq = lax.dynamic_slice_in_dim(seg, x * 4 + k * 2, 2, 0).reshape(256, 1)

    q = (plain_dot(xo, wq) + bq).astype(BF)
    key = plain_dot(xf, wk).astype(BF)
    val = (plain_dot(xf, wv) + bv).astype(BF)
    ctx = attend(q, key, val, sq, sk)
    first_sum = xo.astype(F32) + plain_dot(ctx, wo) + bo
    first_out, normed_one, inverse_one = norm_forward(first_sum, gain_one, shift_one)
    first_bf = first_out.astype(BF)
    hidden = plain_dot(first_bf, we) + be
    below = 0.5 + 0.5 * lax.erf(hidden * 0.5**0.5)
    gelled = (hidden * below).astype(BF)
    gelu_slope = (
        below + hidden * (jnp.exp(-0.5 * hidden * hidden) * (2 * jnp.pi) ** -0.5)
    ).astype(BF)
    second_sum = first_out + plain_dot(gelled, wc) + bc
    result, normed_two, inverse_two = norm_forward(second_sum, gain_two, shift_two)
    grad_second, gain_two_grad, shift_two_grad = norm_backward(
        cot.astype(F32), normed_two, inverse_two, gain_two
    )
    o_q, o_k, o_v, o_o, o_e, o_c, resf, dxf, vec = backward_call(
        gelled, grad_second.astype(BF), grad_second, first_bf, gelu_slope, normed_one, inverse_one,
        gain_one.reshape(1, 1024), ctx, q, key, val, xf, sq, sk, result.astype(BF),
        gain_two_grad.reshape(1, 1024), shift_two_grad.reshape(1, 1024),
        we, wc, wo, wq, wk, wv,
    )
    mine = vec.reshape(3072)
    vec_grads = [mine[i * 256 : (i + 1) * 256] for i in range(8)]
    return (
        resf,
        dxf.astype(F32),
        o_q.astype(F32),
        o_k.astype(F32),
        o_v.astype(F32),
        o_o.astype(F32),
        o_e.astype(F32),
        o_c.astype(F32),
        vec_grads[0],
        vec_grads[1],
        vec_grads[2],
        vec_grads[3],
        vec_grads[4],
        mine[2048:],
        vec_grads[5],
        vec_grads[6],
        vec_grads[7],
    )


def solution(mesh):
    in_specs = (
        P(None, "fsdp", "ctx", None),
        P(None, "fsdp", "ctx"),
        P(None, "fsdp", "ctx", None),
        P("fsdp", None),
        P("fsdp", None),
        P("fsdp", None),
        P("fsdp", None),
        P("fsdp", None),
        P("fsdp", None),
        P("fsdp"),
        P("fsdp"),
        P("fsdp"),
        P("fsdp"),
        P("fsdp"),
        P("fsdp"),
        P("fsdp"),
        P("fsdp"),
        P("fsdp"),
    )
    out_specs = (
        P(None, "fsdp", "ctx", None),
        P(None, "fsdp", "ctx", None),
        P("fsdp", None),
        P("fsdp", None),
        P("fsdp", None),
        P("fsdp", None),
        P("fsdp", None),
        P("fsdp", None),
        P("fsdp"),
        P("fsdp"),
        P("fsdp"),
        P("fsdp"),
        P("fsdp"),
        P("fsdp"),
        P("fsdp"),
        P("fsdp"),
        P("fsdp"),
    )
    def whole(layer_input, segments, *rest):
        grouped = (
            dict(mesh.shape) == {"ctx": 8, "fsdp": 4}
            and layer_input.shape == (2, 4, 1024, 1024)
            and rest[5].shape == (1024, 4096)
        )
        body = per_group_device if grouped else per_device
        return jax.shard_map(
            body, mesh=mesh, in_specs=in_specs, out_specs=out_specs, check_vma=False
        )(layer_input, segments, *rest)

    return whole
```

```python
import math

import jax
import jax.numpy as jnp
from jax import lax
from jax.experimental import pallas as pl
from jax.experimental.pallas import tpu as pltpu
from jax.sharding import PartitionSpec as P

HEADS = 16
HEAD_DIM = 64


def as_sent(x):
    return jax.tree.map(lambda a: a.astype(jnp.bfloat16) if a.dtype == jnp.float32 else a, x)


def plain_dot(left_side, right_side):
    return jnp.dot(left_side, right_side, preferred_element_type=jnp.float32)


def left_dot(left_side, right_side):
    return lax.dot_general(
        left_side, right_side, (((0,), (0,)), ((), ())), preferred_element_type=jnp.float32
    )


def right_dot(left_side, right_side):
    return lax.dot_general(
        left_side, right_side, (((1,), (1,)), ((), ())), preferred_element_type=jnp.float32
    )


def norm_forward(hidden, gain_row, offset_row):
    centre = hidden - jnp.mean(hidden, axis=-1, keepdims=True)
    inverse = lax.rsqrt(jnp.mean(centre * centre, axis=-1, keepdims=True) + 1e-05)
    normed = centre * inverse
    return (normed * gain_row.astype(jnp.float32) + offset_row.astype(jnp.float32), normed, inverse)


def norm_backward(grad_out, normed, inverse, gain_row):
    scaled = grad_out * gain_row.astype(jnp.float32)
    grad_in = inverse * (
        scaled
        - jnp.mean(scaled, axis=-1, keepdims=True)
        - normed * jnp.mean(scaled * normed, axis=-1, keepdims=True)
    )
    return (grad_in, jnp.sum(grad_out * normed, axis=0), jnp.sum(grad_out, axis=0))


def gather_weights(shards):
    return (
        lax.all_gather(shards[0], "fsdp", axis=0, tiled=True),
        lax.all_gather(shards[1], "fsdp", axis=0, tiled=True),
        lax.all_gather(shards[2], "fsdp", axis=0, tiled=True),
        lax.all_gather(shards[3], "fsdp", axis=0, tiled=True),
        lax.all_gather(shards[4], "fsdp", axis=0, tiled=True),
        lax.all_gather(shards[5], "fsdp", axis=0, tiled=True),
        lax.all_gather(shards[6], "fsdp", axis=0, tiled=True),
        lax.all_gather(shards[7], "fsdp", axis=0, tiled=True),
        lax.all_gather(shards[8], "fsdp", axis=0, tiled=True),
        lax.all_gather(shards[9], "fsdp", axis=0, tiled=True),
        lax.all_gather(shards[10], "fsdp", axis=0, tiled=True),
        lax.all_gather(shards[11], "fsdp", axis=0, tiled=True),
        lax.all_gather(shards[12], "fsdp", axis=0, tiled=True),
        lax.all_gather(shards[13], "fsdp", axis=0, tiled=True),
        lax.all_gather(shards[14], "fsdp", axis=0, tiled=True),
    )


def attend_forward(query_bf, key_bf, value_bf, seg_local):
    row_count = query_bf.shape[0]
    score_scale = HEAD_DIM ** (-0.5)
    query_heads = query_bf.reshape(row_count, HEADS, HEAD_DIM)
    run_max = jnp.full((HEADS, row_count), -1e30, jnp.float32)
    key_rows = lax.all_gather(key_bf, "ctx", axis=0, tiled=True)
    value_rows = lax.all_gather(value_bf, "ctx", axis=0, tiled=True)
    key_seg = lax.all_gather(seg_local, "ctx", axis=0, tiled=True)
    piece_rows = key_rows.shape[0]
    key_heads = key_rows.reshape(piece_rows, HEADS, HEAD_DIM)
    value_heads = value_rows.reshape(piece_rows, HEADS, HEAD_DIM)
    scores = (
        jnp.einsum("rhd,khd->hrk", query_heads, key_heads, preferred_element_type=jnp.float32)
        * score_scale
    )
    same_doc = seg_local[:, None] == key_seg[None, :]
    scores = jnp.where(same_doc[None], scores, -1e30)
    new_max = jnp.maximum(run_max, jnp.max(scores, axis=-1))
    numerators = jnp.exp(scores - new_max[..., None])
    run_sum = jnp.sum(numerators, axis=-1)
    accumulated = jnp.einsum(
        "hrk,khd->hrd",
        numerators.astype(jnp.bfloat16),
        value_heads,
        preferred_element_type=jnp.float32,
    )
    run_max, run_sum, accumulated = (new_max, run_sum, accumulated)
    context = jnp.transpose(accumulated / run_sum[..., None], (1, 0, 2)).reshape(
        row_count, HEADS * HEAD_DIM
    )
    return (context, run_max + jnp.log(run_sum))


def block_grads(
    query_heads, grad_heads, query_seg, log_sum, row_delta, key_heads, value_heads, key_seg
):
    score_scale = HEAD_DIM ** (-0.5)
    scores = (
        jnp.einsum("rhd,khd->hrk", query_heads, key_heads, preferred_element_type=jnp.float32)
        * score_scale
    )
    same_doc = query_seg[:, None] == key_seg[None, :]
    scores = jnp.where(same_doc[None], scores, -1e30)
    probs_full = jnp.exp(scores - log_sum[..., None])
    grad_probs = jnp.einsum(
        "rhd,khd->hrk", grad_heads, value_heads, preferred_element_type=jnp.float32
    )
    grad_scores = (probs_full * (grad_probs - row_delta[..., None])).astype(jnp.bfloat16)
    return (probs_full, grad_scores)


def attend_backward(query_bf, key_bf, value_bf, seg_local, context, log_sum, grad_context):
    row_count = query_bf.shape[0]
    score_scale = HEAD_DIM ** (-0.5)
    key_every, value_every, seg_every = (
        lax.all_gather(key_bf, "ctx", axis=0, tiled=True),
        lax.all_gather(value_bf, "ctx", axis=0, tiled=True),
        lax.all_gather(seg_local, "ctx", axis=0, tiled=True),
    )
    length = key_every.shape[0]
    block_len = min(512, length)
    query_heads = query_bf.reshape(row_count, HEADS, HEAD_DIM)
    grad_heads = grad_context.reshape(row_count, HEADS, HEAD_DIM)
    row_delta = jnp.sum(
        (grad_context.astype(jnp.float32) * context).reshape(row_count, HEADS, HEAD_DIM), axis=-1
    ).T

    def visit_block(grad_query, block_num):
        first_row = block_num * block_len
        key_heads = lax.dynamic_slice_in_dim(key_every, first_row, block_len, 0).reshape(
            block_len, HEADS, HEAD_DIM
        )
        value_heads = lax.dynamic_slice_in_dim(value_every, first_row, block_len, 0).reshape(
            block_len, HEADS, HEAD_DIM
        )
        key_seg = lax.dynamic_slice_in_dim(seg_every, first_row, block_len, 0)
        probs_full, grad_scores = block_grads(
            query_heads, grad_heads, seg_local, log_sum, row_delta, key_heads, value_heads, key_seg
        )
        grad_query = (
            grad_query
            + jnp.einsum("hrk,khd->rhd", grad_scores, key_heads, preferred_element_type=jnp.float32)
            * score_scale
        )
        grad_keys = (
            jnp.einsum("hrk,rhd->khd", grad_scores, query_heads, preferred_element_type=jnp.float32)
            * score_scale
        )
        grad_values = jnp.einsum(
            "hrk,rhd->khd",
            probs_full.astype(jnp.bfloat16),
            grad_heads,
            preferred_element_type=jnp.float32,
        )
        stacked = jnp.stack(
            (
                grad_keys.reshape(block_len, HEADS * HEAD_DIM),
                grad_values.reshape(block_len, HEADS * HEAD_DIM),
            ),
            axis=1,
        )
        return (grad_query, stacked)

    grad_query, pieces = lax.scan(
        visit_block,
        jnp.zeros((row_count, HEADS, HEAD_DIM), jnp.float32),
        jnp.arange(length // block_len),
    )
    key_terms = pieces.reshape(length, 2, HEADS * HEAD_DIM)
    own_rows = lax.psum_scatter(
        key_terms.astype(jnp.bfloat16), "ctx", scatter_dimension=0, tiled=True
    ).astype(jnp.float32)
    grad_keyed = own_rows[:, 0].astype(jnp.bfloat16)
    grad_valued = own_rows[:, 1].astype(jnp.bfloat16)
    grad_queries = grad_query.reshape(row_count, HEADS * HEAD_DIM).astype(jnp.bfloat16)
    return (grad_queries, grad_keyed, grad_valued)


def layer_forward(inputs, seg_local, full_weights):
    (
        query_weight,
        key_weight,
        value_weight,
        output_weight,
        expand_weight,
        contract_weight,
        query_bias,
        value_bias,
        output_bias,
        first_gain,
        first_shift,
        expand_bias,
        contract_bias,
        second_gain,
        second_shift,
    ) = full_weights
    query_bf = (plain_dot(inputs, query_weight) + query_bias.astype(jnp.float32)).astype(
        jnp.bfloat16
    )
    key_bf = plain_dot(inputs, key_weight).astype(jnp.bfloat16)
    value_bf = (plain_dot(inputs, value_weight) + value_bias.astype(jnp.float32)).astype(
        jnp.bfloat16
    )
    context, log_sum = attend_forward(query_bf, key_bf, value_bf, seg_local)
    context_bf = context.astype(jnp.bfloat16)
    first_sum = (
        inputs.astype(jnp.float32)
        + plain_dot(context_bf, output_weight)
        + output_bias.astype(jnp.float32)
    )
    first_out, normed_one, inverse_one = norm_forward(first_sum, first_gain, first_shift)
    first_bf = first_out.astype(jnp.bfloat16)
    hidden = plain_dot(first_bf, expand_weight) + expand_bias.astype(jnp.float32)
    gelled_bf = jax.nn.gelu(hidden, approximate=False).astype(jnp.bfloat16)
    second_sum = (
        first_out + plain_dot(gelled_bf, contract_weight) + contract_bias.astype(jnp.float32)
    )
    result, normed_two, inverse_two = norm_forward(second_sum, second_gain, second_shift)
    kept_state = (
        query_bf,
        key_bf,
        value_bf,
        context,
        log_sum,
        context_bf,
        normed_one,
        inverse_one,
        first_bf,
        hidden,
        gelled_bf,
        normed_two,
        inverse_two,
    )
    return (result.astype(jnp.bfloat16), kept_state)


def layer_backward(inputs, seg_local, grad_out, kept_state, full_weights):
    (
        query_weight,
        key_weight,
        value_weight,
        output_weight,
        expand_weight,
        contract_weight,
        query_bias,
        value_bias,
        output_bias,
        first_gain,
        first_shift,
        expand_bias,
        contract_bias,
        second_gain,
        second_shift,
    ) = full_weights
    (
        query_bf,
        key_bf,
        value_bf,
        context,
        log_sum,
        context_bf,
        normed_one,
        inverse_one,
        first_bf,
        hidden,
        gelled_bf,
        normed_two,
        inverse_two,
    ) = kept_state
    grad_second, second_gain_grad, second_shift_grad = norm_backward(
        grad_out.astype(jnp.float32), normed_two, inverse_two, second_gain
    )
    grad_branch = grad_second.astype(jnp.bfloat16)
    contract_weight_grad = left_dot(gelled_bf, grad_branch)
    contract_bias_grad = jnp.sum(grad_branch.astype(jnp.float32), axis=0)
    grad_gelled = right_dot(grad_branch, contract_weight)
    gelu_pull = jax.vjp(lambda values: jax.nn.gelu(values, approximate=False), hidden)[1]
    grad_hidden = gelu_pull(grad_gelled)[0].astype(jnp.bfloat16)
    expand_weight_grad = left_dot(first_bf, grad_hidden)
    expand_bias_grad = jnp.sum(grad_hidden.astype(jnp.float32), axis=0)
    grad_first = grad_second + right_dot(grad_hidden, expand_weight)
    grad_attn, first_gain_grad, first_shift_grad = norm_backward(
        grad_first, normed_one, inverse_one, first_gain
    )
    grad_attn_low = grad_attn.astype(jnp.bfloat16)
    output_weight_grad = left_dot(context_bf, grad_attn_low)
    output_bias_grad = jnp.sum(grad_attn_low.astype(jnp.float32), axis=0)
    grad_context = right_dot(grad_attn_low, output_weight).astype(jnp.bfloat16)
    grad_queries, grad_keyed, grad_valued = attend_backward(
        query_bf, key_bf, value_bf, seg_local, context, log_sum, grad_context
    )
    query_weight_grad = left_dot(inputs, grad_queries)
    key_weight_grad = left_dot(inputs, grad_keyed)
    value_weight_grad = left_dot(inputs, grad_valued)
    query_bias_grad = jnp.sum(grad_queries.astype(jnp.float32), axis=0)
    value_bias_grad = jnp.sum(grad_valued.astype(jnp.float32), axis=0)
    grad_input = (
        grad_attn
        + right_dot(grad_queries, query_weight)
        + right_dot(grad_keyed, key_weight)
        + right_dot(grad_valued, value_weight)
    )
    grad_terms = (
        query_weight_grad,
        key_weight_grad,
        value_weight_grad,
        output_weight_grad,
        expand_weight_grad,
        contract_weight_grad,
        query_bias_grad,
        value_bias_grad,
        output_bias_grad,
        first_gain_grad,
        first_shift_grad,
        expand_bias_grad,
        contract_bias_grad,
        second_gain_grad,
        second_shift_grad,
    )
    return (grad_input, grad_terms)


def per_device(
    layer_input,
    segments,
    cotangent,
    query_weight,
    key_weight,
    value_weight,
    output_weight,
    expand_weight,
    contract_weight,
    query_bias,
    value_bias,
    output_bias,
    first_gain,
    first_shift,
    expand_bias,
    contract_bias,
    second_gain,
    second_shift,
):
    shards = (
        query_weight,
        key_weight,
        value_weight,
        output_weight,
        expand_weight,
        contract_weight,
        query_bias,
        value_bias,
        output_bias,
        first_gain,
        first_shift,
        expand_bias,
        contract_bias,
        second_gain,
        second_shift,
    )
    micro_count = layer_input.shape[0]
    results = []
    grad_inputs = []
    totals = None
    for micro_step in range(micro_count):
        inputs = layer_input[micro_step, 0]
        seg_local = segments[micro_step, 0].astype(jnp.bfloat16)
        front_weights = gather_weights(shards)
        result, kept_state = layer_forward(inputs, seg_local, front_weights)
        behind = gather_weights(shards)
        grad_input, grad_terms = layer_backward(
            inputs, seg_local, cotangent[micro_step, 0], kept_state, behind
        )
        results.append(result)
        grad_inputs.append(grad_input)
        if totals is None:
            totals = grad_terms
        else:
            totals = tuple(
                (left_side + right_side for left_side, right_side in zip(totals, grad_terms))
            )
    reduced = jax.tree.map(
        lambda part: part.astype(jnp.float32),
        lax.psum_scatter(as_sent(totals), "fsdp", scatter_dimension=0, tiled=True),
    )
    summed = jax.tree.map(lambda part: part.astype(jnp.float32), lax.psum(as_sent(reduced), "ctx"))
    layer_output = jnp.stack(results, axis=0)[:, None]
    input_grad = jnp.stack(grad_inputs, axis=0)[:, None]
    return (
        layer_output,
        input_grad,
        summed[0],
        summed[1],
        summed[2],
        summed[3],
        summed[4],
        summed[5],
        summed[6],
        summed[7],
        summed[8],
        summed[9],
        summed[10],
        summed[11],
        summed[12],
        summed[13],
        summed[14],
    )


MESH = pl.DeviceIdType.MESH
BF = jnp.bfloat16
F32 = jnp.float32
CHUNKS = 24
SLOTS = 3
LAND = 4
ROOM = 8
Y_ROWS, X_ROWS = 48, 8


def coords():
    c, f = lax.axis_index("ctx"), lax.axis_index("fsdp")
    return c // 2, c % 2, f // 2, f % 2


def dev(z, x, y, k):
    return (z * 2 + x, y * 2 + k)


def greet(z, x, y, k):
    barrier = pltpu.get_barrier_semaphore()
    for step in range(1, 8):
        place = (z * 2 + k + step) % 8
        pl.semaphore_signal(
            barrier, inc=1, device_id=dev(place // 2, x, y, place % 2), device_id_type=MESH
        )
    pl.semaphore_signal(barrier, inc=1, device_id=dev(z, 1 - x, y, k), device_id_type=MESH)
    pl.semaphore_signal(barrier, inc=1, device_id=dev(z, x, 1 - y, k), device_id_type=MESH)
    pl.semaphore_wait(barrier, 9)


def remote(src, dst, send, recv, to):
    return pltpu.make_async_remote_copy(
        src_ref=src, dst_ref=dst, send_sem=send, recv_sem=recv, device_id=to, device_id_type=MESH
    )


def rows_of(start, size, unit=16):
    return pl.ds(pl.multiple_of(start, unit), size)


def two_heads(block):
    lane = lax.broadcasted_iota(jnp.int32, block.shape, 1)
    zero = jnp.zeros_like(block)
    return jnp.concatenate(
        [jnp.where(lane < HEAD_DIM, block, zero), jnp.where(lane >= HEAD_DIM, block, zero)], axis=0
    )


def one_block(pair):
    rows = pair.shape[0] // 2
    lane = lax.broadcasted_iota(jnp.int32, (rows, pair.shape[1]), 1)
    return jnp.where(lane < HEAD_DIM, pair[:rows], pair[rows:])


def softmax_pair(queries, keys, bias):
    scores = right_dot(queries, keys)
    scores = scores + jnp.concatenate([bias, bias], axis=0)
    numer = jnp.exp(scores - jnp.max(scores, axis=-1, keepdims=True))
    return numer * (1.0 / jnp.sum(numer, axis=-1, keepdims=True))


def layer_kernel(
    inp, cot, seg, wq, wk, wv, wo, we, wc, *rest,
):
    (
        vecs, (fq, fk, fv, fo, fe, fc), (o_q, o_k, o_v, o_o, o_e, o_c), (resf, dxf, vec_out), rest
    ) = (rest[:9], rest[9:15], rest[15:21], rest[21:24], rest[24:])
    (
        s_d, l_d, r_d, b_y, r_y, b_x, r_x, b_1, r_1, b_2, r_2, o_b,
        gh, acc, ga, gal, dctx, dq, dk, dv, bias, we_b, wc_b, w_b,
        dx_p, dx_r, dx_s, dx_y, vec, v_s, v_d, v_r,
        gel, gb, fb, gp, n1, inv1, ctx, q, key, val, xf, res, cotf, segf, vec_in, vecf, row8, row_e,
        ss, rs, ds, dr, a_send, a_recv, v_send, v_recv, w_sem, o_sem,
        i_send, i_recv, g_send, g_recv, p_send, p_recv, f_send, f_recv,
    ) = rest
    dx_b = dctx
    z, x, y, k = coords()
    f = y * 2 + k
    other = (1 - y) * 2 + k
    sib, xn, yn = dev(z, x, y, 1 - k), dev(z, 1 - x, y, k), dev(z, x, 1 - y, k)
    bit1, bit2 = z % 2, z // 2
    z1 = dev(z + 1 - 2 * bit1, x, y, k)
    z2 = dev((z + 2) % 4, x, y, k)
    color = bit1 * 2 + x
    c_x, c_z, c_o = color + 1 - 2 * x, (color + 2) % 4, 3 - color
    own_rows = rows_of(x * 512 + k * 256, 256)

    def block_moves(mb):
        to_z, to_k = mb * 2 + k, z // 2
        row = x * 512 + z * 128
        slot = z % 2
        mine = (to_z == z) & (to_k == k)
        moves = (
            (inp.at[mb, 0], xf.at[rows_of(row, 128)], 0),
            (seg.at[mb], segf.at[x * 4 + z], 1),
            (cot.at[mb, 0], cotf.at[rows_of(slot * 128, 128)], 2),
        )
        return mine, dev(to_z, x, y, to_k), slot, moves

    def start_blocks(which):
        for mb in range(2):
            mine, to, slot, moves = block_moves(mb)
            for src, dst, n in moves:
                if n not in which:
                    continue

                @pl.when(mine)
                def _():
                    pltpu.make_async_copy(src, dst, i_recv.at[n, slot]).start()

                @pl.when(jnp.logical_not(mine))
                def _():
                    remote(src, dst, i_send.at[n, mb], i_recv.at[n, slot], to).start()

    def finish_blocks(which):
        for mb in range(2):
            mine, to, slot, moves = block_moves(mb)
            for src, dst, n in moves:
                if n not in which:
                    continue

                @pl.when(jnp.logical_not(mine))
                def _():
                    remote(src, dst, i_send.at[n, mb], i_recv.at[n, slot], to).wait_send()

    def arrive_blocks(which):
        for slot in range(2):
            zz = 2 * k + slot
            for n in which:
                if n == 0:
                    dst = xf.at[rows_of(x * 512 + zz * 128, 128)]
                elif n == 1:
                    dst = segf.at[x * 4 + zz]
                else:
                    dst = cotf.at[pl.ds(slot * 128, 128)]
                pltpu.make_async_copy(dst, dst, i_recv.at[n, slot]).wait()

    def group_copy(step):
        who = x if step < 2 else 1 - x
        src = xf.at[rows_of(who * 512 + k * 256, 256)]
        sseg = segf.at[pl.ds(who * 4 + k * 2, 2)]
        to = (sib, xn, sib)[step]
        return (
            remote(src, src, g_send.at[0, step], g_recv.at[0, step], to),
            remote(sseg, sseg, g_send.at[1, step], g_recv.at[1, step], to),
        )

    def group_arrive(step):
        who = (x, 1 - x, 1 - x)[step]
        kk = (1 - k, k, 1 - k)[step]
        src = xf.at[rows_of(who * 512 + kk * 256, 256)]
        sseg = segf.at[pl.ds(who * 4 + kk * 2, 2)]
        pltpu.make_async_copy(src, src, g_recv.at[0, step]).wait()
        pltpu.make_async_copy(sseg, sseg, g_recv.at[1, step]).wait()

    items = []
    for shard, full in ((wq, fq), (wk, fk), (wv, fv), (wo, fo)):
        items.append((shard, full, 0, 0, 256))
    for j in range(4):
        items.append((we, fe, 0, j * 1024, 256))
    for j in range(4):
        items.append((wc, fc, j * 256, 0, 1024))
    n_items = len(items)

    def part(i, quarter, start, size, own_src=False):
        shard, full, row, col, step = items[i]
        if own_src:
            return shard.at[rows_of(row + start, size, 8), pl.ds(col, 1024)]
        return full.at[rows_of(quarter * step + row + start, size, 8), pl.ds(col, 1024)]

    def send_copy(i, kind):
        sems = (p_send.at[kind, i], p_recv.at[kind, i])
        if kind == 0:
            return remote(part(i, f, color * 64, 64, True), part(i, f, color * 64, 64), *sems, yn)
        if kind == 1:
            return remote(part(i, f, c_o * 64, Y_ROWS, True), part(i, f, c_o * 64, Y_ROWS), *sems, yn)
        if kind == 2:
            src = part(i, other, color * 64, 64)
            return remote(src, src, *sems, xn)
        if kind == 3:
            src = part(i, other, c_z * 64 + Y_ROWS, X_ROWS)
            return remote(src, src, *sems, xn)
        if kind == 4:
            src = part(i, other, color * 64, 64)
            return remote(src, src, *sems, z1)
        if kind == 5:
            src = part(i, other, c_x * 64 + Y_ROWS + X_ROWS, X_ROWS)
            return remote(src, src, *sems, z1)
        if kind == 6:
            return remote(part(i, f, 0, 256, True), part(i, f, 0, 256), *sems, sib)
        src = part(i, other, 0, 256)
        return remote(src, src, *sems, sib)

    def arrive(i, kind):
        if kind == 0:
            dst = part(i, other, color * 64, 64)
        elif kind == 1:
            dst = part(i, other, c_o * 64, Y_ROWS)
        elif kind == 2:
            dst = part(i, other, c_x * 64, 64)
        elif kind == 3:
            dst = part(i, other, c_o * 64 + Y_ROWS, X_ROWS)
        elif kind == 4:
            dst = part(i, other, c_z * 64, 64)
        elif kind == 5:
            dst = part(i, other, c_o * 64 + Y_ROWS + X_ROWS, X_ROWS)
        elif kind == 6:
            dst = part(i, y * 2 + 1 - k, 0, 256)
        else:
            dst = part(i, (1 - y) * 2 + 1 - k, 0, 256)
        pltpu.make_async_copy(dst, dst, p_recv.at[kind, i]).wait()


    for i in range(8):
        packed = vecs[i][...].astype(F32).reshape(1, 256)
        vec_in[pl.ds(2 * i, 1)] = packed[:, :128]
        vec_in[pl.ds(2 * i + 1, 1)] = packed[:, 128:]
    packed = vecs[8][...].astype(F32).reshape(1, 1024)
    for n in range(8):
        vec_in[pl.ds(16 + n, 1)] = packed[:, n * 128 : n * 128 + 128]
    vecf[f] = vec_in[...]
    vec_copies = (
        remote(vec_in, vecf.at[f], f_send.at[0], f_recv.at[0], yn),
        remote(vec_in, vecf.at[f], f_send.at[1], f_recv.at[1], sib),
        remote(vecf.at[other], vecf.at[other], f_send.at[2], f_recv.at[2], sib),
    )

    def load_square(shard, full, row, step, cols, dst, sem):
        out = []
        for d in range(4):
            quarter = (f + d) % 4
            src = shard.at[pl.ds(row, 256), cols]
            if d > 0:
                src = full.at[rows_of(quarter * step + row, 256), cols]
            out.append(pltpu.make_async_copy(src, dst.at[rows_of(quarter * 256, 256)], sem))
        return out

    def load_c(j):
        slot = j % 2
        sem = w_sem.at[slot]

        @pl.when(j // 2 == f)
        def _():
            src = wc.at[rows_of((j % 2) * 512, 512)]
            pltpu.make_async_copy(src, wc_b.at[slot], sem).start()

        @pl.when(j // 2 != f)
        def _():
            pltpu.make_async_copy(fc.at[rows_of(j * 512, 512)], wc_b.at[slot], sem).start()

    def load_e(j):
        for move in load_square(
            we, fe, 0, 256, rows_of(j * 512, 512, 512), we_b.at[j % 2], w_sem.at[2 + j % 2]
        ):
            move.start()

    def load_w(n):
        shard, full = ((wo, fo), (wk, fk), (wv, fv), (wq, fq))[n]
        for move in load_square(
            shard, full, 0, 256, pl.ds(0, 1024), w_b.at[n], w_sem.at[4 + n]
        ):
            move.start()

    def loaded_w(n):
        pltpu.make_async_copy(w_b.at[n], w_b.at[n], w_sem.at[4 + n]).wait()

    def load_item(i):
        shard, full, row, col, step = items[i]
        arrive(i, 6)
        arrive(i, 7)
        slot = i % 4
        for move in load_square(
            shard, full, row, step, pl.ds(col, 1024), w_b.at[slot], w_sem.at[4 + slot]
        ):
            move.start()

    def item(i):
        slot = i % 4
        pltpu.make_async_copy(w_b.at[slot], w_b.at[slot], w_sem.at[4 + slot]).wait()
        return w_b.at[slot]

    def relay(t):
        for u in (0, 1, 2) if t == 0 else (t + 2,):
            if u < n_items:
                send_copy(u, 0).start()
                send_copy(u, 1).start()
                send_copy(u, 6).start()
        if 1 <= t <= n_items:
            i = t - 1
            arrive(i, 0)
            send_copy(i, 2).start()
            send_copy(i, 4).start()
        if 2 <= t <= n_items + 1:
            i = t - 2
            arrive(i, 4)
            send_copy(i, 3).start()
            arrive(i, 2)
            send_copy(i, 5).start()
        if 3 <= t <= n_items + 2:
            i = t - 3
            arrive(i, 1)
            arrive(i, 3)
            arrive(i, 5)
            send_copy(i, 7).start()

    def fill_rows():
        pltpu.make_async_copy(vec_in, vec_in, f_recv.at[1]).wait()
        pltpu.make_async_copy(vec_in, vec_in, f_recv.at[2]).wait()
        for quarter in range(4):
            for i in range(8):
                for half in range(2):
                    col = quarter * 256 + half * 128
                    row8[pl.ds(i, 1), col : col + 128] = vecf[quarter, pl.ds(2 * i + half, 1)]
            for n in range(8):
                col = quarter * 1024 + n * 128
                row_e[:, col : col + 128] = vecf[quarter, pl.ds(16 + n, 1)]

    def fill_bias():
        for block in range(2):
            own = segf[x * 4 + k * 2 + block].astype(F32)
            down = jnp.transpose(jnp.broadcast_to(own, (128, 128)))
            for n in range(8):
                across = segf[n].astype(F32)
                bias[block * 128 : block * 128 + 128, n * 128 : n * 128 + 128] = jnp.where(
                    down == across, 0.0, -1e30
                )

    def project_own(w):
        q[...] = (plain_dot(xf[own_rows], w[...]) + row8[0:1]).astype(BF)

    def project_all(w, dst, add_row):
        def block(n, carry):
            rows = rows_of(n * 256, 256)
            dst[rows] = (plain_dot(xf[rows], w[...]) + add_row).astype(BF)
            return carry

        lax.fori_loop(0, 4, block, 0)

    def heads(first, last):
        def one(h, carry):
            cols = rows_of(h * 128, 128, 128)
            queries = two_heads(q[:, cols] * BF(HEAD_DIM**-0.5))
            probs = softmax_pair(queries, key[:, cols], bias[...])
            ctx[:, cols] = one_block(plain_dot(probs.astype(BF), val[:, cols])).astype(BF)
            return carry

        lax.fori_loop(first, last, one, 0)

    def norm(v):
        centre = v - jnp.mean(v, axis=-1, keepdims=True)
        inverse = lax.rsqrt(jnp.mean(centre * centre, axis=-1, keepdims=True) + 1e-05)
        return centre * inverse, inverse

    def attention_out(w):
        normed, inverse = norm(
            xf[own_rows].astype(F32) + plain_dot(ctx[...], w[...]) + row8[2:3]
        )
        n1[...] = normed
        inv1[...] = inverse
        first_out = normed * row8[3:4] + row8[4:5]
        acc[...] = first_out
        fb[...] = first_out.astype(BF)

    def expand(j, w):
        def block(n, carry):
            cols = rows_of(n * 256, 256, 256)
            out = rows_of(j * 1024 + n * 256, 256, 256)
            hidden = plain_dot(fb[...], w[:, cols]) + row_e[:, out]
            below = 0.5 + 0.5 * lax.erf(hidden * 0.5**0.5)
            gel[:, out] = (hidden * below).astype(BF)
            bell = jnp.exp(-0.5 * hidden * hidden) * (2 * math.pi) ** -0.5
            gp[:, out] = (below + hidden * bell).astype(BF)
            return carry

        lax.fori_loop(0, 4, block, 0)

    def contract(j, w):
        for quarter in range(4):
            cols = pl.ds(quarter * 1024 + j * 256, 256)
            acc[...] += plain_dot(gel[:, cols], w[quarter * 256 : quarter * 256 + 256])

    def second_norm():
        normed, inverse = norm(acc[...] + row8[5:6])
        res[...] = (normed * row8[6:7] + row8[7:8]).astype(BF)
        grad_out = cotf[...].astype(F32)
        keep(6, column(grad_out * normed))
        keep(7, column(grad_out))
        scaled = grad_out * row8[6:7]
        grad = inverse * (
            scaled
            - jnp.mean(scaled, axis=-1, keepdims=True)
            - normed * jnp.mean(scaled * normed, axis=-1, keepdims=True)
        )
        acc[...] = grad
        low = grad.astype(BF)
        gb[...] = low
        keep(5, column(low))


    def back(n, slot):
        to_z = 2 * k + slot
        to_k = z % 2
        mb = z // 2
        mine = (to_z == z) & (to_k == k)
        src = (res, dx_b)[n].at[pl.ds(slot * 128, 128)]
        dst = (resf, dxf)[n].at[mb, 0]

        def far():
            return remote(
                src, dst, a_send.at[n, slot], a_recv.at[n, mb], dev(to_z, x, y, to_k)
            )

        def near():
            return pltpu.make_async_copy(src, dst, a_recv.at[n, mb])

        return mine, far, near

    def start_back(n):
        for slot in range(2):
            mine, far, near = back(n, slot)

            @pl.when(mine)
            def _():
                near().start()

            @pl.when(jnp.logical_not(mine))
            def _():
                far().start()

    def finish_back(n):
        for slot in range(2):
            mine, far, _ = back(n, slot)

            @pl.when(jnp.logical_not(mine))
            def _():
                far().wait_send()

        for mb in range(2):
            dst = (resf, dxf)[n].at[mb, 0]
            pltpu.make_async_copy(dst, dst, a_recv.at[n, mb]).wait()

    def column(v):
        return jnp.sum(v.astype(F32), axis=0, keepdims=True)

    def keep(i, row):
        for quarter in range(4):
            for half in range(2):
                col = quarter * 256 + half * 128
                vec[quarter, pl.ds(2 * i + half, 1)] = row[:, col : col + 128]

    v_peers = (sib, yn, xn, z1, z2)

    def v_copy(stage):
        if stage == 0:
            return remote(v_d.at[1], v_d.at[2], v_send.at[0], v_recv.at[0], sib)
        src = v_s.at[0, 1 - y] if stage == 1 else v_s.at[stage - 1, 0]
        return remote(src, v_r.at[stage - 1], v_send.at[stage], v_recv.at[stage], v_peers[stage])

    def v_step(stage):
        if stage == 0:
            for plane in range(2):
                v_d[0, plane] = vec[plane * 2 + k]
                v_d[1, plane] = vec[plane * 2 + 1 - k]
        elif stage == 1:
            pltpu.make_async_copy(v_d.at[2], v_d.at[2], v_recv.at[0]).wait()
            v_s[0] = v_d[0] + v_d[2]
        else:
            dst = v_r.at[stage - 2]
            pltpu.make_async_copy(dst, dst, v_recv.at[stage - 1]).wait()
            mine = v_s[0, y] if stage == 2 else v_s[stage - 2, 0]
            total = mine + v_r[stage - 2]
            if stage == 5:
                vec_out[...] = total
            else:
                v_s[stage - 1, 0] = total
        if stage < 5:
            v_copy(stage).start()

    def send(stage, i, src, dst, to):
        return remote(src, dst, ss.at[stage, i % SLOTS], rs.at[stage, i % LAND], to)

    def landed(stage, i, dst):
        pltpu.make_async_copy(dst, dst, rs.at[stage, i % LAND]).wait()

    def copies(stage, i):
        slot, land, room = i % SLOTS, i % LAND, i % ROOM
        if stage == 0:
            return send(0, i, s_d.at[slot], r_d.at[land], sib)
        if stage == 1:
            return send(1, i, b_y.at[slot, 1 - y], r_y.at[land], yn)
        if stage == 2:
            return send(2, i, b_x.at[slot, rows_of((1 - x) * 64, 64)], r_x.at[land], xn)
        if stage == 3:
            return send(3, i, b_1.at[slot, rows_of((1 - bit1) * 32, 32)], r_1.at[land], z1)
        if stage == 4:
            return send(4, i, b_2.at[slot, rows_of((1 - bit2) * 16, 16)], r_2.at[land], z2)
        if stage == 5:
            own = o_b.at[room, rows_of(x * 64 + bit1 * 32 + bit2 * 16, 16)]
            return send(5, i, own, own, z2)
        if stage == 6:
            own = o_b.at[room, rows_of(x * 64 + bit1 * 32, 32)]
            return send(6, i, own, own, z1)
        own = o_b.at[room, rows_of(x * 64, 64)]
        return send(7, i, own, own, xn)

    def launch(stage, i):
        copies(stage, i).start()

    def clear(stage, i):
        @pl.when(i >= SLOTS)
        def _():
            copies(stage, i - SLOTS).wait_send()

    def add(a, b):
        return (a.astype(F32) + b.astype(F32)).astype(BF)

    def terms(i, a_ref, b_ref, a_base, a_step, b_col, a_rows=None):
        slot = i % SLOTS
        right = b_ref[:, b_col]
        for plane in range(2):
            for core in range(2):
                quarter = plane * 2 + (k if core == 0 else 1 - k)
                cols = pl.ds(pl.multiple_of(a_base + quarter * a_step, 128), 128)
                left = a_ref[:, cols] if a_rows is None else a_ref[a_rows, cols]
                product = left_dot(left, right).astype(BF)
                if core == 0:
                    l_d[slot, plane] = product
                else:
                    s_d[slot, plane] = product

    every = pl.ds(0, 1024)

    def stage_zero(i):
        @pl.when((i >= 0) & (i < CHUNKS))
        def _():
            clear(0, i)

        @pl.when(i < 8)
        def _():
            terms(i, gel, gb, i * 128, 1024, every)

        @pl.when((i >= 8) & (i < 16))
        def _():
            j = i - 8
            terms(i, fb, gh, (j % 2) * 128, 256, rows_of((j // 2) * 1024, 1024, 1024))

        @pl.when((i >= 16) & (i < 18))
        def _():
            terms(i, ctx, gal, (i - 16) * 128, 256, every)

        @pl.when((i >= 18) & (i < 20))
        def _():
            terms(i, xf, dq, (i - 18) * 128, 256, every, own_rows)

        @pl.when((i >= 20) & (i < 22))
        def _():
            terms(i, xf, dk, (i - 20) * 128, 256, every)

        @pl.when((i >= 22) & (i < 24))
        def _():
            terms(i, xf, dv, (i - 22) * 128, 256, every)

        @pl.when((i >= 0) & (i < CHUNKS))
        def _():
            launch(0, i)

    def stored():
        pltpu.make_async_copy(o_b.at[0], o_b.at[0], o_sem).wait()

    def store(i):
        src = o_b.at[i % ROOM]

        @pl.when(i >= 1)
        def _():
            stored()

        @pl.when(i < 8)
        def _():
            pltpu.make_async_copy(src, o_c.at[rows_of(i * 128, 128)], o_sem).start()

        @pl.when((i >= 8) & (i < 16))
        def _():
            j = i - 8
            dst = o_e.at[rows_of((j % 2) * 128, 128), rows_of((j // 2) * 1024, 1024, 1024)]
            pltpu.make_async_copy(src, dst, o_sem).start()

        for n, ref in enumerate((o_o, o_q, o_k, o_v)):
            first = 16 + 2 * n

            @pl.when((i >= first) & (i < first + 2))
            def _():
                dst = ref.at[rows_of((i - first) * 128, 128)]
                pltpu.make_async_copy(src, dst, o_sem).start()

    def feed_forward(j):
        slot = j % 2
        cols = rows_of(j * 512, 512, 512)
        pltpu.make_async_copy(wc_b.at[slot], wc_b.at[slot], w_sem.at[slot]).wait()
        pltpu.make_async_copy(we_b.at[slot], we_b.at[slot], w_sem.at[2 + slot]).wait()

        @pl.when(j < 7)
        def _():
            load_c(j + 1)
            load_e(j + 1)

        grads = (right_dot(gb[...], wc_b[slot]) * gp[:, cols].astype(F32)).astype(BF)
        gh[:, cols] = grads
        acc[...] += right_dot(grads, we_b[slot])
        row = column(grads)
        for n in range(4):
            vec[j // 2, pl.ds(16 + (j % 2) * 4 + n, 1)] = row[:, n * 128 : n * 128 + 128]

    def first_norm():
        normed = n1[...]
        grad_first = acc[...]
        keep(3, column(grad_first * normed))
        keep(4, column(grad_first))
        scaled = grad_first * row8[3:4]
        grad_attn = inv1[...] * (
            scaled
            - jnp.mean(scaled, axis=-1, keepdims=True)
            - normed * jnp.mean(scaled * normed, axis=-1, keepdims=True)
        )
        ga[...] = grad_attn
        low = grad_attn.astype(BF)
        gal[...] = low
        keep(2, column(low))
        loaded_w(0)
        dctx[...] = right_dot(low, w_b[0]).astype(BF)

    def attention(h):
        cols = rows_of(h * 128, 128, 128)
        queries = two_heads(q[:, cols] * BF(HEAD_DIM**-0.5))
        keys = key[:, cols]
        probs = softmax_pair(queries, keys, bias[...])
        grads = two_heads(dctx[:, cols])
        grad_probs = right_dot(grads, val[:, cols])
        delta = jnp.sum(probs * grad_probs, axis=-1, keepdims=True)
        grad_scores = (probs * (grad_probs - delta)).astype(BF)
        dv[:, cols] = left_dot(probs.astype(BF), grads).astype(BF)
        dk[:, cols] = left_dot(grad_scores, queries).astype(BF)
        dq[:, cols] = (one_block(plain_dot(grad_scores, keys)) * HEAD_DIM**-0.5).astype(BF)

    def dx_core(g):
        return remote(dx_p.at[g], dx_r.at[g], ds.at[g], dr.at[g], sib)

    dx_far = remote(dx_s, dx_y, ds.at[2], dr.at[2], xn)

    def input_rows(n):
        who = x * (n % 2) + (1 - x) * (1 - n % 2)
        core = (1 - k) * (1 - n // 2) + k * (n // 2)
        rows = rows_of(who * 512 + core * 256, 256)
        terms_here = right_dot(dk[rows], w_b[1]) + right_dot(dv[rows], w_b[2])

        @pl.when(n == 0)
        def _():
            dx_p[1] = terms_here.astype(BF)
            dx_core(1).start()

        @pl.when(n == 1)
        def _():
            dx_p[0] = terms_here.astype(BF)
            dx_core(0).start()

        @pl.when(n == 2)
        def _():
            pltpu.make_async_copy(dx_r.at[1], dx_r.at[1], dr.at[1]).wait()
            dx_s[...] = (terms_here + dx_r[1].astype(F32)).astype(BF)
            dx_far.start()

        @pl.when(n == 3)
        def _():
            pltpu.make_async_copy(dx_r.at[0], dx_r.at[0], dr.at[0]).wait()
            loaded_w(3)
            ga[...] = ga[...] + terms_here + dx_r[0].astype(F32) + right_dot(dq[...], w_b[3])

    greet(z, x, y, k)
    start_blocks((0, 1))
    vec_copies[0].start()
    vec_copies[1].start()
    relay(0)
    relay(1)
    arrive_blocks((0, 1))
    for step in range(2):
        for move in group_copy(step):
            move.start()
    pltpu.make_async_copy(vec_in, vec_in, f_recv.at[0]).wait()
    vec_copies[2].start()
    relay(2)
    relay(3)
    group_arrive(1)
    for move in group_copy(2):
        move.start()
    start_blocks((2,))
    relay(4)
    load_item(0)
    fill_rows()
    relay(5)
    load_item(1)
    project_own(item(0))
    relay(6)
    load_item(2)
    group_arrive(0)
    group_arrive(2)
    fill_bias()
    project_all(item(1), key, 0.0)
    relay(7)
    load_item(3)
    project_all(item(2), val, row8[1:2])
    relay(8)
    load_item(4)
    heads(0, 3)
    relay(9)
    load_item(5)
    heads(3, 6)
    relay(10)
    load_item(6)
    heads(6, 8)
    attention_out(item(3))
    for j in range(4):
        relay(11 + j)
        load_item(7 + j)
        expand(j, item(4 + j))
    load_item(11)
    for j in range(4):
        contract(j, item(8 + j))
    arrive_blocks((2,))
    load_c(0)
    load_e(0)
    for n in range(4):
        load_w(n)
    second_norm()
    start_back(0)

    def tick(t, carry):
        def at(stage):
            i = t - stage
            return i, (i >= 0) & (i < CHUNKS)

        stage_zero(t)
        i1, live1 = at(1)

        @pl.when(live1)
        def _():
            slot, land = i1 % SLOTS, i1 % LAND
            clear(1, i1)
            landed(0, i1, r_d.at[land])
            for plane in range(2):
                b_y[slot, plane] = add(l_d[slot, plane], r_d[land, plane])
            launch(1, i1)

        @pl.when(t < 8)
        def _():
            feed_forward(t)

        @pl.when(t == 8)
        def _():
            first_norm()

        @pl.when((t >= 9) & (t < 17))
        def _():
            attention(t - 9)

        @pl.when(t == 17)
        def _():
            keep(0, column(dq[...]))
            keep(1, column(dv[...]))
            loaded_w(1)
            loaded_w(2)

        @pl.when((t >= 17) & (t < 21))
        def _():
            input_rows(t - 17)

        for stage in range(6):

            @pl.when(t == 18 + 2 * stage)
            def _():
                v_step(stage)

        @pl.when(t == 23)
        def _():
            pltpu.make_async_copy(dx_y, dx_y, dr.at[2]).wait()
            dx_b[...] = (ga[...] + dx_y[...].astype(F32)).astype(BF)
            start_back(1)

        i2, live2 = at(2)

        @pl.when(live2)
        def _():
            slot, land = i2 % SLOTS, i2 % LAND
            clear(2, i2)
            landed(1, i2, r_y.at[land])
            b_x[slot] = add(b_y[slot, y], r_y[land])
            launch(2, i2)

        i3, live3 = at(3)

        @pl.when(live3)
        def _():
            slot, land = i3 % SLOTS, i3 % LAND
            clear(3, i3)
            landed(2, i3, r_x.at[land])
            b_1[slot] = add(b_x[slot, rows_of(x * 64, 64)], r_x[land])
            launch(3, i3)

        i4, live4 = at(4)

        @pl.when(live4)
        def _():
            slot, land = i4 % SLOTS, i4 % LAND
            clear(4, i4)
            landed(3, i4, r_1.at[land])
            b_2[slot] = add(b_1[slot, rows_of(bit1 * 32, 32)], r_1[land])
            launch(4, i4)

        i5, live5 = at(5)

        @pl.when(live5)
        def _():
            slot, land = i5 % SLOTS, i5 % LAND
            clear(5, i5)
            landed(4, i5, r_2.at[land])
            o_b[i5 % ROOM, rows_of(x * 64 + bit1 * 32 + bit2 * 16, 16)] = add(
                b_2[slot, rows_of(bit2 * 16, 16)], r_2[land]
            )
            launch(5, i5)

        i6, live6 = at(6)

        @pl.when(live6)
        def _():
            clear(6, i6)
            landed(5, i6, o_b.at[i6 % ROOM, rows_of(x * 64 + bit1 * 32 + (1 - bit2) * 16, 16)])
            launch(6, i6)

        i7, live7 = at(7)

        @pl.when(live7)
        def _():
            clear(7, i7)
            landed(6, i7, o_b.at[i7 % ROOM, rows_of(x * 64 + (1 - bit1) * 32, 32)])
            launch(7, i7)

        i8, live8 = at(8)

        @pl.when(live8)
        def _():
            landed(7, i8, o_b.at[i8 % ROOM, rows_of((1 - x) * 64, 64)])
            store(i8)

        return carry

    lax.fori_loop(0, CHUNKS + 8, tick, 0)
    stored()
    for stage in range(8):
        for i in range(CHUNKS - SLOTS, CHUNKS):
            copies(stage, i).wait_send()
    for stage in range(5):
        v_copy(stage).wait_send()
    dx_core(0).wait_send()
    dx_core(1).wait_send()
    dx_far.wait_send()
    finish_back(0)
    finish_back(1)
    for i in range(n_items):
        for kind in range(8):
            send_copy(i, kind).wait_send()
    finish_blocks((0, 1, 2))
    for step in range(3):
        for move in group_copy(step):
            move.wait_send()
    for move in vec_copies:
        move.wait_send()


def layer_call(inp, cot, seg, weights, vectors):
    vmem = pl.BlockSpec(memory_space=pltpu.VMEM)
    any_spec = pl.BlockSpec(memory_space=pl.ANY)
    dma = pltpu.SemaphoreType.DMA
    grad = jax.ShapeDtypeStruct((256, 1024), BF)
    square = jax.ShapeDtypeStruct((1024, 1024), BF)
    full_weights = [square] * 4 + [
        jax.ShapeDtypeStruct((1024, 4096), BF), jax.ShapeDtypeStruct((4096, 1024), BF)
    ]
    return pl.pallas_call(
        layer_kernel,
        out_shape=full_weights + [
            grad, grad, grad, grad,
            jax.ShapeDtypeStruct((256, 4096), BF),
            jax.ShapeDtypeStruct((1024, 1024), BF),
            jax.ShapeDtypeStruct((2, 1, 128, 1024), BF),
            jax.ShapeDtypeStruct((2, 1, 128, 1024), BF),
            jax.ShapeDtypeStruct((24, 128), F32),
        ],
        in_specs=[any_spec] * 9 + [vmem] * 9,
        out_specs=[any_spec] * 14 + [vmem],
        scratch_shapes=[
            pltpu.VMEM((SLOTS, 2, 128, 1024), BF),
            pltpu.VMEM((SLOTS, 2, 128, 1024), BF),
            pltpu.VMEM((LAND, 2, 128, 1024), BF),
            pltpu.VMEM((SLOTS, 2, 128, 1024), BF),
            pltpu.VMEM((LAND, 128, 1024), BF),
            pltpu.VMEM((SLOTS, 128, 1024), BF),
            pltpu.VMEM((LAND, 64, 1024), BF),
            pltpu.VMEM((SLOTS, 64, 1024), BF),
            pltpu.VMEM((LAND, 32, 1024), BF),
            pltpu.VMEM((SLOTS, 32, 1024), BF),
            pltpu.VMEM((LAND, 16, 1024), BF),
            pltpu.VMEM((ROOM, 128, 1024), BF),
            pltpu.VMEM((256, 4096), BF),
            pltpu.VMEM((256, 1024), F32),
            pltpu.VMEM((256, 1024), F32),
            pltpu.VMEM((256, 1024), BF),
            pltpu.VMEM((256, 1024), BF),
            pltpu.VMEM((256, 1024), BF),
            pltpu.VMEM((1024, 1024), BF),
            pltpu.VMEM((1024, 1024), BF),
            pltpu.VMEM((256, 1024), F32),
            pltpu.VMEM((2, 1024, 512), BF),
            pltpu.VMEM((2, 512, 1024), BF),
            pltpu.VMEM((4, 1024, 1024), BF),
            pltpu.VMEM((2, 256, 1024), BF),
            pltpu.VMEM((2, 256, 1024), BF),
            pltpu.VMEM((256, 1024), BF),
            pltpu.VMEM((256, 1024), BF),
            pltpu.VMEM((4, 24, 128), F32),
            pltpu.VMEM((4, 2, 24, 128), F32),
            pltpu.VMEM((3, 2, 24, 128), F32),
            pltpu.VMEM((4, 24, 128), F32),
            pltpu.VMEM((256, 4096), BF),
            pltpu.VMEM((256, 1024), BF),
            pltpu.VMEM((256, 1024), BF),
            pltpu.VMEM((256, 4096), BF),
            pltpu.VMEM((256, 1024), F32),
            pltpu.VMEM((256, 1), F32),
            pltpu.VMEM((256, 1024), BF),
            pltpu.VMEM((256, 1024), BF),
            pltpu.VMEM((1024, 1024), BF),
            pltpu.VMEM((1024, 1024), BF),
            pltpu.VMEM((1024, 1024), BF),
            pltpu.VMEM((256, 1024), BF),
            pltpu.VMEM((256, 1024), BF),
            pltpu.VMEM((8, 1, 128), jnp.int32),
            pltpu.VMEM((24, 128), F32),
            pltpu.VMEM((4, 24, 128), F32),
            pltpu.VMEM((8, 1024), F32),
            pltpu.VMEM((1, 4096), F32),
            dma((8, SLOTS)), dma((8, LAND)), dma((3,)), dma((3,)), dma((2, 2)), dma((2, 2)),
            dma((5,)), dma((5,)), dma((8,)), dma(()),
            dma((3, 2)), dma((3, 2)), dma((2, 3)), dma((2, 3)),
            dma((8, 12)), dma((8, 12)), dma((3,)), dma((3,)),
        ],
        compiler_params=pltpu.CompilerParams(
            collective_id=0, has_side_effects=True, vmem_limit_bytes=61 << 20
        ),
        name="layer",
    )(inp, cot, seg, *weights, *vectors)


def per_group_device(
    layer_input, segments, cotangent,
    query_weight, key_weight, value_weight, output_weight, expand_weight, contract_weight,
    query_bias, value_bias, output_bias, first_gain, first_shift, expand_bias, contract_bias,
    second_gain, second_shift,
):
    outs = layer_call(
        layer_input, cotangent, segments,
        (query_weight, key_weight, value_weight, output_weight, expand_weight, contract_weight),
        (
            query_bias, value_bias, output_bias, first_gain, first_shift, contract_bias,
            second_gain, second_shift, expand_bias,
        ),
    )
    o_q, o_k, o_v, o_o, o_e, o_c, resf, dxf, vec = outs[6:]
    mine = vec.reshape(3072)
    vec_grads = [mine[i * 256 : (i + 1) * 256] for i in range(8)]
    return (
        resf,
        dxf.astype(F32),
        o_q.astype(F32),
        o_k.astype(F32),
        o_v.astype(F32),
        o_o.astype(F32),
        o_e.astype(F32),
        o_c.astype(F32),
        vec_grads[0],
        vec_grads[1],
        vec_grads[2],
        vec_grads[3],
        vec_grads[4],
        mine[2048:],
        vec_grads[5],
        vec_grads[6],
        vec_grads[7],
    )


def solution(mesh):
    in_specs = (
        P(None, "fsdp", "ctx", None),
        P(None, "fsdp", "ctx"),
        P(None, "fsdp", "ctx", None),
        P("fsdp", None),
        P("fsdp", None),
        P("fsdp", None),
        P("fsdp", None),
        P("fsdp", None),
        P("fsdp", None),
        P("fsdp"),
        P("fsdp"),
        P("fsdp"),
        P("fsdp"),
        P("fsdp"),
        P("fsdp"),
        P("fsdp"),
        P("fsdp"),
        P("fsdp"),
    )
    out_specs = (
        P(None, "fsdp", "ctx", None),
        P(None, "fsdp", "ctx", None),
        P("fsdp", None),
        P("fsdp", None),
        P("fsdp", None),
        P("fsdp", None),
        P("fsdp", None),
        P("fsdp", None),
        P("fsdp"),
        P("fsdp"),
        P("fsdp"),
        P("fsdp"),
        P("fsdp"),
        P("fsdp"),
        P("fsdp"),
        P("fsdp"),
        P("fsdp"),
    )
    def whole(layer_input, segments, *rest):
        grouped = (
            dict(mesh.shape) == {"ctx": 8, "fsdp": 4}
            and layer_input.shape == (2, 4, 1024, 1024)
            and rest[5].shape == (1024, 4096)
        )
        body = per_group_device if grouped else per_device
        return jax.shard_map(
            body, mesh=mesh, in_specs=in_specs, out_specs=out_specs, check_vma=False
        )(layer_input, segments, *rest)

    return whole
```

```python
import math

import jax
import jax.numpy as jnp
from jax import lax
from jax.experimental import pallas as pl
from jax.experimental.pallas import tpu as pltpu
from jax.sharding import PartitionSpec as P

HEADS = 16
HEAD_DIM = 64


def as_sent(x):
    return jax.tree.map(lambda a: a.astype(jnp.bfloat16) if a.dtype == jnp.float32 else a, x)


def plain_dot(left_side, right_side):
    return jnp.dot(left_side, right_side, preferred_element_type=jnp.float32)


def left_dot(left_side, right_side):
    return lax.dot_general(
        left_side, right_side, (((0,), (0,)), ((), ())), preferred_element_type=jnp.float32
    )


def right_dot(left_side, right_side):
    return lax.dot_general(
        left_side, right_side, (((1,), (1,)), ((), ())), preferred_element_type=jnp.float32
    )


def norm_forward(hidden, gain_row, offset_row):
    centre = hidden - jnp.mean(hidden, axis=-1, keepdims=True)
    inverse = lax.rsqrt(jnp.mean(centre * centre, axis=-1, keepdims=True) + 1e-05)
    normed = centre * inverse
    return (normed * gain_row.astype(jnp.float32) + offset_row.astype(jnp.float32), normed, inverse)


def norm_backward(grad_out, normed, inverse, gain_row):
    scaled = grad_out * gain_row.astype(jnp.float32)
    grad_in = inverse * (
        scaled
        - jnp.mean(scaled, axis=-1, keepdims=True)
        - normed * jnp.mean(scaled * normed, axis=-1, keepdims=True)
    )
    return (grad_in, jnp.sum(grad_out * normed, axis=0), jnp.sum(grad_out, axis=0))


def gather_weights(shards):
    return (
        lax.all_gather(shards[0], "fsdp", axis=0, tiled=True),
        lax.all_gather(shards[1], "fsdp", axis=0, tiled=True),
        lax.all_gather(shards[2], "fsdp", axis=0, tiled=True),
        lax.all_gather(shards[3], "fsdp", axis=0, tiled=True),
        lax.all_gather(shards[4], "fsdp", axis=0, tiled=True),
        lax.all_gather(shards[5], "fsdp", axis=0, tiled=True),
        lax.all_gather(shards[6], "fsdp", axis=0, tiled=True),
        lax.all_gather(shards[7], "fsdp", axis=0, tiled=True),
        lax.all_gather(shards[8], "fsdp", axis=0, tiled=True),
        lax.all_gather(shards[9], "fsdp", axis=0, tiled=True),
        lax.all_gather(shards[10], "fsdp", axis=0, tiled=True),
        lax.all_gather(shards[11], "fsdp", axis=0, tiled=True),
        lax.all_gather(shards[12], "fsdp", axis=0, tiled=True),
        lax.all_gather(shards[13], "fsdp", axis=0, tiled=True),
        lax.all_gather(shards[14], "fsdp", axis=0, tiled=True),
    )


def attend_forward(query_bf, key_bf, value_bf, seg_local):
    row_count = query_bf.shape[0]
    score_scale = HEAD_DIM ** (-0.5)
    query_heads = query_bf.reshape(row_count, HEADS, HEAD_DIM)
    run_max = jnp.full((HEADS, row_count), -1e30, jnp.float32)
    key_rows = lax.all_gather(key_bf, "ctx", axis=0, tiled=True)
    value_rows = lax.all_gather(value_bf, "ctx", axis=0, tiled=True)
    key_seg = lax.all_gather(seg_local, "ctx", axis=0, tiled=True)
    piece_rows = key_rows.shape[0]
    key_heads = key_rows.reshape(piece_rows, HEADS, HEAD_DIM)
    value_heads = value_rows.reshape(piece_rows, HEADS, HEAD_DIM)
    scores = (
        jnp.einsum("rhd,khd->hrk", query_heads, key_heads, preferred_element_type=jnp.float32)
        * score_scale
    )
    same_doc = seg_local[:, None] == key_seg[None, :]
    scores = jnp.where(same_doc[None], scores, -1e30)
    new_max = jnp.maximum(run_max, jnp.max(scores, axis=-1))
    numerators = jnp.exp(scores - new_max[..., None])
    run_sum = jnp.sum(numerators, axis=-1)
    accumulated = jnp.einsum(
        "hrk,khd->hrd",
        numerators.astype(jnp.bfloat16),
        value_heads,
        preferred_element_type=jnp.float32,
    )
    run_max, run_sum, accumulated = (new_max, run_sum, accumulated)
    context = jnp.transpose(accumulated / run_sum[..., None], (1, 0, 2)).reshape(
        row_count, HEADS * HEAD_DIM
    )
    return (context, run_max + jnp.log(run_sum))


def block_grads(
    query_heads, grad_heads, query_seg, log_sum, row_delta, key_heads, value_heads, key_seg
):
    score_scale = HEAD_DIM ** (-0.5)
    scores = (
        jnp.einsum("rhd,khd->hrk", query_heads, key_heads, preferred_element_type=jnp.float32)
        * score_scale
    )
    same_doc = query_seg[:, None] == key_seg[None, :]
    scores = jnp.where(same_doc[None], scores, -1e30)
    probs_full = jnp.exp(scores - log_sum[..., None])
    grad_probs = jnp.einsum(
        "rhd,khd->hrk", grad_heads, value_heads, preferred_element_type=jnp.float32
    )
    grad_scores = (probs_full * (grad_probs - row_delta[..., None])).astype(jnp.bfloat16)
    return (probs_full, grad_scores)


def attend_backward(query_bf, key_bf, value_bf, seg_local, context, log_sum, grad_context):
    row_count = query_bf.shape[0]
    score_scale = HEAD_DIM ** (-0.5)
    key_every, value_every, seg_every = (
        lax.all_gather(key_bf, "ctx", axis=0, tiled=True),
        lax.all_gather(value_bf, "ctx", axis=0, tiled=True),
        lax.all_gather(seg_local, "ctx", axis=0, tiled=True),
    )
    length = key_every.shape[0]
    block_len = min(512, length)
    query_heads = query_bf.reshape(row_count, HEADS, HEAD_DIM)
    grad_heads = grad_context.reshape(row_count, HEADS, HEAD_DIM)
    row_delta = jnp.sum(
        (grad_context.astype(jnp.float32) * context).reshape(row_count, HEADS, HEAD_DIM), axis=-1
    ).T

    def visit_block(grad_query, block_num):
        first_row = block_num * block_len
        key_heads = lax.dynamic_slice_in_dim(key_every, first_row, block_len, 0).reshape(
            block_len, HEADS, HEAD_DIM
        )
        value_heads = lax.dynamic_slice_in_dim(value_every, first_row, block_len, 0).reshape(
            block_len, HEADS, HEAD_DIM
        )
        key_seg = lax.dynamic_slice_in_dim(seg_every, first_row, block_len, 0)
        probs_full, grad_scores = block_grads(
            query_heads, grad_heads, seg_local, log_sum, row_delta, key_heads, value_heads, key_seg
        )
        grad_query = (
            grad_query
            + jnp.einsum("hrk,khd->rhd", grad_scores, key_heads, preferred_element_type=jnp.float32)
            * score_scale
        )
        grad_keys = (
            jnp.einsum("hrk,rhd->khd", grad_scores, query_heads, preferred_element_type=jnp.float32)
            * score_scale
        )
        grad_values = jnp.einsum(
            "hrk,rhd->khd",
            probs_full.astype(jnp.bfloat16),
            grad_heads,
            preferred_element_type=jnp.float32,
        )
        stacked = jnp.stack(
            (
                grad_keys.reshape(block_len, HEADS * HEAD_DIM),
                grad_values.reshape(block_len, HEADS * HEAD_DIM),
            ),
            axis=1,
        )
        return (grad_query, stacked)

    grad_query, pieces = lax.scan(
        visit_block,
        jnp.zeros((row_count, HEADS, HEAD_DIM), jnp.float32),
        jnp.arange(length // block_len),
    )
    key_terms = pieces.reshape(length, 2, HEADS * HEAD_DIM)
    own_rows = lax.psum_scatter(
        key_terms.astype(jnp.bfloat16), "ctx", scatter_dimension=0, tiled=True
    ).astype(jnp.float32)
    grad_keyed = own_rows[:, 0].astype(jnp.bfloat16)
    grad_valued = own_rows[:, 1].astype(jnp.bfloat16)
    grad_queries = grad_query.reshape(row_count, HEADS * HEAD_DIM).astype(jnp.bfloat16)
    return (grad_queries, grad_keyed, grad_valued)


def layer_forward(inputs, seg_local, full_weights):
    (
        query_weight,
        key_weight,
        value_weight,
        output_weight,
        expand_weight,
        contract_weight,
        query_bias,
        value_bias,
        output_bias,
        first_gain,
        first_shift,
        expand_bias,
        contract_bias,
        second_gain,
        second_shift,
    ) = full_weights
    query_bf = (plain_dot(inputs, query_weight) + query_bias.astype(jnp.float32)).astype(
        jnp.bfloat16
    )
    key_bf = plain_dot(inputs, key_weight).astype(jnp.bfloat16)
    value_bf = (plain_dot(inputs, value_weight) + value_bias.astype(jnp.float32)).astype(
        jnp.bfloat16
    )
    context, log_sum = attend_forward(query_bf, key_bf, value_bf, seg_local)
    context_bf = context.astype(jnp.bfloat16)
    first_sum = (
        inputs.astype(jnp.float32)
        + plain_dot(context_bf, output_weight)
        + output_bias.astype(jnp.float32)
    )
    first_out, normed_one, inverse_one = norm_forward(first_sum, first_gain, first_shift)
    first_bf = first_out.astype(jnp.bfloat16)
    hidden = plain_dot(first_bf, expand_weight) + expand_bias.astype(jnp.float32)
    gelled_bf = jax.nn.gelu(hidden, approximate=False).astype(jnp.bfloat16)
    second_sum = (
        first_out + plain_dot(gelled_bf, contract_weight) + contract_bias.astype(jnp.float32)
    )
    result, normed_two, inverse_two = norm_forward(second_sum, second_gain, second_shift)
    kept_state = (
        query_bf,
        key_bf,
        value_bf,
        context,
        log_sum,
        context_bf,
        normed_one,
        inverse_one,
        first_bf,
        hidden,
        gelled_bf,
        normed_two,
        inverse_two,
    )
    return (result.astype(jnp.bfloat16), kept_state)


def layer_backward(inputs, seg_local, grad_out, kept_state, full_weights):
    (
        query_weight,
        key_weight,
        value_weight,
        output_weight,
        expand_weight,
        contract_weight,
        query_bias,
        value_bias,
        output_bias,
        first_gain,
        first_shift,
        expand_bias,
        contract_bias,
        second_gain,
        second_shift,
    ) = full_weights
    (
        query_bf,
        key_bf,
        value_bf,
        context,
        log_sum,
        context_bf,
        normed_one,
        inverse_one,
        first_bf,
        hidden,
        gelled_bf,
        normed_two,
        inverse_two,
    ) = kept_state
    grad_second, second_gain_grad, second_shift_grad = norm_backward(
        grad_out.astype(jnp.float32), normed_two, inverse_two, second_gain
    )
    grad_branch = grad_second.astype(jnp.bfloat16)
    contract_weight_grad = left_dot(gelled_bf, grad_branch)
    contract_bias_grad = jnp.sum(grad_branch.astype(jnp.float32), axis=0)
    grad_gelled = right_dot(grad_branch, contract_weight)
    gelu_pull = jax.vjp(lambda values: jax.nn.gelu(values, approximate=False), hidden)[1]
    grad_hidden = gelu_pull(grad_gelled)[0].astype(jnp.bfloat16)
    expand_weight_grad = left_dot(first_bf, grad_hidden)
    expand_bias_grad = jnp.sum(grad_hidden.astype(jnp.float32), axis=0)
    grad_first = grad_second + right_dot(grad_hidden, expand_weight)
    grad_attn, first_gain_grad, first_shift_grad = norm_backward(
        grad_first, normed_one, inverse_one, first_gain
    )
    grad_attn_low = grad_attn.astype(jnp.bfloat16)
    output_weight_grad = left_dot(context_bf, grad_attn_low)
    output_bias_grad = jnp.sum(grad_attn_low.astype(jnp.float32), axis=0)
    grad_context = right_dot(grad_attn_low, output_weight).astype(jnp.bfloat16)
    grad_queries, grad_keyed, grad_valued = attend_backward(
        query_bf, key_bf, value_bf, seg_local, context, log_sum, grad_context
    )
    query_weight_grad = left_dot(inputs, grad_queries)
    key_weight_grad = left_dot(inputs, grad_keyed)
    value_weight_grad = left_dot(inputs, grad_valued)
    query_bias_grad = jnp.sum(grad_queries.astype(jnp.float32), axis=0)
    value_bias_grad = jnp.sum(grad_valued.astype(jnp.float32), axis=0)
    grad_input = (
        grad_attn
        + right_dot(grad_queries, query_weight)
        + right_dot(grad_keyed, key_weight)
        + right_dot(grad_valued, value_weight)
    )
    grad_terms = (
        query_weight_grad,
        key_weight_grad,
        value_weight_grad,
        output_weight_grad,
        expand_weight_grad,
        contract_weight_grad,
        query_bias_grad,
        value_bias_grad,
        output_bias_grad,
        first_gain_grad,
        first_shift_grad,
        expand_bias_grad,
        contract_bias_grad,
        second_gain_grad,
        second_shift_grad,
    )
    return (grad_input, grad_terms)


def per_device(
    layer_input,
    segments,
    cotangent,
    query_weight,
    key_weight,
    value_weight,
    output_weight,
    expand_weight,
    contract_weight,
    query_bias,
    value_bias,
    output_bias,
    first_gain,
    first_shift,
    expand_bias,
    contract_bias,
    second_gain,
    second_shift,
):
    shards = (
        query_weight,
        key_weight,
        value_weight,
        output_weight,
        expand_weight,
        contract_weight,
        query_bias,
        value_bias,
        output_bias,
        first_gain,
        first_shift,
        expand_bias,
        contract_bias,
        second_gain,
        second_shift,
    )
    micro_count = layer_input.shape[0]
    results = []
    grad_inputs = []
    totals = None
    for micro_step in range(micro_count):
        inputs = layer_input[micro_step, 0]
        seg_local = segments[micro_step, 0].astype(jnp.bfloat16)
        front_weights = gather_weights(shards)
        result, kept_state = layer_forward(inputs, seg_local, front_weights)
        behind = gather_weights(shards)
        grad_input, grad_terms = layer_backward(
            inputs, seg_local, cotangent[micro_step, 0], kept_state, behind
        )
        results.append(result)
        grad_inputs.append(grad_input)
        if totals is None:
            totals = grad_terms
        else:
            totals = tuple(
                (left_side + right_side for left_side, right_side in zip(totals, grad_terms))
            )
    reduced = jax.tree.map(
        lambda part: part.astype(jnp.float32),
        lax.psum_scatter(as_sent(totals), "fsdp", scatter_dimension=0, tiled=True),
    )
    summed = jax.tree.map(lambda part: part.astype(jnp.float32), lax.psum(as_sent(reduced), "ctx"))
    layer_output = jnp.stack(results, axis=0)[:, None]
    input_grad = jnp.stack(grad_inputs, axis=0)[:, None]
    return (
        layer_output,
        input_grad,
        summed[0],
        summed[1],
        summed[2],
        summed[3],
        summed[4],
        summed[5],
        summed[6],
        summed[7],
        summed[8],
        summed[9],
        summed[10],
        summed[11],
        summed[12],
        summed[13],
        summed[14],
    )


MESH = pl.DeviceIdType.MESH
BF = jnp.bfloat16
F32 = jnp.float32
CHUNKS = 24
SLOTS = 3
LAND = 6
LAND_D = 4
ROOM = 10
LAG = (0, 1, 3, 5, 6, 7, 8, 9, 11)
Z_FROM, Z_TO = 12, 14
Y_ROWS, X_ROWS, Z_ROWS = 40, 16, 8


def coords():
    c, f = lax.axis_index("ctx"), lax.axis_index("fsdp")
    return c // 2, c % 2, f // 2, f % 2


def dev(z, x, y, k):
    return (z * 2 + x, y * 2 + k)


def greet(z, x, y, k):
    barrier = pltpu.get_barrier_semaphore()
    for step in range(1, 8):
        place = (z * 2 + k + step) % 8
        pl.semaphore_signal(
            barrier, inc=1, device_id=dev(place // 2, x, y, place % 2), device_id_type=MESH
        )
    pl.semaphore_signal(barrier, inc=1, device_id=dev(z, 1 - x, y, k), device_id_type=MESH)
    pl.semaphore_signal(barrier, inc=1, device_id=dev(z, x, 1 - y, k), device_id_type=MESH)
    pl.semaphore_wait(barrier, 9)


def remote(src, dst, send, recv, to):
    return pltpu.make_async_remote_copy(
        src_ref=src, dst_ref=dst, send_sem=send, recv_sem=recv, device_id=to, device_id_type=MESH
    )


def rows_of(start, size, unit=16):
    return pl.ds(pl.multiple_of(start, unit), size)


def two_heads(block):
    lane = lax.broadcasted_iota(jnp.int32, block.shape, 1)
    zero = jnp.zeros_like(block)
    return jnp.concatenate(
        [jnp.where(lane < HEAD_DIM, block, zero), jnp.where(lane >= HEAD_DIM, block, zero)], axis=0
    )


def one_block(pair):
    rows = pair.shape[0] // 2
    lane = lax.broadcasted_iota(jnp.int32, (rows, pair.shape[1]), 1)
    return jnp.where(lane < HEAD_DIM, pair[:rows], pair[rows:])


def softmax_pair(queries, keys, bias):
    scores = right_dot(queries, keys)
    scores = scores + jnp.concatenate([bias, bias], axis=0)
    numer = jnp.exp(scores - jnp.max(scores, axis=-1, keepdims=True))
    return numer * (1.0 / jnp.sum(numer, axis=-1, keepdims=True))


def layer_kernel(
    inp, cot, seg, wq, wk, wv, wo, we, wc, *rest,
):
    (
        vecs, (fq, fk, fv, fo, fe, fc), (o_q, o_k, o_v, o_o, o_e, o_c), (resf, dxf, vec_out), rest
    ) = (rest[:9], rest[9:15], rest[15:21], rest[21:24], rest[24:])
    (
        s_d, l_d, r_d, b_y, r_y, b_x, r_x, b_1, r_1, b_2, r_2, o_b,
        gh, acc, ga, gal, dctx, dq, dk, dv, bias, we_b, wc_b, w_b,
        dx_r, dx_y, vec, v_s, v_d, v_r,
        gel, gb, fb, gp, n1, inv1, ctx, q, key, val, xf, res, segf, vec_in, vecf, row8, row_e,
        ss, rs, ds, dr, a_send, a_recv, v_send, v_recv, w_sem, o_sem,
        i_send, i_recv, g_send, g_recv, p_send, p_recv, f_send, f_recv,
    ) = rest
    dx_b, dx_s = dctx, gb
    cotf = gh.at[:, pl.ds(0, 1024)]
    z, x, y, k = coords()
    f = y * 2 + k
    other = (1 - y) * 2 + k
    sib, xn, yn = dev(z, x, y, 1 - k), dev(z, 1 - x, y, k), dev(z, x, 1 - y, k)
    bit1, bit2 = z % 2, z // 2
    z1 = dev(z + 1 - 2 * bit1, x, y, k)
    z2 = dev((z + 2) % 4, x, y, k)
    color = bit1 * 2 + x
    c_x, c_z, c_o = color + 1 - 2 * x, (color + 2) % 4, 3 - color
    own_rows = rows_of(x * 512 + k * 256, 256)

    def block_moves(mb):
        to_z, to_k = mb * 2 + k, z // 2
        row = x * 512 + z * 128
        slot = z % 2
        mine = (to_z == z) & (to_k == k)
        moves = (
            (inp.at[mb, 0], xf.at[rows_of(row, 128)], 0),
            (seg.at[mb], segf.at[x * 4 + z], 1),
            (cot.at[mb, 0], cotf.at[rows_of(slot * 128, 128)], 2),
        )
        return mine, dev(to_z, x, y, to_k), slot, moves

    def start_blocks(which):
        for mb in range(2):
            mine, to, slot, moves = block_moves(mb)
            for src, dst, n in moves:
                if n not in which:
                    continue

                @pl.when(mine)
                def _():
                    pltpu.make_async_copy(src, dst, i_recv.at[n, slot]).start()

                @pl.when(jnp.logical_not(mine))
                def _():
                    remote(src, dst, i_send.at[n, mb], i_recv.at[n, slot], to).start()

    def finish_blocks(which):
        for mb in range(2):
            mine, to, slot, moves = block_moves(mb)
            for src, dst, n in moves:
                if n not in which:
                    continue

                @pl.when(jnp.logical_not(mine))
                def _():
                    remote(src, dst, i_send.at[n, mb], i_recv.at[n, slot], to).wait_send()

    def arrive_blocks(which):
        for slot in range(2):
            zz = 2 * k + slot
            for n in which:
                if n == 0:
                    dst = xf.at[rows_of(x * 512 + zz * 128, 128)]
                elif n == 1:
                    dst = segf.at[x * 4 + zz]
                else:
                    dst = cotf.at[pl.ds(slot * 128, 128)]
                pltpu.make_async_copy(dst, dst, i_recv.at[n, slot]).wait()

    def group_copy(step):
        who = x if step < 2 else 1 - x
        src = xf.at[rows_of(who * 512 + k * 256, 256)]
        sseg = segf.at[pl.ds(who * 4 + k * 2, 2)]
        to = (sib, xn, sib)[step]
        return (
            remote(src, src, g_send.at[0, step], g_recv.at[0, step], to),
            remote(sseg, sseg, g_send.at[1, step], g_recv.at[1, step], to),
        )

    def group_arrive(step):
        who = (x, 1 - x, 1 - x)[step]
        kk = (1 - k, k, 1 - k)[step]
        src = xf.at[rows_of(who * 512 + kk * 256, 256)]
        sseg = segf.at[pl.ds(who * 4 + kk * 2, 2)]
        pltpu.make_async_copy(src, src, g_recv.at[0, step]).wait()
        pltpu.make_async_copy(sseg, sseg, g_recv.at[1, step]).wait()

    items = []
    for shard, full in ((wq, fq), (wk, fk), (wv, fv), (wo, fo)):
        items.append((shard, full, 0, 0, 256))
    for j in range(4):
        items.append((we, fe, 0, j * 1024, 256))
    for j in range(4):
        items.append((wc, fc, j * 256, 0, 1024))
    n_items = len(items)

    def part(i, quarter, start, size, own_src=False):
        shard, full, row, col, step = items[i]
        if own_src:
            return shard.at[rows_of(row + start, size, 8), pl.ds(col, 1024)]
        return full.at[rows_of(quarter * step + row + start, size, 8), pl.ds(col, 1024)]

    def send_copy(i, kind):
        sems = (p_send.at[kind, i], p_recv.at[kind, i])
        if kind == 0:
            return remote(part(i, f, color * 64, 64, True), part(i, f, color * 64, 64), *sems, yn)
        if kind == 1:
            return remote(part(i, f, c_o * 64, Y_ROWS, True), part(i, f, c_o * 64, Y_ROWS), *sems, yn)
        if kind == 2:
            src = part(i, other, color * 64, 64)
            return remote(src, src, *sems, xn)
        if kind == 3:
            src = part(i, other, c_z * 64 + Y_ROWS, X_ROWS)
            return remote(src, src, *sems, xn)
        if kind == 4:
            src = part(i, other, color * 64, 64)
            return remote(src, src, *sems, z1)
        if kind == 5:
            src = part(i, other, c_x * 64 + Y_ROWS + X_ROWS, Z_ROWS)
            return remote(src, src, *sems, z1)
        if kind == 6:
            return remote(part(i, f, 0, 256, True), part(i, f, 0, 256), *sems, sib)
        src = part(i, other, 0, 256)
        return remote(src, src, *sems, sib)

    def arrive(i, kind):
        if kind == 0:
            dst = part(i, other, color * 64, 64)
        elif kind == 1:
            dst = part(i, other, c_o * 64, Y_ROWS)
        elif kind == 2:
            dst = part(i, other, c_x * 64, 64)
        elif kind == 3:
            dst = part(i, other, c_o * 64 + Y_ROWS, X_ROWS)
        elif kind == 4:
            dst = part(i, other, c_z * 64, 64)
        elif kind == 5:
            dst = part(i, other, c_o * 64 + Y_ROWS + X_ROWS, Z_ROWS)
        elif kind == 6:
            dst = part(i, y * 2 + 1 - k, 0, 256)
        else:
            dst = part(i, (1 - y) * 2 + 1 - k, 0, 256)
        pltpu.make_async_copy(dst, dst, p_recv.at[kind, i]).wait()


    for i in range(8):
        packed = vecs[i][...].astype(F32).reshape(1, 256)
        vec_in[pl.ds(2 * i, 1)] = packed[:, :128]
        vec_in[pl.ds(2 * i + 1, 1)] = packed[:, 128:]
    packed = vecs[8][...].astype(F32).reshape(1, 1024)
    for n in range(8):
        vec_in[pl.ds(16 + n, 1)] = packed[:, n * 128 : n * 128 + 128]
    vecf[f] = vec_in[...]
    vec_copies = (
        remote(vec_in, vecf.at[f], f_send.at[0], f_recv.at[0], yn),
        remote(vec_in, vecf.at[f], f_send.at[1], f_recv.at[1], sib),
        remote(vecf.at[other], vecf.at[other], f_send.at[2], f_recv.at[2], sib),
    )

    def load_square(shard, full, row, step, cols, dst, sem):
        out = []
        for d in range(4):
            quarter = (f + d) % 4
            src = shard.at[pl.ds(row, 256), cols]
            if d > 0:
                src = full.at[rows_of(quarter * step + row, 256), cols]
            out.append(pltpu.make_async_copy(src, dst.at[rows_of(quarter * 256, 256)], sem))
        return out

    def load_c(j):
        slot = j % 2
        sem = w_sem.at[slot]

        @pl.when(j // 2 == f)
        def _():
            src = wc.at[rows_of((j % 2) * 512, 512)]
            pltpu.make_async_copy(src, wc_b.at[slot], sem).start()

        @pl.when(j // 2 != f)
        def _():
            pltpu.make_async_copy(fc.at[rows_of(j * 512, 512)], wc_b.at[slot], sem).start()

    def load_e(j):
        for move in load_square(
            we, fe, 0, 256, rows_of(j * 512, 512, 512), we_b.at[j % 2], w_sem.at[2 + j % 2]
        ):
            move.start()

    def load_w(n):
        shard, full = ((wo, fo), (wk, fk), (wv, fv), (wq, fq))[n]
        for move in load_square(
            shard, full, 0, 256, pl.ds(0, 1024), w_b.at[n], w_sem.at[4 + n]
        ):
            move.start()

    def loaded_w(n):
        pltpu.make_async_copy(w_b.at[n], w_b.at[n], w_sem.at[4 + n]).wait()

    def load_item(i):
        shard, full, row, col, step = items[i]
        arrive(i, 6)
        arrive(i, 7)
        slot = i % 4
        for move in load_square(
            shard, full, row, step, pl.ds(col, 1024), w_b.at[slot], w_sem.at[4 + slot]
        ):
            move.start()

    def item(i):
        slot = i % 4
        pltpu.make_async_copy(w_b.at[slot], w_b.at[slot], w_sem.at[4 + slot]).wait()
        return w_b.at[slot]

    def relay(t):
        for u in (0, 1, 2) if t == 0 else (t + 2,):
            if u < n_items:
                send_copy(u, 0).start()
                send_copy(u, 1).start()
                send_copy(u, 6).start()
        if 1 <= t <= n_items:
            i = t - 1
            arrive(i, 0)
            send_copy(i, 2).start()
            send_copy(i, 4).start()
        if 2 <= t <= n_items + 1:
            i = t - 2
            arrive(i, 4)
            send_copy(i, 3).start()
            arrive(i, 2)
            send_copy(i, 5).start()
        if 3 <= t <= n_items + 2:
            i = t - 3
            arrive(i, 1)
            arrive(i, 3)
            arrive(i, 5)
            send_copy(i, 7).start()

    def fill_rows():
        pltpu.make_async_copy(vec_in, vec_in, f_recv.at[1]).wait()
        pltpu.make_async_copy(vec_in, vec_in, f_recv.at[2]).wait()
        for quarter in range(4):
            for i in range(8):
                for half in range(2):
                    col = quarter * 256 + half * 128
                    row8[pl.ds(i, 1), col : col + 128] = vecf[quarter, pl.ds(2 * i + half, 1)]
            for n in range(8):
                col = quarter * 1024 + n * 128
                row_e[:, col : col + 128] = vecf[quarter, pl.ds(16 + n, 1)]

    def fill_bias():
        for block in range(2):
            own = segf[x * 4 + k * 2 + block].astype(F32)
            down = jnp.transpose(jnp.broadcast_to(own, (128, 128)))
            for n in range(8):
                across = segf[n].astype(F32)
                bias[block * 128 : block * 128 + 128, n * 128 : n * 128 + 128] = jnp.where(
                    down == across, 0.0, -1e30
                )

    def project_own(w):
        q[...] = (plain_dot(xf[own_rows], w[...]) + row8[0:1]).astype(BF)

    def project_all(w, dst, add_row):
        def block(n, carry):
            rows = rows_of(n * 256, 256)
            dst[rows] = (plain_dot(xf[rows], w[...]) + add_row).astype(BF)
            return carry

        lax.fori_loop(0, 4, block, 0)

    def heads(first, last):
        def one(h, carry):
            cols = rows_of(h * 128, 128, 128)
            queries = two_heads(q[:, cols] * BF(HEAD_DIM**-0.5))
            probs = softmax_pair(queries, key[:, cols], bias[...])
            ctx[:, cols] = one_block(plain_dot(probs.astype(BF), val[:, cols])).astype(BF)
            return carry

        lax.fori_loop(first, last, one, 0)

    def norm(v):
        centre = v - jnp.mean(v, axis=-1, keepdims=True)
        inverse = lax.rsqrt(jnp.mean(centre * centre, axis=-1, keepdims=True) + 1e-05)
        return centre * inverse, inverse

    def attention_out(w):
        normed, inverse = norm(
            xf[own_rows].astype(F32) + plain_dot(ctx[...], w[...]) + row8[2:3]
        )
        n1[...] = normed
        inv1[...] = inverse
        first_out = normed * row8[3:4] + row8[4:5]
        acc[...] = first_out
        fb[...] = first_out.astype(BF)

    def expand(j, w):
        def block(n, carry):
            cols = rows_of(n * 256, 256, 256)
            out = rows_of(j * 1024 + n * 256, 256, 256)
            hidden = plain_dot(fb[...], w[:, cols]) + row_e[:, out]
            below = 0.5 + 0.5 * lax.erf(hidden * 0.5**0.5)
            gel[:, out] = (hidden * below).astype(BF)
            bell = jnp.exp(-0.5 * hidden * hidden) * (2 * math.pi) ** -0.5
            gp[:, out] = (below + hidden * bell).astype(BF)
            return carry

        lax.fori_loop(0, 4, block, 0)

    def contract(j, w):
        for quarter in range(4):
            cols = pl.ds(quarter * 1024 + j * 256, 256)
            acc[...] += plain_dot(gel[:, cols], w[quarter * 256 : quarter * 256 + 256])

    def second_norm():
        normed, inverse = norm(acc[...] + row8[5:6])
        res[...] = (normed * row8[6:7] + row8[7:8]).astype(BF)
        grad_out = cotf[...].astype(F32)
        keep(6, column(grad_out * normed))
        keep(7, column(grad_out))
        scaled = grad_out * row8[6:7]
        grad = inverse * (
            scaled
            - jnp.mean(scaled, axis=-1, keepdims=True)
            - normed * jnp.mean(scaled * normed, axis=-1, keepdims=True)
        )
        acc[...] = grad
        low = grad.astype(BF)
        gb[...] = low
        keep(5, column(low))


    def back(n, slot):
        to_z = 2 * k + slot
        to_k = z % 2
        mb = z // 2
        mine = (to_z == z) & (to_k == k)
        src = (res, dx_b)[n].at[pl.ds(slot * 128, 128)]
        dst = (resf, dxf)[n].at[mb, 0]

        def far():
            return remote(
                src, dst, a_send.at[n, slot], a_recv.at[n, mb], dev(to_z, x, y, to_k)
            )

        def near():
            return pltpu.make_async_copy(src, dst, a_recv.at[n, mb])

        return mine, far, near

    def start_back(n):
        for slot in range(2):
            mine, far, near = back(n, slot)

            @pl.when(mine)
            def _():
                near().start()

            @pl.when(jnp.logical_not(mine))
            def _():
                far().start()

    def finish_back(n):
        for slot in range(2):
            mine, far, _ = back(n, slot)

            @pl.when(jnp.logical_not(mine))
            def _():
                far().wait_send()

        for mb in range(2):
            dst = (resf, dxf)[n].at[mb, 0]
            pltpu.make_async_copy(dst, dst, a_recv.at[n, mb]).wait()

    def column(v):
        return jnp.sum(v.astype(F32), axis=0, keepdims=True)

    def keep(i, row):
        for quarter in range(4):
            for half in range(2):
                col = quarter * 256 + half * 128
                vec[quarter, pl.ds(2 * i + half, 1)] = row[:, col : col + 128]

    v_peers = (sib, yn, xn, z1, z2)

    def v_copy(stage):
        if stage == 0:
            return remote(v_d.at[1], v_d.at[2], v_send.at[0], v_recv.at[0], sib)
        src = v_s.at[0, 1 - y] if stage == 1 else v_s.at[stage - 1, 0]
        return remote(src, v_r.at[stage - 1], v_send.at[stage], v_recv.at[stage], v_peers[stage])

    def v_step(stage):
        if stage == 0:
            for plane in range(2):
                v_d[0, plane] = vec[plane * 2 + k]
                v_d[1, plane] = vec[plane * 2 + 1 - k]
        elif stage == 1:
            pltpu.make_async_copy(v_d.at[2], v_d.at[2], v_recv.at[0]).wait()
            v_s[0] = v_d[0] + v_d[2]
        else:
            dst = v_r.at[stage - 2]
            pltpu.make_async_copy(dst, dst, v_recv.at[stage - 1]).wait()
            mine = v_s[0, y] if stage == 2 else v_s[stage - 2, 0]
            total = mine + v_r[stage - 2]
            if stage == 5:
                vec_out[...] = total
            else:
                v_s[stage - 1, 0] = total
        if stage < 5:
            v_copy(stage).start()

    def send(stage, i, src, dst, to):
        return remote(src, dst, ss.at[stage, i % SLOTS], rs.at[stage, i % LAND], to)

    def landed(stage, i, dst):
        pltpu.make_async_copy(dst, dst, rs.at[stage, i % LAND]).wait()

    def order(i):
        late = (i // Z_FROM) * (1 - i // Z_TO) if Z_FROM < Z_TO else 0
        bits = tuple(
            (1 - late) * p + late * q
            for p, q in ((x, bit1), (bit1, bit2), (bit2, x))
        )
        peers = tuple(
            tuple((1 - late) * p + late * q for p, q in zip(one, two))
            for one, two in ((xn, z1), (z1, z2), (z2, xn))
        )
        return bits, peers

    def copies(stage, i):
        slot, land, room = i % SLOTS, i % LAND, i % ROOM
        (first, second, third), peers = order(i)
        if stage == 0:
            return send(0, i, s_d.at[slot], r_d.at[i % LAND_D], sib)
        if stage == 1:
            return send(1, i, b_y.at[slot, 1 - y], r_y.at[land], yn)
        if stage == 2:
            return send(2, i, b_x.at[slot, rows_of((1 - first) * 64, 64)], r_x.at[land], peers[0])
        if stage == 3:
            return send(3, i, b_1.at[slot, rows_of((1 - second) * 32, 32)], r_1.at[land], peers[1])
        if stage == 4:
            return send(4, i, b_2.at[slot, rows_of((1 - third) * 16, 16)], r_2.at[land], peers[2])
        if stage == 5:
            own = o_b.at[room, rows_of(first * 64 + second * 32 + third * 16, 16)]
            return send(5, i, own, own, peers[2])
        if stage == 6:
            own = o_b.at[room, rows_of(first * 64 + second * 32, 32)]
            return send(6, i, own, own, peers[1])
        own = o_b.at[room, rows_of(first * 64, 64)]
        return send(7, i, own, own, peers[0])

    def launch(stage, i):
        copies(stage, i).start()

    def clear(stage, i):
        @pl.when(i >= SLOTS)
        def _():
            copies(stage, i - SLOTS).wait_send()

    def add(a, b):
        return (a.astype(F32) + b.astype(F32)).astype(BF)

    def terms(i, a_ref, b_ref, a_base, a_step, b_col, a_rows=None):
        slot = i % SLOTS
        right = b_ref[:, b_col]
        for plane in range(2):
            for core in range(2):
                quarter = plane * 2 + (k if core == 0 else 1 - k)
                cols = pl.ds(pl.multiple_of(a_base + quarter * a_step, 128), 128)
                left = a_ref[:, cols] if a_rows is None else a_ref[a_rows, cols]
                product = left_dot(left, right).astype(BF)
                if core == 0:
                    l_d[slot, plane] = product
                else:
                    s_d[slot, plane] = product

    every = pl.ds(0, 1024)

    def stage_zero(i):
        @pl.when((i >= 0) & (i < CHUNKS))
        def _():
            clear(0, i)

        @pl.when(i < 8)
        def _():
            terms(i, gel, gb, i * 128, 1024, every)

        @pl.when((i >= 8) & (i < 16))
        def _():
            j = i - 8
            terms(i, fb, gh, (j % 2) * 128, 256, rows_of((j // 2) * 1024, 1024, 1024))

        @pl.when((i >= 16) & (i < 18))
        def _():
            terms(i, ctx, gal, (i - 16) * 128, 256, every)

        @pl.when((i >= 18) & (i < 20))
        def _():
            terms(i, xf, dq, (i - 18) * 128, 256, every, own_rows)

        @pl.when((i >= 20) & (i < 22))
        def _():
            terms(i, xf, dk, (i - 20) * 128, 256, every)

        @pl.when((i >= 22) & (i < 24))
        def _():
            terms(i, xf, dv, (i - 22) * 128, 256, every)

        @pl.when((i >= 0) & (i < CHUNKS))
        def _():
            launch(0, i)

    def stored():
        pltpu.make_async_copy(o_b.at[0], o_b.at[0], o_sem).wait()

    def store(i):
        src = o_b.at[i % ROOM]

        @pl.when(i >= 1)
        def _():
            stored()

        @pl.when(i < 8)
        def _():
            pltpu.make_async_copy(src, o_c.at[rows_of(i * 128, 128)], o_sem).start()

        @pl.when((i >= 8) & (i < 16))
        def _():
            j = i - 8
            dst = o_e.at[rows_of((j % 2) * 128, 128), rows_of((j // 2) * 1024, 1024, 1024)]
            pltpu.make_async_copy(src, dst, o_sem).start()

        for n, ref in enumerate((o_o, o_q, o_k, o_v)):
            first = 16 + 2 * n

            @pl.when((i >= first) & (i < first + 2))
            def _():
                dst = ref.at[rows_of((i - first) * 128, 128)]
                pltpu.make_async_copy(src, dst, o_sem).start()

    def feed_forward(j):
        slot = j % 2
        cols = rows_of(j * 512, 512, 512)
        pltpu.make_async_copy(wc_b.at[slot], wc_b.at[slot], w_sem.at[slot]).wait()
        pltpu.make_async_copy(we_b.at[slot], we_b.at[slot], w_sem.at[2 + slot]).wait()

        grads = (right_dot(gb[...], wc_b[slot]) * gp[:, cols].astype(F32)).astype(BF)
        gh[:, cols] = grads
        acc[...] += right_dot(grads, we_b[slot])
        row = column(grads)
        for n in range(4):
            vec[j // 2, pl.ds(16 + (j % 2) * 4 + n, 1)] = row[:, n * 128 : n * 128 + 128]

        @pl.when(j < 6)
        def _():
            load_c(j + 2)
            load_e(j + 2)

    def first_norm():
        normed = n1[...]
        grad_first = acc[...]
        keep(3, column(grad_first * normed))
        keep(4, column(grad_first))
        scaled = grad_first * row8[3:4]
        grad_attn = inv1[...] * (
            scaled
            - jnp.mean(scaled, axis=-1, keepdims=True)
            - normed * jnp.mean(scaled * normed, axis=-1, keepdims=True)
        )
        ga[...] = grad_attn
        low = grad_attn.astype(BF)
        gal[...] = low
        keep(2, column(low))
        loaded_w(0)
        dctx[...] = right_dot(low, w_b[0]).astype(BF)

    def attention(h):
        cols = rows_of(h * 128, 128, 128)
        queries = two_heads(q[:, cols] * BF(HEAD_DIM**-0.5))
        keys = key[:, cols]
        probs = softmax_pair(queries, keys, bias[...])
        grads = two_heads(dctx[:, cols])
        grad_probs = right_dot(grads, val[:, cols])
        delta = jnp.sum(probs * grad_probs, axis=-1, keepdims=True)
        grad_scores = (probs * (grad_probs - delta)).astype(BF)
        dv[:, cols] = left_dot(probs.astype(BF), grads).astype(BF)
        dk[:, cols] = left_dot(grad_scores, queries).astype(BF)
        dq[:, cols] = (one_block(plain_dot(grad_scores, keys)) * HEAD_DIM**-0.5).astype(BF)

    def dx_core(g):
        return remote(gel.at[:, pl.ds(g * 1024, 1024)], dx_r.at[g], ds.at[g], dr.at[g], sib)

    dx_far = remote(dx_s, dx_y, ds.at[2], dr.at[2], xn)

    def input_rows(n):
        who = x * (n % 2) + (1 - x) * (1 - n % 2)
        core = (1 - k) * (1 - n // 2) + k * (n // 2)
        rows = rows_of(who * 512 + core * 256, 256)
        terms_here = right_dot(dk[rows], w_b[1]) + right_dot(dv[rows], w_b[2])

        @pl.when(n == 0)
        def _():
            gel[:, pl.ds(1024, 1024)] = terms_here.astype(BF)
            dx_core(1).start()

        @pl.when(n == 1)
        def _():
            gel[:, pl.ds(0, 1024)] = terms_here.astype(BF)
            dx_core(0).start()

        @pl.when(n == 2)
        def _():
            pltpu.make_async_copy(dx_r.at[1], dx_r.at[1], dr.at[1]).wait()
            dx_s[...] = (terms_here + dx_r[1].astype(F32)).astype(BF)
            dx_far.start()

        @pl.when(n == 3)
        def _():
            pltpu.make_async_copy(dx_r.at[0], dx_r.at[0], dr.at[0]).wait()
            loaded_w(3)
            ga[...] = ga[...] + terms_here + dx_r[0].astype(F32) + right_dot(dq[...], w_b[3])

    greet(z, x, y, k)
    start_blocks((0, 1))
    vec_copies[0].start()
    vec_copies[1].start()
    relay(0)
    relay(1)
    arrive_blocks((0, 1))
    for step in range(2):
        for move in group_copy(step):
            move.start()
    pltpu.make_async_copy(vec_in, vec_in, f_recv.at[0]).wait()
    vec_copies[2].start()
    relay(2)
    relay(3)
    group_arrive(1)
    for move in group_copy(2):
        move.start()
    start_blocks((2,))
    relay(4)
    load_item(0)
    fill_rows()
    relay(5)
    load_item(1)
    project_own(item(0))
    relay(6)
    load_item(2)
    group_arrive(0)
    group_arrive(2)
    fill_bias()
    project_all(item(1), key, 0.0)
    relay(7)
    load_item(3)
    project_all(item(2), val, row8[1:2])
    relay(8)
    load_item(4)
    heads(0, 3)
    relay(9)
    load_item(5)
    heads(3, 6)
    relay(10)
    load_item(6)
    heads(6, 8)
    attention_out(item(3))
    for j in range(4):
        relay(11 + j)
        load_item(7 + j)
        expand(j, item(4 + j))
    load_item(11)
    for j in range(4):
        contract(j, item(8 + j))
    arrive_blocks((2,))
    for j in range(2):
        load_c(j)
        load_e(j)
    for n in range(4):
        load_w(n)
    second_norm()
    start_back(0)

    def tick(t, carry):
        def at(stage):
            i = t - LAG[stage]
            return i, (i >= 0) & (i < CHUNKS)

        stage_zero(t)
        i1, live1 = at(1)

        @pl.when(live1)
        def _():
            slot, land = i1 % SLOTS, i1 % LAND_D
            clear(1, i1)
            landed(0, i1, r_d.at[i1 % LAND_D])
            for plane in range(2):
                b_y[slot, plane] = add(l_d[slot, plane], r_d[land, plane])
            launch(1, i1)

        @pl.when(t < 4)
        def _():
            def one(n, c):
                feed_forward(2 * t + n)
                return c

            lax.fori_loop(0, 2, one, 0)

        @pl.when(t == 4)
        def _():
            first_norm()

        @pl.when((t >= 5) & (t < 13))
        def _():
            attention(t - 5)

        @pl.when(t == 13)
        def _():
            keep(0, column(dq[...]))
            keep(1, column(dv[...]))
            loaded_w(1)
            loaded_w(2)

        @pl.when((t >= 13) & (t < 17))
        def _():
            input_rows(t - 13)

        for stage in range(6):

            @pl.when(t == 14 + 2 * stage)
            def _():
                v_step(stage)

        @pl.when(t == 18)
        def _():
            pltpu.make_async_copy(dx_y, dx_y, dr.at[2]).wait()
            dx_b[...] = (ga[...] + dx_y[...].astype(F32)).astype(BF)
            start_back(1)

        i2, live2 = at(2)

        @pl.when(live2)
        def _():
            slot, land = i2 % SLOTS, i2 % LAND
            clear(2, i2)
            landed(1, i2, r_y.at[land])
            b_x[slot] = add(b_y[slot, y], r_y[land])
            launch(2, i2)

        i3, live3 = at(3)

        @pl.when(live3)
        def _():
            slot, land = i3 % SLOTS, i3 % LAND
            clear(3, i3)
            landed(2, i3, r_x.at[land])
            first = order(i3)[0][0]
            b_1[slot] = add(b_x[slot, rows_of(first * 64, 64)], r_x[land])
            launch(3, i3)

        i4, live4 = at(4)

        @pl.when(live4)
        def _():
            slot, land = i4 % SLOTS, i4 % LAND
            clear(4, i4)
            landed(3, i4, r_1.at[land])
            second = order(i4)[0][1]
            b_2[slot] = add(b_1[slot, rows_of(second * 32, 32)], r_1[land])
            launch(4, i4)

        i5, live5 = at(5)

        @pl.when(live5)
        def _():
            slot, land = i5 % SLOTS, i5 % LAND
            clear(5, i5)
            landed(4, i5, r_2.at[land])
            first, second, third = order(i5)[0]
            o_b[i5 % ROOM, rows_of(first * 64 + second * 32 + third * 16, 16)] = add(
                b_2[slot, rows_of(third * 16, 16)], r_2[land]
            )
            launch(5, i5)

        i6, live6 = at(6)

        @pl.when(live6)
        def _():
            clear(6, i6)
            first, second, third = order(i6)[0]
            row = first * 64 + second * 32 + (1 - third) * 16
            landed(5, i6, o_b.at[i6 % ROOM, rows_of(row, 16)])
            launch(6, i6)

        i7, live7 = at(7)

        @pl.when(live7)
        def _():
            clear(7, i7)
            first, second, _ = order(i7)[0]
            landed(6, i7, o_b.at[i7 % ROOM, rows_of(first * 64 + (1 - second) * 32, 32)])
            launch(7, i7)

        i8, live8 = at(8)

        @pl.when(live8)
        def _():
            first = order(i8)[0][0]
            landed(7, i8, o_b.at[i8 % ROOM, rows_of((1 - first) * 64, 64)])
            store(i8)

        return carry

    lax.fori_loop(0, CHUNKS + LAG[8], tick, 0)
    stored()
    for stage in range(8):
        for i in range(CHUNKS - SLOTS, CHUNKS):
            copies(stage, i).wait_send()
    for stage in range(5):
        v_copy(stage).wait_send()
    dx_core(0).wait_send()
    dx_core(1).wait_send()
    dx_far.wait_send()
    finish_back(0)
    finish_back(1)
    for i in range(n_items):
        for kind in range(8):
            send_copy(i, kind).wait_send()
    finish_blocks((0, 1, 2))
    for step in range(3):
        for move in group_copy(step):
            move.wait_send()
    for move in vec_copies:
        move.wait_send()


def layer_call(inp, cot, seg, weights, vectors):
    vmem = pl.BlockSpec(memory_space=pltpu.VMEM)
    any_spec = pl.BlockSpec(memory_space=pl.ANY)
    dma = pltpu.SemaphoreType.DMA
    grad = jax.ShapeDtypeStruct((256, 1024), BF)
    square = jax.ShapeDtypeStruct((1024, 1024), BF)
    full_weights = [square] * 4 + [
        jax.ShapeDtypeStruct((1024, 4096), BF), jax.ShapeDtypeStruct((4096, 1024), BF)
    ]
    return pl.pallas_call(
        layer_kernel,
        out_shape=full_weights + [
            grad, grad, grad, grad,
            jax.ShapeDtypeStruct((256, 4096), BF),
            jax.ShapeDtypeStruct((1024, 1024), BF),
            jax.ShapeDtypeStruct((2, 1, 128, 1024), BF),
            jax.ShapeDtypeStruct((2, 1, 128, 1024), BF),
            jax.ShapeDtypeStruct((24, 128), F32),
        ],
        in_specs=[any_spec] * 9 + [vmem] * 9,
        out_specs=[any_spec] * 14 + [vmem],
        scratch_shapes=[
            pltpu.VMEM((SLOTS, 2, 128, 1024), BF),
            pltpu.VMEM((SLOTS, 2, 128, 1024), BF),
            pltpu.VMEM((LAND_D, 2, 128, 1024), BF),
            pltpu.VMEM((SLOTS, 2, 128, 1024), BF),
            pltpu.VMEM((LAND, 128, 1024), BF),
            pltpu.VMEM((SLOTS, 128, 1024), BF),
            pltpu.VMEM((LAND, 64, 1024), BF),
            pltpu.VMEM((SLOTS, 64, 1024), BF),
            pltpu.VMEM((LAND, 32, 1024), BF),
            pltpu.VMEM((SLOTS, 32, 1024), BF),
            pltpu.VMEM((LAND, 16, 1024), BF),
            pltpu.VMEM((ROOM, 128, 1024), BF),
            pltpu.VMEM((256, 4096), BF),
            pltpu.VMEM((256, 1024), F32),
            pltpu.VMEM((256, 1024), F32),
            pltpu.VMEM((256, 1024), BF),
            pltpu.VMEM((256, 1024), BF),
            pltpu.VMEM((256, 1024), BF),
            pltpu.VMEM((1024, 1024), BF),
            pltpu.VMEM((1024, 1024), BF),
            pltpu.VMEM((256, 1024), F32),
            pltpu.VMEM((2, 1024, 512), BF),
            pltpu.VMEM((2, 512, 1024), BF),
            pltpu.VMEM((4, 1024, 1024), BF),
            pltpu.VMEM((2, 256, 1024), BF),
            pltpu.VMEM((256, 1024), BF),
            pltpu.VMEM((4, 24, 128), F32),
            pltpu.VMEM((4, 2, 24, 128), F32),
            pltpu.VMEM((3, 2, 24, 128), F32),
            pltpu.VMEM((4, 24, 128), F32),
            pltpu.VMEM((256, 4096), BF),
            pltpu.VMEM((256, 1024), BF),
            pltpu.VMEM((256, 1024), BF),
            pltpu.VMEM((256, 4096), BF),
            pltpu.VMEM((256, 1024), F32),
            pltpu.VMEM((256, 1), F32),
            pltpu.VMEM((256, 1024), BF),
            pltpu.VMEM((256, 1024), BF),
            pltpu.VMEM((1024, 1024), BF),
            pltpu.VMEM((1024, 1024), BF),
            pltpu.VMEM((1024, 1024), BF),
            pltpu.VMEM((256, 1024), BF),
            pltpu.VMEM((8, 1, 128), jnp.int32),
            pltpu.VMEM((24, 128), F32),
            pltpu.VMEM((4, 24, 128), F32),
            pltpu.VMEM((8, 1024), F32),
            pltpu.VMEM((1, 4096), F32),
            dma((8, SLOTS)), dma((8, LAND)), dma((3,)), dma((3,)), dma((2, 2)), dma((2, 2)),
            dma((5,)), dma((5,)), dma((8,)), dma(()),
            dma((3, 2)), dma((3, 2)), dma((2, 3)), dma((2, 3)),
            dma((8, 12)), dma((8, 12)), dma((3,)), dma((3,)),
        ],
        compiler_params=pltpu.CompilerParams(
            collective_id=0, has_side_effects=True, vmem_limit_bytes=61 << 20
        ),
        name="layer",
    )(inp, cot, seg, *weights, *vectors)


def widen_kernel(*refs):
    ins, outs = refs[:9], refs[9:]
    for src, dst in zip(ins[:8], outs[:8]):
        dst[...] = src[...].astype(dst.dtype)
    vec, smalls = ins[8], outs[8:]

    @pl.when(pl.program_id(0) == 0)
    def _():
        for i in range(8):
            for half in range(2):
                smalls[i][pl.ds(half * 128, 128)] = vec[2 * i + half]
        for n in range(8):
            smalls[8][pl.ds(n * 128, 128)] = vec[16 + n]


def widen(narrow, vec):
    steps = 8
    in_specs, out_specs, shapes = [], [], []
    for n, v in enumerate(narrow):
        at = v.ndim - 2
        block = v.shape[:at] + (v.shape[at] // steps,) + v.shape[at + 1 :]

        def place(i, at=at, rank=v.ndim):
            return tuple(i if d == at else 0 for d in range(rank))

        in_specs.append(pl.BlockSpec(block, place))
        out_specs.append(pl.BlockSpec(block, place))
        shapes.append(jax.ShapeDtypeStruct(v.shape, BF if n == 7 else F32))
    in_specs.append(pl.BlockSpec((24, 128), lambda i: (0, 0)))
    for size in (256,) * 8 + (1024,):
        out_specs.append(pl.BlockSpec((size,), lambda i: (0,)))
        shapes.append(jax.ShapeDtypeStruct((size,), F32))
    return pl.pallas_call(
        widen_kernel,
        grid=(steps,),
        out_shape=shapes,
        in_specs=in_specs,
        out_specs=out_specs,
        compiler_params=pltpu.CompilerParams(vmem_limit_bytes=61 << 20),
        name="widen",
    )(*narrow, vec)


def per_group_device(
    layer_input, segments, cotangent,
    query_weight, key_weight, value_weight, output_weight, expand_weight, contract_weight,
    query_bias, value_bias, output_bias, first_gain, first_shift, expand_bias, contract_bias,
    second_gain, second_shift,
):
    outs = layer_call(
        layer_input, cotangent, segments,
        (query_weight, key_weight, value_weight, output_weight, expand_weight, contract_weight),
        (
            query_bias, value_bias, output_bias, first_gain, first_shift, contract_bias,
            second_gain, second_shift, expand_bias,
        ),
    )
    o_q, o_k, o_v, o_o, o_e, o_c, resf, dxf, vec = outs[6:]
    wide = widen((o_q, o_k, o_v, o_o, o_e, o_c, dxf, resf), vec)
    g_q, g_k, g_v, g_o, g_e, g_c, input_grad, layer_output = wide[:8]
    b_q, b_v, b_o, g_one, s_one, b_c, g_two, s_two, b_e = wide[8:]
    return (
        layer_output, input_grad, g_q, g_k, g_v, g_o, g_e, g_c,
        b_q, b_v, b_o, g_one, s_one, b_e, b_c, g_two, s_two,
    )


def solution(mesh):
    in_specs = (
        P(None, "fsdp", "ctx", None),
        P(None, "fsdp", "ctx"),
        P(None, "fsdp", "ctx", None),
        P("fsdp", None),
        P("fsdp", None),
        P("fsdp", None),
        P("fsdp", None),
        P("fsdp", None),
        P("fsdp", None),
        P("fsdp"),
        P("fsdp"),
        P("fsdp"),
        P("fsdp"),
        P("fsdp"),
        P("fsdp"),
        P("fsdp"),
        P("fsdp"),
        P("fsdp"),
    )
    out_specs = (
        P(None, "fsdp", "ctx", None),
        P(None, "fsdp", "ctx", None),
        P("fsdp", None),
        P("fsdp", None),
        P("fsdp", None),
        P("fsdp", None),
        P("fsdp", None),
        P("fsdp", None),
        P("fsdp"),
        P("fsdp"),
        P("fsdp"),
        P("fsdp"),
        P("fsdp"),
        P("fsdp"),
        P("fsdp"),
        P("fsdp"),
        P("fsdp"),
    )
    def whole(layer_input, segments, *rest):
        grouped = (
            dict(mesh.shape) == {"ctx": 8, "fsdp": 4}
            and layer_input.shape == (2, 4, 1024, 1024)
            and rest[5].shape == (1024, 4096)
        )
        body = per_group_device if grouped else per_device
        return jax.shard_map(
            body, mesh=mesh, in_specs=in_specs, out_specs=out_specs, check_vma=False
        )(layer_input, segments, *rest)

    return whole
```

```python
import math

import jax
import jax.numpy as jnp
from jax import lax
from jax.experimental import pallas as pl
from jax.experimental.pallas import tpu as pltpu
from jax.sharding import PartitionSpec as P

HEADS = 16
HEAD_DIM = 64


def as_sent(x):
    return jax.tree.map(lambda a: a.astype(jnp.bfloat16) if a.dtype == jnp.float32 else a, x)


def plain_dot(left_side, right_side):
    return jnp.dot(left_side, right_side, preferred_element_type=jnp.float32)


def left_dot(left_side, right_side):
    return lax.dot_general(
        left_side, right_side, (((0,), (0,)), ((), ())), preferred_element_type=jnp.float32
    )


def right_dot(left_side, right_side):
    return lax.dot_general(
        left_side, right_side, (((1,), (1,)), ((), ())), preferred_element_type=jnp.float32
    )


def norm_forward(hidden, gain_row, offset_row):
    centre = hidden - jnp.mean(hidden, axis=-1, keepdims=True)
    inverse = lax.rsqrt(jnp.mean(centre * centre, axis=-1, keepdims=True) + 1e-05)
    normed = centre * inverse
    return (normed * gain_row.astype(jnp.float32) + offset_row.astype(jnp.float32), normed, inverse)


def norm_backward(grad_out, normed, inverse, gain_row):
    scaled = grad_out * gain_row.astype(jnp.float32)
    grad_in = inverse * (
        scaled
        - jnp.mean(scaled, axis=-1, keepdims=True)
        - normed * jnp.mean(scaled * normed, axis=-1, keepdims=True)
    )
    return (grad_in, jnp.sum(grad_out * normed, axis=0), jnp.sum(grad_out, axis=0))


def gather_weights(shards):
    return (
        lax.all_gather(shards[0], "fsdp", axis=0, tiled=True),
        lax.all_gather(shards[1], "fsdp", axis=0, tiled=True),
        lax.all_gather(shards[2], "fsdp", axis=0, tiled=True),
        lax.all_gather(shards[3], "fsdp", axis=0, tiled=True),
        lax.all_gather(shards[4], "fsdp", axis=0, tiled=True),
        lax.all_gather(shards[5], "fsdp", axis=0, tiled=True),
        lax.all_gather(shards[6], "fsdp", axis=0, tiled=True),
        lax.all_gather(shards[7], "fsdp", axis=0, tiled=True),
        lax.all_gather(shards[8], "fsdp", axis=0, tiled=True),
        lax.all_gather(shards[9], "fsdp", axis=0, tiled=True),
        lax.all_gather(shards[10], "fsdp", axis=0, tiled=True),
        lax.all_gather(shards[11], "fsdp", axis=0, tiled=True),
        lax.all_gather(shards[12], "fsdp", axis=0, tiled=True),
        lax.all_gather(shards[13], "fsdp", axis=0, tiled=True),
        lax.all_gather(shards[14], "fsdp", axis=0, tiled=True),
    )


def attend_forward(query_bf, key_bf, value_bf, seg_local):
    row_count = query_bf.shape[0]
    score_scale = HEAD_DIM ** (-0.5)
    query_heads = query_bf.reshape(row_count, HEADS, HEAD_DIM)
    run_max = jnp.full((HEADS, row_count), -1e30, jnp.float32)
    key_rows = lax.all_gather(key_bf, "ctx", axis=0, tiled=True)
    value_rows = lax.all_gather(value_bf, "ctx", axis=0, tiled=True)
    key_seg = lax.all_gather(seg_local, "ctx", axis=0, tiled=True)
    piece_rows = key_rows.shape[0]
    key_heads = key_rows.reshape(piece_rows, HEADS, HEAD_DIM)
    value_heads = value_rows.reshape(piece_rows, HEADS, HEAD_DIM)
    scores = (
        jnp.einsum("rhd,khd->hrk", query_heads, key_heads, preferred_element_type=jnp.float32)
        * score_scale
    )
    same_doc = seg_local[:, None] == key_seg[None, :]
    scores = jnp.where(same_doc[None], scores, -1e30)
    new_max = jnp.maximum(run_max, jnp.max(scores, axis=-1))
    numerators = jnp.exp(scores - new_max[..., None])
    run_sum = jnp.sum(numerators, axis=-1)
    accumulated = jnp.einsum(
        "hrk,khd->hrd",
        numerators.astype(jnp.bfloat16),
        value_heads,
        preferred_element_type=jnp.float32,
    )
    run_max, run_sum, accumulated = (new_max, run_sum, accumulated)
    context = jnp.transpose(accumulated / run_sum[..., None], (1, 0, 2)).reshape(
        row_count, HEADS * HEAD_DIM
    )
    return (context, run_max + jnp.log(run_sum))


def block_grads(
    query_heads, grad_heads, query_seg, log_sum, row_delta, key_heads, value_heads, key_seg
):
    score_scale = HEAD_DIM ** (-0.5)
    scores = (
        jnp.einsum("rhd,khd->hrk", query_heads, key_heads, preferred_element_type=jnp.float32)
        * score_scale
    )
    same_doc = query_seg[:, None] == key_seg[None, :]
    scores = jnp.where(same_doc[None], scores, -1e30)
    probs_full = jnp.exp(scores - log_sum[..., None])
    grad_probs = jnp.einsum(
        "rhd,khd->hrk", grad_heads, value_heads, preferred_element_type=jnp.float32
    )
    grad_scores = (probs_full * (grad_probs - row_delta[..., None])).astype(jnp.bfloat16)
    return (probs_full, grad_scores)


def attend_backward(query_bf, key_bf, value_bf, seg_local, context, log_sum, grad_context):
    row_count = query_bf.shape[0]
    score_scale = HEAD_DIM ** (-0.5)
    key_every, value_every, seg_every = (
        lax.all_gather(key_bf, "ctx", axis=0, tiled=True),
        lax.all_gather(value_bf, "ctx", axis=0, tiled=True),
        lax.all_gather(seg_local, "ctx", axis=0, tiled=True),
    )
    length = key_every.shape[0]
    block_len = min(512, length)
    query_heads = query_bf.reshape(row_count, HEADS, HEAD_DIM)
    grad_heads = grad_context.reshape(row_count, HEADS, HEAD_DIM)
    row_delta = jnp.sum(
        (grad_context.astype(jnp.float32) * context).reshape(row_count, HEADS, HEAD_DIM), axis=-1
    ).T

    def visit_block(grad_query, block_num):
        first_row = block_num * block_len
        key_heads = lax.dynamic_slice_in_dim(key_every, first_row, block_len, 0).reshape(
            block_len, HEADS, HEAD_DIM
        )
        value_heads = lax.dynamic_slice_in_dim(value_every, first_row, block_len, 0).reshape(
            block_len, HEADS, HEAD_DIM
        )
        key_seg = lax.dynamic_slice_in_dim(seg_every, first_row, block_len, 0)
        probs_full, grad_scores = block_grads(
            query_heads, grad_heads, seg_local, log_sum, row_delta, key_heads, value_heads, key_seg
        )
        grad_query = (
            grad_query
            + jnp.einsum("hrk,khd->rhd", grad_scores, key_heads, preferred_element_type=jnp.float32)
            * score_scale
        )
        grad_keys = (
            jnp.einsum("hrk,rhd->khd", grad_scores, query_heads, preferred_element_type=jnp.float32)
            * score_scale
        )
        grad_values = jnp.einsum(
            "hrk,rhd->khd",
            probs_full.astype(jnp.bfloat16),
            grad_heads,
            preferred_element_type=jnp.float32,
        )
        stacked = jnp.stack(
            (
                grad_keys.reshape(block_len, HEADS * HEAD_DIM),
                grad_values.reshape(block_len, HEADS * HEAD_DIM),
            ),
            axis=1,
        )
        return (grad_query, stacked)

    grad_query, pieces = lax.scan(
        visit_block,
        jnp.zeros((row_count, HEADS, HEAD_DIM), jnp.float32),
        jnp.arange(length // block_len),
    )
    key_terms = pieces.reshape(length, 2, HEADS * HEAD_DIM)
    own_rows = lax.psum_scatter(
        key_terms.astype(jnp.bfloat16), "ctx", scatter_dimension=0, tiled=True
    ).astype(jnp.float32)
    grad_keyed = own_rows[:, 0].astype(jnp.bfloat16)
    grad_valued = own_rows[:, 1].astype(jnp.bfloat16)
    grad_queries = grad_query.reshape(row_count, HEADS * HEAD_DIM).astype(jnp.bfloat16)
    return (grad_queries, grad_keyed, grad_valued)


def layer_forward(inputs, seg_local, full_weights):
    (
        query_weight,
        key_weight,
        value_weight,
        output_weight,
        expand_weight,
        contract_weight,
        query_bias,
        value_bias,
        output_bias,
        first_gain,
        first_shift,
        expand_bias,
        contract_bias,
        second_gain,
        second_shift,
    ) = full_weights
    query_bf = (plain_dot(inputs, query_weight) + query_bias.astype(jnp.float32)).astype(
        jnp.bfloat16
    )
    key_bf = plain_dot(inputs, key_weight).astype(jnp.bfloat16)
    value_bf = (plain_dot(inputs, value_weight) + value_bias.astype(jnp.float32)).astype(
        jnp.bfloat16
    )
    context, log_sum = attend_forward(query_bf, key_bf, value_bf, seg_local)
    context_bf = context.astype(jnp.bfloat16)
    first_sum = (
        inputs.astype(jnp.float32)
        + plain_dot(context_bf, output_weight)
        + output_bias.astype(jnp.float32)
    )
    first_out, normed_one, inverse_one = norm_forward(first_sum, first_gain, first_shift)
    first_bf = first_out.astype(jnp.bfloat16)
    hidden = plain_dot(first_bf, expand_weight) + expand_bias.astype(jnp.float32)
    gelled_bf = jax.nn.gelu(hidden, approximate=False).astype(jnp.bfloat16)
    second_sum = (
        first_out + plain_dot(gelled_bf, contract_weight) + contract_bias.astype(jnp.float32)
    )
    result, normed_two, inverse_two = norm_forward(second_sum, second_gain, second_shift)
    kept_state = (
        query_bf,
        key_bf,
        value_bf,
        context,
        log_sum,
        context_bf,
        normed_one,
        inverse_one,
        first_bf,
        hidden,
        gelled_bf,
        normed_two,
        inverse_two,
    )
    return (result.astype(jnp.bfloat16), kept_state)


def layer_backward(inputs, seg_local, grad_out, kept_state, full_weights):
    (
        query_weight,
        key_weight,
        value_weight,
        output_weight,
        expand_weight,
        contract_weight,
        query_bias,
        value_bias,
        output_bias,
        first_gain,
        first_shift,
        expand_bias,
        contract_bias,
        second_gain,
        second_shift,
    ) = full_weights
    (
        query_bf,
        key_bf,
        value_bf,
        context,
        log_sum,
        context_bf,
        normed_one,
        inverse_one,
        first_bf,
        hidden,
        gelled_bf,
        normed_two,
        inverse_two,
    ) = kept_state
    grad_second, second_gain_grad, second_shift_grad = norm_backward(
        grad_out.astype(jnp.float32), normed_two, inverse_two, second_gain
    )
    grad_branch = grad_second.astype(jnp.bfloat16)
    contract_weight_grad = left_dot(gelled_bf, grad_branch)
    contract_bias_grad = jnp.sum(grad_branch.astype(jnp.float32), axis=0)
    grad_gelled = right_dot(grad_branch, contract_weight)
    gelu_pull = jax.vjp(lambda values: jax.nn.gelu(values, approximate=False), hidden)[1]
    grad_hidden = gelu_pull(grad_gelled)[0].astype(jnp.bfloat16)
    expand_weight_grad = left_dot(first_bf, grad_hidden)
    expand_bias_grad = jnp.sum(grad_hidden.astype(jnp.float32), axis=0)
    grad_first = grad_second + right_dot(grad_hidden, expand_weight)
    grad_attn, first_gain_grad, first_shift_grad = norm_backward(
        grad_first, normed_one, inverse_one, first_gain
    )
    grad_attn_low = grad_attn.astype(jnp.bfloat16)
    output_weight_grad = left_dot(context_bf, grad_attn_low)
    output_bias_grad = jnp.sum(grad_attn_low.astype(jnp.float32), axis=0)
    grad_context = right_dot(grad_attn_low, output_weight).astype(jnp.bfloat16)
    grad_queries, grad_keyed, grad_valued = attend_backward(
        query_bf, key_bf, value_bf, seg_local, context, log_sum, grad_context
    )
    query_weight_grad = left_dot(inputs, grad_queries)
    key_weight_grad = left_dot(inputs, grad_keyed)
    value_weight_grad = left_dot(inputs, grad_valued)
    query_bias_grad = jnp.sum(grad_queries.astype(jnp.float32), axis=0)
    value_bias_grad = jnp.sum(grad_valued.astype(jnp.float32), axis=0)
    grad_input = (
        grad_attn
        + right_dot(grad_queries, query_weight)
        + right_dot(grad_keyed, key_weight)
        + right_dot(grad_valued, value_weight)
    )
    grad_terms = (
        query_weight_grad,
        key_weight_grad,
        value_weight_grad,
        output_weight_grad,
        expand_weight_grad,
        contract_weight_grad,
        query_bias_grad,
        value_bias_grad,
        output_bias_grad,
        first_gain_grad,
        first_shift_grad,
        expand_bias_grad,
        contract_bias_grad,
        second_gain_grad,
        second_shift_grad,
    )
    return (grad_input, grad_terms)


def per_device(
    layer_input,
    segments,
    cotangent,
    query_weight,
    key_weight,
    value_weight,
    output_weight,
    expand_weight,
    contract_weight,
    query_bias,
    value_bias,
    output_bias,
    first_gain,
    first_shift,
    expand_bias,
    contract_bias,
    second_gain,
    second_shift,
):
    shards = (
        query_weight,
        key_weight,
        value_weight,
        output_weight,
        expand_weight,
        contract_weight,
        query_bias,
        value_bias,
        output_bias,
        first_gain,
        first_shift,
        expand_bias,
        contract_bias,
        second_gain,
        second_shift,
    )
    micro_count = layer_input.shape[0]
    results = []
    grad_inputs = []
    totals = None
    for micro_step in range(micro_count):
        inputs = layer_input[micro_step, 0]
        seg_local = segments[micro_step, 0].astype(jnp.bfloat16)
        front_weights = gather_weights(shards)
        result, kept_state = layer_forward(inputs, seg_local, front_weights)
        behind = gather_weights(shards)
        grad_input, grad_terms = layer_backward(
            inputs, seg_local, cotangent[micro_step, 0], kept_state, behind
        )
        results.append(result)
        grad_inputs.append(grad_input)
        if totals is None:
            totals = grad_terms
        else:
            totals = tuple(
                (left_side + right_side for left_side, right_side in zip(totals, grad_terms))
            )
    reduced = jax.tree.map(
        lambda part: part.astype(jnp.float32),
        lax.psum_scatter(as_sent(totals), "fsdp", scatter_dimension=0, tiled=True),
    )
    summed = jax.tree.map(lambda part: part.astype(jnp.float32), lax.psum(as_sent(reduced), "ctx"))
    layer_output = jnp.stack(results, axis=0)[:, None]
    input_grad = jnp.stack(grad_inputs, axis=0)[:, None]
    return (
        layer_output,
        input_grad,
        summed[0],
        summed[1],
        summed[2],
        summed[3],
        summed[4],
        summed[5],
        summed[6],
        summed[7],
        summed[8],
        summed[9],
        summed[10],
        summed[11],
        summed[12],
        summed[13],
        summed[14],
    )


MESH = pl.DeviceIdType.MESH
BF = jnp.bfloat16
F32 = jnp.float32
CHUNKS = 24
SLOTS = 3
LAND = 6
LAND_D = 4
ROOM = 10
LAG = (0, 0, 2, 4, 5, 6, 7, 8, 10)
Z_FROM, Z_TO = 12, 14
SPLIT = ((64, 0, 0), (48, 16, 0))
EARLY = 4


def coords():
    c, f = lax.axis_index("ctx"), lax.axis_index("fsdp")
    return c // 2, c % 2, f // 2, f % 2


def dev(z, x, y, k):
    return (z * 2 + x, y * 2 + k)


def greet(z, x, y, k):
    barrier = pltpu.get_barrier_semaphore()
    for step in range(1, 8):
        place = (z * 2 + k + step) % 8
        pl.semaphore_signal(
            barrier, inc=1, device_id=dev(place // 2, x, y, place % 2), device_id_type=MESH
        )
    pl.semaphore_signal(barrier, inc=1, device_id=dev(z, 1 - x, y, k), device_id_type=MESH)
    pl.semaphore_signal(barrier, inc=1, device_id=dev(z, x, 1 - y, k), device_id_type=MESH)
    pl.semaphore_wait(barrier, 9)


def remote(src, dst, send, recv, to):
    return pltpu.make_async_remote_copy(
        src_ref=src, dst_ref=dst, send_sem=send, recv_sem=recv, device_id=to, device_id_type=MESH
    )


def rows_of(start, size, unit=16):
    return pl.ds(pl.multiple_of(start, unit), size)


def two_heads(block):
    lane = lax.broadcasted_iota(jnp.int32, block.shape, 1)
    zero = jnp.zeros_like(block)
    return jnp.concatenate(
        [jnp.where(lane < HEAD_DIM, block, zero), jnp.where(lane >= HEAD_DIM, block, zero)], axis=0
    )


def one_block(pair):
    rows = pair.shape[0] // 2
    lane = lax.broadcasted_iota(jnp.int32, (rows, pair.shape[1]), 1)
    return jnp.where(lane < HEAD_DIM, pair[:rows], pair[rows:])


def softmax_pair(queries, keys, bias):
    scores = right_dot(queries, keys)
    scores = scores + jnp.concatenate([bias, bias], axis=0)
    numer = jnp.exp(scores - jnp.max(scores, axis=-1, keepdims=True))
    return numer * (1.0 / jnp.sum(numer, axis=-1, keepdims=True))


def layer_kernel(
    inp, cot, seg, wq, wk, wv, wo, we, wc, *rest,
):
    (
        vecs, (fq, fk, fv, fo, fe, fc), (o_q, o_k, o_v, o_o, o_e, o_c), (resf, dxf, vec_out), rest
    ) = (rest[:9], rest[9:15], rest[15:21], rest[21:24], rest[24:])
    (
        s_d, l_d, r_d, b_y, r_y, b_x, r_x, b_1, r_1, b_2, r_2, o_b,
        gh, acc, ga, gal, dctx, dq, dk, dv, bias, we_b, wc_b, w_b,
        dx_r, dx_y, vec, v_s, v_d, v_r,
        gel, gb, fb, gp, n1, inv1, ctx, q, key, val, xf, res, segf, vec_in, vecf, row8, row_e,
        ss, rs, ds, dr, a_send, a_recv, v_send, v_recv, w_sem, o_sem,
        i_send, i_recv, g_send, g_recv, p_send, p_recv, f_send, f_recv,
    ) = rest
    dx_b, dx_s = dctx, gb
    cotf = gh.at[:, pl.ds(0, 1024)]
    z, x, y, k = coords()
    f = y * 2 + k
    other = (1 - y) * 2 + k
    sib, xn, yn = dev(z, x, y, 1 - k), dev(z, 1 - x, y, k), dev(z, x, 1 - y, k)
    bit1, bit2 = z % 2, z // 2
    z1 = dev(z + 1 - 2 * bit1, x, y, k)
    z2 = dev((z + 2) % 4, x, y, k)
    color = bit1 * 2 + x
    c_x, c_z, c_o = color + 1 - 2 * x, (color + 2) % 4, 3 - color
    own_rows = rows_of(x * 512 + k * 256, 256)

    def block_moves(mb):
        to_z, to_k = mb * 2 + k, z // 2
        row = x * 512 + z * 128
        slot = z % 2
        mine = (to_z == z) & (to_k == k)
        moves = (
            (inp.at[mb, 0], xf.at[rows_of(row, 128)], 0),
            (seg.at[mb], segf.at[x * 4 + z], 1),
            (cot.at[mb, 0], cotf.at[rows_of(slot * 128, 128)], 2),
        )
        return mine, dev(to_z, x, y, to_k), slot, moves

    def start_blocks(which):
        for mb in range(2):
            mine, to, slot, moves = block_moves(mb)
            for src, dst, n in moves:
                if n not in which:
                    continue

                @pl.when(mine)
                def _():
                    pltpu.make_async_copy(src, dst, i_recv.at[n, slot]).start()

                @pl.when(jnp.logical_not(mine))
                def _():
                    remote(src, dst, i_send.at[n, mb], i_recv.at[n, slot], to).start()

    def finish_blocks(which):
        for mb in range(2):
            mine, to, slot, moves = block_moves(mb)
            for src, dst, n in moves:
                if n not in which:
                    continue

                @pl.when(jnp.logical_not(mine))
                def _():
                    remote(src, dst, i_send.at[n, mb], i_recv.at[n, slot], to).wait_send()

    def arrive_block(slot, which):
        zz = 2 * k + slot
        for n in which:
            if n == 0:
                dst = xf.at[rows_of(x * 512 + zz * 128, 128)]
            elif n == 1:
                dst = segf.at[x * 4 + zz]
            else:
                dst = cotf.at[pl.ds(slot * 128, 128)]
            pltpu.make_async_copy(dst, dst, i_recv.at[n, slot]).wait()

    def group_copy(step, block):
        who = x if step < 2 else 1 - x
        src = xf.at[rows_of(who * 512 + k * 256 + block * 128, 128)]
        sseg = segf.at[who * 4 + k * 2 + block]
        to = (sib, xn, sib)[step]
        return (
            remote(src, src, g_send.at[0, step, block], g_recv.at[0, step, block], to),
            remote(sseg, sseg, g_send.at[1, step, block], g_recv.at[1, step, block], to),
        )

    def group_start(step, block):
        for move in group_copy(step, block):
            move.start()

    def group_arrive(step, block):
        who = (x, 1 - x, 1 - x)[step]
        kk = (1 - k, k, 1 - k)[step]
        src = xf.at[rows_of(who * 512 + kk * 256 + block * 128, 128)]
        sseg = segf.at[who * 4 + kk * 2 + block]
        pltpu.make_async_copy(src, src, g_recv.at[0, step, block]).wait()
        pltpu.make_async_copy(sseg, sseg, g_recv.at[1, step, block]).wait()

    items = []
    for shard, full in ((wq, fq), (wk, fk), (wv, fv), (wo, fo)):
        items.append((shard, full, 0, 0, 256))
    for j in range(4):
        items.append((we, fe, 0, j * 1024, 256))
    for j in range(4):
        items.append((wc, fc, j * 256, 0, 1024))
    n_items = len(items)

    def split(i):
        return SPLIT[0] if i < EARLY else SPLIT[1]

    def part(i, quarter, start, size, own_src=False):
        shard, full, row, col, step = items[i]
        if own_src:
            return shard.at[rows_of(row + start, size, 8), pl.ds(col, 1024)]
        return full.at[rows_of(quarter * step + row + start, size, 8), pl.ds(col, 1024)]

    def send_copy(i, kind):
        sems = (p_send.at[kind, i], p_recv.at[kind, i])
        if kind == 0:
            return remote(part(i, f, color * 64, 64, True), part(i, f, color * 64, 64), *sems, yn)
        if kind == 1:
            rows = split(i)[0]
            return remote(part(i, f, c_o * 64, rows, True), part(i, f, c_o * 64, rows), *sems, yn)
        if kind == 2:
            src = part(i, other, color * 64, 64)
            return remote(src, src, *sems, xn)
        if kind == 3:
            src = part(i, other, c_z * 64 + split(i)[0], split(i)[1])
            return remote(src, src, *sems, xn)
        if kind == 4:
            src = part(i, other, color * 64, 64)
            return remote(src, src, *sems, z1)
        if kind == 5:
            src = part(i, other, c_x * 64 + 64 - split(i)[2], split(i)[2])
            return remote(src, src, *sems, z1)
        if kind == 6:
            return remote(part(i, f, 0, 256, True), part(i, f, 0, 256), *sems, sib)
        src = part(i, other, 0, 256)
        return remote(src, src, *sems, sib)

    def arrive(i, kind):
        if kind == 0:
            dst = part(i, other, color * 64, 64)
        elif kind == 1:
            dst = part(i, other, c_o * 64, split(i)[0])
        elif kind == 2:
            dst = part(i, other, c_x * 64, 64)
        elif kind == 3:
            dst = part(i, other, c_o * 64 + split(i)[0], split(i)[1])
        elif kind == 4:
            dst = part(i, other, c_z * 64, 64)
        elif kind == 5:
            dst = part(i, other, c_o * 64 + 64 - split(i)[2], split(i)[2])
        elif kind == 6:
            dst = part(i, y * 2 + 1 - k, 0, 256)
        else:
            dst = part(i, (1 - y) * 2 + 1 - k, 0, 256)
        pltpu.make_async_copy(dst, dst, p_recv.at[kind, i]).wait()


    for i in range(8):
        packed = vecs[i][...].astype(F32).reshape(1, 256)
        vec_in[pl.ds(2 * i, 1)] = packed[:, :128]
        vec_in[pl.ds(2 * i + 1, 1)] = packed[:, 128:]
    packed = vecs[8][...].astype(F32).reshape(1, 1024)
    for n in range(8):
        vec_in[pl.ds(16 + n, 1)] = packed[:, n * 128 : n * 128 + 128]
    vecf[f] = vec_in[...]
    vec_copies = (
        remote(vec_in, vecf.at[f], f_send.at[0], f_recv.at[0], yn),
        remote(vec_in, vecf.at[f], f_send.at[1], f_recv.at[1], sib),
        remote(vecf.at[other], vecf.at[other], f_send.at[2], f_recv.at[2], sib),
    )

    def load_square(shard, full, row, step, cols, dst, sem):
        out = []
        for d in range(4):
            quarter = (f + d) % 4
            src = shard.at[pl.ds(row, 256), cols]
            if d > 0:
                src = full.at[rows_of(quarter * step + row, 256), cols]
            out.append(pltpu.make_async_copy(src, dst.at[rows_of(quarter * 256, 256)], sem))
        return out

    def load_c(j):
        slot = j % 2
        sem = w_sem.at[slot]

        @pl.when(j // 2 == f)
        def _():
            src = wc.at[rows_of((j % 2) * 512, 512)]
            pltpu.make_async_copy(src, wc_b.at[slot], sem).start()

        @pl.when(j // 2 != f)
        def _():
            pltpu.make_async_copy(fc.at[rows_of(j * 512, 512)], wc_b.at[slot], sem).start()

    def load_e(j):
        for move in load_square(
            we, fe, 0, 256, rows_of(j * 512, 512, 512), we_b.at[j % 2], w_sem.at[2 + j % 2]
        ):
            move.start()

    def load_w(n):
        shard, full = ((wo, fo), (wk, fk), (wv, fv), (wq, fq))[n]
        for move in load_square(
            shard, full, 0, 256, pl.ds(0, 1024), w_b.at[n], w_sem.at[4 + n]
        ):
            move.start()

    def loaded_w(n):
        pltpu.make_async_copy(w_b.at[n], w_b.at[n], w_sem.at[4 + n]).wait()

    def load_item(i):
        shard, full, row, col, step = items[i]
        arrive(i, 6)
        arrive(i, 7)
        slot = i % 4
        for move in load_square(
            shard, full, row, step, pl.ds(col, 1024), w_b.at[slot], w_sem.at[4 + slot]
        ):
            move.start()

    def item(i):
        slot = i % 4
        pltpu.make_async_copy(w_b.at[slot], w_b.at[slot], w_sem.at[4 + slot]).wait()
        return w_b.at[slot]

    def relay(t):
        for u in (0, 1, 2) if t == 0 else (t + 2,):
            if u < n_items:
                send_copy(u, 0).start()
                send_copy(u, 1).start()
                send_copy(u, 6).start()
        if 1 <= t <= n_items:
            i = t - 1
            arrive(i, 0)
            send_copy(i, 2).start()
            send_copy(i, 4).start()
        if EARLY <= t - 3 < n_items:
            i = t - 3
            arrive(i, 4)
            send_copy(i, 3).start()
            arrive(i, 2)
            if split(i)[2]:
                send_copy(i, 5).start()
        if 0 <= t - 3 < EARLY:
            i = t - 3
            arrive(i, 1)
            arrive(i, 2)
            arrive(i, 4)
            send_copy(i, 7).start()
        if EARLY <= t - 6 < n_items:
            i = t - 6
            arrive(i, 1)
            arrive(i, 3)
            if split(i)[2]:
                arrive(i, 5)
            send_copy(i, 7).start()

    def fill_rows():
        pltpu.make_async_copy(vec_in, vec_in, f_recv.at[1]).wait()
        pltpu.make_async_copy(vec_in, vec_in, f_recv.at[2]).wait()
        for quarter in range(4):
            for i in range(8):
                for half in range(2):
                    col = quarter * 256 + half * 128
                    row8[pl.ds(i, 1), col : col + 128] = vecf[quarter, pl.ds(2 * i + half, 1)]
            for n in range(8):
                col = quarter * 1024 + n * 128
                row_e[:, col : col + 128] = vecf[quarter, pl.ds(16 + n, 1)]

    def fill_bias():
        for block in range(2):
            own = segf[x * 4 + k * 2 + block].astype(F32)
            down = jnp.transpose(jnp.broadcast_to(own, (128, 128)))
            for n in range(8):
                across = segf[n].astype(F32)
                bias[block * 128 : block * 128 + 128, n * 128 : n * 128 + 128] = jnp.where(
                    down == across, 0.0, -1e30
                )

    def project_own(w):
        q[...] = (plain_dot(xf[own_rows], w[...]) + row8[0:1]).astype(BF)

    def project_all(w, dst, add_row):
        def block(n, carry):
            rows = rows_of(n * 256, 256)
            dst[rows] = (plain_dot(xf[rows], w[...]) + add_row).astype(BF)
            return carry

        lax.fori_loop(0, 4, block, 0)

    def heads(first, last):
        def one(h, carry):
            cols = rows_of(h * 128, 128, 128)
            queries = two_heads(q[:, cols] * BF(HEAD_DIM**-0.5))
            probs = softmax_pair(queries, key[:, cols], bias[...])
            ctx[:, cols] = one_block(plain_dot(probs.astype(BF), val[:, cols])).astype(BF)
            return carry

        lax.fori_loop(first, last, one, 0)

    def norm(v):
        centre = v - jnp.mean(v, axis=-1, keepdims=True)
        inverse = lax.rsqrt(jnp.mean(centre * centre, axis=-1, keepdims=True) + 1e-05)
        return centre * inverse, inverse

    def attention_out(w):
        normed, inverse = norm(
            xf[own_rows].astype(F32) + plain_dot(ctx[...], w[...]) + row8[2:3]
        )
        n1[...] = normed
        inv1[...] = inverse
        first_out = normed * row8[3:4] + row8[4:5]
        acc[...] = first_out
        fb[...] = first_out.astype(BF)

    def expand(j, w):
        def block(n, carry):
            cols = rows_of(n * 256, 256, 256)
            out = rows_of(j * 1024 + n * 256, 256, 256)
            hidden = plain_dot(fb[...], w[:, cols]) + row_e[:, out]
            below = 0.5 + 0.5 * lax.erf(hidden * 0.5**0.5)
            gel[:, out] = (hidden * below).astype(BF)
            bell = jnp.exp(-0.5 * hidden * hidden) * (2 * math.pi) ** -0.5
            gp[:, out] = (below + hidden * bell).astype(BF)
            return carry

        lax.fori_loop(0, 4, block, 0)

    def contract(j, w):
        for quarter in range(4):
            cols = pl.ds(quarter * 1024 + j * 256, 256)
            acc[...] += plain_dot(gel[:, cols], w[quarter * 256 : quarter * 256 + 256])

    def second_norm():
        normed, inverse = norm(acc[...] + row8[5:6])
        res[...] = (normed * row8[6:7] + row8[7:8]).astype(BF)
        grad_out = cotf[...].astype(F32)
        keep(6, column(grad_out * normed))
        keep(7, column(grad_out))
        scaled = grad_out * row8[6:7]
        grad = inverse * (
            scaled
            - jnp.mean(scaled, axis=-1, keepdims=True)
            - normed * jnp.mean(scaled * normed, axis=-1, keepdims=True)
        )
        acc[...] = grad
        low = grad.astype(BF)
        gb[...] = low
        keep(5, column(low))


    def back(n, slot):
        to_z = 2 * k + slot
        to_k = z % 2
        mb = z // 2
        mine = (to_z == z) & (to_k == k)
        src = (res, dx_b)[n].at[pl.ds(slot * 128, 128)]
        dst = (resf, dxf)[n].at[mb, 0]

        def far():
            return remote(
                src, dst, a_send.at[n, slot], a_recv.at[n, mb], dev(to_z, x, y, to_k)
            )

        def near():
            return pltpu.make_async_copy(src, dst, a_recv.at[n, mb])

        return mine, far, near

    def start_back(n):
        for slot in range(2):
            mine, far, near = back(n, slot)

            @pl.when(mine)
            def _():
                near().start()

            @pl.when(jnp.logical_not(mine))
            def _():
                far().start()

    def finish_back(n):
        for slot in range(2):
            mine, far, _ = back(n, slot)

            @pl.when(jnp.logical_not(mine))
            def _():
                far().wait_send()

        for mb in range(2):
            dst = (resf, dxf)[n].at[mb, 0]
            pltpu.make_async_copy(dst, dst, a_recv.at[n, mb]).wait()

    def column(v):
        return jnp.sum(v.astype(F32), axis=0, keepdims=True)

    def keep(i, row):
        for quarter in range(4):
            for half in range(2):
                col = quarter * 256 + half * 128
                vec[quarter, pl.ds(2 * i + half, 1)] = row[:, col : col + 128]

    v_peers = (sib, yn, xn, z1, z2)

    def v_copy(stage):
        if stage == 0:
            return remote(v_d.at[1], v_d.at[2], v_send.at[0], v_recv.at[0], sib)
        src = v_s.at[0, 1 - y] if stage == 1 else v_s.at[stage - 1, 0]
        return remote(src, v_r.at[stage - 1], v_send.at[stage], v_recv.at[stage], v_peers[stage])

    def v_step(stage):
        if stage == 0:
            for plane in range(2):
                v_d[0, plane] = vec[plane * 2 + k]
                v_d[1, plane] = vec[plane * 2 + 1 - k]
        elif stage == 1:
            pltpu.make_async_copy(v_d.at[2], v_d.at[2], v_recv.at[0]).wait()
            v_s[0] = v_d[0] + v_d[2]
        else:
            dst = v_r.at[stage - 2]
            pltpu.make_async_copy(dst, dst, v_recv.at[stage - 1]).wait()
            mine = v_s[0, y] if stage == 2 else v_s[stage - 2, 0]
            total = mine + v_r[stage - 2]
            if stage == 5:
                vec_out[...] = total
            else:
                v_s[stage - 1, 0] = total
        if stage < 5:
            v_copy(stage).start()

    def send(stage, i, src, dst, to):
        return remote(src, dst, ss.at[stage, i % SLOTS], rs.at[stage, i % LAND], to)

    def landed(stage, i, dst):
        pltpu.make_async_copy(dst, dst, rs.at[stage, i % LAND]).wait()

    def order(i):
        late = (i // Z_FROM) * (1 - i // Z_TO) if Z_FROM < Z_TO else 0
        bits = tuple(
            (1 - late) * p + late * q
            for p, q in ((x, bit1), (bit1, bit2), (bit2, x))
        )
        peers = tuple(
            tuple((1 - late) * p + late * q for p, q in zip(one, two))
            for one, two in ((xn, z1), (z1, z2), (z2, xn))
        )
        return bits, peers

    def copies(stage, i):
        slot, land, room = i % SLOTS, i % LAND, i % ROOM
        (first, second, third), peers = order(i)
        if stage == 0:
            return send(0, i, s_d.at[slot], r_d.at[i % LAND_D], sib)
        if stage == 1:
            return send(1, i, b_y.at[slot, 1 - y], r_y.at[land], yn)
        if stage == 2:
            return send(2, i, b_x.at[slot, rows_of((1 - first) * 64, 64)], r_x.at[land], peers[0])
        if stage == 3:
            return send(3, i, b_1.at[slot, rows_of((1 - second) * 32, 32)], r_1.at[land], peers[1])
        if stage == 4:
            return send(4, i, b_2.at[slot, rows_of((1 - third) * 16, 16)], r_2.at[land], peers[2])
        if stage == 5:
            own = o_b.at[room, rows_of(first * 64 + second * 32 + third * 16, 16)]
            return send(5, i, own, own, peers[2])
        if stage == 6:
            own = o_b.at[room, rows_of(first * 64 + second * 32, 32)]
            return send(6, i, own, own, peers[1])
        own = o_b.at[room, rows_of(first * 64, 64)]
        return send(7, i, own, own, peers[0])

    def launch(stage, i):
        copies(stage, i).start()

    def clear(stage, i):
        @pl.when(i >= SLOTS)
        def _():
            copies(stage, i - SLOTS).wait_send()

    def add(a, b):
        return (a.astype(F32) + b.astype(F32)).astype(BF)

    def terms(i, a_ref, b_ref, a_base, a_step, b_col, a_rows=None):
        slot = i % SLOTS
        right = b_ref[:, b_col]
        for plane in range(2):
            for core in range(2):
                quarter = plane * 2 + (k if core == 0 else 1 - k)
                cols = pl.ds(pl.multiple_of(a_base + quarter * a_step, 128), 128)
                left = a_ref[:, cols] if a_rows is None else a_ref[a_rows, cols]
                product = left_dot(left, right).astype(BF)
                if core == 0:
                    l_d[slot, plane] = product
                else:
                    s_d[slot, plane] = product

    every = pl.ds(0, 1024)

    def stage_zero(i):
        @pl.when((i >= 0) & (i < CHUNKS))
        def _():
            clear(0, i)

        @pl.when(i < 8)
        def _():
            terms(i, gel, gb, i * 128, 1024, every)

        @pl.when((i >= 8) & (i < 16))
        def _():
            j = i - 8
            terms(i, fb, gh, (j % 2) * 128, 256, rows_of((j // 2) * 1024, 1024, 1024))

        @pl.when((i >= 16) & (i < 18))
        def _():
            terms(i, ctx, gal, (i - 16) * 128, 256, every)

        @pl.when((i >= 18) & (i < 20))
        def _():
            terms(i, xf, dq, (i - 18) * 128, 256, every, own_rows)

        @pl.when((i >= 20) & (i < 22))
        def _():
            terms(i, xf, dk, (i - 20) * 128, 256, every)

        @pl.when((i >= 22) & (i < 24))
        def _():
            terms(i, xf, dv, (i - 22) * 128, 256, every)

        @pl.when((i >= 0) & (i < CHUNKS))
        def _():
            launch(0, i)

    def stored():
        pltpu.make_async_copy(o_b.at[0], o_b.at[0], o_sem).wait()

    def store(i):
        src = o_b.at[i % ROOM]

        @pl.when(i >= 1)
        def _():
            stored()

        @pl.when(i < 8)
        def _():
            pltpu.make_async_copy(src, o_c.at[rows_of(i * 128, 128)], o_sem).start()

        @pl.when((i >= 8) & (i < 16))
        def _():
            j = i - 8
            dst = o_e.at[rows_of((j % 2) * 128, 128), rows_of((j // 2) * 1024, 1024, 1024)]
            pltpu.make_async_copy(src, dst, o_sem).start()

        for n, ref in enumerate((o_o, o_q, o_k, o_v)):
            first = 16 + 2 * n

            @pl.when((i >= first) & (i < first + 2))
            def _():
                dst = ref.at[rows_of((i - first) * 128, 128)]
                pltpu.make_async_copy(src, dst, o_sem).start()

    def feed_forward(j):
        slot = j % 2
        cols = rows_of(j * 512, 512, 512)
        pltpu.make_async_copy(wc_b.at[slot], wc_b.at[slot], w_sem.at[slot]).wait()
        pltpu.make_async_copy(we_b.at[slot], we_b.at[slot], w_sem.at[2 + slot]).wait()

        grads = (right_dot(gb[...], wc_b[slot]) * gp[:, cols].astype(F32)).astype(BF)
        gh[:, cols] = grads
        acc[...] += right_dot(grads, we_b[slot])
        row = column(grads)
        for n in range(4):
            vec[j // 2, pl.ds(16 + (j % 2) * 4 + n, 1)] = row[:, n * 128 : n * 128 + 128]

        @pl.when(j < 6)
        def _():
            load_c(j + 2)
            load_e(j + 2)

    def first_norm():
        normed = n1[...]
        grad_first = acc[...]
        keep(3, column(grad_first * normed))
        keep(4, column(grad_first))
        scaled = grad_first * row8[3:4]
        grad_attn = inv1[...] * (
            scaled
            - jnp.mean(scaled, axis=-1, keepdims=True)
            - normed * jnp.mean(scaled * normed, axis=-1, keepdims=True)
        )
        ga[...] = grad_attn
        low = grad_attn.astype(BF)
        gal[...] = low
        keep(2, column(low))
        loaded_w(0)
        dctx[...] = right_dot(low, w_b[0]).astype(BF)

    def attention(h):
        cols = rows_of(h * 128, 128, 128)
        queries = two_heads(q[:, cols] * BF(HEAD_DIM**-0.5))
        keys = key[:, cols]
        probs = softmax_pair(queries, keys, bias[...])
        grads = two_heads(dctx[:, cols])
        grad_probs = right_dot(grads, val[:, cols])
        delta = jnp.sum(probs * grad_probs, axis=-1, keepdims=True)
        grad_scores = (probs * (grad_probs - delta)).astype(BF)
        dv[:, cols] = left_dot(probs.astype(BF), grads).astype(BF)
        dk[:, cols] = left_dot(grad_scores, queries).astype(BF)
        dq[:, cols] = (one_block(plain_dot(grad_scores, keys)) * HEAD_DIM**-0.5).astype(BF)

    def dx_core(g):
        return remote(gel.at[:, pl.ds(g * 1024, 1024)], dx_r.at[g], ds.at[g], dr.at[g], sib)

    dx_far = remote(dx_s, dx_y, ds.at[2], dr.at[2], xn)

    def input_rows(n):
        who = x * (n % 2) + (1 - x) * (1 - n % 2)
        core = (1 - k) * (1 - n // 2) + k * (n // 2)
        rows = rows_of(who * 512 + core * 256, 256)
        terms_here = right_dot(dk[rows], w_b[1]) + right_dot(dv[rows], w_b[2])

        @pl.when(n == 0)
        def _():
            gel[:, pl.ds(1024, 1024)] = terms_here.astype(BF)
            dx_core(1).start()

        @pl.when(n == 1)
        def _():
            gel[:, pl.ds(0, 1024)] = terms_here.astype(BF)
            dx_core(0).start()

        @pl.when(n == 2)
        def _():
            pltpu.make_async_copy(dx_r.at[1], dx_r.at[1], dr.at[1]).wait()
            dx_s[...] = (terms_here + dx_r[1].astype(F32)).astype(BF)
            dx_far.start()

        @pl.when(n == 3)
        def _():
            pltpu.make_async_copy(dx_r.at[0], dx_r.at[0], dr.at[0]).wait()
            loaded_w(3)
            ga[...] = ga[...] + terms_here + dx_r[0].astype(F32) + right_dot(dq[...], w_b[3])

    greet(z, x, y, k)
    start_blocks((0, 1))
    vec_copies[0].start()
    vec_copies[1].start()
    relay(0)
    relay(1)
    for block in range(2):
        arrive_block(block, (0, 1))
        group_start(0, block)
        group_start(1, block)
    pltpu.make_async_copy(vec_in, vec_in, f_recv.at[0]).wait()
    vec_copies[2].start()
    start_blocks((2,))
    relay(2)
    group_arrive(1, 0)
    group_start(2, 0)
    relay(3)
    group_arrive(1, 1)
    group_start(2, 1)
    load_item(0)
    fill_rows()
    for step in (0, 2):
        for block in range(2):
            group_arrive(step, block)
    fill_bias()
    relay(4)
    project_own(item(0))
    load_item(1)
    relay(5)
    project_all(item(1), key, 0.0)
    load_item(2)
    relay(6)
    project_all(item(2), val, row8[1:2])
    load_item(3)
    relay(7)
    heads(0, 3)
    relay(8)
    heads(3, 6)
    relay(9)
    heads(6, 8)
    relay(10)
    attention_out(item(3))
    load_item(4)
    for j in range(4):
        relay(11 + j)
        expand(j, item(4 + j))
        load_item(5 + j)
    for j in range(3):
        relay(15 + j)
        contract(j, item(8 + j))
        load_item(9 + j)
    contract(3, item(11))
    for slot in range(2):
        arrive_block(slot, (2,))
    for j in range(2):
        load_c(j)
        load_e(j)
    for n in range(4):
        load_w(n)
    second_norm()
    start_back(0)

    def tick(t, carry):
        def at(stage):
            i = t - LAG[stage]
            return i, (i >= 0) & (i < CHUNKS)

        stage_zero(t)
        @pl.when(t < 4)
        def _():
            def one(n, c):
                feed_forward(2 * t + n)
                return c

            lax.fori_loop(0, 2, one, 0)

        @pl.when(t == 4)
        def _():
            first_norm()

        @pl.when((t >= 5) & (t < 13))
        def _():
            attention(t - 5)

        @pl.when(t == 13)
        def _():
            keep(0, column(dq[...]))
            keep(1, column(dv[...]))
            loaded_w(1)
            loaded_w(2)

        @pl.when((t >= 13) & (t < 17))
        def _():
            input_rows(t - 13)

        for stage in range(6):

            @pl.when(t == 14 + 2 * stage)
            def _():
                v_step(stage)

        @pl.when(t == 18)
        def _():
            pltpu.make_async_copy(dx_y, dx_y, dr.at[2]).wait()
            dx_b[...] = (ga[...] + dx_y[...].astype(F32)).astype(BF)
            start_back(1)

        i1, live1 = at(1)

        @pl.when(live1)
        def _():
            slot, land = i1 % SLOTS, i1 % LAND_D
            clear(1, i1)
            landed(0, i1, r_d.at[i1 % LAND_D])
            for plane in range(2):
                b_y[slot, plane] = add(l_d[slot, plane], r_d[land, plane])
            launch(1, i1)

        i2, live2 = at(2)

        @pl.when(live2)
        def _():
            slot, land = i2 % SLOTS, i2 % LAND
            clear(2, i2)
            landed(1, i2, r_y.at[land])
            b_x[slot] = add(b_y[slot, y], r_y[land])
            launch(2, i2)

        i3, live3 = at(3)

        @pl.when(live3)
        def _():
            slot, land = i3 % SLOTS, i3 % LAND
            clear(3, i3)
            landed(2, i3, r_x.at[land])
            first = order(i3)[0][0]
            b_1[slot] = add(b_x[slot, rows_of(first * 64, 64)], r_x[land])
            launch(3, i3)

        i4, live4 = at(4)

        @pl.when(live4)
        def _():
            slot, land = i4 % SLOTS, i4 % LAND
            clear(4, i4)
            landed(3, i4, r_1.at[land])
            second = order(i4)[0][1]
            b_2[slot] = add(b_1[slot, rows_of(second * 32, 32)], r_1[land])
            launch(4, i4)

        i5, live5 = at(5)

        @pl.when(live5)
        def _():
            slot, land = i5 % SLOTS, i5 % LAND
            clear(5, i5)
            landed(4, i5, r_2.at[land])
            first, second, third = order(i5)[0]
            o_b[i5 % ROOM, rows_of(first * 64 + second * 32 + third * 16, 16)] = add(
                b_2[slot, rows_of(third * 16, 16)], r_2[land]
            )
            launch(5, i5)

        i6, live6 = at(6)

        @pl.when(live6)
        def _():
            clear(6, i6)
            first, second, third = order(i6)[0]
            row = first * 64 + second * 32 + (1 - third) * 16
            landed(5, i6, o_b.at[i6 % ROOM, rows_of(row, 16)])
            launch(6, i6)

        i7, live7 = at(7)

        @pl.when(live7)
        def _():
            clear(7, i7)
            first, second, _ = order(i7)[0]
            landed(6, i7, o_b.at[i7 % ROOM, rows_of(first * 64 + (1 - second) * 32, 32)])
            launch(7, i7)

        i8, live8 = at(8)

        @pl.when(live8)
        def _():
            first = order(i8)[0][0]
            landed(7, i8, o_b.at[i8 % ROOM, rows_of((1 - first) * 64, 64)])
            store(i8)

        return carry

    lax.fori_loop(0, CHUNKS + LAG[8], tick, 0)
    stored()
    for stage in range(8):
        for i in range(CHUNKS - SLOTS, CHUNKS):
            copies(stage, i).wait_send()
    for stage in range(5):
        v_copy(stage).wait_send()
    dx_core(0).wait_send()
    dx_core(1).wait_send()
    dx_far.wait_send()
    finish_back(0)
    finish_back(1)
    for i in range(n_items):
        for kind in range(8):
            if kind not in (3, 5) or split(i)[kind // 2]:
                send_copy(i, kind).wait_send()
    finish_blocks((0, 1, 2))
    for step in range(3):
        for block in range(2):
            for move in group_copy(step, block):
                move.wait_send()
    for move in vec_copies:
        move.wait_send()


def layer_call(inp, cot, seg, weights, vectors):
    vmem = pl.BlockSpec(memory_space=pltpu.VMEM)
    any_spec = pl.BlockSpec(memory_space=pl.ANY)
    dma = pltpu.SemaphoreType.DMA
    grad = jax.ShapeDtypeStruct((256, 1024), BF)
    square = jax.ShapeDtypeStruct((1024, 1024), BF)
    full_weights = [square] * 4 + [
        jax.ShapeDtypeStruct((1024, 4096), BF), jax.ShapeDtypeStruct((4096, 1024), BF)
    ]
    return pl.pallas_call(
        layer_kernel,
        out_shape=full_weights + [
            grad, grad, grad, grad,
            jax.ShapeDtypeStruct((256, 4096), BF),
            jax.ShapeDtypeStruct((1024, 1024), BF),
            jax.ShapeDtypeStruct((2, 1, 128, 1024), BF),
            jax.ShapeDtypeStruct((2, 1, 128, 1024), BF),
            jax.ShapeDtypeStruct((24, 128), F32),
        ],
        in_specs=[any_spec] * 9 + [vmem] * 9,
        out_specs=[any_spec] * 14 + [vmem],
        scratch_shapes=[
            pltpu.VMEM((SLOTS, 2, 128, 1024), BF),
            pltpu.VMEM((SLOTS, 2, 128, 1024), BF),
            pltpu.VMEM((LAND_D, 2, 128, 1024), BF),
            pltpu.VMEM((SLOTS, 2, 128, 1024), BF),
            pltpu.VMEM((LAND, 128, 1024), BF),
            pltpu.VMEM((SLOTS, 128, 1024), BF),
            pltpu.VMEM((LAND, 64, 1024), BF),
            pltpu.VMEM((SLOTS, 64, 1024), BF),
            pltpu.VMEM((LAND, 32, 1024), BF),
            pltpu.VMEM((SLOTS, 32, 1024), BF),
            pltpu.VMEM((LAND, 16, 1024), BF),
            pltpu.VMEM((ROOM, 128, 1024), BF),
            pltpu.VMEM((256, 4096), BF),
            pltpu.VMEM((256, 1024), F32),
            pltpu.VMEM((256, 1024), F32),
            pltpu.VMEM((256, 1024), BF),
            pltpu.VMEM((256, 1024), BF),
            pltpu.VMEM((256, 1024), BF),
            pltpu.VMEM((1024, 1024), BF),
            pltpu.VMEM((1024, 1024), BF),
            pltpu.VMEM((256, 1024), F32),
            pltpu.VMEM((2, 1024, 512), BF),
            pltpu.VMEM((2, 512, 1024), BF),
            pltpu.VMEM((4, 1024, 1024), BF),
            pltpu.VMEM((2, 256, 1024), BF),
            pltpu.VMEM((256, 1024), BF),
            pltpu.VMEM((4, 24, 128), F32),
            pltpu.VMEM((4, 2, 24, 128), F32),
            pltpu.VMEM((3, 2, 24, 128), F32),
            pltpu.VMEM((4, 24, 128), F32),
            pltpu.VMEM((256, 4096), BF),
            pltpu.VMEM((256, 1024), BF),
            pltpu.VMEM((256, 1024), BF),
            pltpu.VMEM((256, 4096), BF),
            pltpu.VMEM((256, 1024), F32),
            pltpu.VMEM((256, 1), F32),
            pltpu.VMEM((256, 1024), BF),
            pltpu.VMEM((256, 1024), BF),
            pltpu.VMEM((1024, 1024), BF),
            pltpu.VMEM((1024, 1024), BF),
            pltpu.VMEM((1024, 1024), BF),
            pltpu.VMEM((256, 1024), BF),
            pltpu.VMEM((8, 1, 128), jnp.int32),
            pltpu.VMEM((24, 128), F32),
            pltpu.VMEM((4, 24, 128), F32),
            pltpu.VMEM((8, 1024), F32),
            pltpu.VMEM((1, 4096), F32),
            dma((8, SLOTS)), dma((8, LAND)), dma((3,)), dma((3,)), dma((2, 2)), dma((2, 2)),
            dma((5,)), dma((5,)), dma((8,)), dma(()),
            dma((3, 2)), dma((3, 2)), dma((2, 3, 2)), dma((2, 3, 2)),
            dma((8, 12)), dma((8, 12)), dma((3,)), dma((3,)),
        ],
        compiler_params=pltpu.CompilerParams(
            collective_id=0, has_side_effects=True, vmem_limit_bytes=61 << 20
        ),
        name="layer",
    )(inp, cot, seg, *weights, *vectors)


def widen_kernel(*refs):
    ins, outs = refs[:9], refs[9:]
    for src, dst in zip(ins[:8], outs[:8]):
        dst[...] = src[...].astype(dst.dtype)
    vec, smalls = ins[8], outs[8:]

    @pl.when(pl.program_id(0) == 0)
    def _():
        for i in range(8):
            for half in range(2):
                smalls[i][pl.ds(half * 128, 128)] = vec[2 * i + half]
        for n in range(8):
            smalls[8][pl.ds(n * 128, 128)] = vec[16 + n]


def widen(narrow, vec):
    steps = 8
    in_specs, out_specs, shapes = [], [], []
    for n, v in enumerate(narrow):
        at = v.ndim - 2
        block = v.shape[:at] + (v.shape[at] // steps,) + v.shape[at + 1 :]

        def place(i, at=at, rank=v.ndim):
            return tuple(i if d == at else 0 for d in range(rank))

        in_specs.append(pl.BlockSpec(block, place))
        out_specs.append(pl.BlockSpec(block, place))
        shapes.append(jax.ShapeDtypeStruct(v.shape, BF if n == 7 else F32))
    in_specs.append(pl.BlockSpec((24, 128), lambda i: (0, 0)))
    for size in (256,) * 8 + (1024,):
        out_specs.append(pl.BlockSpec((size,), lambda i: (0,)))
        shapes.append(jax.ShapeDtypeStruct((size,), F32))
    return pl.pallas_call(
        widen_kernel,
        grid=(steps,),
        out_shape=shapes,
        in_specs=in_specs,
        out_specs=out_specs,
        compiler_params=pltpu.CompilerParams(vmem_limit_bytes=61 << 20),
        name="widen",
    )(*narrow, vec)


def per_group_device(
    layer_input, segments, cotangent,
    query_weight, key_weight, value_weight, output_weight, expand_weight, contract_weight,
    query_bias, value_bias, output_bias, first_gain, first_shift, expand_bias, contract_bias,
    second_gain, second_shift,
):
    outs = layer_call(
        layer_input, cotangent, segments,
        (query_weight, key_weight, value_weight, output_weight, expand_weight, contract_weight),
        (
            query_bias, value_bias, output_bias, first_gain, first_shift, contract_bias,
            second_gain, second_shift, expand_bias,
        ),
    )
    o_q, o_k, o_v, o_o, o_e, o_c, resf, dxf, vec = outs[6:]
    wide = widen((o_q, o_k, o_v, o_o, o_e, o_c, dxf, resf), vec)
    g_q, g_k, g_v, g_o, g_e, g_c, input_grad, layer_output = wide[:8]
    b_q, b_v, b_o, g_one, s_one, b_c, g_two, s_two, b_e = wide[8:]
    return (
        layer_output, input_grad, g_q, g_k, g_v, g_o, g_e, g_c,
        b_q, b_v, b_o, g_one, s_one, b_e, b_c, g_two, s_two,
    )


def solution(mesh):
    in_specs = (
        P(None, "fsdp", "ctx", None),
        P(None, "fsdp", "ctx"),
        P(None, "fsdp", "ctx", None),
        P("fsdp", None),
        P("fsdp", None),
        P("fsdp", None),
        P("fsdp", None),
        P("fsdp", None),
        P("fsdp", None),
        P("fsdp"),
        P("fsdp"),
        P("fsdp"),
        P("fsdp"),
        P("fsdp"),
        P("fsdp"),
        P("fsdp"),
        P("fsdp"),
        P("fsdp"),
    )
    out_specs = (
        P(None, "fsdp", "ctx", None),
        P(None, "fsdp", "ctx", None),
        P("fsdp", None),
        P("fsdp", None),
        P("fsdp", None),
        P("fsdp", None),
        P("fsdp", None),
        P("fsdp", None),
        P("fsdp"),
        P("fsdp"),
        P("fsdp"),
        P("fsdp"),
        P("fsdp"),
        P("fsdp"),
        P("fsdp"),
        P("fsdp"),
        P("fsdp"),
    )
    def whole(layer_input, segments, *rest):
        grouped = (
            dict(mesh.shape) == {"ctx": 8, "fsdp": 4}
            and layer_input.shape == (2, 4, 1024, 1024)
            and rest[5].shape == (1024, 4096)
        )
        body = per_group_device if grouped else per_device
        return jax.shard_map(
            body, mesh=mesh, in_specs=in_specs, out_specs=out_specs, check_vma=False
        )(layer_input, segments, *rest)

    return whole
```

```python
import math

import jax
import jax.numpy as jnp
from jax import lax
from jax.experimental import pallas as pl
from jax.experimental.pallas import tpu as pltpu
from jax.sharding import PartitionSpec as P

HEADS = 16
HEAD_DIM = 64


def as_sent(x):
    return jax.tree.map(lambda a: a.astype(jnp.bfloat16) if a.dtype == jnp.float32 else a, x)


def plain_dot(left_side, right_side):
    return jnp.dot(left_side, right_side, preferred_element_type=jnp.float32)


def left_dot(left_side, right_side):
    return lax.dot_general(
        left_side, right_side, (((0,), (0,)), ((), ())), preferred_element_type=jnp.float32
    )


def right_dot(left_side, right_side):
    return lax.dot_general(
        left_side, right_side, (((1,), (1,)), ((), ())), preferred_element_type=jnp.float32
    )


def norm_forward(hidden, gain_row, offset_row):
    centre = hidden - jnp.mean(hidden, axis=-1, keepdims=True)
    inverse = lax.rsqrt(jnp.mean(centre * centre, axis=-1, keepdims=True) + 1e-05)
    normed = centre * inverse
    return (normed * gain_row.astype(jnp.float32) + offset_row.astype(jnp.float32), normed, inverse)


def norm_backward(grad_out, normed, inverse, gain_row):
    scaled = grad_out * gain_row.astype(jnp.float32)
    grad_in = inverse * (
        scaled
        - jnp.mean(scaled, axis=-1, keepdims=True)
        - normed * jnp.mean(scaled * normed, axis=-1, keepdims=True)
    )
    return (grad_in, jnp.sum(grad_out * normed, axis=0), jnp.sum(grad_out, axis=0))


def gather_weights(shards):
    return (
        lax.all_gather(shards[0], "fsdp", axis=0, tiled=True),
        lax.all_gather(shards[1], "fsdp", axis=0, tiled=True),
        lax.all_gather(shards[2], "fsdp", axis=0, tiled=True),
        lax.all_gather(shards[3], "fsdp", axis=0, tiled=True),
        lax.all_gather(shards[4], "fsdp", axis=0, tiled=True),
        lax.all_gather(shards[5], "fsdp", axis=0, tiled=True),
        lax.all_gather(shards[6], "fsdp", axis=0, tiled=True),
        lax.all_gather(shards[7], "fsdp", axis=0, tiled=True),
        lax.all_gather(shards[8], "fsdp", axis=0, tiled=True),
        lax.all_gather(shards[9], "fsdp", axis=0, tiled=True),
        lax.all_gather(shards[10], "fsdp", axis=0, tiled=True),
        lax.all_gather(shards[11], "fsdp", axis=0, tiled=True),
        lax.all_gather(shards[12], "fsdp", axis=0, tiled=True),
        lax.all_gather(shards[13], "fsdp", axis=0, tiled=True),
        lax.all_gather(shards[14], "fsdp", axis=0, tiled=True),
    )


def attend_forward(query_bf, key_bf, value_bf, seg_local):
    row_count = query_bf.shape[0]
    score_scale = HEAD_DIM ** (-0.5)
    query_heads = query_bf.reshape(row_count, HEADS, HEAD_DIM)
    run_max = jnp.full((HEADS, row_count), -1e30, jnp.float32)
    key_rows = lax.all_gather(key_bf, "ctx", axis=0, tiled=True)
    value_rows = lax.all_gather(value_bf, "ctx", axis=0, tiled=True)
    key_seg = lax.all_gather(seg_local, "ctx", axis=0, tiled=True)
    piece_rows = key_rows.shape[0]
    key_heads = key_rows.reshape(piece_rows, HEADS, HEAD_DIM)
    value_heads = value_rows.reshape(piece_rows, HEADS, HEAD_DIM)
    scores = (
        jnp.einsum("rhd,khd->hrk", query_heads, key_heads, preferred_element_type=jnp.float32)
        * score_scale
    )
    same_doc = seg_local[:, None] == key_seg[None, :]
    scores = jnp.where(same_doc[None], scores, -1e30)
    new_max = jnp.maximum(run_max, jnp.max(scores, axis=-1))
    numerators = jnp.exp(scores - new_max[..., None])
    run_sum = jnp.sum(numerators, axis=-1)
    accumulated = jnp.einsum(
        "hrk,khd->hrd",
        numerators.astype(jnp.bfloat16),
        value_heads,
        preferred_element_type=jnp.float32,
    )
    run_max, run_sum, accumulated = (new_max, run_sum, accumulated)
    context = jnp.transpose(accumulated / run_sum[..., None], (1, 0, 2)).reshape(
        row_count, HEADS * HEAD_DIM
    )
    return (context, run_max + jnp.log(run_sum))


def block_grads(
    query_heads, grad_heads, query_seg, log_sum, row_delta, key_heads, value_heads, key_seg
):
    score_scale = HEAD_DIM ** (-0.5)
    scores = (
        jnp.einsum("rhd,khd->hrk", query_heads, key_heads, preferred_element_type=jnp.float32)
        * score_scale
    )
    same_doc = query_seg[:, None] == key_seg[None, :]
    scores = jnp.where(same_doc[None], scores, -1e30)
    probs_full = jnp.exp(scores - log_sum[..., None])
    grad_probs = jnp.einsum(
        "rhd,khd->hrk", grad_heads, value_heads, preferred_element_type=jnp.float32
    )
    grad_scores = (probs_full * (grad_probs - row_delta[..., None])).astype(jnp.bfloat16)
    return (probs_full, grad_scores)


def attend_backward(query_bf, key_bf, value_bf, seg_local, context, log_sum, grad_context):
    row_count = query_bf.shape[0]
    score_scale = HEAD_DIM ** (-0.5)
    key_every, value_every, seg_every = (
        lax.all_gather(key_bf, "ctx", axis=0, tiled=True),
        lax.all_gather(value_bf, "ctx", axis=0, tiled=True),
        lax.all_gather(seg_local, "ctx", axis=0, tiled=True),
    )
    length = key_every.shape[0]
    block_len = min(512, length)
    query_heads = query_bf.reshape(row_count, HEADS, HEAD_DIM)
    grad_heads = grad_context.reshape(row_count, HEADS, HEAD_DIM)
    row_delta = jnp.sum(
        (grad_context.astype(jnp.float32) * context).reshape(row_count, HEADS, HEAD_DIM), axis=-1
    ).T

    def visit_block(grad_query, block_num):
        first_row = block_num * block_len
        key_heads = lax.dynamic_slice_in_dim(key_every, first_row, block_len, 0).reshape(
            block_len, HEADS, HEAD_DIM
        )
        value_heads = lax.dynamic_slice_in_dim(value_every, first_row, block_len, 0).reshape(
            block_len, HEADS, HEAD_DIM
        )
        key_seg = lax.dynamic_slice_in_dim(seg_every, first_row, block_len, 0)
        probs_full, grad_scores = block_grads(
            query_heads, grad_heads, seg_local, log_sum, row_delta, key_heads, value_heads, key_seg
        )
        grad_query = (
            grad_query
            + jnp.einsum("hrk,khd->rhd", grad_scores, key_heads, preferred_element_type=jnp.float32)
            * score_scale
        )
        grad_keys = (
            jnp.einsum("hrk,rhd->khd", grad_scores, query_heads, preferred_element_type=jnp.float32)
            * score_scale
        )
        grad_values = jnp.einsum(
            "hrk,rhd->khd",
            probs_full.astype(jnp.bfloat16),
            grad_heads,
            preferred_element_type=jnp.float32,
        )
        stacked = jnp.stack(
            (
                grad_keys.reshape(block_len, HEADS * HEAD_DIM),
                grad_values.reshape(block_len, HEADS * HEAD_DIM),
            ),
            axis=1,
        )
        return (grad_query, stacked)

    grad_query, pieces = lax.scan(
        visit_block,
        jnp.zeros((row_count, HEADS, HEAD_DIM), jnp.float32),
        jnp.arange(length // block_len),
    )
    key_terms = pieces.reshape(length, 2, HEADS * HEAD_DIM)
    own_rows = lax.psum_scatter(
        key_terms.astype(jnp.bfloat16), "ctx", scatter_dimension=0, tiled=True
    ).astype(jnp.float32)
    grad_keyed = own_rows[:, 0].astype(jnp.bfloat16)
    grad_valued = own_rows[:, 1].astype(jnp.bfloat16)
    grad_queries = grad_query.reshape(row_count, HEADS * HEAD_DIM).astype(jnp.bfloat16)
    return (grad_queries, grad_keyed, grad_valued)


def layer_forward(inputs, seg_local, full_weights):
    (
        query_weight,
        key_weight,
        value_weight,
        output_weight,
        expand_weight,
        contract_weight,
        query_bias,
        value_bias,
        output_bias,
        first_gain,
        first_shift,
        expand_bias,
        contract_bias,
        second_gain,
        second_shift,
    ) = full_weights
    query_bf = (plain_dot(inputs, query_weight) + query_bias.astype(jnp.float32)).astype(
        jnp.bfloat16
    )
    key_bf = plain_dot(inputs, key_weight).astype(jnp.bfloat16)
    value_bf = (plain_dot(inputs, value_weight) + value_bias.astype(jnp.float32)).astype(
        jnp.bfloat16
    )
    context, log_sum = attend_forward(query_bf, key_bf, value_bf, seg_local)
    context_bf = context.astype(jnp.bfloat16)
    first_sum = (
        inputs.astype(jnp.float32)
        + plain_dot(context_bf, output_weight)
        + output_bias.astype(jnp.float32)
    )
    first_out, normed_one, inverse_one = norm_forward(first_sum, first_gain, first_shift)
    first_bf = first_out.astype(jnp.bfloat16)
    hidden = plain_dot(first_bf, expand_weight) + expand_bias.astype(jnp.float32)
    gelled_bf = jax.nn.gelu(hidden, approximate=False).astype(jnp.bfloat16)
    second_sum = (
        first_out + plain_dot(gelled_bf, contract_weight) + contract_bias.astype(jnp.float32)
    )
    result, normed_two, inverse_two = norm_forward(second_sum, second_gain, second_shift)
    kept_state = (
        query_bf,
        key_bf,
        value_bf,
        context,
        log_sum,
        context_bf,
        normed_one,
        inverse_one,
        first_bf,
        hidden,
        gelled_bf,
        normed_two,
        inverse_two,
    )
    return (result.astype(jnp.bfloat16), kept_state)


def layer_backward(inputs, seg_local, grad_out, kept_state, full_weights):
    (
        query_weight,
        key_weight,
        value_weight,
        output_weight,
        expand_weight,
        contract_weight,
        query_bias,
        value_bias,
        output_bias,
        first_gain,
        first_shift,
        expand_bias,
        contract_bias,
        second_gain,
        second_shift,
    ) = full_weights
    (
        query_bf,
        key_bf,
        value_bf,
        context,
        log_sum,
        context_bf,
        normed_one,
        inverse_one,
        first_bf,
        hidden,
        gelled_bf,
        normed_two,
        inverse_two,
    ) = kept_state
    grad_second, second_gain_grad, second_shift_grad = norm_backward(
        grad_out.astype(jnp.float32), normed_two, inverse_two, second_gain
    )
    grad_branch = grad_second.astype(jnp.bfloat16)
    contract_weight_grad = left_dot(gelled_bf, grad_branch)
    contract_bias_grad = jnp.sum(grad_branch.astype(jnp.float32), axis=0)
    grad_gelled = right_dot(grad_branch, contract_weight)
    gelu_pull = jax.vjp(lambda values: jax.nn.gelu(values, approximate=False), hidden)[1]
    grad_hidden = gelu_pull(grad_gelled)[0].astype(jnp.bfloat16)
    expand_weight_grad = left_dot(first_bf, grad_hidden)
    expand_bias_grad = jnp.sum(grad_hidden.astype(jnp.float32), axis=0)
    grad_first = grad_second + right_dot(grad_hidden, expand_weight)
    grad_attn, first_gain_grad, first_shift_grad = norm_backward(
        grad_first, normed_one, inverse_one, first_gain
    )
    grad_attn_low = grad_attn.astype(jnp.bfloat16)
    output_weight_grad = left_dot(context_bf, grad_attn_low)
    output_bias_grad = jnp.sum(grad_attn_low.astype(jnp.float32), axis=0)
    grad_context = right_dot(grad_attn_low, output_weight).astype(jnp.bfloat16)
    grad_queries, grad_keyed, grad_valued = attend_backward(
        query_bf, key_bf, value_bf, seg_local, context, log_sum, grad_context
    )
    query_weight_grad = left_dot(inputs, grad_queries)
    key_weight_grad = left_dot(inputs, grad_keyed)
    value_weight_grad = left_dot(inputs, grad_valued)
    query_bias_grad = jnp.sum(grad_queries.astype(jnp.float32), axis=0)
    value_bias_grad = jnp.sum(grad_valued.astype(jnp.float32), axis=0)
    grad_input = (
        grad_attn
        + right_dot(grad_queries, query_weight)
        + right_dot(grad_keyed, key_weight)
        + right_dot(grad_valued, value_weight)
    )
    grad_terms = (
        query_weight_grad,
        key_weight_grad,
        value_weight_grad,
        output_weight_grad,
        expand_weight_grad,
        contract_weight_grad,
        query_bias_grad,
        value_bias_grad,
        output_bias_grad,
        first_gain_grad,
        first_shift_grad,
        expand_bias_grad,
        contract_bias_grad,
        second_gain_grad,
        second_shift_grad,
    )
    return (grad_input, grad_terms)


def per_device(
    layer_input,
    segments,
    cotangent,
    query_weight,
    key_weight,
    value_weight,
    output_weight,
    expand_weight,
    contract_weight,
    query_bias,
    value_bias,
    output_bias,
    first_gain,
    first_shift,
    expand_bias,
    contract_bias,
    second_gain,
    second_shift,
):
    shards = (
        query_weight,
        key_weight,
        value_weight,
        output_weight,
        expand_weight,
        contract_weight,
        query_bias,
        value_bias,
        output_bias,
        first_gain,
        first_shift,
        expand_bias,
        contract_bias,
        second_gain,
        second_shift,
    )
    micro_count = layer_input.shape[0]
    results = []
    grad_inputs = []
    totals = None
    for micro_step in range(micro_count):
        inputs = layer_input[micro_step, 0]
        seg_local = segments[micro_step, 0].astype(jnp.bfloat16)
        front_weights = gather_weights(shards)
        result, kept_state = layer_forward(inputs, seg_local, front_weights)
        behind = gather_weights(shards)
        grad_input, grad_terms = layer_backward(
            inputs, seg_local, cotangent[micro_step, 0], kept_state, behind
        )
        results.append(result)
        grad_inputs.append(grad_input)
        if totals is None:
            totals = grad_terms
        else:
            totals = tuple(
                (left_side + right_side for left_side, right_side in zip(totals, grad_terms))
            )
    reduced = jax.tree.map(
        lambda part: part.astype(jnp.float32),
        lax.psum_scatter(as_sent(totals), "fsdp", scatter_dimension=0, tiled=True),
    )
    summed = jax.tree.map(lambda part: part.astype(jnp.float32), lax.psum(as_sent(reduced), "ctx"))
    layer_output = jnp.stack(results, axis=0)[:, None]
    input_grad = jnp.stack(grad_inputs, axis=0)[:, None]
    return (
        layer_output,
        input_grad,
        summed[0],
        summed[1],
        summed[2],
        summed[3],
        summed[4],
        summed[5],
        summed[6],
        summed[7],
        summed[8],
        summed[9],
        summed[10],
        summed[11],
        summed[12],
        summed[13],
        summed[14],
    )


MESH = pl.DeviceIdType.MESH
BF = jnp.bfloat16
F32 = jnp.float32
CHUNKS = 24
SLOTS = 3
LAND = 6
LAND_D = 4
ROOM = 10
LAG = (0, 0, 2, 4, 5, 6, 7, 8, 10)
Z_FROM, Z_TO = 12, 14
SPLIT = ((64, 0, 0), (40, 24, 0))
EARLY, LATE = 4, 10


def coords():
    c, f = lax.axis_index("ctx"), lax.axis_index("fsdp")
    return c // 2, c % 2, f // 2, f % 2


def dev(z, x, y, k):
    return (z * 2 + x, y * 2 + k)


def greet(z, x, y, k):
    barrier = pltpu.get_barrier_semaphore()
    for step in range(1, 8):
        place = (z * 2 + k + step) % 8
        pl.semaphore_signal(
            barrier, inc=1, device_id=dev(place // 2, x, y, place % 2), device_id_type=MESH
        )
    pl.semaphore_signal(barrier, inc=1, device_id=dev(z, 1 - x, y, k), device_id_type=MESH)
    pl.semaphore_signal(barrier, inc=1, device_id=dev(z, x, 1 - y, k), device_id_type=MESH)
    pl.semaphore_wait(barrier, 9)


def remote(src, dst, send, recv, to):
    return pltpu.make_async_remote_copy(
        src_ref=src, dst_ref=dst, send_sem=send, recv_sem=recv, device_id=to, device_id_type=MESH
    )


def rows_of(start, size, unit=16):
    return pl.ds(pl.multiple_of(start, unit), size)


def two_heads(block):
    lane = lax.broadcasted_iota(jnp.int32, block.shape, 1)
    zero = jnp.zeros_like(block)
    return jnp.concatenate(
        [jnp.where(lane < HEAD_DIM, block, zero), jnp.where(lane >= HEAD_DIM, block, zero)], axis=0
    )


def one_block(pair):
    rows = pair.shape[0] // 2
    lane = lax.broadcasted_iota(jnp.int32, (rows, pair.shape[1]), 1)
    return jnp.where(lane < HEAD_DIM, pair[:rows], pair[rows:])


def softmax_pair(queries, keys, bias):
    scores = right_dot(queries, keys)
    scores = scores + jnp.concatenate([bias, bias], axis=0)
    numer = jnp.exp(scores - jnp.max(scores, axis=-1, keepdims=True))
    return numer * (1.0 / jnp.sum(numer, axis=-1, keepdims=True))


def layer_kernel(
    inp, cot, seg, wq, wk, wv, wo, we, wc, *rest,
):
    (
        vecs, (fq, fk, fv, fo, fe, fc), (o_q, o_k, o_v, o_o, o_e, o_c), (resf, dxf, vec_out), rest
    ) = (rest[:9], rest[9:15], rest[15:21], rest[21:24], rest[24:])
    (
        s_d, l_d, r_d, b_y, r_y, b_x, r_x, b_1, r_1, b_2, r_2, o_b,
        gh, acc, ga, gal, dctx, dq, dk, dv, bias, we_b, wc_b, w_b,
        dx_r, dx_y, vec, v_s, v_d, v_r,
        gel, gb, fb, gp, n1, inv1, ctx, q, key, val, xf, res, segf, vec_in, vecf, row8, row_e,
        ss, rs, ds, dr, a_send, a_recv, v_send, v_recv, w_sem, o_sem,
        i_send, i_recv, g_send, g_recv, p_send, p_recv, f_send, f_recv,
    ) = rest
    dx_b, dx_s = dctx, gb
    cotf = gh.at[:, pl.ds(0, 1024)]
    z, x, y, k = coords()
    f = y * 2 + k
    other = (1 - y) * 2 + k
    sib, xn, yn = dev(z, x, y, 1 - k), dev(z, 1 - x, y, k), dev(z, x, 1 - y, k)
    bit1, bit2 = z % 2, z // 2
    z1 = dev(z + 1 - 2 * bit1, x, y, k)
    z2 = dev((z + 2) % 4, x, y, k)
    color = bit1 * 2 + x
    c_x, c_z, c_o = color + 1 - 2 * x, (color + 2) % 4, 3 - color
    own_rows = rows_of(x * 512 + k * 256, 256)

    def block_moves(mb):
        to_z, to_k = mb * 2 + k, z // 2
        row = x * 512 + z * 128
        slot = z % 2
        mine = (to_z == z) & (to_k == k)
        moves = (
            (inp.at[mb, 0], xf.at[rows_of(row, 128)], 0),
            (seg.at[mb], segf.at[x * 4 + z], 1),
            (cot.at[mb, 0], cotf.at[rows_of(slot * 128, 128)], 2),
        )
        return mine, dev(to_z, x, y, to_k), slot, moves

    def start_blocks(which):
        for mb in range(2):
            mine, to, slot, moves = block_moves(mb)
            for src, dst, n in moves:
                if n not in which:
                    continue

                @pl.when(mine)
                def _():
                    pltpu.make_async_copy(src, dst, i_recv.at[n, slot]).start()

                @pl.when(jnp.logical_not(mine))
                def _():
                    remote(src, dst, i_send.at[n, mb], i_recv.at[n, slot], to).start()

    def finish_blocks(which):
        for mb in range(2):
            mine, to, slot, moves = block_moves(mb)
            for src, dst, n in moves:
                if n not in which:
                    continue

                @pl.when(jnp.logical_not(mine))
                def _():
                    remote(src, dst, i_send.at[n, mb], i_recv.at[n, slot], to).wait_send()

    def arrive_block(slot, which):
        zz = 2 * k + slot
        for n in which:
            if n == 0:
                dst = xf.at[rows_of(x * 512 + zz * 128, 128)]
            elif n == 1:
                dst = segf.at[x * 4 + zz]
            else:
                dst = cotf.at[pl.ds(slot * 128, 128)]
            pltpu.make_async_copy(dst, dst, i_recv.at[n, slot]).wait()

    def group_copy(step, block):
        who = x if step < 2 else 1 - x
        src = xf.at[rows_of(who * 512 + k * 256 + block * 128, 128)]
        sseg = segf.at[who * 4 + k * 2 + block]
        to = (sib, xn, sib)[step]
        return (
            remote(src, src, g_send.at[0, step, block], g_recv.at[0, step, block], to),
            remote(sseg, sseg, g_send.at[1, step, block], g_recv.at[1, step, block], to),
        )

    def group_start(step, block):
        for move in group_copy(step, block):
            move.start()

    def group_arrive(step, block):
        who = (x, 1 - x, 1 - x)[step]
        kk = (1 - k, k, 1 - k)[step]
        src = xf.at[rows_of(who * 512 + kk * 256 + block * 128, 128)]
        sseg = segf.at[who * 4 + kk * 2 + block]
        pltpu.make_async_copy(src, src, g_recv.at[0, step, block]).wait()
        pltpu.make_async_copy(sseg, sseg, g_recv.at[1, step, block]).wait()

    items = []
    for shard, full in ((wq, fq), (wk, fk), (wv, fv), (wo, fo)):
        items.append((shard, full, 0, 0, 256))
    for j in range(4):
        items.append((we, fe, 0, j * 1024, 256))
    for j in range(4):
        items.append((wc, fc, j * 256, 0, 1024))
    n_items = len(items)

    def direct(i):
        return i < EARLY or LATE <= i < n_items

    def split(i):
        return SPLIT[0] if direct(i) else SPLIT[1]

    def part(i, quarter, start, size, own_src=False):
        shard, full, row, col, step = items[i]
        if own_src:
            return shard.at[rows_of(row + start, size, 8), pl.ds(col, 1024)]
        return full.at[rows_of(quarter * step + row + start, size, 8), pl.ds(col, 1024)]

    def send_copy(i, kind):
        sems = (p_send.at[kind, i], p_recv.at[kind, i])
        if kind == 0:
            return remote(part(i, f, color * 64, 64, True), part(i, f, color * 64, 64), *sems, yn)
        if kind == 1:
            rows = split(i)[0]
            return remote(part(i, f, c_o * 64, rows, True), part(i, f, c_o * 64, rows), *sems, yn)
        if kind == 2:
            src = part(i, other, color * 64, 64)
            return remote(src, src, *sems, xn)
        if kind == 3:
            src = part(i, other, c_z * 64 + split(i)[0], split(i)[1])
            return remote(src, src, *sems, xn)
        if kind == 4:
            src = part(i, other, color * 64, 64)
            return remote(src, src, *sems, z1)
        if kind == 5:
            src = part(i, other, c_x * 64 + 64 - split(i)[2], split(i)[2])
            return remote(src, src, *sems, z1)
        if kind == 6:
            return remote(part(i, f, 0, 256, True), part(i, f, 0, 256), *sems, sib)
        src = part(i, other, 0, 256)
        return remote(src, src, *sems, sib)

    def arrive(i, kind):
        if kind == 0:
            dst = part(i, other, color * 64, 64)
        elif kind == 1:
            dst = part(i, other, c_o * 64, split(i)[0])
        elif kind == 2:
            dst = part(i, other, c_x * 64, 64)
        elif kind == 3:
            dst = part(i, other, c_o * 64 + split(i)[0], split(i)[1])
        elif kind == 4:
            dst = part(i, other, c_z * 64, 64)
        elif kind == 5:
            dst = part(i, other, c_o * 64 + 64 - split(i)[2], split(i)[2])
        elif kind == 6:
            dst = part(i, y * 2 + 1 - k, 0, 256)
        else:
            dst = part(i, (1 - y) * 2 + 1 - k, 0, 256)
        pltpu.make_async_copy(dst, dst, p_recv.at[kind, i]).wait()


    for i in range(8):
        packed = vecs[i][...].astype(F32).reshape(1, 256)
        vec_in[pl.ds(2 * i, 1)] = packed[:, :128]
        vec_in[pl.ds(2 * i + 1, 1)] = packed[:, 128:]
    packed = vecs[8][...].astype(F32).reshape(1, 1024)
    for n in range(8):
        vec_in[pl.ds(16 + n, 1)] = packed[:, n * 128 : n * 128 + 128]
    vecf[f] = vec_in[...]
    vec_copies = (
        remote(vec_in, vecf.at[f], f_send.at[0], f_recv.at[0], yn),
        remote(vec_in, vecf.at[f], f_send.at[1], f_recv.at[1], sib),
        remote(vecf.at[other], vecf.at[other], f_send.at[2], f_recv.at[2], sib),
    )

    def load_square(shard, full, row, step, cols, dst, sem):
        out = []
        for d in range(4):
            quarter = (f + d) % 4
            src = shard.at[pl.ds(row, 256), cols]
            if d > 0:
                src = full.at[rows_of(quarter * step + row, 256), cols]
            out.append(pltpu.make_async_copy(src, dst.at[rows_of(quarter * 256, 256)], sem))
        return out

    def load_c(j):
        slot = j % 2
        sem = w_sem.at[slot]

        @pl.when(j // 2 == f)
        def _():
            src = wc.at[rows_of((j % 2) * 512, 512)]
            pltpu.make_async_copy(src, wc_b.at[slot], sem).start()

        @pl.when(j // 2 != f)
        def _():
            pltpu.make_async_copy(fc.at[rows_of(j * 512, 512)], wc_b.at[slot], sem).start()

    def load_e(j):
        for move in load_square(
            we, fe, 0, 256, rows_of(j * 512, 512, 512), we_b.at[j % 2], w_sem.at[2 + j % 2]
        ):
            move.start()

    def load_w(n):
        shard, full = ((wo, fo), (wk, fk), (wv, fv), (wq, fq))[n]
        for move in load_square(
            shard, full, 0, 256, pl.ds(0, 1024), w_b.at[n], w_sem.at[4 + n]
        ):
            move.start()

    def loaded_w(n):
        pltpu.make_async_copy(w_b.at[n], w_b.at[n], w_sem.at[4 + n]).wait()

    def load_item(i):
        shard, full, row, col, step = items[i]
        arrive(i, 6)
        arrive(i, 7)
        slot = i % 4
        for move in load_square(
            shard, full, row, step, pl.ds(col, 1024), w_b.at[slot], w_sem.at[4 + slot]
        ):
            move.start()

    def item(i):
        slot = i % 4
        pltpu.make_async_copy(w_b.at[slot], w_b.at[slot], w_sem.at[4 + slot]).wait()
        return w_b.at[slot]

    def relay(t):
        for u in (0, 1, 2) if t == 0 else (t + 2,):
            if u < n_items:
                send_copy(u, 0).start()
                send_copy(u, 1).start()
                send_copy(u, 6).start()
        if 1 <= t <= n_items:
            i = t - 1
            arrive(i, 0)
            send_copy(i, 2).start()
            send_copy(i, 4).start()
        if 0 <= t - 3 < n_items and not direct(t - 3):
            i = t - 3
            arrive(i, 4)
            send_copy(i, 3).start()
            arrive(i, 2)
            if split(i)[2]:
                send_copy(i, 5).start()
        if 0 <= t - 3 and direct(t - 3):
            i = t - 3
            arrive(i, 1)
            arrive(i, 2)
            arrive(i, 4)
            send_copy(i, 7).start()
        if 0 <= t - 6 < n_items and not direct(t - 6):
            i = t - 6
            arrive(i, 1)
            arrive(i, 3)
            if split(i)[2]:
                arrive(i, 5)
            send_copy(i, 7).start()

    def fill_rows():
        pltpu.make_async_copy(vec_in, vec_in, f_recv.at[1]).wait()
        pltpu.make_async_copy(vec_in, vec_in, f_recv.at[2]).wait()
        for quarter in range(4):
            for i in range(8):
                for half in range(2):
                    col = quarter * 256 + half * 128
                    row8[pl.ds(i, 1), col : col + 128] = vecf[quarter, pl.ds(2 * i + half, 1)]
            for n in range(8):
                col = quarter * 1024 + n * 128
                row_e[:, col : col + 128] = vecf[quarter, pl.ds(16 + n, 1)]

    def fill_bias():
        for block in range(2):
            own = segf[x * 4 + k * 2 + block].astype(F32)
            down = jnp.transpose(jnp.broadcast_to(own, (128, 128)))
            for n in range(8):
                across = segf[n].astype(F32)
                bias[block * 128 : block * 128 + 128, n * 128 : n * 128 + 128] = jnp.where(
                    down == across, 0.0, -1e30
                )

    def project_own(w):
        q[...] = (plain_dot(xf[own_rows], w[...]) + row8[0:1]).astype(BF)

    def project_all(w, dst, add_row):
        def block(n, carry):
            rows = rows_of(n * 256, 256)
            dst[rows] = (plain_dot(xf[rows], w[...]) + add_row).astype(BF)
            return carry

        lax.fori_loop(0, 4, block, 0)

    def heads(first, last):
        def one(h, carry):
            cols = rows_of(h * 128, 128, 128)
            queries = two_heads(q[:, cols] * BF(HEAD_DIM**-0.5))
            probs = softmax_pair(queries, key[:, cols], bias[...])
            ctx[:, cols] = one_block(plain_dot(probs.astype(BF), val[:, cols])).astype(BF)
            return carry

        lax.fori_loop(first, last, one, 0)

    def norm(v):
        centre = v - jnp.mean(v, axis=-1, keepdims=True)
        inverse = lax.rsqrt(jnp.mean(centre * centre, axis=-1, keepdims=True) + 1e-05)
        return centre * inverse, inverse

    def attention_out(w):
        normed, inverse = norm(
            xf[own_rows].astype(F32) + plain_dot(ctx[...], w[...]) + row8[2:3]
        )
        n1[...] = normed
        inv1[...] = inverse
        first_out = normed * row8[3:4] + row8[4:5]
        acc[...] = first_out
        fb[...] = first_out.astype(BF)

    def expand(j, w):
        def block(n, carry):
            cols = rows_of(n * 256, 256, 256)
            out = rows_of(j * 1024 + n * 256, 256, 256)
            hidden = plain_dot(fb[...], w[:, cols]) + row_e[:, out]
            below = 0.5 + 0.5 * lax.erf(hidden * 0.5**0.5)
            gel[:, out] = (hidden * below).astype(BF)
            bell = jnp.exp(-0.5 * hidden * hidden) * (2 * math.pi) ** -0.5
            gp[:, out] = (below + hidden * bell).astype(BF)
            return carry

        lax.fori_loop(0, 4, block, 0)

    def contract(j, w):
        for quarter in range(4):
            cols = pl.ds(quarter * 1024 + j * 256, 256)
            acc[...] += plain_dot(gel[:, cols], w[quarter * 256 : quarter * 256 + 256])

    def second_norm():
        normed, inverse = norm(acc[...] + row8[5:6])
        res[...] = (normed * row8[6:7] + row8[7:8]).astype(BF)
        grad_out = cotf[...].astype(F32)
        keep(6, column(grad_out * normed))
        keep(7, column(grad_out))
        scaled = grad_out * row8[6:7]
        grad = inverse * (
            scaled
            - jnp.mean(scaled, axis=-1, keepdims=True)
            - normed * jnp.mean(scaled * normed, axis=-1, keepdims=True)
        )
        acc[...] = grad
        low = grad.astype(BF)
        gb[...] = low
        keep(5, column(low))


    def back(n, slot):
        to_z = 2 * k + slot
        to_k = z % 2
        mb = z // 2
        mine = (to_z == z) & (to_k == k)
        src = (res, dx_b)[n].at[pl.ds(slot * 128, 128)]
        dst = (resf, dxf)[n].at[mb, 0]

        def far():
            return remote(
                src, dst, a_send.at[n, slot], a_recv.at[n, mb], dev(to_z, x, y, to_k)
            )

        def near():
            return pltpu.make_async_copy(src, dst, a_recv.at[n, mb])

        return mine, far, near

    def start_back(n):
        for slot in range(2):
            mine, far, near = back(n, slot)

            @pl.when(mine)
            def _():
                near().start()

            @pl.when(jnp.logical_not(mine))
            def _():
                far().start()

    def finish_back(n):
        for slot in range(2):
            mine, far, _ = back(n, slot)

            @pl.when(jnp.logical_not(mine))
            def _():
                far().wait_send()

        for mb in range(2):
            dst = (resf, dxf)[n].at[mb, 0]
            pltpu.make_async_copy(dst, dst, a_recv.at[n, mb]).wait()

    def column(v):
        return jnp.sum(v.astype(F32), axis=0, keepdims=True)

    def keep(i, row):
        for quarter in range(4):
            for half in range(2):
                col = quarter * 256 + half * 128
                vec[quarter, pl.ds(2 * i + half, 1)] = row[:, col : col + 128]

    v_peers = (sib, yn, xn, z1, z2)

    def v_copy(stage):
        if stage == 0:
            return remote(v_d.at[1], v_d.at[2], v_send.at[0], v_recv.at[0], sib)
        src = v_s.at[0, 1 - y] if stage == 1 else v_s.at[stage - 1, 0]
        return remote(src, v_r.at[stage - 1], v_send.at[stage], v_recv.at[stage], v_peers[stage])

    def v_step(stage):
        if stage == 0:
            for plane in range(2):
                v_d[0, plane] = vec[plane * 2 + k]
                v_d[1, plane] = vec[plane * 2 + 1 - k]
        elif stage == 1:
            pltpu.make_async_copy(v_d.at[2], v_d.at[2], v_recv.at[0]).wait()
            v_s[0] = v_d[0] + v_d[2]
        else:
            dst = v_r.at[stage - 2]
            pltpu.make_async_copy(dst, dst, v_recv.at[stage - 1]).wait()
            mine = v_s[0, y] if stage == 2 else v_s[stage - 2, 0]
            total = mine + v_r[stage - 2]
            if stage == 5:
                vec_out[...] = total
            else:
                v_s[stage - 1, 0] = total
        if stage < 5:
            v_copy(stage).start()

    def send(stage, i, src, dst, to):
        return remote(src, dst, ss.at[stage, i % SLOTS], rs.at[stage, i % LAND], to)

    def landed(stage, i, dst):
        pltpu.make_async_copy(dst, dst, rs.at[stage, i % LAND]).wait()

    def order(i):
        late = (i // Z_FROM) * (1 - i // Z_TO) if Z_FROM < Z_TO else 0
        bits = tuple(
            (1 - late) * p + late * q
            for p, q in ((x, bit1), (bit1, bit2), (bit2, x))
        )
        peers = tuple(
            tuple((1 - late) * p + late * q for p, q in zip(one, two))
            for one, two in ((xn, z1), (z1, z2), (z2, xn))
        )
        return bits, peers

    def copies(stage, i):
        slot, land, room = i % SLOTS, i % LAND, i % ROOM
        (first, second, third), peers = order(i)
        if stage == 0:
            return send(0, i, s_d.at[slot], r_d.at[i % LAND_D], sib)
        if stage == 1:
            return send(1, i, b_y.at[slot, 1 - y], r_y.at[land], yn)
        if stage == 2:
            return send(2, i, b_x.at[slot, rows_of((1 - first) * 64, 64)], r_x.at[land], peers[0])
        if stage == 3:
            return send(3, i, b_1.at[slot, rows_of((1 - second) * 32, 32)], r_1.at[land], peers[1])
        if stage == 4:
            return send(4, i, b_2.at[slot, rows_of((1 - third) * 16, 16)], r_2.at[land], peers[2])
        if stage == 5:
            own = o_b.at[room, rows_of(first * 64 + second * 32 + third * 16, 16)]
            return send(5, i, own, own, peers[2])
        if stage == 6:
            own = o_b.at[room, rows_of(first * 64 + second * 32, 32)]
            return send(6, i, own, own, peers[1])
        own = o_b.at[room, rows_of(first * 64, 64)]
        return send(7, i, own, own, peers[0])

    def launch(stage, i):
        copies(stage, i).start()

    def clear(stage, i):
        @pl.when(i >= SLOTS)
        def _():
            copies(stage, i - SLOTS).wait_send()

    def add(a, b):
        return (a.astype(F32) + b.astype(F32)).astype(BF)

    def terms(i, a_ref, b_ref, a_base, a_step, b_col, a_rows=None):
        slot = i % SLOTS
        right = b_ref[:, b_col]
        for plane in range(2):
            for core in range(2):
                quarter = plane * 2 + (k if core == 0 else 1 - k)
                cols = pl.ds(pl.multiple_of(a_base + quarter * a_step, 128), 128)
                left = a_ref[:, cols] if a_rows is None else a_ref[a_rows, cols]
                product = left_dot(left, right).astype(BF)
                if core == 0:
                    l_d[slot, plane] = product
                else:
                    s_d[slot, plane] = product

    every = pl.ds(0, 1024)

    def stage_zero(i):
        @pl.when((i >= 0) & (i < CHUNKS))
        def _():
            clear(0, i)

        @pl.when(i < 8)
        def _():
            terms(i, gel, gb, i * 128, 1024, every)

        @pl.when((i >= 8) & (i < 16))
        def _():
            j = i - 8
            terms(i, fb, gh, (j % 2) * 128, 256, rows_of((j // 2) * 1024, 1024, 1024))

        @pl.when((i >= 16) & (i < 18))
        def _():
            terms(i, ctx, gal, (i - 16) * 128, 256, every)

        @pl.when((i >= 18) & (i < 20))
        def _():
            terms(i, xf, dq, (i - 18) * 128, 256, every, own_rows)

        @pl.when((i >= 20) & (i < 22))
        def _():
            terms(i, xf, dk, (i - 20) * 128, 256, every)

        @pl.when((i >= 22) & (i < 24))
        def _():
            terms(i, xf, dv, (i - 22) * 128, 256, every)

        @pl.when((i >= 0) & (i < CHUNKS))
        def _():
            launch(0, i)

    def stored():
        pltpu.make_async_copy(o_b.at[0], o_b.at[0], o_sem).wait()

    def store(i):
        src = o_b.at[i % ROOM]

        @pl.when(i >= 1)
        def _():
            stored()

        @pl.when(i < 8)
        def _():
            pltpu.make_async_copy(src, o_c.at[rows_of(i * 128, 128)], o_sem).start()

        @pl.when((i >= 8) & (i < 16))
        def _():
            j = i - 8
            dst = o_e.at[rows_of((j % 2) * 128, 128), rows_of((j // 2) * 1024, 1024, 1024)]
            pltpu.make_async_copy(src, dst, o_sem).start()

        for n, ref in enumerate((o_o, o_q, o_k, o_v)):
            first = 16 + 2 * n

            @pl.when((i >= first) & (i < first + 2))
            def _():
                dst = ref.at[rows_of((i - first) * 128, 128)]
                pltpu.make_async_copy(src, dst, o_sem).start()

    def feed_forward(j):
        slot = j % 2
        cols = rows_of(j * 512, 512, 512)
        pltpu.make_async_copy(wc_b.at[slot], wc_b.at[slot], w_sem.at[slot]).wait()
        pltpu.make_async_copy(we_b.at[slot], we_b.at[slot], w_sem.at[2 + slot]).wait()

        grads = (right_dot(gb[...], wc_b[slot]) * gp[:, cols].astype(F32)).astype(BF)
        gh[:, cols] = grads
        acc[...] += right_dot(grads, we_b[slot])
        row = column(grads)
        for n in range(4):
            vec[j // 2, pl.ds(16 + (j % 2) * 4 + n, 1)] = row[:, n * 128 : n * 128 + 128]

        @pl.when(j < 6)
        def _():
            load_c(j + 2)
            load_e(j + 2)

    def first_norm():
        normed = n1[...]
        grad_first = acc[...]
        keep(3, column(grad_first * normed))
        keep(4, column(grad_first))
        scaled = grad_first * row8[3:4]
        grad_attn = inv1[...] * (
            scaled
            - jnp.mean(scaled, axis=-1, keepdims=True)
            - normed * jnp.mean(scaled * normed, axis=-1, keepdims=True)
        )
        ga[...] = grad_attn
        low = grad_attn.astype(BF)
        gal[...] = low
        keep(2, column(low))
        loaded_w(0)
        dctx[...] = right_dot(low, w_b[0]).astype(BF)

    def attention(h):
        cols = rows_of(h * 128, 128, 128)
        queries = two_heads(q[:, cols] * BF(HEAD_DIM**-0.5))
        keys = key[:, cols]
        probs = softmax_pair(queries, keys, bias[...])
        grads = two_heads(dctx[:, cols])
        grad_probs = right_dot(grads, val[:, cols])
        delta = jnp.sum(probs * grad_probs, axis=-1, keepdims=True)
        grad_scores = (probs * (grad_probs - delta)).astype(BF)
        dv[:, cols] = left_dot(probs.astype(BF), grads).astype(BF)
        dk[:, cols] = left_dot(grad_scores, queries).astype(BF)
        dq[:, cols] = (one_block(plain_dot(grad_scores, keys)) * HEAD_DIM**-0.5).astype(BF)

    def dx_core(g):
        return remote(gel.at[:, pl.ds(g * 1024, 1024)], dx_r.at[g], ds.at[g], dr.at[g], sib)

    dx_far = remote(dx_s, dx_y, ds.at[2], dr.at[2], xn)

    def input_rows(n):
        who = x * (n % 2) + (1 - x) * (1 - n % 2)
        core = (1 - k) * (1 - n // 2) + k * (n // 2)
        rows = rows_of(who * 512 + core * 256, 256)
        terms_here = right_dot(dk[rows], w_b[1]) + right_dot(dv[rows], w_b[2])

        @pl.when(n == 0)
        def _():
            gel[:, pl.ds(1024, 1024)] = terms_here.astype(BF)
            dx_core(1).start()

        @pl.when(n == 1)
        def _():
            gel[:, pl.ds(0, 1024)] = terms_here.astype(BF)
            dx_core(0).start()

        @pl.when(n == 2)
        def _():
            pltpu.make_async_copy(dx_r.at[1], dx_r.at[1], dr.at[1]).wait()
            dx_s[...] = (terms_here + dx_r[1].astype(F32)).astype(BF)
            dx_far.start()

        @pl.when(n == 3)
        def _():
            pltpu.make_async_copy(dx_r.at[0], dx_r.at[0], dr.at[0]).wait()
            loaded_w(3)
            ga[...] = ga[...] + terms_here + dx_r[0].astype(F32) + right_dot(dq[...], w_b[3])

    greet(z, x, y, k)
    start_blocks((0, 1))
    vec_copies[0].start()
    vec_copies[1].start()
    relay(0)
    relay(1)
    for block in range(2):
        arrive_block(block, (0, 1))
        group_start(0, block)
        group_start(1, block)
    pltpu.make_async_copy(vec_in, vec_in, f_recv.at[0]).wait()
    vec_copies[2].start()
    start_blocks((2,))
    relay(2)
    group_arrive(1, 0)
    group_start(2, 0)
    relay(3)
    group_arrive(1, 1)
    group_start(2, 1)
    load_item(0)
    fill_rows()
    for step in (0, 2):
        for block in range(2):
            group_arrive(step, block)
    fill_bias()
    relay(4)
    project_own(item(0))
    load_item(1)
    relay(5)
    project_all(item(1), key, 0.0)
    load_item(2)
    relay(6)
    project_all(item(2), val, row8[1:2])
    load_item(3)
    relay(7)
    heads(0, 3)
    relay(8)
    heads(3, 6)
    relay(9)
    heads(6, 8)
    relay(10)
    attention_out(item(3))
    load_item(4)
    for j in range(4):
        relay(11 + j)
        expand(j, item(4 + j))
        load_item(5 + j)
    relay(15)
    for j in range(1, 4):
        load_item(8 + j)
    for j in range(4):
        contract(j, item(8 + j))
    for slot in range(2):
        arrive_block(slot, (2,))
    for j in range(2):
        load_c(j)
        load_e(j)
    for n in range(4):
        load_w(n)
    second_norm()
    start_back(0)

    def tick(t, carry):
        def at(stage):
            i = t - LAG[stage]
            return i, (i >= 0) & (i < CHUNKS)

        stage_zero(t)
        @pl.when(t < 4)
        def _():
            def one(n, c):
                feed_forward(2 * t + n)
                return c

            lax.fori_loop(0, 2, one, 0)

        @pl.when(t == 4)
        def _():
            first_norm()

        @pl.when((t >= 5) & (t < 13))
        def _():
            attention(t - 5)

        @pl.when(t == 13)
        def _():
            keep(0, column(dq[...]))
            keep(1, column(dv[...]))
            loaded_w(1)
            loaded_w(2)

        @pl.when((t >= 13) & (t < 17))
        def _():
            input_rows(t - 13)

        for stage in range(6):

            @pl.when(t == 14 + 2 * stage)
            def _():
                v_step(stage)

        @pl.when(t == 18)
        def _():
            pltpu.make_async_copy(dx_y, dx_y, dr.at[2]).wait()
            dx_b[...] = (ga[...] + dx_y[...].astype(F32)).astype(BF)
            start_back(1)

        i1, live1 = at(1)

        @pl.when(live1)
        def _():
            slot, land = i1 % SLOTS, i1 % LAND_D
            clear(1, i1)
            landed(0, i1, r_d.at[i1 % LAND_D])
            for plane in range(2):
                b_y[slot, plane] = add(l_d[slot, plane], r_d[land, plane])
            launch(1, i1)

        i2, live2 = at(2)

        @pl.when(live2)
        def _():
            slot, land = i2 % SLOTS, i2 % LAND
            clear(2, i2)
            landed(1, i2, r_y.at[land])
            b_x[slot] = add(b_y[slot, y], r_y[land])
            launch(2, i2)

        i3, live3 = at(3)

        @pl.when(live3)
        def _():
            slot, land = i3 % SLOTS, i3 % LAND
            clear(3, i3)
            landed(2, i3, r_x.at[land])
            first = order(i3)[0][0]
            b_1[slot] = add(b_x[slot, rows_of(first * 64, 64)], r_x[land])
            launch(3, i3)

        i4, live4 = at(4)

        @pl.when(live4)
        def _():
            slot, land = i4 % SLOTS, i4 % LAND
            clear(4, i4)
            landed(3, i4, r_1.at[land])
            second = order(i4)[0][1]
            b_2[slot] = add(b_1[slot, rows_of(second * 32, 32)], r_1[land])
            launch(4, i4)

        i5, live5 = at(5)

        @pl.when(live5)
        def _():
            slot, land = i5 % SLOTS, i5 % LAND
            clear(5, i5)
            landed(4, i5, r_2.at[land])
            first, second, third = order(i5)[0]
            o_b[i5 % ROOM, rows_of(first * 64 + second * 32 + third * 16, 16)] = add(
                b_2[slot, rows_of(third * 16, 16)], r_2[land]
            )
            launch(5, i5)

        i6, live6 = at(6)

        @pl.when(live6)
        def _():
            clear(6, i6)
            first, second, third = order(i6)[0]
            row = first * 64 + second * 32 + (1 - third) * 16
            landed(5, i6, o_b.at[i6 % ROOM, rows_of(row, 16)])
            launch(6, i6)

        i7, live7 = at(7)

        @pl.when(live7)
        def _():
            clear(7, i7)
            first, second, _ = order(i7)[0]
            landed(6, i7, o_b.at[i7 % ROOM, rows_of(first * 64 + (1 - second) * 32, 32)])
            launch(7, i7)

        i8, live8 = at(8)

        @pl.when(live8)
        def _():
            first = order(i8)[0][0]
            landed(7, i8, o_b.at[i8 % ROOM, rows_of((1 - first) * 64, 64)])
            store(i8)

        return carry

    lax.fori_loop(0, CHUNKS + LAG[8], tick, 0)
    stored()
    for stage in range(8):
        for i in range(CHUNKS - SLOTS, CHUNKS):
            copies(stage, i).wait_send()
    for stage in range(5):
        v_copy(stage).wait_send()
    dx_core(0).wait_send()
    dx_core(1).wait_send()
    dx_far.wait_send()
    finish_back(0)
    finish_back(1)
    for i in range(n_items):
        for kind in range(8):
            if kind not in (3, 5) or split(i)[kind // 2]:
                send_copy(i, kind).wait_send()
    finish_blocks((0, 1, 2))
    for step in range(3):
        for block in range(2):
            for move in group_copy(step, block):
                move.wait_send()
    for move in vec_copies:
        move.wait_send()


def layer_call(inp, cot, seg, weights, vectors):
    vmem = pl.BlockSpec(memory_space=pltpu.VMEM)
    any_spec = pl.BlockSpec(memory_space=pl.ANY)
    dma = pltpu.SemaphoreType.DMA
    grad = jax.ShapeDtypeStruct((256, 1024), BF)
    square = jax.ShapeDtypeStruct((1024, 1024), BF)
    full_weights = [square] * 4 + [
        jax.ShapeDtypeStruct((1024, 4096), BF), jax.ShapeDtypeStruct((4096, 1024), BF)
    ]
    return pl.pallas_call(
        layer_kernel,
        out_shape=full_weights + [
            grad, grad, grad, grad,
            jax.ShapeDtypeStruct((256, 4096), BF),
            jax.ShapeDtypeStruct((1024, 1024), BF),
            jax.ShapeDtypeStruct((2, 1, 128, 1024), BF),
            jax.ShapeDtypeStruct((2, 1, 128, 1024), BF),
            jax.ShapeDtypeStruct((24, 128), F32),
        ],
        in_specs=[any_spec] * 9 + [vmem] * 9,
        out_specs=[any_spec] * 14 + [vmem],
        scratch_shapes=[
            pltpu.VMEM((SLOTS, 2, 128, 1024), BF),
            pltpu.VMEM((SLOTS, 2, 128, 1024), BF),
            pltpu.VMEM((LAND_D, 2, 128, 1024), BF),
            pltpu.VMEM((SLOTS, 2, 128, 1024), BF),
            pltpu.VMEM((LAND, 128, 1024), BF),
            pltpu.VMEM((SLOTS, 128, 1024), BF),
            pltpu.VMEM((LAND, 64, 1024), BF),
            pltpu.VMEM((SLOTS, 64, 1024), BF),
            pltpu.VMEM((LAND, 32, 1024), BF),
            pltpu.VMEM((SLOTS, 32, 1024), BF),
            pltpu.VMEM((LAND, 16, 1024), BF),
            pltpu.VMEM((ROOM, 128, 1024), BF),
            pltpu.VMEM((256, 4096), BF),
            pltpu.VMEM((256, 1024), F32),
            pltpu.VMEM((256, 1024), F32),
            pltpu.VMEM((256, 1024), BF),
            pltpu.VMEM((256, 1024), BF),
            pltpu.VMEM((256, 1024), BF),
            pltpu.VMEM((1024, 1024), BF),
            pltpu.VMEM((1024, 1024), BF),
            pltpu.VMEM((256, 1024), F32),
            pltpu.VMEM((2, 1024, 512), BF),
            pltpu.VMEM((2, 512, 1024), BF),
            pltpu.VMEM((4, 1024, 1024), BF),
            pltpu.VMEM((2, 256, 1024), BF),
            pltpu.VMEM((256, 1024), BF),
            pltpu.VMEM((4, 24, 128), F32),
            pltpu.VMEM((4, 2, 24, 128), F32),
            pltpu.VMEM((3, 2, 24, 128), F32),
            pltpu.VMEM((4, 24, 128), F32),
            pltpu.VMEM((256, 4096), BF),
            pltpu.VMEM((256, 1024), BF),
            pltpu.VMEM((256, 1024), BF),
            pltpu.VMEM((256, 4096), BF),
            pltpu.VMEM((256, 1024), F32),
            pltpu.VMEM((256, 1), F32),
            pltpu.VMEM((256, 1024), BF),
            pltpu.VMEM((256, 1024), BF),
            pltpu.VMEM((1024, 1024), BF),
            pltpu.VMEM((1024, 1024), BF),
            pltpu.VMEM((1024, 1024), BF),
            pltpu.VMEM((256, 1024), BF),
            pltpu.VMEM((8, 1, 128), jnp.int32),
            pltpu.VMEM((24, 128), F32),
            pltpu.VMEM((4, 24, 128), F32),
            pltpu.VMEM((8, 1024), F32),
            pltpu.VMEM((1, 4096), F32),
            dma((8, SLOTS)), dma((8, LAND)), dma((3,)), dma((3,)), dma((2, 2)), dma((2, 2)),
            dma((5,)), dma((5,)), dma((8,)), dma(()),
            dma((3, 2)), dma((3, 2)), dma((2, 3, 2)), dma((2, 3, 2)),
            dma((8, 12)), dma((8, 12)), dma((3,)), dma((3,)),
        ],
        compiler_params=pltpu.CompilerParams(
            collective_id=0, has_side_effects=True, vmem_limit_bytes=61 << 20
        ),
        name="layer",
    )(inp, cot, seg, *weights, *vectors)


def widen_kernel(*refs):
    ins, outs = refs[:9], refs[9:]
    for src, dst in zip(ins[:8], outs[:8]):
        dst[...] = src[...].astype(dst.dtype)
    vec, smalls = ins[8], outs[8:]

    @pl.when(pl.program_id(0) == 0)
    def _():
        for i in range(8):
            for half in range(2):
                smalls[i][pl.ds(half * 128, 128)] = vec[2 * i + half]
        for n in range(8):
            smalls[8][pl.ds(n * 128, 128)] = vec[16 + n]


def widen(narrow, vec):
    steps = 2
    in_specs, out_specs, shapes = [], [], []
    for n, v in enumerate(narrow):
        at = v.ndim - 2
        block = v.shape[:at] + (v.shape[at] // steps,) + v.shape[at + 1 :]

        def place(i, at=at, rank=v.ndim):
            return tuple(i if d == at else 0 for d in range(rank))

        in_specs.append(pl.BlockSpec(block, place))
        out_specs.append(pl.BlockSpec(block, place))
        shapes.append(jax.ShapeDtypeStruct(v.shape, BF if n == 7 else F32))
    in_specs.append(pl.BlockSpec((24, 128), lambda i: (0, 0)))
    for size in (256,) * 8 + (1024,):
        out_specs.append(pl.BlockSpec((size,), lambda i: (0,)))
        shapes.append(jax.ShapeDtypeStruct((size,), F32))
    return pl.pallas_call(
        widen_kernel,
        grid=(steps,),
        out_shape=shapes,
        in_specs=in_specs,
        out_specs=out_specs,
        compiler_params=pltpu.CompilerParams(vmem_limit_bytes=61 << 20),
        name="widen",
    )(*narrow, vec)


def per_group_device(
    layer_input, segments, cotangent,
    query_weight, key_weight, value_weight, output_weight, expand_weight, contract_weight,
    query_bias, value_bias, output_bias, first_gain, first_shift, expand_bias, contract_bias,
    second_gain, second_shift,
):
    outs = layer_call(
        layer_input, cotangent, segments,
        (query_weight, key_weight, value_weight, output_weight, expand_weight, contract_weight),
        (
            query_bias, value_bias, output_bias, first_gain, first_shift, contract_bias,
            second_gain, second_shift, expand_bias,
        ),
    )
    o_q, o_k, o_v, o_o, o_e, o_c, resf, dxf, vec = outs[6:]
    wide = widen((o_q, o_k, o_v, o_o, o_e, o_c, dxf, resf), vec)
    g_q, g_k, g_v, g_o, g_e, g_c, input_grad, layer_output = wide[:8]
    b_q, b_v, b_o, g_one, s_one, b_c, g_two, s_two, b_e = wide[8:]
    return (
        layer_output, input_grad, g_q, g_k, g_v, g_o, g_e, g_c,
        b_q, b_v, b_o, g_one, s_one, b_e, b_c, g_two, s_two,
    )


def solution(mesh):
    in_specs = (
        P(None, "fsdp", "ctx", None),
        P(None, "fsdp", "ctx"),
        P(None, "fsdp", "ctx", None),
        P("fsdp", None),
        P("fsdp", None),
        P("fsdp", None),
        P("fsdp", None),
        P("fsdp", None),
        P("fsdp", None),
        P("fsdp"),
        P("fsdp"),
        P("fsdp"),
        P("fsdp"),
        P("fsdp"),
        P("fsdp"),
        P("fsdp"),
        P("fsdp"),
        P("fsdp"),
    )
    out_specs = (
        P(None, "fsdp", "ctx", None),
        P(None, "fsdp", "ctx", None),
        P("fsdp", None),
        P("fsdp", None),
        P("fsdp", None),
        P("fsdp", None),
        P("fsdp", None),
        P("fsdp", None),
        P("fsdp"),
        P("fsdp"),
        P("fsdp"),
        P("fsdp"),
        P("fsdp"),
        P("fsdp"),
        P("fsdp"),
        P("fsdp"),
        P("fsdp"),
    )
    def whole(layer_input, segments, *rest):
        grouped = (
            dict(mesh.shape) == {"ctx": 8, "fsdp": 4}
            and layer_input.shape == (2, 4, 1024, 1024)
            and rest[5].shape == (1024, 4096)
        )
        body = per_group_device if grouped else per_device
        return jax.shard_map(
            body, mesh=mesh, in_specs=in_specs, out_specs=out_specs, check_vma=False
        )(layer_input, segments, *rest)

    return whole
```

```python
import math

import jax
import jax.numpy as jnp
from jax import lax
from jax.experimental import pallas as pl
from jax.experimental.pallas import tpu as pltpu
from jax.sharding import PartitionSpec as P

HEADS = 16
HEAD_DIM = 64


def as_sent(x):
    return jax.tree.map(lambda a: a.astype(jnp.bfloat16) if a.dtype == jnp.float32 else a, x)


def plain_dot(left_side, right_side):
    return jnp.dot(left_side, right_side, preferred_element_type=jnp.float32)


def left_dot(left_side, right_side):
    return lax.dot_general(
        left_side, right_side, (((0,), (0,)), ((), ())), preferred_element_type=jnp.float32
    )


def right_dot(left_side, right_side):
    return lax.dot_general(
        left_side, right_side, (((1,), (1,)), ((), ())), preferred_element_type=jnp.float32
    )


def norm_forward(hidden, gain_row, offset_row):
    centre = hidden - jnp.mean(hidden, axis=-1, keepdims=True)
    inverse = lax.rsqrt(jnp.mean(centre * centre, axis=-1, keepdims=True) + 1e-05)
    normed = centre * inverse
    return (normed * gain_row.astype(jnp.float32) + offset_row.astype(jnp.float32), normed, inverse)


def norm_backward(grad_out, normed, inverse, gain_row):
    scaled = grad_out * gain_row.astype(jnp.float32)
    grad_in = inverse * (
        scaled
        - jnp.mean(scaled, axis=-1, keepdims=True)
        - normed * jnp.mean(scaled * normed, axis=-1, keepdims=True)
    )
    return (grad_in, jnp.sum(grad_out * normed, axis=0), jnp.sum(grad_out, axis=0))


def gather_weights(shards):
    return (
        lax.all_gather(shards[0], "fsdp", axis=0, tiled=True),
        lax.all_gather(shards[1], "fsdp", axis=0, tiled=True),
        lax.all_gather(shards[2], "fsdp", axis=0, tiled=True),
        lax.all_gather(shards[3], "fsdp", axis=0, tiled=True),
        lax.all_gather(shards[4], "fsdp", axis=0, tiled=True),
        lax.all_gather(shards[5], "fsdp", axis=0, tiled=True),
        lax.all_gather(shards[6], "fsdp", axis=0, tiled=True),
        lax.all_gather(shards[7], "fsdp", axis=0, tiled=True),
        lax.all_gather(shards[8], "fsdp", axis=0, tiled=True),
        lax.all_gather(shards[9], "fsdp", axis=0, tiled=True),
        lax.all_gather(shards[10], "fsdp", axis=0, tiled=True),
        lax.all_gather(shards[11], "fsdp", axis=0, tiled=True),
        lax.all_gather(shards[12], "fsdp", axis=0, tiled=True),
        lax.all_gather(shards[13], "fsdp", axis=0, tiled=True),
        lax.all_gather(shards[14], "fsdp", axis=0, tiled=True),
    )


def attend_forward(query_bf, key_bf, value_bf, seg_local):
    row_count = query_bf.shape[0]
    score_scale = HEAD_DIM ** (-0.5)
    query_heads = query_bf.reshape(row_count, HEADS, HEAD_DIM)
    run_max = jnp.full((HEADS, row_count), -1e30, jnp.float32)
    key_rows = lax.all_gather(key_bf, "ctx", axis=0, tiled=True)
    value_rows = lax.all_gather(value_bf, "ctx", axis=0, tiled=True)
    key_seg = lax.all_gather(seg_local, "ctx", axis=0, tiled=True)
    piece_rows = key_rows.shape[0]
    key_heads = key_rows.reshape(piece_rows, HEADS, HEAD_DIM)
    value_heads = value_rows.reshape(piece_rows, HEADS, HEAD_DIM)
    scores = (
        jnp.einsum("rhd,khd->hrk", query_heads, key_heads, preferred_element_type=jnp.float32)
        * score_scale
    )
    same_doc = seg_local[:, None] == key_seg[None, :]
    scores = jnp.where(same_doc[None], scores, -1e30)
    new_max = jnp.maximum(run_max, jnp.max(scores, axis=-1))
    numerators = jnp.exp(scores - new_max[..., None])
    run_sum = jnp.sum(numerators, axis=-1)
    accumulated = jnp.einsum(
        "hrk,khd->hrd",
        numerators.astype(jnp.bfloat16),
        value_heads,
        preferred_element_type=jnp.float32,
    )
    run_max, run_sum, accumulated = (new_max, run_sum, accumulated)
    context = jnp.transpose(accumulated / run_sum[..., None], (1, 0, 2)).reshape(
        row_count, HEADS * HEAD_DIM
    )
    return (context, run_max + jnp.log(run_sum))


def block_grads(
    query_heads, grad_heads, query_seg, log_sum, row_delta, key_heads, value_heads, key_seg
):
    score_scale = HEAD_DIM ** (-0.5)
    scores = (
        jnp.einsum("rhd,khd->hrk", query_heads, key_heads, preferred_element_type=jnp.float32)
        * score_scale
    )
    same_doc = query_seg[:, None] == key_seg[None, :]
    scores = jnp.where(same_doc[None], scores, -1e30)
    probs_full = jnp.exp(scores - log_sum[..., None])
    grad_probs = jnp.einsum(
        "rhd,khd->hrk", grad_heads, value_heads, preferred_element_type=jnp.float32
    )
    grad_scores = (probs_full * (grad_probs - row_delta[..., None])).astype(jnp.bfloat16)
    return (probs_full, grad_scores)


def attend_backward(query_bf, key_bf, value_bf, seg_local, context, log_sum, grad_context):
    row_count = query_bf.shape[0]
    score_scale = HEAD_DIM ** (-0.5)
    key_every, value_every, seg_every = (
        lax.all_gather(key_bf, "ctx", axis=0, tiled=True),
        lax.all_gather(value_bf, "ctx", axis=0, tiled=True),
        lax.all_gather(seg_local, "ctx", axis=0, tiled=True),
    )
    length = key_every.shape[0]
    block_len = min(512, length)
    query_heads = query_bf.reshape(row_count, HEADS, HEAD_DIM)
    grad_heads = grad_context.reshape(row_count, HEADS, HEAD_DIM)
    row_delta = jnp.sum(
        (grad_context.astype(jnp.float32) * context).reshape(row_count, HEADS, HEAD_DIM), axis=-1
    ).T

    def visit_block(grad_query, block_num):
        first_row = block_num * block_len
        key_heads = lax.dynamic_slice_in_dim(key_every, first_row, block_len, 0).reshape(
            block_len, HEADS, HEAD_DIM
        )
        value_heads = lax.dynamic_slice_in_dim(value_every, first_row, block_len, 0).reshape(
            block_len, HEADS, HEAD_DIM
        )
        key_seg = lax.dynamic_slice_in_dim(seg_every, first_row, block_len, 0)
        probs_full, grad_scores = block_grads(
            query_heads, grad_heads, seg_local, log_sum, row_delta, key_heads, value_heads, key_seg
        )
        grad_query = (
            grad_query
            + jnp.einsum("hrk,khd->rhd", grad_scores, key_heads, preferred_element_type=jnp.float32)
            * score_scale
        )
        grad_keys = (
            jnp.einsum("hrk,rhd->khd", grad_scores, query_heads, preferred_element_type=jnp.float32)
            * score_scale
        )
        grad_values = jnp.einsum(
            "hrk,rhd->khd",
            probs_full.astype(jnp.bfloat16),
            grad_heads,
            preferred_element_type=jnp.float32,
        )
        stacked = jnp.stack(
            (
                grad_keys.reshape(block_len, HEADS * HEAD_DIM),
                grad_values.reshape(block_len, HEADS * HEAD_DIM),
            ),
            axis=1,
        )
        return (grad_query, stacked)

    grad_query, pieces = lax.scan(
        visit_block,
        jnp.zeros((row_count, HEADS, HEAD_DIM), jnp.float32),
        jnp.arange(length // block_len),
    )
    key_terms = pieces.reshape(length, 2, HEADS * HEAD_DIM)
    own_rows = lax.psum_scatter(
        key_terms.astype(jnp.bfloat16), "ctx", scatter_dimension=0, tiled=True
    ).astype(jnp.float32)
    grad_keyed = own_rows[:, 0].astype(jnp.bfloat16)
    grad_valued = own_rows[:, 1].astype(jnp.bfloat16)
    grad_queries = grad_query.reshape(row_count, HEADS * HEAD_DIM).astype(jnp.bfloat16)
    return (grad_queries, grad_keyed, grad_valued)


def layer_forward(inputs, seg_local, full_weights):
    (
        query_weight,
        key_weight,
        value_weight,
        output_weight,
        expand_weight,
        contract_weight,
        query_bias,
        value_bias,
        output_bias,
        first_gain,
        first_shift,
        expand_bias,
        contract_bias,
        second_gain,
        second_shift,
    ) = full_weights
    query_bf = (plain_dot(inputs, query_weight) + query_bias.astype(jnp.float32)).astype(
        jnp.bfloat16
    )
    key_bf = plain_dot(inputs, key_weight).astype(jnp.bfloat16)
    value_bf = (plain_dot(inputs, value_weight) + value_bias.astype(jnp.float32)).astype(
        jnp.bfloat16
    )
    context, log_sum = attend_forward(query_bf, key_bf, value_bf, seg_local)
    context_bf = context.astype(jnp.bfloat16)
    first_sum = (
        inputs.astype(jnp.float32)
        + plain_dot(context_bf, output_weight)
        + output_bias.astype(jnp.float32)
    )
    first_out, normed_one, inverse_one = norm_forward(first_sum, first_gain, first_shift)
    first_bf = first_out.astype(jnp.bfloat16)
    hidden = plain_dot(first_bf, expand_weight) + expand_bias.astype(jnp.float32)
    gelled_bf = jax.nn.gelu(hidden, approximate=False).astype(jnp.bfloat16)
    second_sum = (
        first_out + plain_dot(gelled_bf, contract_weight) + contract_bias.astype(jnp.float32)
    )
    result, normed_two, inverse_two = norm_forward(second_sum, second_gain, second_shift)
    kept_state = (
        query_bf,
        key_bf,
        value_bf,
        context,
        log_sum,
        context_bf,
        normed_one,
        inverse_one,
        first_bf,
        hidden,
        gelled_bf,
        normed_two,
        inverse_two,
    )
    return (result.astype(jnp.bfloat16), kept_state)


def layer_backward(inputs, seg_local, grad_out, kept_state, full_weights):
    (
        query_weight,
        key_weight,
        value_weight,
        output_weight,
        expand_weight,
        contract_weight,
        query_bias,
        value_bias,
        output_bias,
        first_gain,
        first_shift,
        expand_bias,
        contract_bias,
        second_gain,
        second_shift,
    ) = full_weights
    (
        query_bf,
        key_bf,
        value_bf,
        context,
        log_sum,
        context_bf,
        normed_one,
        inverse_one,
        first_bf,
        hidden,
        gelled_bf,
        normed_two,
        inverse_two,
    ) = kept_state
    grad_second, second_gain_grad, second_shift_grad = norm_backward(
        grad_out.astype(jnp.float32), normed_two, inverse_two, second_gain
    )
    grad_branch = grad_second.astype(jnp.bfloat16)
    contract_weight_grad = left_dot(gelled_bf, grad_branch)
    contract_bias_grad = jnp.sum(grad_branch.astype(jnp.float32), axis=0)
    grad_gelled = right_dot(grad_branch, contract_weight)
    gelu_pull = jax.vjp(lambda values: jax.nn.gelu(values, approximate=False), hidden)[1]
    grad_hidden = gelu_pull(grad_gelled)[0].astype(jnp.bfloat16)
    expand_weight_grad = left_dot(first_bf, grad_hidden)
    expand_bias_grad = jnp.sum(grad_hidden.astype(jnp.float32), axis=0)
    grad_first = grad_second + right_dot(grad_hidden, expand_weight)
    grad_attn, first_gain_grad, first_shift_grad = norm_backward(
        grad_first, normed_one, inverse_one, first_gain
    )
    grad_attn_low = grad_attn.astype(jnp.bfloat16)
    output_weight_grad = left_dot(context_bf, grad_attn_low)
    output_bias_grad = jnp.sum(grad_attn_low.astype(jnp.float32), axis=0)
    grad_context = right_dot(grad_attn_low, output_weight).astype(jnp.bfloat16)
    grad_queries, grad_keyed, grad_valued = attend_backward(
        query_bf, key_bf, value_bf, seg_local, context, log_sum, grad_context
    )
    query_weight_grad = left_dot(inputs, grad_queries)
    key_weight_grad = left_dot(inputs, grad_keyed)
    value_weight_grad = left_dot(inputs, grad_valued)
    query_bias_grad = jnp.sum(grad_queries.astype(jnp.float32), axis=0)
    value_bias_grad = jnp.sum(grad_valued.astype(jnp.float32), axis=0)
    grad_input = (
        grad_attn
        + right_dot(grad_queries, query_weight)
        + right_dot(grad_keyed, key_weight)
        + right_dot(grad_valued, value_weight)
    )
    grad_terms = (
        query_weight_grad,
        key_weight_grad,
        value_weight_grad,
        output_weight_grad,
        expand_weight_grad,
        contract_weight_grad,
        query_bias_grad,
        value_bias_grad,
        output_bias_grad,
        first_gain_grad,
        first_shift_grad,
        expand_bias_grad,
        contract_bias_grad,
        second_gain_grad,
        second_shift_grad,
    )
    return (grad_input, grad_terms)


def per_device(
    layer_input,
    segments,
    cotangent,
    query_weight,
    key_weight,
    value_weight,
    output_weight,
    expand_weight,
    contract_weight,
    query_bias,
    value_bias,
    output_bias,
    first_gain,
    first_shift,
    expand_bias,
    contract_bias,
    second_gain,
    second_shift,
):
    shards = (
        query_weight,
        key_weight,
        value_weight,
        output_weight,
        expand_weight,
        contract_weight,
        query_bias,
        value_bias,
        output_bias,
        first_gain,
        first_shift,
        expand_bias,
        contract_bias,
        second_gain,
        second_shift,
    )
    micro_count = layer_input.shape[0]
    results = []
    grad_inputs = []
    totals = None
    for micro_step in range(micro_count):
        inputs = layer_input[micro_step, 0]
        seg_local = segments[micro_step, 0].astype(jnp.bfloat16)
        front_weights = gather_weights(shards)
        result, kept_state = layer_forward(inputs, seg_local, front_weights)
        behind = gather_weights(shards)
        grad_input, grad_terms = layer_backward(
            inputs, seg_local, cotangent[micro_step, 0], kept_state, behind
        )
        results.append(result)
        grad_inputs.append(grad_input)
        if totals is None:
            totals = grad_terms
        else:
            totals = tuple(
                (left_side + right_side for left_side, right_side in zip(totals, grad_terms))
            )
    reduced = jax.tree.map(
        lambda part: part.astype(jnp.float32),
        lax.psum_scatter(as_sent(totals), "fsdp", scatter_dimension=0, tiled=True),
    )
    summed = jax.tree.map(lambda part: part.astype(jnp.float32), lax.psum(as_sent(reduced), "ctx"))
    layer_output = jnp.stack(results, axis=0)[:, None]
    input_grad = jnp.stack(grad_inputs, axis=0)[:, None]
    return (
        layer_output,
        input_grad,
        summed[0],
        summed[1],
        summed[2],
        summed[3],
        summed[4],
        summed[5],
        summed[6],
        summed[7],
        summed[8],
        summed[9],
        summed[10],
        summed[11],
        summed[12],
        summed[13],
        summed[14],
    )


MESH = pl.DeviceIdType.MESH
BF = jnp.bfloat16
F32 = jnp.float32
CHUNKS = 24
SLOTS = 3
LAND = 6
LAND_D = 4
ROOM = 10
LAG = (0, 0, 2, 4, 5, 6, 7, 8, 10)
Z_FROM, Z_TO = 12, 14
SPLIT = ((64, 0, 0), (40, 24, 0))
EARLY, LATE = 4, 9


def coords():
    c, f = lax.axis_index("ctx"), lax.axis_index("fsdp")
    return c // 2, c % 2, f // 2, f % 2


def dev(z, x, y, k):
    return (z * 2 + x, y * 2 + k)


def greet(z, x, y, k):
    barrier = pltpu.get_barrier_semaphore()
    for step in range(1, 8):
        place = (z * 2 + k + step) % 8
        pl.semaphore_signal(
            barrier, inc=1, device_id=dev(place // 2, x, y, place % 2), device_id_type=MESH
        )
    pl.semaphore_signal(barrier, inc=1, device_id=dev(z, 1 - x, y, k), device_id_type=MESH)
    pl.semaphore_signal(barrier, inc=1, device_id=dev(z, x, 1 - y, k), device_id_type=MESH)
    pl.semaphore_wait(barrier, 9)


def remote(src, dst, send, recv, to):
    return pltpu.make_async_remote_copy(
        src_ref=src, dst_ref=dst, send_sem=send, recv_sem=recv, device_id=to, device_id_type=MESH
    )


def rows_of(start, size, unit=16):
    return pl.ds(pl.multiple_of(start, unit), size)


def two_heads(block):
    lane = lax.broadcasted_iota(jnp.int32, block.shape, 1)
    zero = jnp.zeros_like(block)
    return jnp.concatenate(
        [jnp.where(lane < HEAD_DIM, block, zero), jnp.where(lane >= HEAD_DIM, block, zero)], axis=0
    )


def one_block(pair):
    rows = pair.shape[0] // 2
    lane = lax.broadcasted_iota(jnp.int32, (rows, pair.shape[1]), 1)
    return jnp.where(lane < HEAD_DIM, pair[:rows], pair[rows:])


def softmax_pair(queries, keys, bias):
    scores = right_dot(queries, keys)
    scores = scores + jnp.concatenate([bias, bias], axis=0)
    numer = jnp.exp(scores - jnp.max(scores, axis=-1, keepdims=True))
    return numer * (1.0 / jnp.sum(numer, axis=-1, keepdims=True))


def layer_kernel(
    inp, cot, seg, wq, wk, wv, wo, we, wc, *rest,
):
    (
        vecs, (fq, fk, fv, fo, fe, fc), (o_q, o_k, o_v, o_o, o_e, o_c), (resf, dxf, vec_out), rest
    ) = (rest[:9], rest[9:15], rest[15:21], rest[21:24], rest[24:])
    (
        s_d, l_d, r_d, b_y, r_y, b_x, r_x, b_1, r_1, b_2, r_2, o_b,
        gh, acc, ga, gal, dctx, dq, dk, dv, bias, we_b, wc_b, w_b,
        dx_r, dx_y, vec, v_s, v_d, v_r,
        gel, gb, fb, gp, n1, inv1, ctx, q, key, val, xf, res, segf, vec_in, vecf, row8, row_e,
        ss, rs, ds, dr, a_send, a_recv, v_send, v_recv, w_sem, o_sem,
        i_send, i_recv, g_send, g_recv, p_send, p_recv, f_send, f_recv,
    ) = rest
    dx_b, dx_s = dctx, gb
    cotf = gh.at[:, pl.ds(0, 1024)]
    z, x, y, k = coords()
    f = y * 2 + k
    other = (1 - y) * 2 + k
    sib, xn, yn = dev(z, x, y, 1 - k), dev(z, 1 - x, y, k), dev(z, x, 1 - y, k)
    bit1, bit2 = z % 2, z // 2
    z1 = dev(z + 1 - 2 * bit1, x, y, k)
    z2 = dev((z + 2) % 4, x, y, k)
    color = bit1 * 2 + x
    c_x, c_z, c_o = color + 1 - 2 * x, (color + 2) % 4, 3 - color
    own_rows = rows_of(x * 512 + k * 256, 256)

    def block_moves(mb):
        to_z, to_k = mb * 2 + k, z // 2
        row = x * 512 + z * 128
        slot = z % 2
        mine = (to_z == z) & (to_k == k)
        moves = (
            (inp.at[mb, 0], xf.at[rows_of(row, 128)], 0),
            (seg.at[mb], segf.at[x * 4 + z], 1),
            (cot.at[mb, 0], cotf.at[rows_of(slot * 128, 128)], 2),
        )
        return mine, dev(to_z, x, y, to_k), slot, moves

    def start_blocks(which):
        for mb in range(2):
            mine, to, slot, moves = block_moves(mb)
            for src, dst, n in moves:
                if n not in which:
                    continue

                @pl.when(mine)
                def _():
                    pltpu.make_async_copy(src, dst, i_recv.at[n, slot]).start()

                @pl.when(jnp.logical_not(mine))
                def _():
                    remote(src, dst, i_send.at[n, mb], i_recv.at[n, slot], to).start()

    def finish_blocks(which):
        for mb in range(2):
            mine, to, slot, moves = block_moves(mb)
            for src, dst, n in moves:
                if n not in which:
                    continue

                @pl.when(jnp.logical_not(mine))
                def _():
                    remote(src, dst, i_send.at[n, mb], i_recv.at[n, slot], to).wait_send()

    def arrive_block(slot, which):
        zz = 2 * k + slot
        for n in which:
            if n == 0:
                dst = xf.at[rows_of(x * 512 + zz * 128, 128)]
            elif n == 1:
                dst = segf.at[x * 4 + zz]
            else:
                dst = cotf.at[pl.ds(slot * 128, 128)]
            pltpu.make_async_copy(dst, dst, i_recv.at[n, slot]).wait()

    def group_copy(step, block):
        who = x if step < 2 else 1 - x
        src = xf.at[rows_of(who * 512 + k * 256 + block * 128, 128)]
        sseg = segf.at[who * 4 + k * 2 + block]
        to = (sib, xn, sib)[step]
        return (
            remote(src, src, g_send.at[0, step, block], g_recv.at[0, step, block], to),
            remote(sseg, sseg, g_send.at[1, step, block], g_recv.at[1, step, block], to),
        )

    def group_start(step, block):
        for move in group_copy(step, block):
            move.start()

    def group_arrive(step, block):
        who = (x, 1 - x, 1 - x)[step]
        kk = (1 - k, k, 1 - k)[step]
        src = xf.at[rows_of(who * 512 + kk * 256 + block * 128, 128)]
        sseg = segf.at[who * 4 + kk * 2 + block]
        pltpu.make_async_copy(src, src, g_recv.at[0, step, block]).wait()
        pltpu.make_async_copy(sseg, sseg, g_recv.at[1, step, block]).wait()

    items = []
    for shard, full in ((wq, fq), (wk, fk), (wv, fv), (wo, fo)):
        items.append((shard, full, 0, 0, 256))
    for j in range(4):
        items.append((we, fe, 0, j * 1024, 256))
    for j in range(4):
        items.append((wc, fc, j * 256, 0, 1024))
    n_items = len(items)

    def direct(i):
        return i < EARLY or LATE <= i < n_items

    def split(i):
        return SPLIT[0] if direct(i) else SPLIT[1]

    def part(i, quarter, start, size, own_src=False):
        shard, full, row, col, step = items[i]
        if own_src:
            return shard.at[rows_of(row + start, size, 8), pl.ds(col, 1024)]
        return full.at[rows_of(quarter * step + row + start, size, 8), pl.ds(col, 1024)]

    def send_copy(i, kind):
        sems = (p_send.at[kind, i], p_recv.at[kind, i])
        if kind == 0:
            return remote(part(i, f, color * 64, 64, True), part(i, f, color * 64, 64), *sems, yn)
        if kind == 1:
            rows = split(i)[0]
            return remote(part(i, f, c_o * 64, rows, True), part(i, f, c_o * 64, rows), *sems, yn)
        if kind == 2:
            src = part(i, other, color * 64, 64)
            return remote(src, src, *sems, xn)
        if kind == 3:
            src = part(i, other, c_z * 64 + split(i)[0], split(i)[1])
            return remote(src, src, *sems, xn)
        if kind == 4:
            src = part(i, other, color * 64, 64)
            return remote(src, src, *sems, z1)
        if kind == 5:
            src = part(i, other, c_x * 64 + 64 - split(i)[2], split(i)[2])
            return remote(src, src, *sems, z1)
        if kind == 6:
            return remote(part(i, f, 0, 256, True), part(i, f, 0, 256), *sems, sib)
        src = part(i, other, 0, 256)
        return remote(src, src, *sems, sib)

    def arrive(i, kind):
        if kind == 0:
            dst = part(i, other, color * 64, 64)
        elif kind == 1:
            dst = part(i, other, c_o * 64, split(i)[0])
        elif kind == 2:
            dst = part(i, other, c_x * 64, 64)
        elif kind == 3:
            dst = part(i, other, c_o * 64 + split(i)[0], split(i)[1])
        elif kind == 4:
            dst = part(i, other, c_z * 64, 64)
        elif kind == 5:
            dst = part(i, other, c_o * 64 + 64 - split(i)[2], split(i)[2])
        elif kind == 6:
            dst = part(i, y * 2 + 1 - k, 0, 256)
        else:
            dst = part(i, (1 - y) * 2 + 1 - k, 0, 256)
        pltpu.make_async_copy(dst, dst, p_recv.at[kind, i]).wait()


    for i in range(8):
        packed = vecs[i][...].astype(F32).reshape(1, 256)
        vec_in[pl.ds(2 * i, 1)] = packed[:, :128]
        vec_in[pl.ds(2 * i + 1, 1)] = packed[:, 128:]
    packed = vecs[8][...].astype(F32).reshape(1, 1024)
    for n in range(8):
        vec_in[pl.ds(16 + n, 1)] = packed[:, n * 128 : n * 128 + 128]
    vecf[f] = vec_in[...]
    vec_copies = (
        remote(vec_in, vecf.at[f], f_send.at[0], f_recv.at[0], yn),
        remote(vec_in, vecf.at[f], f_send.at[1], f_recv.at[1], sib),
        remote(vecf.at[other], vecf.at[other], f_send.at[2], f_recv.at[2], sib),
    )

    def load_square(shard, full, row, step, cols, dst, sem):
        out = []
        for d in range(4):
            quarter = (f + d) % 4
            src = shard.at[pl.ds(row, 256), cols]
            if d > 0:
                src = full.at[rows_of(quarter * step + row, 256), cols]
            out.append(pltpu.make_async_copy(src, dst.at[rows_of(quarter * 256, 256)], sem))
        return out

    def load_c(j):
        slot = j % 2
        sem = w_sem.at[slot]

        @pl.when(j // 2 == f)
        def _():
            src = wc.at[rows_of((j % 2) * 512, 512)]
            pltpu.make_async_copy(src, wc_b.at[slot], sem).start()

        @pl.when(j // 2 != f)
        def _():
            pltpu.make_async_copy(fc.at[rows_of(j * 512, 512)], wc_b.at[slot], sem).start()

    def load_e(j):
        for move in load_square(
            we, fe, 0, 256, rows_of(j * 512, 512, 512), we_b.at[j % 2], w_sem.at[2 + j % 2]
        ):
            move.start()

    def load_w(n):
        shard, full = ((wo, fo), (wk, fk), (wv, fv), (wq, fq))[n]
        for move in load_square(
            shard, full, 0, 256, pl.ds(0, 1024), w_b.at[n], w_sem.at[4 + n]
        ):
            move.start()

    def loaded_w(n):
        pltpu.make_async_copy(w_b.at[n], w_b.at[n], w_sem.at[4 + n]).wait()

    def load_item(i):
        shard, full, row, col, step = items[i]
        arrive(i, 6)
        arrive(i, 7)
        slot = i % 4
        for move in load_square(
            shard, full, row, step, pl.ds(col, 1024), w_b.at[slot], w_sem.at[4 + slot]
        ):
            move.start()

    def item(i):
        slot = i % 4
        pltpu.make_async_copy(w_b.at[slot], w_b.at[slot], w_sem.at[4 + slot]).wait()
        return w_b.at[slot]

    def relay(t):
        for u in (0, 1, 2) if t == 0 else (t + 2,):
            if u < n_items:
                send_copy(u, 0).start()
                send_copy(u, 1).start()
                send_copy(u, 6).start()
        if 1 <= t <= n_items:
            i = t - 1
            arrive(i, 0)
            send_copy(i, 2).start()
            send_copy(i, 4).start()
        if 0 <= t - 3 < n_items and not direct(t - 3):
            i = t - 3
            arrive(i, 4)
            send_copy(i, 3).start()
            arrive(i, 2)
            if split(i)[2]:
                send_copy(i, 5).start()
        if 0 <= t - 3 and direct(t - 3):
            i = t - 3
            arrive(i, 1)
            arrive(i, 2)
            arrive(i, 4)
            send_copy(i, 7).start()
        if 0 <= t - 6 < n_items and not direct(t - 6):
            i = t - 6
            arrive(i, 1)
            arrive(i, 3)
            if split(i)[2]:
                arrive(i, 5)
            send_copy(i, 7).start()

    def fill_rows():
        pltpu.make_async_copy(vec_in, vec_in, f_recv.at[1]).wait()
        pltpu.make_async_copy(vec_in, vec_in, f_recv.at[2]).wait()
        for quarter in range(4):
            for i in range(8):
                for half in range(2):
                    col = quarter * 256 + half * 128
                    row8[pl.ds(i, 1), col : col + 128] = vecf[quarter, pl.ds(2 * i + half, 1)]
            for n in range(8):
                col = quarter * 1024 + n * 128
                row_e[:, col : col + 128] = vecf[quarter, pl.ds(16 + n, 1)]

    def fill_bias():
        for block in range(2):
            own = segf[x * 4 + k * 2 + block].astype(F32)
            down = jnp.transpose(jnp.broadcast_to(own, (128, 128)))
            for n in range(8):
                across = segf[n].astype(F32)
                bias[block * 128 : block * 128 + 128, n * 128 : n * 128 + 128] = jnp.where(
                    down == across, 0.0, -1e30
                )

    def project_own(w):
        q[...] = (plain_dot(xf[own_rows], w[...]) + row8[0:1]).astype(BF)

    def project_all(w, dst, add_row):
        def block(n, carry):
            rows = rows_of(n * 256, 256)
            dst[rows] = (plain_dot(xf[rows], w[...]) + add_row).astype(BF)
            return carry

        lax.fori_loop(0, 4, block, 0)

    def heads(first, last):
        def one(h, carry):
            cols = rows_of(h * 128, 128, 128)
            queries = two_heads(q[:, cols] * BF(HEAD_DIM**-0.5))
            probs = softmax_pair(queries, key[:, cols], bias[...])
            ctx[:, cols] = one_block(plain_dot(probs.astype(BF), val[:, cols])).astype(BF)
            return carry

        lax.fori_loop(first, last, one, 0)

    def norm(v):
        centre = v - jnp.mean(v, axis=-1, keepdims=True)
        inverse = lax.rsqrt(jnp.mean(centre * centre, axis=-1, keepdims=True) + 1e-05)
        return centre * inverse, inverse

    def attention_out(w):
        normed, inverse = norm(
            xf[own_rows].astype(F32) + plain_dot(ctx[...], w[...]) + row8[2:3]
        )
        n1[...] = normed
        inv1[...] = inverse
        first_out = normed * row8[3:4] + row8[4:5]
        acc[...] = first_out
        fb[...] = first_out.astype(BF)

    def expand(j, w):
        def block(n, carry):
            cols = rows_of(n * 256, 256, 256)
            out = rows_of(j * 1024 + n * 256, 256, 256)
            hidden = plain_dot(fb[...], w[:, cols]) + row_e[:, out]
            below = 0.5 + 0.5 * lax.erf(hidden * 0.5**0.5)
            gel[:, out] = (hidden * below).astype(BF)
            bell = jnp.exp(-0.5 * hidden * hidden) * (2 * math.pi) ** -0.5
            gp[:, out] = (below + hidden * bell).astype(BF)
            return carry

        lax.fori_loop(0, 4, block, 0)

    def contract(j, w):
        for quarter in range(4):
            cols = pl.ds(quarter * 1024 + j * 256, 256)
            acc[...] += plain_dot(gel[:, cols], w[quarter * 256 : quarter * 256 + 256])

    def second_norm():
        normed, inverse = norm(acc[...] + row8[5:6])
        res[...] = (normed * row8[6:7] + row8[7:8]).astype(BF)
        grad_out = cotf[...].astype(F32)
        keep(6, column(grad_out * normed))
        keep(7, column(grad_out))
        scaled = grad_out * row8[6:7]
        grad = inverse * (
            scaled
            - jnp.mean(scaled, axis=-1, keepdims=True)
            - normed * jnp.mean(scaled * normed, axis=-1, keepdims=True)
        )
        acc[...] = grad
        low = grad.astype(BF)
        gb[...] = low
        keep(5, column(low))


    def back(n, slot):
        to_z = 2 * k + slot
        to_k = z % 2
        mb = z // 2
        mine = (to_z == z) & (to_k == k)
        src = (res, dx_b)[n].at[pl.ds(slot * 128, 128)]
        dst = (resf, dxf)[n].at[mb, 0]

        def far():
            return remote(
                src, dst, a_send.at[n, slot], a_recv.at[n, mb], dev(to_z, x, y, to_k)
            )

        def near():
            return pltpu.make_async_copy(src, dst, a_recv.at[n, mb])

        return mine, far, near

    def start_back(n):
        for slot in range(2):
            mine, far, near = back(n, slot)

            @pl.when(mine)
            def _():
                near().start()

            @pl.when(jnp.logical_not(mine))
            def _():
                far().start()

    def finish_back(n):
        for slot in range(2):
            mine, far, _ = back(n, slot)

            @pl.when(jnp.logical_not(mine))
            def _():
                far().wait_send()

        for mb in range(2):
            dst = (resf, dxf)[n].at[mb, 0]
            pltpu.make_async_copy(dst, dst, a_recv.at[n, mb]).wait()

    def column(v):
        return jnp.sum(v.astype(F32), axis=0, keepdims=True)

    def keep(i, row):
        for quarter in range(4):
            for half in range(2):
                col = quarter * 256 + half * 128
                vec[quarter, pl.ds(2 * i + half, 1)] = row[:, col : col + 128]

    v_peers = (sib, yn, xn, z1, z2)

    def v_copy(stage):
        if stage == 0:
            return remote(v_d.at[1], v_d.at[2], v_send.at[0], v_recv.at[0], sib)
        src = v_s.at[0, 1 - y] if stage == 1 else v_s.at[stage - 1, 0]
        return remote(src, v_r.at[stage - 1], v_send.at[stage], v_recv.at[stage], v_peers[stage])

    def v_step(stage):
        if stage == 0:
            for plane in range(2):
                v_d[0, plane] = vec[plane * 2 + k]
                v_d[1, plane] = vec[plane * 2 + 1 - k]
        elif stage == 1:
            pltpu.make_async_copy(v_d.at[2], v_d.at[2], v_recv.at[0]).wait()
            v_s[0] = v_d[0] + v_d[2]
        else:
            dst = v_r.at[stage - 2]
            pltpu.make_async_copy(dst, dst, v_recv.at[stage - 1]).wait()
            mine = v_s[0, y] if stage == 2 else v_s[stage - 2, 0]
            total = mine + v_r[stage - 2]
            if stage == 5:
                vec_out[...] = total
            else:
                v_s[stage - 1, 0] = total
        if stage < 5:
            v_copy(stage).start()

    def send(stage, i, src, dst, to):
        return remote(src, dst, ss.at[stage, i % SLOTS], rs.at[stage, i % LAND], to)

    def landed(stage, i, dst):
        pltpu.make_async_copy(dst, dst, rs.at[stage, i % LAND]).wait()

    def order(i):
        late = (i // Z_FROM) * (1 - i // Z_TO) if Z_FROM < Z_TO else 0
        bits = tuple(
            (1 - late) * p + late * q
            for p, q in ((x, bit1), (bit1, bit2), (bit2, x))
        )
        peers = tuple(
            tuple((1 - late) * p + late * q for p, q in zip(one, two))
            for one, two in ((xn, z1), (z1, z2), (z2, xn))
        )
        return bits, peers

    def copies(stage, i):
        slot, land, room = i % SLOTS, i % LAND, i % ROOM
        (first, second, third), peers = order(i)
        if stage == 0:
            return send(0, i, s_d.at[slot], r_d.at[i % LAND_D], sib)
        if stage == 1:
            return send(1, i, b_y.at[slot, 1 - y], r_y.at[land], yn)
        if stage == 2:
            return send(2, i, b_x.at[slot, rows_of((1 - first) * 64, 64)], r_x.at[land], peers[0])
        if stage == 3:
            return send(3, i, b_1.at[slot, rows_of((1 - second) * 32, 32)], r_1.at[land], peers[1])
        if stage == 4:
            return send(4, i, b_2.at[slot, rows_of((1 - third) * 16, 16)], r_2.at[land], peers[2])
        if stage == 5:
            own = o_b.at[room, rows_of(first * 64 + second * 32 + third * 16, 16)]
            return send(5, i, own, own, peers[2])
        if stage == 6:
            own = o_b.at[room, rows_of(first * 64 + second * 32, 32)]
            return send(6, i, own, own, peers[1])
        own = o_b.at[room, rows_of(first * 64, 64)]
        return send(7, i, own, own, peers[0])

    def launch(stage, i):
        copies(stage, i).start()

    def clear(stage, i):
        @pl.when(i >= SLOTS)
        def _():
            copies(stage, i - SLOTS).wait_send()

    def add(a, b):
        return (a.astype(F32) + b.astype(F32)).astype(BF)

    def terms(i, a_ref, b_ref, a_base, a_step, b_col, a_rows=None):
        slot = i % SLOTS
        right = b_ref[:, b_col]
        for plane in range(2):
            for core in range(2):
                quarter = plane * 2 + (k if core == 0 else 1 - k)
                cols = pl.ds(pl.multiple_of(a_base + quarter * a_step, 128), 128)
                left = a_ref[:, cols] if a_rows is None else a_ref[a_rows, cols]
                product = left_dot(left, right).astype(BF)
                if core == 0:
                    l_d[slot, plane] = product
                else:
                    s_d[slot, plane] = product

    every = pl.ds(0, 1024)

    def stage_zero(i):
        @pl.when((i >= 0) & (i < CHUNKS))
        def _():
            clear(0, i)

        @pl.when(i < 8)
        def _():
            terms(i, gel, gb, i * 128, 1024, every)

        @pl.when((i >= 8) & (i < 16))
        def _():
            j = i - 8
            terms(i, fb, gh, (j % 2) * 128, 256, rows_of((j // 2) * 1024, 1024, 1024))

        @pl.when((i >= 16) & (i < 18))
        def _():
            terms(i, ctx, gal, (i - 16) * 128, 256, every)

        @pl.when((i >= 18) & (i < 20))
        def _():
            terms(i, xf, dq, (i - 18) * 128, 256, every, own_rows)

        @pl.when((i >= 20) & (i < 22))
        def _():
            terms(i, xf, dk, (i - 20) * 128, 256, every)

        @pl.when((i >= 22) & (i < 24))
        def _():
            terms(i, xf, dv, (i - 22) * 128, 256, every)

        @pl.when((i >= 0) & (i < CHUNKS))
        def _():
            launch(0, i)

    def stored():
        pltpu.make_async_copy(o_b.at[0], o_b.at[0], o_sem).wait()

    def store(i):
        src = o_b.at[i % ROOM]

        @pl.when(i >= 1)
        def _():
            stored()

        @pl.when(i < 8)
        def _():
            pltpu.make_async_copy(src, o_c.at[rows_of(i * 128, 128)], o_sem).start()

        @pl.when((i >= 8) & (i < 16))
        def _():
            j = i - 8
            dst = o_e.at[rows_of((j % 2) * 128, 128), rows_of((j // 2) * 1024, 1024, 1024)]
            pltpu.make_async_copy(src, dst, o_sem).start()

        for n, ref in enumerate((o_o, o_q, o_k, o_v)):
            first = 16 + 2 * n

            @pl.when((i >= first) & (i < first + 2))
            def _():
                dst = ref.at[rows_of((i - first) * 128, 128)]
                pltpu.make_async_copy(src, dst, o_sem).start()

    def feed_forward(j):
        slot = j % 2
        cols = rows_of(j * 512, 512, 512)
        pltpu.make_async_copy(wc_b.at[slot], wc_b.at[slot], w_sem.at[slot]).wait()
        pltpu.make_async_copy(we_b.at[slot], we_b.at[slot], w_sem.at[2 + slot]).wait()

        grads = (right_dot(gb[...], wc_b[slot]) * gp[:, cols].astype(F32)).astype(BF)
        gh[:, cols] = grads
        acc[...] += right_dot(grads, we_b[slot])
        row = column(grads)
        for n in range(4):
            vec[j // 2, pl.ds(16 + (j % 2) * 4 + n, 1)] = row[:, n * 128 : n * 128 + 128]

        @pl.when(j < 6)
        def _():
            load_c(j + 2)
            load_e(j + 2)

    def first_norm():
        normed = n1[...]
        grad_first = acc[...]
        keep(3, column(grad_first * normed))
        keep(4, column(grad_first))
        scaled = grad_first * row8[3:4]
        grad_attn = inv1[...] * (
            scaled
            - jnp.mean(scaled, axis=-1, keepdims=True)
            - normed * jnp.mean(scaled * normed, axis=-1, keepdims=True)
        )
        ga[...] = grad_attn
        low = grad_attn.astype(BF)
        gal[...] = low
        keep(2, column(low))
        loaded_w(0)
        dctx[...] = right_dot(low, w_b[0]).astype(BF)

    def attention(h):
        cols = rows_of(h * 128, 128, 128)
        queries = two_heads(q[:, cols] * BF(HEAD_DIM**-0.5))
        keys = key[:, cols]
        probs = softmax_pair(queries, keys, bias[...])
        grads = two_heads(dctx[:, cols])
        grad_probs = right_dot(grads, val[:, cols])
        delta = jnp.sum(probs * grad_probs, axis=-1, keepdims=True)
        grad_scores = (probs * (grad_probs - delta)).astype(BF)
        dv[:, cols] = left_dot(probs.astype(BF), grads).astype(BF)
        dk[:, cols] = left_dot(grad_scores, queries).astype(BF)
        dq[:, cols] = (one_block(plain_dot(grad_scores, keys)) * HEAD_DIM**-0.5).astype(BF)

    def dx_core(g):
        return remote(gel.at[:, pl.ds(g * 1024, 1024)], dx_r.at[g], ds.at[g], dr.at[g], sib)

    dx_far = remote(dx_s, dx_y, ds.at[2], dr.at[2], xn)

    def input_rows(n):
        who = x * (n % 2) + (1 - x) * (1 - n % 2)
        core = (1 - k) * (1 - n // 2) + k * (n // 2)
        rows = rows_of(who * 512 + core * 256, 256)
        terms_here = right_dot(dk[rows], w_b[1]) + right_dot(dv[rows], w_b[2])

        @pl.when(n == 0)
        def _():
            gel[:, pl.ds(1024, 1024)] = terms_here.astype(BF)
            dx_core(1).start()

        @pl.when(n == 1)
        def _():
            gel[:, pl.ds(0, 1024)] = terms_here.astype(BF)
            dx_core(0).start()

        @pl.when(n == 2)
        def _():
            pltpu.make_async_copy(dx_r.at[1], dx_r.at[1], dr.at[1]).wait()
            dx_s[...] = (terms_here + dx_r[1].astype(F32)).astype(BF)
            dx_far.start()

        @pl.when(n == 3)
        def _():
            pltpu.make_async_copy(dx_r.at[0], dx_r.at[0], dr.at[0]).wait()
            loaded_w(3)
            ga[...] = ga[...] + terms_here + dx_r[0].astype(F32) + right_dot(dq[...], w_b[3])

    greet(z, x, y, k)
    start_blocks((0, 1))
    vec_copies[0].start()
    vec_copies[1].start()
    relay(0)
    relay(1)
    for block in range(2):
        arrive_block(block, (0, 1))
        group_start(0, block)
        group_start(1, block)
    pltpu.make_async_copy(vec_in, vec_in, f_recv.at[0]).wait()
    vec_copies[2].start()
    start_blocks((2,))
    relay(2)
    group_arrive(1, 0)
    group_start(2, 0)
    relay(3)
    group_arrive(1, 1)
    group_start(2, 1)
    load_item(0)
    fill_rows()
    for step in (0, 2):
        for block in range(2):
            group_arrive(step, block)
    fill_bias()
    relay(4)
    project_own(item(0))
    load_item(1)
    relay(5)
    project_all(item(1), key, 0.0)
    load_item(2)
    relay(6)
    project_all(item(2), val, row8[1:2])
    load_item(3)
    relay(7)
    heads(0, 3)
    relay(8)
    heads(3, 6)
    relay(9)
    heads(6, 8)
    relay(10)
    attention_out(item(3))
    load_item(4)
    for j in range(4):
        relay(11 + j)
        expand(j, item(4 + j))
        load_item(5 + j)
    relay(15)
    for j in range(1, 4):
        load_item(8 + j)
    for j in range(4):
        contract(j, item(8 + j))
    for slot in range(2):
        arrive_block(slot, (2,))
    for j in range(2):
        load_c(j)
        load_e(j)
    for n in range(4):
        load_w(n)
    second_norm()
    start_back(0)

    def tick(t, carry):
        def at(stage):
            i = t - LAG[stage]
            return i, (i >= 0) & (i < CHUNKS)

        stage_zero(t)
        @pl.when(t < 4)
        def _():
            def one(n, c):
                feed_forward(2 * t + n)
                return c

            lax.fori_loop(0, 2, one, 0)

        @pl.when(t == 4)
        def _():
            first_norm()

        @pl.when((t >= 5) & (t < 13))
        def _():
            attention(t - 5)

        @pl.when(t == 13)
        def _():
            keep(0, column(dq[...]))
            keep(1, column(dv[...]))
            loaded_w(1)
            loaded_w(2)

        @pl.when((t >= 13) & (t < 17))
        def _():
            input_rows(t - 13)

        for stage in range(6):

            @pl.when(t == 14 + 2 * stage)
            def _():
                v_step(stage)

        @pl.when(t == 18)
        def _():
            pltpu.make_async_copy(dx_y, dx_y, dr.at[2]).wait()
            dx_b[...] = (ga[...] + dx_y[...].astype(F32)).astype(BF)
            start_back(1)

        i1, live1 = at(1)

        @pl.when(live1)
        def _():
            slot, land = i1 % SLOTS, i1 % LAND_D
            clear(1, i1)
            landed(0, i1, r_d.at[i1 % LAND_D])
            for plane in range(2):
                b_y[slot, plane] = add(l_d[slot, plane], r_d[land, plane])
            launch(1, i1)

        i2, live2 = at(2)

        @pl.when(live2)
        def _():
            slot, land = i2 % SLOTS, i2 % LAND
            clear(2, i2)
            landed(1, i2, r_y.at[land])
            b_x[slot] = add(b_y[slot, y], r_y[land])
            launch(2, i2)

        i3, live3 = at(3)

        @pl.when(live3)
        def _():
            slot, land = i3 % SLOTS, i3 % LAND
            clear(3, i3)
            landed(2, i3, r_x.at[land])
            first = order(i3)[0][0]
            b_1[slot] = add(b_x[slot, rows_of(first * 64, 64)], r_x[land])
            launch(3, i3)

        i4, live4 = at(4)

        @pl.when(live4)
        def _():
            slot, land = i4 % SLOTS, i4 % LAND
            clear(4, i4)
            landed(3, i4, r_1.at[land])
            second = order(i4)[0][1]
            b_2[slot] = add(b_1[slot, rows_of(second * 32, 32)], r_1[land])
            launch(4, i4)

        i5, live5 = at(5)

        @pl.when(live5)
        def _():
            slot, land = i5 % SLOTS, i5 % LAND
            clear(5, i5)
            landed(4, i5, r_2.at[land])
            first, second, third = order(i5)[0]
            o_b[i5 % ROOM, rows_of(first * 64 + second * 32 + third * 16, 16)] = add(
                b_2[slot, rows_of(third * 16, 16)], r_2[land]
            )
            launch(5, i5)

        i6, live6 = at(6)

        @pl.when(live6)
        def _():
            clear(6, i6)
            first, second, third = order(i6)[0]
            row = first * 64 + second * 32 + (1 - third) * 16
            landed(5, i6, o_b.at[i6 % ROOM, rows_of(row, 16)])
            launch(6, i6)

        i7, live7 = at(7)

        @pl.when(live7)
        def _():
            clear(7, i7)
            first, second, _ = order(i7)[0]
            landed(6, i7, o_b.at[i7 % ROOM, rows_of(first * 64 + (1 - second) * 32, 32)])
            launch(7, i7)

        i8, live8 = at(8)

        @pl.when(live8)
        def _():
            first = order(i8)[0][0]
            landed(7, i8, o_b.at[i8 % ROOM, rows_of((1 - first) * 64, 64)])
            store(i8)

        return carry

    lax.fori_loop(0, CHUNKS + LAG[8], tick, 0)
    stored()
    for stage in range(8):
        for i in range(CHUNKS - SLOTS, CHUNKS):
            copies(stage, i).wait_send()
    for stage in range(5):
        v_copy(stage).wait_send()
    dx_core(0).wait_send()
    dx_core(1).wait_send()
    dx_far.wait_send()
    finish_back(0)
    finish_back(1)
    for i in range(n_items):
        for kind in range(8):
            if kind not in (3, 5) or split(i)[kind // 2]:
                send_copy(i, kind).wait_send()
    finish_blocks((0, 1, 2))
    for step in range(3):
        for block in range(2):
            for move in group_copy(step, block):
                move.wait_send()
    for move in vec_copies:
        move.wait_send()


def layer_call(inp, cot, seg, weights, vectors):
    vmem = pl.BlockSpec(memory_space=pltpu.VMEM)
    any_spec = pl.BlockSpec(memory_space=pl.ANY)
    dma = pltpu.SemaphoreType.DMA
    grad = jax.ShapeDtypeStruct((256, 1024), BF)
    square = jax.ShapeDtypeStruct((1024, 1024), BF)
    full_weights = [square] * 4 + [
        jax.ShapeDtypeStruct((1024, 4096), BF), jax.ShapeDtypeStruct((4096, 1024), BF)
    ]
    return pl.pallas_call(
        layer_kernel,
        out_shape=full_weights + [
            grad, grad, grad, grad,
            jax.ShapeDtypeStruct((256, 4096), BF),
            jax.ShapeDtypeStruct((1024, 1024), BF),
            jax.ShapeDtypeStruct((2, 1, 128, 1024), BF),
            jax.ShapeDtypeStruct((2, 1, 128, 1024), BF),
            jax.ShapeDtypeStruct((24, 128), F32),
        ],
        in_specs=[any_spec] * 9 + [vmem] * 9,
        out_specs=[any_spec] * 14 + [vmem],
        scratch_shapes=[
            pltpu.VMEM((SLOTS, 2, 128, 1024), BF),
            pltpu.VMEM((SLOTS, 2, 128, 1024), BF),
            pltpu.VMEM((LAND_D, 2, 128, 1024), BF),
            pltpu.VMEM((SLOTS, 2, 128, 1024), BF),
            pltpu.VMEM((LAND, 128, 1024), BF),
            pltpu.VMEM((SLOTS, 128, 1024), BF),
            pltpu.VMEM((LAND, 64, 1024), BF),
            pltpu.VMEM((SLOTS, 64, 1024), BF),
            pltpu.VMEM((LAND, 32, 1024), BF),
            pltpu.VMEM((SLOTS, 32, 1024), BF),
            pltpu.VMEM((LAND, 16, 1024), BF),
            pltpu.VMEM((ROOM, 128, 1024), BF),
            pltpu.VMEM((256, 4096), BF),
            pltpu.VMEM((256, 1024), F32),
            pltpu.VMEM((256, 1024), F32),
            pltpu.VMEM((256, 1024), BF),
            pltpu.VMEM((256, 1024), BF),
            pltpu.VMEM((256, 1024), BF),
            pltpu.VMEM((1024, 1024), BF),
            pltpu.VMEM((1024, 1024), BF),
            pltpu.VMEM((256, 1024), F32),
            pltpu.VMEM((2, 1024, 512), BF),
            pltpu.VMEM((2, 512, 1024), BF),
            pltpu.VMEM((4, 1024, 1024), BF),
            pltpu.VMEM((2, 256, 1024), BF),
            pltpu.VMEM((256, 1024), BF),
            pltpu.VMEM((4, 24, 128), F32),
            pltpu.VMEM((4, 2, 24, 128), F32),
            pltpu.VMEM((3, 2, 24, 128), F32),
            pltpu.VMEM((4, 24, 128), F32),
            pltpu.VMEM((256, 4096), BF),
            pltpu.VMEM((256, 1024), BF),
            pltpu.VMEM((256, 1024), BF),
            pltpu.VMEM((256, 4096), BF),
            pltpu.VMEM((256, 1024), F32),
            pltpu.VMEM((256, 1), F32),
            pltpu.VMEM((256, 1024), BF),
            pltpu.VMEM((256, 1024), BF),
            pltpu.VMEM((1024, 1024), BF),
            pltpu.VMEM((1024, 1024), BF),
            pltpu.VMEM((1024, 1024), BF),
            pltpu.VMEM((256, 1024), BF),
            pltpu.VMEM((8, 1, 128), jnp.int32),
            pltpu.VMEM((24, 128), F32),
            pltpu.VMEM((4, 24, 128), F32),
            pltpu.VMEM((8, 1024), F32),
            pltpu.VMEM((1, 4096), F32),
            dma((8, SLOTS)), dma((8, LAND)), dma((3,)), dma((3,)), dma((2, 2)), dma((2, 2)),
            dma((5,)), dma((5,)), dma((8,)), dma(()),
            dma((3, 2)), dma((3, 2)), dma((2, 3, 2)), dma((2, 3, 2)),
            dma((8, 12)), dma((8, 12)), dma((3,)), dma((3,)),
        ],
        compiler_params=pltpu.CompilerParams(
            collective_id=0, has_side_effects=True, vmem_limit_bytes=61 << 20
        ),
        name="layer",
    )(inp, cot, seg, *weights, *vectors)


def widen_kernel(*refs):
    ins, outs = refs[:9], refs[9:]
    for src, dst in zip(ins[:8], outs[:8]):
        dst[...] = src[...].astype(dst.dtype)
    vec, smalls = ins[8], outs[8:]

    @pl.when(pl.program_id(0) == 0)
    def _():
        for i in range(8):
            for half in range(2):
                smalls[i][pl.ds(half * 128, 128)] = vec[2 * i + half]
        for n in range(8):
            smalls[8][pl.ds(n * 128, 128)] = vec[16 + n]


def widen(narrow, vec):
    steps = 2
    in_specs, out_specs, shapes = [], [], []
    for n, v in enumerate(narrow):
        at = v.ndim - 2
        block = v.shape[:at] + (v.shape[at] // steps,) + v.shape[at + 1 :]

        def place(i, at=at, rank=v.ndim):
            return tuple(i if d == at else 0 for d in range(rank))

        in_specs.append(pl.BlockSpec(block, place))
        out_specs.append(pl.BlockSpec(block, place))
        shapes.append(jax.ShapeDtypeStruct(v.shape, BF if n == 7 else F32))
    in_specs.append(pl.BlockSpec((24, 128), lambda i: (0, 0)))
    for size in (256,) * 8 + (1024,):
        out_specs.append(pl.BlockSpec((size,), lambda i: (0,)))
        shapes.append(jax.ShapeDtypeStruct((size,), F32))
    return pl.pallas_call(
        widen_kernel,
        grid=(steps,),
        out_shape=shapes,
        in_specs=in_specs,
        out_specs=out_specs,
        compiler_params=pltpu.CompilerParams(vmem_limit_bytes=61 << 20),
        name="widen",
    )(*narrow, vec)


def per_group_device(
    layer_input, segments, cotangent,
    query_weight, key_weight, value_weight, output_weight, expand_weight, contract_weight,
    query_bias, value_bias, output_bias, first_gain, first_shift, expand_bias, contract_bias,
    second_gain, second_shift,
):
    outs = layer_call(
        layer_input, cotangent, segments,
        (query_weight, key_weight, value_weight, output_weight, expand_weight, contract_weight),
        (
            query_bias, value_bias, output_bias, first_gain, first_shift, contract_bias,
            second_gain, second_shift, expand_bias,
        ),
    )
    o_q, o_k, o_v, o_o, o_e, o_c, resf, dxf, vec = outs[6:]
    wide = widen((o_q, o_k, o_v, o_o, o_e, o_c, dxf, resf), vec)
    g_q, g_k, g_v, g_o, g_e, g_c, input_grad, layer_output = wide[:8]
    b_q, b_v, b_o, g_one, s_one, b_c, g_two, s_two, b_e = wide[8:]
    return (
        layer_output, input_grad, g_q, g_k, g_v, g_o, g_e, g_c,
        b_q, b_v, b_o, g_one, s_one, b_e, b_c, g_two, s_two,
    )


def solution(mesh):
    in_specs = (
        P(None, "fsdp", "ctx", None),
        P(None, "fsdp", "ctx"),
        P(None, "fsdp", "ctx", None),
        P("fsdp", None),
        P("fsdp", None),
        P("fsdp", None),
        P("fsdp", None),
        P("fsdp", None),
        P("fsdp", None),
        P("fsdp"),
        P("fsdp"),
        P("fsdp"),
        P("fsdp"),
        P("fsdp"),
        P("fsdp"),
        P("fsdp"),
        P("fsdp"),
        P("fsdp"),
    )
    out_specs = (
        P(None, "fsdp", "ctx", None),
        P(None, "fsdp", "ctx", None),
        P("fsdp", None),
        P("fsdp", None),
        P("fsdp", None),
        P("fsdp", None),
        P("fsdp", None),
        P("fsdp", None),
        P("fsdp"),
        P("fsdp"),
        P("fsdp"),
        P("fsdp"),
        P("fsdp"),
        P("fsdp"),
        P("fsdp"),
        P("fsdp"),
        P("fsdp"),
    )
    def whole(layer_input, segments, *rest):
        grouped = (
            dict(mesh.shape) == {"ctx": 8, "fsdp": 4}
            and layer_input.shape == (2, 4, 1024, 1024)
            and rest[5].shape == (1024, 4096)
        )
        body = per_group_device if grouped else per_device
        return jax.shard_map(
            body, mesh=mesh, in_specs=in_specs, out_specs=out_specs, check_vma=False
        )(layer_input, segments, *rest)

    return whole
```
